32 devices in a mesh: wide: 16 (over z, x, core), narrow: 2 (over y).
Axes of the slice: x: 2, y: 2, z: 4, core: 2. Of those that a mesh axis runs over, the one named last changes fastest.
Arguments:
- frames: bfloat16 [4096, 1024], P(('wide', 'narrow')), may hold values from -13 to 13
- lengths: int32 [32, 4], P(('wide', 'narrow')), may hold values from 1 to 96, 128 in all within a row
- out_grad: bfloat16 [4096, 1024], P(('wide', 'narrow')), may hold values from -6 to 6
- up_weight: float32 [2, 1024, 4096], P(None, ('wide', 'narrow')), may hold values from -0.1875 to 0.1875
- down_weight: float32 [2, 4096, 1024], P(None, ('wide', 'narrow')), may hold values from -0.09375 to 0.09375
- square_weight: float32 [8, 1024, 1024], P(None, ('wide', 'narrow')), may hold values from -0.75 to 0.75
- chan_weight: float32 [45, 1024], P(None, ('wide', 'narrow')), may hold values from -1.2 to 1.3
- up_moment: float32 [2, 1024, 4096], P(None, ('wide', 'narrow')), may hold values from -80 to 80
- down_moment: float32 [2, 4096, 1024], P(None, ('wide', 'narrow')), may hold values from -80 to 80
- square_moment: float32 [8, 1024, 1024], P(None, ('wide', 'narrow')), may hold values from -80 to 80
- chan_moment: float32 [45, 1024], P(None, ('wide', 'narrow')), may hold values from -80 to 80
- up_average: float32 [2, 1024, 4096], P(None, ('wide', 'narrow')), may hold values from -0.1875 to 0.1875
- down_average: float32 [2, 4096, 1024], P(None, ('wide', 'narrow')), may hold values from -0.09375 to 0.09375
- square_average: float32 [8, 1024, 1024], P(None, ('wide', 'narrow')), may hold values from -0.1875 to 0.1875
- chan_average: float32 [45, 1024], P(None, ('wide', 'narrow')), may hold values from -3 to 3
Outputs:
- output: bfloat16 [4096, 1024], P(('wide', 'narrow'))
- frames_grad: bfloat16 [4096, 1024], P(('wide', 'narrow'))
- up_grad: float32 [2, 1024, 4096], P(None, ('wide', 'narrow'))
- down_grad: float32 [2, 4096, 1024], P(None, ('wide', 'narrow'))
- square_grad: float32 [8, 1024, 1024], P(None, ('wide', 'narrow'))
- chan_grad: float32 [45, 1024], P(None, ('wide', 'narrow'))
- up_moment_new: float32 [2, 1024, 4096], P(None, ('wide', 'narrow'))
- down_moment_new: float32 [2, 4096, 1024], P(None, ('wide', 'narrow'))
- square_moment_new: float32 [8, 1024, 1024], P(None, ('wide', 'narrow'))
- chan_moment_new: float32 [45, 1024], P(None, ('wide', 'narrow'))
- up_weight_new: float32 [2, 1024, 4096], P(None, ('wide', 'narrow'))
- down_weight_new: float32 [2, 4096, 1024], P(None, ('wide', 'narrow'))
- square_weight_new: float32 [8, 1024, 1024], P(None, ('wide', 'narrow'))
- chan_weight_new: float32 [45, 1024], P(None, ('wide', 'narrow'))
- up_average_new: float32 [2, 1024, 4096], P(None, ('wide', 'narrow'))
- down_average_new: float32 [2, 4096, 1024], P(None, ('wide', 'narrow'))
- square_average_new: float32 [8, 1024, 1024], P(None, ('wide', 'narrow'))
- chan_average_new: float32 [45, 1024], P(None, ('wide', 'narrow'))
- bias_grad: float32 [2, 1024], P(None, ('wide', 'narrow'))
The draws below stay inside these ranges and needn't reach their ends.
Inputs may be any that keep to these rules, and one draw needn't show every extreme that they name: `lengths`: each row sums to 128; its largest entry is 96.
All inputs are finite; a program needn't handle non-finite values.
Results may differ from the reference program's by a relative error of at most 0.018.
Values may be sent and summed in bfloat16 or wider, within the bound.
No kernel may reach another device: no remote copies, remote signals or barrier semaphores. Data moves between devices by JAX's collectives and lax.ppermute only.
A program may use at most 256 MiB of HBM per device.

```python
import math
from functools import partial
import jax
import jax.numpy as jnp
import numpy as np
from jax import lax

D = 1024
HEADS = 16
HEAD_DIM = 64
FF = 4096
KERNEL = 31
TOK_DEV = 128
ITEMS = 3
ITEM_MOST = 96
CHAN_ROWS = 45
TOKENS = 4096
DEVICES = 32


def draw_frames(key, part):
    keys = jax.random.split(key, 2)
    bucket_count = TOKENS // TOK_DEV
    place = (jnp.arange(TOKENS, dtype=jnp.int32) // TOK_DEV).astype(jnp.float32) / max(bucket_count - 1, 1)
    noise = jax.random.truncated_normal(keys[0], -4.0, 4.0, (TOKENS, D), jnp.float32)
    strength = 0.5 + 2.5 * place
    direction = jax.random.truncated_normal(keys[1], -3.0, 3.0, (D,), jnp.float32)
    return (noise + strength[:, None] * direction[None, :]).astype(jnp.bfloat16)


def draw_square_weight(key, part):
    base = jax.random.truncated_normal(key, -4.0, 4.0, (8, D, D), jnp.float32)
    boost = jnp.where(jnp.arange(8) == 3, 6.0, 1.0).astype(jnp.float32)
    return base * D ** (-0.5) * boost[:, None, None]


def draw_chan_weight(key, part):
    keys = jax.random.split(key, 6)
    taps = 0.3 * jax.random.truncated_normal(keys[0], -4.0, 4.0, (KERNEL, D), jnp.float32)
    shifts = 0.1 * jax.random.truncated_normal(keys[2], -4.0, 4.0, (5, D), jnp.float32)
    biases = 0.3 * jax.random.truncated_normal(keys[5], -4.0, 4.0, (2, D), jnp.float32)
    gains = jax.random.uniform(keys[1], (5, D), jnp.float32, 0.7, 1.3)
    batch_gain = jax.random.uniform(keys[3], (1, D), jnp.float32, 0.7, 1.3)
    batch_shift = 0.1 * jax.random.truncated_normal(keys[4], -4.0, 4.0, (1, D), jnp.float32)
    return jnp.concatenate([taps, gains, shifts, batch_gain, batch_shift, biases], axis=0)


def levels(rng, extent, cuts, least, high):
    gain, own = 1.0, jax.random.fold_in(rng, 6)
    for axis_at, blocks in cuts:
        heights = jnp.exp(jax.random.uniform(jax.random.fold_in(own, axis_at), (blocks,), jnp.float32, least / len(cuts), high / len(cuts)))
        gain = gain * jnp.repeat(heights, extent[axis_at] // blocks).reshape([-1 if axis == axis_at else 1 for axis in range(len(extent))])
    return gain


def split_up(amount, total, limit, lean):
    portions = [(1 << 20) // math.isqrt(rank ** lean) + 1 for rank in range(2, amount + 1)]
    spare, holding = total - limit - (amount - 1), [1] * (amount - 1)
    while spare > 0:
        free = [i for i in range(amount - 1) if holding[i] < limit]
        mass, left = sum([portions[i] for i in free]), spare
        for i in free:
            more = min(limit - holding[i], max(1, left * portions[i] // mass), spare)
            holding[i] = holding[i] + more
            spare = spare - more
    return np.array([limit] + holding)


def uneven(own_key, number_of, total, limit, skew):
    if number_of == 2:
        one = jax.random.randint(own_key, (), max(1, total - limit), min(limit, total - 1) + 1)
        return jnp.stack([one, total - one])
    tallies = jnp.asarray(split_up(number_of, total, limit, skew), jnp.int32)
    twos = (number_of - 1) // 2
    donor, taker = tallies[1:1 + 2 * twos:2], tallies[2:2 + 2 * twos:2]
    margin = jnp.minimum(donor - 1, limit - taker)
    passed = jax.random.randint(jax.random.fold_in(own_key, 1), (twos,), 0, 1 << 20) % (margin + 1)
    tallies = tallies.at[1:1 + 2 * twos:2].set(donor - passed).at[2:2 + 2 * twos:2].set(taker + passed)
    return tallies[jax.random.permutation(jax.random.fold_in(own_key, 2), number_of)]


def gaussian(own_key, shape, scale, most, cuts=(), kind=jnp.bfloat16):
    values = jax.random.normal(own_key, shape, jnp.float32) * scale
    if len(cuts) > 0:
        values = levels(own_key, shape, cuts, -0.22, 0.18) * values
    return jnp.clip(values, min=-most, max=most).astype(kind)


def setup_inputs(seed: int = 0) -> dict:
    splits = jax.random.split(jax.random.key(seed), 16)
    frames = draw_frames(jax.random.fold_in(splits[15], 71), 0)
    lengths = jax.vmap(lambda own: uneven(own, ITEMS + 1, TOK_DEV, ITEM_MOST, 2))(jax.random.split(splits[1], DEVICES)).reshape((DEVICES, ITEMS + 1)).astype(jnp.int32)
    out_grad = gaussian(splits[2], (TOKENS, D), 1.0, 6.0, ((0, 32),))
    up_weight = gaussian(splits[3], (2, D, FF), D ** -0.5, 0.1875, ((1, 32),), jnp.float32)
    down_weight = gaussian(splits[4], (2, FF, D), FF ** -0.5, 0.09375, ((1, 32),), jnp.float32)
    square_weight = draw_square_weight(jax.random.fold_in(splits[15], 71), 0)
    chan_weight = draw_chan_weight(jax.random.fold_in(splits[15], 71), 0)
    up_moment = gaussian(splits[7], (2, D, FF), (0.2 * TOKENS ** 0.5), 80.0, ((1, 32),), jnp.float32)
    down_moment = gaussian(splits[8], (2, FF, D), (0.2 * TOKENS ** 0.5), 80.0, ((1, 32),), jnp.float32)
    square_moment = gaussian(splits[9], (8, D, D), (0.2 * TOKENS ** 0.5), 80.0, ((1, 32),), jnp.float32)
    chan_moment = gaussian(splits[10], (CHAN_ROWS, D), (0.2 * TOKENS ** 0.5), 80.0, ((1, 32),), jnp.float32)
    up_average = gaussian(splits[11], (2, D, FF), D ** -0.5, 0.1875, ((1, 32),), jnp.float32)
    down_average = gaussian(splits[12], (2, FF, D), FF ** -0.5, 0.09375, ((1, 32),), jnp.float32)
    square_average = gaussian(splits[13], (8, D, D), D ** -0.5, 0.1875, ((1, 32),), jnp.float32)
    chan_average = gaussian(splits[14], (CHAN_ROWS, D), 0.5, 3.0, ((1, 32),), jnp.float32)
    return {"frames": frames, "lengths": lengths, "out_grad": out_grad, "up_weight": up_weight, "down_weight": down_weight, "square_weight": square_weight, "chan_weight": chan_weight, "up_moment": up_moment, "down_moment": down_moment, "square_moment": square_moment, "chan_moment": chan_moment, "up_average": up_average, "down_average": down_average, "square_average": square_average, "chan_average": chan_average}


@jax.custom_vjp
def low(v):
    return lax.optimization_barrier(v.astype(jnp.bfloat16)).astype(jnp.float32)

@jax.custom_vjp
def low_back(v):
    return v

def low_keep(v):
    return (low(v), None)

def low_pass(kept, grad):
    return (grad,)

def back_keep(v):
    return (v, None)

def back_low(kept, grad):
    return (low(grad),)
low.defvjp(low_keep, low_pass)
low_back.defvjp(back_keep, back_low)
EPSILON = 1e-05
MOMENTUM_DECAY = 0.9
AVERAGE_DECAY = 0.9
RATE_UP = 0.05
RATE_DOWN = 0.026
RATE_SQUARE = 0.05
RATE_CHANNEL = 0.5
MASKED_SCORE = -1e+30
FULL_PRECISION = lax.Precision.HIGHEST

def matmul(left, right):
    return jnp.dot(left, right, precision=FULL_PRECISION, preferred_element_type=jnp.float32)

def swish_unit(values):
    return values * jax.nn.sigmoid(values)

def layer_norm(values, gain_row, shift_row):
    centre = values - lax.optimization_barrier(jnp.mean(values, axis=-1, keepdims=True))
    spread = lax.optimization_barrier(jnp.mean(centre * centre, axis=-1, keepdims=True))
    return centre * lax.rsqrt(spread + EPSILON) * gain_row + shift_row

def item_segments(length_row, slot_count, item_count):
    bounds = jnp.cumsum(length_row[:item_count], dtype=jnp.int32)
    where_at = jnp.arange(slot_count, dtype=jnp.int32)
    return lax.optimization_barrier(jnp.sum((where_at[:, None] >= bounds[None, :]).astype(jnp.int32), axis=1, dtype=jnp.int32))

def offset_table(slot_count, model_width):
    offsets = jnp.arange(2 * slot_count - 1, dtype=jnp.float32) - (slot_count - 1)
    freqs = jnp.exp(-jnp.log(10000.0) * jnp.arange(0, model_width, 2, dtype=jnp.float32) / model_width)
    angles = offsets[:, None] * freqs[None, :]
    return jnp.concatenate([jnp.sin(angles), jnp.cos(angles)], axis=1)

def shift_relative_scores(unshifted_position_scores):
    slot_count = unshifted_position_scores.shape[-2]
    leading = unshifted_position_scores.shape[:-2]
    padded = jnp.pad(unshifted_position_scores, [(0, 0)] * len(leading) + [(0, 0), (0, 1)])
    flat_rows = padded.reshape(leading + (2 * slot_count * slot_count,))
    flat_rows = flat_rows[..., slot_count - 1:slot_count - 1 + slot_count * (2 * slot_count - 1)]
    return flat_rows.reshape(leading + (slot_count, 2 * slot_count - 1))[..., :slot_count]

def depth_conv(glu_rows, tap_rows, segment):
    slot_count = glu_rows.shape[0]
    half_width = tap_rows.shape[0] // 2
    padded = jnp.pad(glu_rows, ((half_width, half_width), (0, 0)))
    segment_pad = jnp.pad(segment, (half_width, half_width), constant_values=-1)
    total = jnp.zeros_like(glu_rows)
    for tap_index in range(tap_rows.shape[0]):
        nearby = lax.slice_in_dim(padded, tap_index, tap_index + slot_count, axis=0)
        match = lax.slice_in_dim(segment_pad, tap_index, tap_index + slot_count, axis=0) == segment
        total = total + jnp.where(match[:, None], nearby, 0.0) * tap_rows[tap_index]
    return total

def section_front(stream_zero, segment, up_low, down_low, square_low, chan_low):
    valid = (segment < ITEMS).astype(jnp.float32)[:, None]
    normed_one = low(layer_norm(stream_zero, chan_low[KERNEL], chan_low[KERNEL + 5]))
    before_one = low_back(matmul(normed_one, up_low[0]))
    branch_one = low_back(matmul(low(swish_unit(before_one)), down_low[0]))
    stream_one = stream_zero + 0.5 * branch_one
    normed_two = low(layer_norm(stream_one, chan_low[KERNEL + 1], chan_low[KERNEL + 6]))
    query_rows = low_back(matmul(normed_two, square_low[0]))
    key_rows = low(low_back(matmul(normed_two, square_low[1]))).reshape(TOK_DEV, HEADS, HEAD_DIM)
    value_rows = low(low_back(matmul(normed_two, square_low[2]))).reshape(TOK_DEV, HEADS, HEAD_DIM)
    place_table = low(offset_table(TOK_DEV, D))
    position_embed_rows = low(low_back(matmul(place_table, square_low[4]))).reshape(2 * TOK_DEV - 1, HEADS, HEAD_DIM)
    query_c = low(query_rows + chan_low[KERNEL + 12]).reshape(TOK_DEV, HEADS, HEAD_DIM)
    query_position_side = low(query_rows + chan_low[KERNEL + 13]).reshape(TOK_DEV, HEADS, HEAD_DIM)
    content = jnp.einsum('thd,shd->hts', query_c, key_rows, precision=FULL_PRECISION)
    relative_position = shift_relative_scores(jnp.einsum('yia,xia->iyx', query_position_side, position_embed_rows, precision=FULL_PRECISION))
    scores = low_back((content + relative_position) * HEAD_DIM ** (-0.5))
    same_item = segment[:, None] == segment[None, :]
    scores = jnp.where(same_item[None], scores, MASKED_SCORE)
    soft_weights = low(jax.nn.softmax(scores, axis=-1))
    mixed_rows = low_back(jnp.einsum('hts,shd->thd', soft_weights, value_rows, precision=FULL_PRECISION).reshape(TOK_DEV, D))
    stream_two = stream_one + low_back(matmul(low(mixed_rows), square_low[3]))
    normed_three = low(layer_norm(stream_two, chan_low[KERNEL + 2], chan_low[KERNEL + 7]))
    gate_first = low_back(matmul(normed_three, square_low[5]))
    gate_second = low_back(matmul(normed_three, square_low[6]))
    glu_rows = gate_first * jax.nn.sigmoid(gate_second) * valid
    return (stream_two, depth_conv(glu_rows, chan_low[:KERNEL], segment))

def section_back(stream_two, conv_rows, segment, mean_rows, spread_inv, up_low, down_low, square_low, chan_low):
    valid = (segment < ITEMS).astype(jnp.float32)[:, None]
    batch_normed = (conv_rows - mean_rows) * spread_inv * chan_low[KERNEL + 10] + chan_low[KERNEL + 11]
    stream_three = stream_two + low_back(matmul(low(swish_unit(batch_normed)), square_low[7]))
    normed_four = low(layer_norm(stream_three, chan_low[KERNEL + 3], chan_low[KERNEL + 8]))
    before_four = low_back(matmul(normed_four, up_low[1]))
    branch_four = low_back(matmul(low(swish_unit(before_four)), down_low[1]))
    stream_four = stream_three + 0.5 * branch_four
    return layer_norm(stream_four, chan_low[KERNEL + 4], chan_low[KERNEL + 9]) * valid

def nesterov(weight, moment, average, grad_rows, rate, rate_scale):
    moment_new = MOMENTUM_DECAY * moment + grad_rows
    weight_new = weight - rate * rate_scale * (grad_rows + MOMENTUM_DECAY * moment_new)
    average_new = AVERAGE_DECAY * average + (1.0 - AVERAGE_DECAY) * weight_new
    return (moment_new, weight_new, average_new)

def reference(frames, lengths, out_grad, up_weight, down_weight, square_weight, chan_weight, up_moment, down_moment, square_moment, chan_moment, up_average, down_average, square_average, chan_average):
    segment = jax.vmap(partial(item_segments, slot_count=TOK_DEV, item_count=ITEMS))(lengths)
    valid = (segment < ITEMS).astype(jnp.float32)
    frame_count = jnp.sum(valid)

    def forward(frames_float, up_float, down_float, square_float, chan_float):
        up_low = low(up_float)
        down_low = low(down_float)
        square_low = low(square_float)
        chan_low = low(chan_float)
        buckets = frames_float.reshape(DEVICES, TOK_DEV, D)

        def front(inputs):
            return section_front(inputs[0], inputs[1], up_low, down_low, square_low, chan_low)
        stream_two, conv_rows = lax.map(jax.checkpoint(front), (buckets, segment))
        valid_rows = valid[..., None]
        mean_rows = lax.optimization_barrier(jnp.sum(conv_rows * valid_rows, axis=(0, 1))) / frame_count
        centred = (conv_rows - mean_rows) * valid_rows
        variance = lax.optimization_barrier(jnp.sum(centred * centred, axis=(0, 1))) / frame_count
        spread_inv = lax.rsqrt(variance + EPSILON)

        def back(inputs):
            return section_back(inputs[0], inputs[1], inputs[2], mean_rows, spread_inv, up_low, down_low, square_low, chan_low)
        final_rows = lax.map(jax.checkpoint(back), (stream_two, conv_rows, segment))
        return final_rows.reshape(TOKENS, D)
    output, pull = jax.vjp(forward, frames.astype(jnp.float32), up_weight, down_weight, square_weight, chan_weight)
    frames_grad, up_grad, down_grad, square_grad, chan_grad = pull(out_grad.astype(jnp.float32))
    rate_scale = lax.rsqrt(frame_count)
    up_new = nesterov(up_weight, up_moment, up_average, up_grad, RATE_UP, rate_scale)
    down_new = nesterov(down_weight, down_moment, down_average, down_grad, RATE_DOWN, rate_scale)
    square_new = nesterov(square_weight, square_moment, square_average, square_grad, RATE_SQUARE, rate_scale)
    chan_new = nesterov(chan_weight, chan_moment, chan_average, chan_grad, RATE_CHANNEL, rate_scale)
    bias_grad = chan_grad[KERNEL + 12:KERNEL + 14]
    return (output.astype(jnp.bfloat16), frames_grad.astype(jnp.bfloat16), up_grad, down_grad, square_grad, chan_grad, up_new[0], down_new[0], square_new[0], chan_new[0], up_new[1], down_new[1], square_new[1], chan_new[1], up_new[2], down_new[2], square_new[2], chan_new[2], bias_grad)
```

```python
import jax
import jax.numpy as jnp
from jax import lax
from jax.sharding import Mesh
from jax.sharding import PartitionSpec as P

HEADS = 16
EPSILON = 1e-05
MOMENTUM_DECAY = 0.9
AVERAGE_DECAY = 0.9
RATE_UP = 0.05
RATE_DOWN = 0.026
RATE_SQUARE = 0.05
RATE_CHANNEL = 0.5
MASKED_SCORE = -1e30
BF16 = jnp.bfloat16
F32 = jnp.float32
ALL = ("z", "x", "c", "y")


def mm(left, right):
    return jnp.dot(left, right, preferred_element_type=F32)


def mm_tn(left, right):
    return lax.dot_general(left, right, (((0,), (0,)), ((), ())), preferred_element_type=F32)


def mm_nt(left, right):
    return lax.dot_general(left, right, (((1,), (1,)), ((), ())), preferred_element_type=F32)


def swap(values, axis, bit=1):
    size = lax.axis_size(axis)
    return lax.ppermute(values, axis, [(i, i ^ bit) for i in range(size)])


def swish_grad(values):
    sig = jax.nn.sigmoid(values)
    return sig * (1.0 + values * (1.0 - sig))


def normalize(values):
    centre = values - jnp.mean(values, axis=-1, keepdims=True)
    scale = lax.rsqrt(jnp.mean(centre * centre, axis=-1, keepdims=True) + EPSILON)
    return centre * scale, scale


def layer_norm(values, gain_row, shift_row):
    return normalize(values)[0] * gain_row + shift_row


def layer_norm_back(values, gain_row, grad):
    unit, scale = normalize(values)
    grad_unit = grad * gain_row
    inner = jnp.mean(grad_unit, axis=-1, keepdims=True)
    cross = jnp.mean(grad_unit * unit, axis=-1, keepdims=True)
    grad_in = scale * (grad_unit - inner - unit * cross)
    return grad_in, jnp.sum(grad * unit, axis=0), jnp.sum(grad, axis=0)


def team_gather(values, wide_team):
    half = values.shape[0] // 2
    from_x = swap(values, "x")
    from_c = swap(values, "c")
    if not wide_team:
        return [jnp.concatenate([values, from_c]), jnp.concatenate([from_x, swap(from_x, "c")])]
    from_y = swap(values, "y")
    far = jnp.concatenate([swap(from_x[:half], "y"), swap(from_y[half:], "x")])
    return [
        jnp.concatenate([values, from_c]),
        jnp.concatenate([from_x, swap(from_x, "c")]),
        jnp.concatenate([from_y, swap(from_y, "c")]),
        jnp.concatenate([far, swap(far, "c")]),
    ]


def team_gather_small(values, wide_team):
    near = [values, swap(values, "c")]
    across = swap(jnp.stack(near), "x")
    rows = near + [across[0], across[1]]
    if wide_team:
        side = swap(jnp.stack(rows), "y")
        rows = rows + [side[i] for i in range(4)]
    return rows


def team_scatter(pairs, wide_team):
    slots = pairs[0].shape[0] // 2
    half = slots // 2

    def chip_sum(pair):
        return pair[:slots] + swap(pair[slots:].astype(BF16), "c").astype(F32)

    if not wide_team:
        across = swap(chip_sum(pairs[1]).astype(BF16), "x")
        return chip_sum(pairs[0]) + across.astype(F32)
    far = chip_sum(pairs[3]).astype(BF16)
    far_x = swap(far[:half], "x").astype(F32)
    far_y = swap(far[half:], "y").astype(F32)
    to_y = chip_sum(pairs[2])
    to_x = chip_sum(pairs[1])
    to_y = jnp.concatenate([to_y[:half] + far_x, to_y[half:]]).astype(BF16)
    to_x = jnp.concatenate([to_x[:half], to_x[half:] + far_y]).astype(BF16)
    from_x, from_y = swap(to_x, "x"), swap(to_y, "y")
    return chip_sum(pairs[0]) + from_x.astype(F32) + from_y.astype(F32)


def item_segments(length_rows, slot_count):
    item_count = length_rows.shape[1] - 1
    bounds = jnp.cumsum(length_rows[:, :item_count], axis=1, dtype=jnp.int32)
    where_at = jnp.arange(slot_count, dtype=jnp.int32)
    return jnp.sum(
        (where_at[None, :, None] >= bounds[:, None, :]).astype(jnp.int32), axis=2, dtype=jnp.int32
    )


def offset_table(slot_count, model_width):
    offsets = jnp.arange(2 * slot_count - 1, dtype=F32) - (slot_count - 1)
    freqs = jnp.exp(-jnp.log(10000.0) * jnp.arange(0, model_width, 2, dtype=F32) / model_width)
    angles = offsets[:, None] * freqs[None, :]
    return jnp.concatenate([jnp.sin(angles), jnp.cos(angles)], axis=1)


def shift_scores(wide_scores):
    slots = wide_scores.shape[-2]
    lead = wide_scores.shape[:-2]
    padded = jnp.pad(wide_scores, [(0, 0)] * len(lead) + [(0, 0), (0, 1)])
    flat = padded.reshape(lead + (2 * slots * slots,))
    flat = flat[..., slots - 1 : slots - 1 + slots * (2 * slots - 1)]
    return flat.reshape(lead + (slots, 2 * slots - 1))[..., :slots]


def depth_conv(rows, taps, segment, flip):
    slots = rows.shape[1]
    tap_count = taps.shape[0]
    reach = tap_count // 2
    padded = jnp.pad(rows, ((0, 0), (reach, reach), (0, 0)))
    segment_pad = jnp.pad(segment, ((0, 0), (reach, reach)), constant_values=-1)
    total = jnp.zeros_like(rows)
    for k in range(tap_count):
        near = lax.slice_in_dim(padded, k, k + slots, axis=1)
        match = lax.slice_in_dim(segment_pad, k, k + slots, axis=1) == segment
        tap = taps[tap_count - 1 - k] if flip else taps[k]
        total = total + jnp.where(match[:, :, None], near, 0.0) * tap
    return total


def tap_grads(rows, grad, tap_count, segment):
    slots = rows.shape[1]
    reach = tap_count // 2
    padded = jnp.pad(rows, ((0, 0), (reach, reach), (0, 0)))
    segment_pad = jnp.pad(segment, ((0, 0), (reach, reach)), constant_values=-1)
    terms = []
    for k in range(tap_count):
        near = lax.slice_in_dim(padded, k, k + slots, axis=1)
        match = lax.slice_in_dim(segment_pad, k, k + slots, axis=1) == segment
        terms.append(jnp.sum(jnp.where(match[:, :, None], near, 0.0) * grad, axis=(0, 1)))
    return jnp.stack(terms)


def nesterov(weight, moment, average, grad_rows, rate, rate_scale):
    moment_new = MOMENTUM_DECAY * moment + grad_rows
    weight_new = weight - rate * rate_scale * (grad_rows + MOMENTUM_DECAY * moment_new)
    average_new = AVERAGE_DECAY * average + (1.0 - AVERAGE_DECAY) * weight_new
    return (moment_new, weight_new, average_new)


def make_step(planes, sides):
    wide_team = sides == 2
    team_axes = ("x", "c", "y") if wide_team else ("x", "c")
    team = 8 if wide_team else 4
    outer_bits = [("z", 1 << i) for i in range((planes - 1).bit_length())]
    if not wide_team:
        outer_bits += [("y", 1 << i) for i in range((sides - 1).bit_length())]
    head_aligned = wide_team and planes * 4 == HEADS

    def side_rows(rows):
        return rows if wide_team else lax.all_gather(rows, "y", axis=0, tiled=True)

    def side_scatter(rows):
        if wide_team:
            return rows
        return lax.psum_scatter(rows, "y", scatter_dimension=0, tiled=True)

    def split_hidden(rows):
        r, f = rows.shape
        return rows.reshape(r, planes, team, f // (planes * team)).transpose(2, 0, 1, 3).reshape(
            team, r, f // team
        )

    def join_hidden(blocks):
        _, r, f = blocks.shape
        return blocks.reshape(team, r, planes, f // planes).transpose(1, 2, 0, 3).reshape(
            r, team * f
        )

    def split_heads(rows):
        r, d = rows.shape
        if not head_aligned:
            return rows.reshape(r, team, d // team).transpose(1, 0, 2)
        size = d // HEADS
        rows = rows.reshape(r, sides, planes // sides, 2, 2, size)
        return rows.transpose(3, 4, 1, 0, 2, 5).reshape(team, r, d // team)

    def join_heads(blocks):
        _, r, f = blocks.shape
        if not head_aligned:
            return blocks.transpose(1, 0, 2).reshape(r, team * f)
        size = team * f // HEADS
        blocks = blocks.reshape(2, 2, sides, r, planes // sides, size)
        return blocks.transpose(3, 2, 4, 0, 1, 5).reshape(r, team * f)

    def team_swap(blocks):
        return lax.all_to_all(blocks, team_axes, split_axis=0, concat_axis=0, tiled=True)

    def plane_gather(rows):
        return lax.all_gather(rows, "z", axis=0, tiled=False)

    def plane_scatter(rows):
        return lax.psum_scatter(rows, "z", scatter_dimension=0, tiled=False)

    def outer_sum(values):
        for axis, bit in outer_bits:
            values = values + swap(values, axis, bit)
        return values

    def outer_moments(count, mean, spread):
        for axis, bit in outer_bits:
            packed = jnp.stack([count, mean, spread])
            other = swap(packed, axis, bit)
            total = count + other[0]
            gap = other[1] - mean
            spread = spread + other[2] + gap * gap * (count * other[0] / total)
            mean = (count * mean + other[0] * other[1]) / total
            count = total
        return count, mean, spread

    def step(
        frames,
        lengths,
        out_grad,
        up_weight,
        down_weight,
        square_weight,
        chan_weight,
        up_moment,
        down_moment,
        square_moment,
        chan_moment,
        up_average,
        down_average,
        square_average,
        chan_average,
    ):
        slots, width = frames.shape
        head_size = width // HEADS
        team_heads = HEADS // team
        score_scale = head_size ** (-0.5)
        item_count = lengths.shape[1] - 1
        chan_rows = chan_weight.shape[0]
        tap_count = chan_rows - 14
        hidden = up_weight.shape[2]
        team_hidden = hidden // team
        team_width = width // team
        buckets = team
        x_at, c_at, y_at = lax.axis_index("x"), lax.axis_index("c"), lax.axis_index("y")
        team_at = (x_at * 2 + c_at) * 2 + y_at if wide_team else x_at * 2 + c_at

        up_low = up_weight.astype(BF16)
        down_low = down_weight.astype(BF16)
        square_low = square_weight.astype(BF16)
        chan_low = chan_weight.astype(BF16)

        chan_side = chan_low if wide_team else lax.all_gather(chan_low, "y", axis=0)
        chan_flat = chan_side.reshape(-1)
        chan_size = chan_flat.shape[0]
        chan_lines = -(-chan_size // team_hidden)
        chan_flat = jnp.pad(chan_flat, (0, chan_lines * team_hidden - chan_size))
        chan_block = jnp.broadcast_to(
            chan_flat.reshape(1, chan_lines, team_hidden), (team, chan_lines, team_hidden)
        )
        first_up = split_hidden(side_rows(up_low[0]))
        rows_in = first_up.shape[1]
        first = team_swap(jnp.concatenate([first_up, chan_block], axis=1))
        first = jnp.concatenate(
            [
                first[:, :rows_in].reshape(team * rows_in, team_hidden),
                first[:, rows_in:].reshape(team * chan_lines, team_hidden),
            ]
        )
        first = plane_gather(first)
        up_one = first[:, : team * rows_in].reshape(width, team_hidden)
        chan_all = first[:, team * rows_in :].reshape(planes, team, chan_lines * team_hidden)
        chan_all = chan_all[:, :, :chan_size].reshape(
            planes, team, 1 if wide_team else sides, chan_rows, chan_weight.shape[1]
        )
        chan_float = chan_all.transpose(3, 0, 1, 2, 4).reshape(chan_rows, width).astype(F32)

        down_rows = side_rows(down_low[0]).shape[0]
        mix_low, conv_out_low = square_low[3], side_rows(square_low[7])
        conv_rows_in = conv_out_low.shape[0]
        if head_aligned:
            mix_side = lax.all_gather(mix_low, "y", axis=0, tiled=True)
            head_rows = mix_side.shape[0]
            second = plane_gather(jnp.concatenate([side_rows(down_low[0]), mix_side, conv_out_low]))
            mix_all = second[:, down_rows : down_rows + head_rows]
            per_side = planes // sides
            mix_full = lax.dynamic_slice_in_dim(mix_all, y_at * per_side, per_side, axis=0)
            mix_full = mix_full.reshape(team_width, width)
        else:
            head_rows = 0
            second = plane_gather(jnp.concatenate([side_rows(down_low[0]), conv_out_low]))
            mix_all = lax.all_gather(mix_low, ALL, axis=0, tiled=True)
            mix_full = lax.dynamic_slice_in_dim(mix_all, team_at * team_width, team_width, axis=0)
        down_one = second[:, :down_rows].reshape(team_hidden, width)
        conv_out = second[:, down_rows + head_rows :].reshape(team_width, width)

        third = jnp.concatenate(
            [split_heads(side_rows(square_low[i])) for i in (0, 1, 2, 4)]
            + [split_hidden(side_rows(square_low[i])) for i in (5, 6)],
            axis=2,
        )
        third = plane_gather(team_swap(third).reshape(-1, 6 * team_width))
        third = third.reshape(width, 6 * team_width)
        qkv_in = third[:, : 3 * team_width]
        place_in = third[:, 3 * team_width : 4 * team_width]
        gate_in = third[:, 4 * team_width :]

        up_two = plane_gather(
            team_swap(split_hidden(side_rows(up_low[1]))).reshape(-1, team_hidden)
        ).reshape(width, team_hidden)
        down_two = plane_gather(side_rows(down_low[1])).reshape(team_hidden, width)

        def own_hidden(rows):
            rows = rows.reshape(rows.shape[0], planes, team, -1)
            rows = lax.dynamic_index_in_dim(rows, team_at, axis=2, keepdims=False)
            return rows.reshape(rows.shape[0], team_width)

        def own_heads(rows):
            blocks = split_heads(rows)
            return lax.dynamic_index_in_dim(blocks, team_at, axis=0, keepdims=False)

        taps = own_hidden(chan_float[:tap_count])
        batch_rows = own_hidden(chan_float[tap_count + 10 : tap_count + 12])
        batch_gain, batch_shift = batch_rows[0], batch_rows[1]
        bias_rows = own_heads(chan_float[tap_count + 12 : tap_count + 14])
        bias_content, bias_place = bias_rows[0], bias_rows[1]
        gains = [chan_float[tap_count + j] for j in range(5)]
        shifts = [chan_float[tap_count + 5 + j] for j in range(5)]

        team_lengths = jnp.concatenate(team_gather_small(lengths, wide_team))
        segment = item_segments(team_lengths, slots)
        valid_team = (segment < item_count).astype(F32)[:, :, None]
        valid = valid_team[0]

        def gather(values):
            return team_gather(values, wide_team)

        def scatter(pairs):
            return team_scatter(pairs, wide_team)

        def feed_forward(stream, gain, shift, up, down):
            normed = gather(layer_norm(stream, gain, shift).astype(BF16))
            before = [mm(n, up) for n in normed]
            active = [(a * jax.nn.sigmoid(a)).astype(BF16) for a in before]
            branch = scatter([mm(s, down) for s in active])
            return stream + 0.5 * branch, (normed, before, active)

        def feed_backward(grad_stream, stream, gain, up, down, saved):
            normed, before, active = saved
            grads = gather((0.5 * grad_stream).astype(BF16))
            grad_before = [
                (mm_nt(g, down) * swish_grad(a)).astype(BF16) for g, a in zip(grads, before)
            ]
            grad_normed = scatter([mm_nt(g, up) for g in grad_before])
            down_term = mm_tn(jnp.concatenate(active), jnp.concatenate(grads))
            up_term = mm_tn(jnp.concatenate(normed), jnp.concatenate(grad_before))
            grad_in, gain_term, shift_term = layer_norm_back(stream, gain, grad_normed)
            return grad_stream + grad_in, up_term, down_term, gain_term, shift_term

        stream_zero = frames.astype(F32)
        stream_one, saved_one = feed_forward(stream_zero, gains[0], shifts[0], up_one, down_one)

        normed_two = gather(layer_norm(stream_one, gains[1], shifts[1]).astype(BF16))
        normed_two = jnp.concatenate(normed_two)
        qkv = mm(normed_two, qkv_in)
        query = qkv[:, :team_width]

        def to_heads(rows):
            return rows.reshape(-1, slots, team_heads, head_size).transpose(0, 2, 1, 3)

        def from_heads(rows):
            return rows.transpose(0, 2, 1, 3).reshape(-1, team_width)

        query_c = to_heads((query + bias_content).astype(BF16))
        query_p = to_heads((query + bias_place).astype(BF16))
        key = to_heads(qkv[:, team_width : 2 * team_width].astype(BF16))
        value = to_heads(qkv[:, 2 * team_width :].astype(BF16))
        table = offset_table(slots, width).astype(BF16)
        place = mm(table, place_in).astype(BF16).reshape(-1, team_heads, head_size)

        wide_scores = jnp.einsum("bhid,ohd->bhio", query_p, place, preferred_element_type=F32)
        content = jnp.einsum("bhid,bhjd->bhij", query_c, key, preferred_element_type=F32)
        scores = (content + shift_scores(wide_scores)) * score_scale
        same = segment[:, :, None] == segment[:, None, :]
        scores = jnp.where(same[:, None], scores, MASKED_SCORE)
        probs = jax.nn.softmax(scores, axis=-1)
        probs_low = probs.astype(BF16)
        mixed = jnp.einsum("bhij,bhjd->bhid", probs_low, value, preferred_element_type=F32)
        mixed = from_heads(mixed.astype(BF16))
        pair_rows = 2 * slots
        pair_count = team // 2

        def in_pairs(rows):
            return [rows[p * pair_rows : (p + 1) * pair_rows] for p in range(pair_count)]

        stream_two = stream_one + scatter([mm(m, mix_full) for m in in_pairs(mixed)])

        normed_three = gather(layer_norm(stream_two, gains[2], shifts[2]).astype(BF16))
        normed_three = jnp.concatenate(normed_three)
        gates = mm(normed_three, gate_in).reshape(buckets, slots, 2 * team_width)
        gate_a, gate_b = gates[:, :, :team_width], gates[:, :, team_width:]
        gate_sig = jax.nn.sigmoid(gate_b)
        glu = gate_a * gate_sig * valid_team
        conv = depth_conv(glu, taps, segment, False)
        local_count = jnp.sum(valid_team)
        local_mean = jnp.sum(conv * valid_team, axis=(0, 1)) / local_count
        local_gap = (conv - local_mean) * valid_team
        local_spread = jnp.sum(local_gap * local_gap, axis=(0, 1))
        count_row, mean, spread = outer_moments(
            jnp.broadcast_to(local_count, local_mean.shape), local_mean, local_spread
        )
        frame_count = count_row[0]
        spread_inv = lax.rsqrt(spread / frame_count + EPSILON)
        unit = (conv - mean) * spread_inv
        batch_normed = unit * batch_gain + batch_shift
        active_conv = (batch_normed * jax.nn.sigmoid(batch_normed)).astype(BF16)
        active_conv = active_conv.reshape(-1, team_width)
        stream_three = stream_two + scatter([mm(s, conv_out) for s in in_pairs(active_conv)])

        stream_four, saved_four = feed_forward(
            stream_three, gains[3], shifts[3], up_two, down_two
        )
        output = (layer_norm(stream_four, gains[4], shifts[4]) * valid).astype(BF16)

        grad_final = out_grad.astype(F32) * valid
        grad_four, gain_four, shift_four = layer_norm_back(stream_four, gains[4], grad_final)
        grad_three, up_second, down_second, gain_three, shift_three = feed_backward(
            grad_four, stream_three, gains[3], up_two, down_two, saved_four
        )
        down_second = plane_scatter(down_second.astype(BF16).reshape(planes, -1, width))
        up_second = plane_scatter(up_second.astype(BF16).reshape(planes, -1, team_hidden))

        grads = jnp.concatenate(gather(grad_three.astype(BF16)))
        conv_out_term = mm_tn(active_conv, grads)
        grad_active = mm_nt(grads, conv_out).reshape(buckets, slots, team_width)
        grad_batch = grad_active * swish_grad(batch_normed)
        batch_gain_term = jnp.sum(grad_batch * unit, axis=(0, 1))
        batch_shift_term = jnp.sum(grad_batch, axis=(0, 1))
        grad_unit = grad_batch * batch_gain
        sums = outer_sum(
            jnp.stack(
                [
                    jnp.sum(grad_unit * valid_team, axis=(0, 1)),
                    jnp.sum(grad_unit * unit * valid_team, axis=(0, 1)),
                ]
            )
        )
        grad_conv = (
            valid_team
            * spread_inv
            * (grad_unit - sums[0] / frame_count - unit * (sums[1] / frame_count))
        )
        tap_term = tap_grads(glu, grad_conv, tap_count, segment)
        grad_glu = depth_conv(grad_conv, taps, segment, True) * valid_team
        grad_a = (grad_glu * gate_sig).astype(BF16)
        grad_b = (grad_glu * gate_a * gate_sig * (1.0 - gate_sig)).astype(BF16)
        grad_gates = jnp.concatenate([grad_a, grad_b], axis=2).reshape(-1, 2 * team_width)
        gate_term = mm_tn(normed_three, grad_gates)
        grad_normed = scatter([mm_nt(g, gate_in) for g in in_pairs(grad_gates)])
        grad_in, gain_two, shift_two = layer_norm_back(stream_two, gains[2], grad_normed)
        grad_two = grad_three + grad_in

        grads = jnp.concatenate(gather(grad_two.astype(BF16)))
        mix_term = mm_tn(mixed, grads)
        grad_mixed = to_heads(mm_nt(grads, mix_full).astype(BF16))
        grad_probs = jnp.einsum("bhid,bhjd->bhij", grad_mixed, value, preferred_element_type=F32)
        grad_value = jnp.einsum(
            "bhij,bhid->bhjd", probs_low, grad_mixed, preferred_element_type=F32
        )
        grad_scores = probs * (
            grad_probs - jnp.sum(probs * grad_probs, axis=-1, keepdims=True)
        )
        grad_scaled = grad_scores.astype(BF16) * score_scale
        grad_qc = jnp.einsum("bhij,bhjd->bhid", grad_scaled, key, preferred_element_type=F32)
        grad_key = jnp.einsum("bhij,bhid->bhjd", grad_scaled, query_c, preferred_element_type=F32)
        _, shift_pull = jax.vjp(shift_scores, wide_scores)
        grad_wide = shift_pull(grad_scaled.astype(F32))[0].astype(BF16)
        grad_qp = jnp.einsum("bhio,ohd->bhid", grad_wide, place, preferred_element_type=F32)
        grad_place = jnp.einsum("bhio,bhid->ohd", grad_wide, query_p, preferred_element_type=F32)
        place_term = mm_tn(table, grad_place.reshape(-1, team_width).astype(BF16))
        bias_content_term = jnp.sum(grad_qc, axis=(0, 2)).reshape(team_width)
        bias_place_term = jnp.sum(grad_qp, axis=(0, 2)).reshape(team_width)
        grad_qkv = jnp.concatenate(
            [
                from_heads((grad_qc + grad_qp).astype(BF16)),
                from_heads(grad_key.astype(BF16)),
                from_heads(grad_value.astype(BF16)),
            ],
            axis=1,
        )
        qkv_term = mm_tn(normed_two, grad_qkv)
        grad_normed = scatter([mm_nt(g, qkv_in) for g in in_pairs(grad_qkv)])
        grad_in, gain_one, shift_one = layer_norm_back(stream_one, gains[1], grad_normed)
        grad_one = grad_two + grad_in

        mix_term = mix_term.astype(BF16)
        conv_out_term = conv_out_term.astype(BF16).reshape(planes, -1, width)
        if head_aligned:
            per_side = planes // sides
            spread_rows = jnp.zeros((planes, head_rows, width), BF16)
            spread_rows = lax.dynamic_update_slice_in_dim(
                spread_rows, mix_term.reshape(per_side, head_rows, width), y_at * per_side, axis=0
            )
            rows_term = plane_scatter(jnp.concatenate([spread_rows, conv_out_term], axis=1))
            mix_own = rows_term[:head_rows]
            mix_own = mix_own.astype(F32) + swap(mix_own, "y").astype(F32)
            per_device = head_rows // sides
            mix_grad = lax.dynamic_slice_in_dim(mix_own, y_at * per_device, per_device, axis=0)
            conv_out_grad = rows_term[head_rows:].astype(F32)
        else:
            spread_rows = jnp.zeros((width, width), BF16)
            spread_rows = lax.dynamic_update_slice_in_dim(
                spread_rows, mix_term, team_at * team_width, axis=0
            )
            mix_grad = lax.psum_scatter(spread_rows, ALL, scatter_dimension=0, tiled=True)
            mix_grad = mix_grad.astype(F32)
            conv_out_grad = side_scatter(plane_scatter(conv_out_term)).astype(F32)
        columns_term = jnp.concatenate([qkv_term, place_term, gate_term], axis=1).astype(BF16)
        columns_term = plane_scatter(columns_term.reshape(planes, -1, 6 * team_width))

        grad_zero, up_first, down_first, gain_zero, shift_zero = feed_backward(
            grad_one, stream_zero, gains[0], up_one, down_one, saved_one
        )
        frames_grad = grad_zero.astype(BF16)
        down_first = plane_scatter(down_first.astype(BF16).reshape(planes, -1, width))
        up_first = plane_scatter(up_first.astype(BF16).reshape(planes, -1, team_hidden))

        def from_team(rows, columns):
            return team_swap(rows.reshape(team, -1, columns))

        up_grad = jnp.stack(
            [
                side_scatter(join_hidden(from_team(rows, team_hidden))).astype(F32)
                for rows in (up_first, up_second)
            ]
        )
        down_grad = jnp.stack(
            [side_scatter(down_first).astype(F32), side_scatter(down_second).astype(F32)]
        )
        blocks = from_team(columns_term, 6 * team_width)

        def block(i):
            return blocks[:, :, i * team_width : (i + 1) * team_width]

        square_grad = jnp.stack(
            [side_scatter(join_heads(block(i))).astype(F32) for i in range(3)]
            + [mix_grad, side_scatter(join_heads(block(3))).astype(F32)]
            + [side_scatter(join_hidden(block(i))).astype(F32) for i in (4, 5)]
            + [conv_out_grad]
        )

        zero_blocks = jnp.zeros((team, 2, team_width), F32)
        bias_terms = join_heads(
            lax.dynamic_update_slice_in_dim(
                zero_blocks,
                jnp.stack([bias_content_term, bias_place_term])[None],
                team_at,
                axis=0,
            )
        )
        feature_terms = jnp.concatenate(
            [
                jnp.stack(
                    [
                        gain_zero,
                        gain_one,
                        gain_two,
                        gain_three,
                        gain_four,
                        shift_zero,
                        shift_one,
                        shift_two,
                        shift_three,
                        shift_four,
                    ]
                ),
                bias_terms,
            ]
        )
        feature_terms = jnp.sum(team_swap(split_hidden(feature_terms)), axis=0)
        chan_term = jnp.concatenate(
            [
                tap_term,
                feature_terms[:10],
                jnp.stack([batch_gain_term, batch_shift_term]),
                feature_terms[10:],
            ]
        )
        chan_term = outer_sum(chan_term).reshape(chan_rows, planes, -1)
        chan_term = lax.dynamic_index_in_dim(chan_term, lax.axis_index("z"), 1, keepdims=False)
        if not wide_team:
            chan_term = lax.dynamic_index_in_dim(
                chan_term.reshape(chan_rows, sides, -1), y_at, 1, keepdims=False
            )
        chan_grad = chan_term

        rate_scale = lax.rsqrt(frame_count)
        up_new = nesterov(up_weight, up_moment, up_average, up_grad, RATE_UP, rate_scale)
        down_new = nesterov(down_weight, down_moment, down_average, down_grad, RATE_DOWN, rate_scale)
        square_new = nesterov(
            square_weight, square_moment, square_average, square_grad, RATE_SQUARE, rate_scale
        )
        chan_new = nesterov(
            chan_weight, chan_moment, chan_average, chan_grad, RATE_CHANNEL, rate_scale
        )
        bias_grad = chan_grad[tap_count + 12 : tap_count + 14]
        return (
            output,
            frames_grad,
            up_grad,
            down_grad,
            square_grad,
            chan_grad,
            up_new[0],
            down_new[0],
            square_new[0],
            chan_new[0],
            up_new[1],
            down_new[1],
            square_new[1],
            chan_new[1],
            up_new[2],
            down_new[2],
            square_new[2],
            chan_new[2],
            bias_grad,
        )

    return step


def solution(mesh):
    wide, narrow = mesh.shape["wide"], mesh.shape["narrow"]
    planes = wide // 4
    inner = Mesh(mesh.devices.reshape(planes, 2, 2, narrow), ALL)
    token = P(ALL, None)
    matrix = P(None, ALL, None)
    vector = P(None, ALL)
    group = (matrix, matrix, matrix, vector)
    return jax.shard_map(
        make_step(planes, narrow),
        mesh=inner,
        in_specs=(token, token, token) + group * 3,
        out_specs=(token, token) + group * 4 + (vector,),
        check_vma=False,
    )
```

```python
import functools

import jax
import jax.numpy as jnp
from jax import lax
from jax.experimental import pallas as pl
from jax.experimental.pallas import tpu as pltpu
from jax.sharding import Mesh
from jax.sharding import PartitionSpec as P

HEADS = 16
EPSILON = 1e-05
MOMENTUM_DECAY = 0.9
AVERAGE_DECAY = 0.9
RATE_UP = 0.05
RATE_DOWN = 0.026
RATE_SQUARE = 0.05
RATE_CHANNEL = 0.5
MASKED_SCORE = -1e30
BF16 = jnp.bfloat16
F32 = jnp.float32
ALL = ("z", "x", "c", "y")
LANES = 128
PAD = 16
BLOCK = 256
CARRY = 16
ROOM = 6 << 20


def mm(left, right):
    return jnp.dot(left, right, preferred_element_type=F32)


def mm_tn(left, right):
    return lax.dot_general(left, right, (((0,), (0,)), ((), ())), preferred_element_type=F32)


def mm_nt(left, right):
    return lax.dot_general(left, right, (((1,), (1,)), ((), ())), preferred_element_type=F32)


def swap(values, axis, bit=1):
    size = lax.axis_size(axis)
    return lax.ppermute(values, axis, [(i, i ^ bit) for i in range(size)])


def sigmoid(values):
    return 1.0 / (1.0 + jnp.exp(-values))


def swish_grad(values):
    sig = sigmoid(values)
    return sig * (1.0 + values * (1.0 - sig))


def normalize(values):
    centre = values - jnp.mean(values, axis=-1, keepdims=True)
    scale = lax.rsqrt(jnp.mean(centre * centre, axis=-1, keepdims=True) + EPSILON)
    return centre * scale, scale


def shape(dims, dtype):
    return jax.ShapeDtypeStruct(tuple(dims), dtype)


def size_of(item):
    total = 1
    for n in item.shape:
        total *= n
    return total * item.dtype.itemsize


def kernel_call(body, outs, args, scalars=(), flops=0, scratch=()):
    moved = sum(size_of(a) for a in args) + sum(size_of(o) for o in outs)
    return pl.pallas_call(
        body,
        out_shape=tuple(outs),
        in_specs=[pl.BlockSpec(memory_space=pltpu.SMEM)] * len(scalars)
        + [pl.BlockSpec(memory_space=pltpu.VMEM)] * len(args),
        out_specs=tuple(pl.BlockSpec(memory_space=pltpu.VMEM) for _ in outs),
        scratch_shapes=list(scratch),
        compiler_params=pltpu.CompilerParams(vmem_limit_bytes=moved + ROOM),
        cost_estimate=pl.CostEstimate(flops=int(flops), bytes_accessed=moved, transcendentals=0),
    )(*scalars, *args)


def store_partial(mine_refs, mate_ref, i, slots, value):
    mine_refs[i][...] = value[:slots]
    mate_ref[i] = value[slots:].astype(BF16)


def up_product(rows, ref):
    planes = ref.shape[0]
    depth = rows.shape[1] // planes
    total = mm(rows[:, :depth], ref[0, :depth, :])
    for p in range(1, planes):
        total = total + mm(rows[:, p * depth : (p + 1) * depth], ref[p, :depth, :])
    return total


def up_product_back(rows, ref, width):
    planes = ref.shape[0]
    depth = width // planes
    return jnp.concatenate([mm_nt(rows, ref[p, :depth, :]) for p in range(planes)], axis=1)


def down_blocks(ref, width):
    planes, hidden = ref.shape[0], ref.shape[2]
    depth, rows = width // planes, hidden // planes
    return [
        jnp.concatenate(
            [ref[p, depth + b * rows : depth + (b + 1) * rows, :] for p in range(planes)]
        )
        for b in range(width // hidden)
    ]


def down_product(rows, blocks):
    return jnp.concatenate([mm(rows, block) for block in blocks], axis=1)


def down_product_back(rows, blocks):
    size = blocks[0].shape[1]
    total = mm_nt(rows[:, :size], blocks[0])
    for b in range(1, len(blocks)):
        total = total + mm_nt(rows[:, b * size : (b + 1) * size], blocks[b])
    return total


def square_columns(ref, p, depth, first, last):
    parts = []
    while first < last:
        block = first // BLOCK
        stop = min(last, (block + 1) * BLOCK)
        lanes = slice(first - block * BLOCK, stop - block * BLOCK)
        parts.append(ref[p, block * depth : (block + 1) * depth, lanes])
        first = stop
    return jnp.concatenate(parts, axis=1) if len(parts) > 1 else parts[0]


def square_product(rows, ref, first, last):
    planes = ref.shape[0]
    depth = rows.shape[1] // planes
    total = None
    for p in range(planes):
        term = mm(rows[:, p * depth : (p + 1) * depth], square_columns(ref, p, depth, first, last))
        total = term if total is None else total + term
    return total


def square_product_back(rows, ref, width, first, last):
    planes = ref.shape[0]
    depth = width // planes
    return jnp.concatenate(
        [mm_nt(rows, square_columns(ref, p, depth, first, last)) for p in range(planes)], axis=1
    )


def output_rows(ref, p, width, size, mix, conv, want_mix):
    base = (6 * size // BLOCK) * (width // ref.shape[0])
    parts = []
    for b in range(width // BLOCK):
        at = base + b * (mix + conv) + (0 if want_mix else mix)
        rows = ref[pl.ds(p, 1), at : at + (mix if want_mix else conv), :]
        parts.append(rows.reshape(rows.shape[1:]))
    return jnp.concatenate(parts, axis=1)


def forward_kernel(k, with_norm, *refs):
    mine, mate, refs = refs[:k], refs[k : 2 * k], refs[2 * k :]
    if with_norm:
        norm_ref, refs = refs[0], refs[1:]
    pack_ref, refs = refs[0], refs[1:]
    out_mine, out_mate, before_ref, active_ref = refs[:k], refs[k], refs[k + 1], refs[k + 2]
    slots, width = mine[0].shape
    blocks = down_blocks(pack_ref, width)
    for i in range(k):
        rows = jnp.concatenate([mine[i][...], mate[i][...]])
        at = pl.ds(2 * i * slots, 2 * slots)
        if with_norm:
            unit, _ = normalize(rows.astype(F32))
            rows = (unit * norm_ref[0:1, :] + norm_ref[1:2, :]).astype(BF16)
            refs[k + 3][at, :] = rows
        before = up_product(rows, pack_ref)
        before_ref[at, :] = before
        active = (before * sigmoid(before)).astype(BF16)
        active_ref[at, :] = active
        store_partial(out_mine, out_mate, i, slots, down_product(active, blocks))


def forward_call(pieces, pack, norm=None):
    mine, mate = pieces
    k, (slots, width) = len(mine), mine[0].shape
    hidden = pack.shape[2]
    rows = 2 * k * slots
    outs = [shape((slots, width), F32)] * k + [
        shape((k, slots, width), BF16),
        shape((rows, hidden), F32),
        shape((rows, hidden), BF16),
    ]
    args = list(mine) + list(mate)
    if norm is not None:
        outs.append(shape((rows, width), BF16))
        args.append(norm)
    result = kernel_call(
        functools.partial(forward_kernel, k, norm is not None),
        outs,
        args + [pack],
        flops=4 * rows * width * hidden,
    )
    return (result[:k], result[k]), result[k + 1 :]


def backward_kernel(k, *refs):
    mine, mate, refs = refs[:k], refs[k : 2 * k], refs[2 * k :]
    pack_ref, before_ref, refs = refs[0], refs[1], refs[2:]
    out_mine, out_mate, grad_ref = refs[:k], refs[k], refs[k + 1]
    slots, width = mine[0].shape
    blocks = down_blocks(pack_ref, width)
    for i in range(k):
        at = pl.ds(2 * i * slots, 2 * slots)
        rows = jnp.concatenate([mine[i][...], mate[i][...]])
        grad = down_product_back(rows, blocks) * swish_grad(before_ref[at, :])
        grad = grad.astype(BF16)
        grad_ref[at, :] = grad
        store_partial(out_mine, out_mate, i, slots, up_product_back(grad, pack_ref, width))


def backward_call(pieces, pack, before):
    mine, mate = pieces
    k, (slots, width) = len(mine), mine[0].shape
    rows, hidden = before.shape
    outs = [shape((slots, width), F32)] * k + [
        shape((k, slots, width), BF16),
        shape((rows, hidden), BF16),
    ]
    result = kernel_call(
        functools.partial(backward_kernel, k),
        outs,
        list(mine) + list(mate) + [pack, before],
        flops=4 * rows * width * hidden,
    )
    return (result[:k], result[k]), result[k + 1]


def joined(refs):
    return jnp.concatenate([r[...] for r in refs])


def take(refs, counts):
    groups, at = [], 0
    for n in counts:
        groups.append(refs[at : at + n])
        at += n
    return groups + [refs[at:]]


def put(out_refs, plane_ref, planes, write):
    if len(out_refs) == 1 and planes > 1:
        for p in range(planes):
            write(out_refs[0].at[p], p)
    else:
        for d in range(planes):
            write(out_refs[d], plane_ref[0] ^ d)


def rows_at(ref, p, rows, lanes=slice(None)):
    return ref[pl.ds(pl.multiple_of(p * rows, rows), rows), lanes]


def feed_weight_kernel(counts, planes, outs, *refs):
    plane_ref, refs = refs[0], refs[1:]
    normed, grads, active, rows, refs = take(refs, counts)
    out_refs, (up_ref, down_ref) = refs[:outs], refs[outs:]
    width, hidden = up_ref.shape
    depth, below = width // planes, hidden // planes
    down_ref[...] = mm_tn(joined(active), joined(rows))
    up_ref[...] = mm_tn(joined(normed), joined(grads))

    def write(out, p):
        out[:depth, :] = rows_at(up_ref, p, depth).astype(BF16)
        for b in range(width // hidden):
            at = depth + b * below
            lanes = slice(b * hidden, (b + 1) * hidden)
            out[at : at + below, :] = rows_at(down_ref, p, below, lanes).astype(BF16)

    put(out_refs, plane_ref, planes, write)


def feed_weight_call(normed, grads, active, rows, plane, planes, by_plane):
    width, hidden = normed[0].shape[1], grads[0].shape[1]
    lines = width // planes + (hidden // planes) * (width // hidden)
    one = shape((lines, hidden), BF16)
    outs = [shape((planes, lines, hidden), BF16)] if by_plane else [one] * planes
    groups = (normed, grads, active, rows)
    tokens = sum(a.shape[0] for a in grads)
    return kernel_call(
        functools.partial(feed_weight_kernel, [len(g) for g in groups], planes, len(outs)),
        outs,
        [a for g in groups for a in g],
        scalars=(plane,),
        flops=4 * width * hidden * tokens,
        scratch=[pltpu.VMEM((width, hidden), F32), pltpu.VMEM((hidden, width), F32)],
    )


def write_columns(out, total_ref, p, depth):
    for b in range(total_ref.shape[1] // BLOCK):
        lanes = slice(b * BLOCK, (b + 1) * BLOCK)
        out[b * depth : (b + 1) * depth, :] = rows_at(total_ref, p, depth, lanes).astype(BF16)


def write_output_rows(out, base, rows):
    count = rows.shape[0]
    for b in range(rows.shape[1] // BLOCK):
        at = base + b * count
        out[at : at + count, :] = rows[:, b * BLOCK : (b + 1) * BLOCK].astype(BF16)


def conv_weight_kernel(counts, planes, *refs):
    plane_ref, refs = refs[0], refs[1:]
    normed, grads, active, rows, refs = take(refs, counts)
    out_ref, gate_ref, row_ref = refs
    depth = gate_ref.shape[0] // planes
    below = row_ref.shape[0] // planes
    base = (gate_ref.shape[1] // BLOCK) * depth
    gate_ref[...] = mm_tn(joined(normed), joined(grads))
    row_ref[...] = mm_tn(joined(active), joined(rows))

    def write(out, p):
        write_columns(out, gate_ref, p, depth)
        write_output_rows(out, base, rows_at(row_ref, p, below))

    put([out_ref], plane_ref, planes, write)


def conv_weight_call(normed, grads, active, rows, plane, planes):
    width, gates, size = normed[0].shape[1], grads[0].shape[1], active[0].shape[1]
    lines = (gates // BLOCK) * (width // planes) + (width // BLOCK) * (size // planes)
    groups = (normed, grads, active, rows)
    tokens = sum(a.shape[0] for a in grads)
    return kernel_call(
        functools.partial(conv_weight_kernel, [len(g) for g in groups], planes),
        [shape((planes, lines, BLOCK), BF16)],
        [a for g in groups for a in g],
        scalars=(plane,),
        flops=2 * width * (gates + size) * tokens,
        scratch=[pltpu.VMEM((width, gates), F32), pltpu.VMEM((size, width), F32)],
    )[0]


def mix_weight_kernel(counts, planes, per_side, *refs):
    plane_ref, side_ref, refs = refs[0], refs[1], refs[2:]
    normed, grads, mixed, rows, place, refs = take(refs, counts)
    table_ref, near_ref, far_ref = place
    out_ref, total_ref, row_ref = refs
    depth = total_ref.shape[0] // planes
    base = (total_ref.shape[1] // BLOCK) * depth
    right = joined(grads)
    qkv = right.shape[1]
    total_ref[:, :qkv] = mm_tn(joined(normed), right)
    total_ref[:, qkv:] = mm_tn(table_ref[...], (near_ref[...] + far_ref[...]).astype(BF16))
    if per_side:
        row_ref[...] = mm_tn(joined(mixed), joined(rows))

    def write(out, p):
        write_columns(out, total_ref, p, depth)
        if per_side:
            below = row_ref.shape[0] // per_side
            place = p - side_ref[0] * per_side
            held = (place >= 0) & (place < per_side)
            share = held.astype(jnp.int32).astype(F32)
            head = rows_at(row_ref, jnp.where(held, place, 0), below) * share
            write_output_rows(out, base, head)

    put([out_ref], plane_ref, planes, write)


def mix_weight_call(normed, grads, mixed, rows, place, plane, side, planes, per_side):
    width, qkv, size = normed[0].shape[1], grads[0].shape[1], mixed[0].shape[1]
    total = qkv + size
    lines = (total // BLOCK) * (width // planes)
    if per_side:
        lines += (width // BLOCK) * (size // per_side)
    groups = (normed, grads, mixed, rows, place)
    tokens = sum(a.shape[0] for a in grads)
    return kernel_call(
        functools.partial(mix_weight_kernel, [len(g) for g in groups], planes, per_side),
        [shape((planes, lines, BLOCK), BF16)],
        [a for g in groups for a in g],
        scalars=(plane, side),
        flops=2 * width * (total + size) * tokens,
        scratch=[pltpu.VMEM((width, total), F32), pltpu.VMEM((size, width), F32)],
    )[0]


def stack_kernel(planes, *refs):
    plane_ref, ups, downs, out_ref = refs[0], refs[1 : 1 + planes], refs[1 + planes : -1], refs[-1]
    depth = ups[0].shape[0]
    for d in range(planes):
        at = pl.ds(plane_ref[0] ^ d, 1)
        out_ref[at, :depth, :] = ups[d][...].reshape((1,) + ups[d].shape)
        out_ref[at, depth:, :] = downs[d][...].reshape((1,) + downs[d].shape)


def channel_kernel(planes, sides, head_size, *refs):
    at_ref, pieces, refs = refs[0], refs[1 : 1 + planes], refs[1 + planes :]
    norm_refs, (tap_ref, batch_ref, bias_ref, length_ref, wide_ref) = refs[:5], refs[5:]
    plane, member, side, core = at_ref[0], at_ref[1], at_ref[2], at_ref[3]
    team, rows = pieces[0].shape[0], pieces[0].shape[1] - CARRY
    size = tap_ref.shape[1]
    listed = [pieces[0][m, rows : rows + 1, :].astype(F32) for m in range(team)]
    one = jnp.concatenate([listed[4], listed[3]])
    two = jnp.concatenate([listed[1], listed[6]])
    table = [
        listed[0],
        listed[2],
        jnp.where(core == 0, one, two),
        jnp.where(core == 0, two, one),
        listed[5],
        listed[7],
    ]
    length_ref[...] = jnp.concatenate(table).astype(jnp.int32)[:, : length_ref.shape[1]]
    for d in range(planes):
        for m in range(team):
            at = ((plane ^ d) * team + (member ^ m)) * rows
            wide_ref[pl.ds(pl.multiple_of(at, rows), rows), :] = pieces[d][m, :rows, :].astype(F32)
    every = wide_ref[...].T
    taps = tap_ref.shape[0] - 1
    for j in range(5):
        first = every[taps + j : taps + j + 1]
        norm_refs[j][...] = jnp.concatenate([first, every[taps + 5 + j : taps + 6 + j]])
    own = [
        wide_ref[pl.ds(pl.multiple_of((p * team + member) * rows, rows), rows), :]
        for p in range(planes)
    ]
    own = jnp.concatenate(own).T
    tap_ref[...] = own[: taps + 1]
    batch_ref[...] = own[taps + 10 : taps + 12]
    heads = size // head_size
    own = [
        wide_ref[
            pl.ds(
                pl.multiple_of(
                    (side * heads + h) * team * rows + (member // sides) * head_size, head_size
                ),
                head_size,
            ),
            :,
        ]
        for h in range(heads)
    ]
    own = jnp.concatenate(own).T
    bias_ref[...] = own[taps + 12 : taps + 14]


def chunk_order(pieces):
    rows = []
    for mine, mate in zip(*pieces):
        rows += [mine, mate]
    return rows


def item_bounds(length_ref, b=0):
    ends = [length_ref[b, 0]]
    for j in range(1, length_ref.shape[1] - 1):
        ends.append(ends[-1] + length_ref[b, j])
    return ends


def item_index(ends, where_at):
    total = (where_at >= ends[0]).astype(jnp.int32)
    for end in ends[1:]:
        total = total + (where_at >= end).astype(jnp.int32)
    return total


def head_masks(slots, head_size):
    lane = lax.broadcasted_iota(jnp.int32, (slots, LANES), 1)
    return [
        (lane >= h * head_size) & (lane < (h + 1) * head_size) for h in range(LANES // head_size)
    ]


def attention_kernel(k, first, head_size, rows_held, *refs):
    length_ref, side_ref, refs = refs[0], refs[1], refs[2:]
    mine, mate, refs = refs[:k], refs[k : 2 * k], refs[2 * k :]
    column_ref, mix_ref, bias_ref, place_ref, refs = refs[0], refs[1], refs[2], refs[3], refs[4:]
    out_mine, out_mate, saved_ref, probs_ref, mixed_ref = (
        refs[:k],
        refs[k],
        refs[k + 1],
        refs[k + 2],
        refs[k + 3],
    )
    slots, width = mine[0].shape
    size = place_ref.shape[1]
    mix = mix_rows(mix_ref, side_ref, width, size, rows_held)
    scale = head_size ** (-0.5)
    row_at = lax.broadcasted_iota(jnp.int32, (slots, slots), 0)
    column_at = lax.broadcasted_iota(jnp.int32, (slots, slots), 1)
    masks = head_masks(slots, head_size)
    for i in range(k):
        rows = jnp.concatenate([mine[i][...], mate[i][...]])
        qkv = square_product(rows, column_ref, 0, 3 * size)
        query = qkv[:, :size]
        query_c = (query + bias_ref[0:1, :]).astype(BF16)
        query_p = (query + bias_ref[1:2, :]).astype(BF16)
        key = qkv[:, size : 2 * size].astype(BF16)
        value = qkv[:, 2 * size :].astype(BF16)
        at = pl.ds(2 * i * slots, 2 * slots)
        saved_ref[at, 0:size] = query_c
        saved_ref[at, size : 2 * size] = query_p
        saved_ref[at, 2 * size : 3 * size] = key
        saved_ref[at, 3 * size : 4 * size] = value
        halves = []
        for j in range(2):
            b = 2 * i + j
            part = slice(j * slots, (j + 1) * slots)
            ends = item_bounds(length_ref, first + b)
            same = item_index(ends, row_at) == item_index(ends, column_at)
            blocks = []
            for lo in range(0, size, LANES):
                lanes = slice(lo, lo + LANES)
                mixed = jnp.zeros((slots, LANES), F32)
                for h, mask in enumerate(masks):
                    qc = jnp.where(mask, query_c[part, lanes], 0)
                    qp = jnp.where(mask, query_p[part, lanes], 0)
                    wide = mm_nt(qp, place_ref[:, lanes])
                    moved = pltpu.roll(wide, slots + 1, 1, stride=1, stride_axis=0)
                    scores = (mm_nt(qc, key[part, lanes]) + moved[:, :slots]) * scale
                    scores = jnp.where(same, scores, MASKED_SCORE)
                    top = jnp.max(scores, axis=-1, keepdims=True)
                    weights = jnp.exp(scores - top)
                    probs = weights / jnp.sum(weights, axis=-1, keepdims=True)
                    probs_ref[b, (lo // LANES) * len(masks) + h] = probs
                    mixed = jnp.where(mask, mm(probs.astype(BF16), value[part, lanes]), mixed)
                blocks.append(mixed)
            halves.append(jnp.concatenate(blocks, axis=1) if len(blocks) > 1 else blocks[0])
        mixed = jnp.concatenate(halves).astype(BF16)
        mixed_ref[at, :] = mixed
        store_partial(out_mine, out_mate, i, slots, mm(mixed, mix))


def mix_rows(mix_ref, side_ref, width, size, rows_held):
    per_side, mix, conv = rows_held
    if not per_side:
        return mix_ref[...]
    return jnp.concatenate(
        [
            output_rows(mix_ref, side_ref[0] * per_side + h, width, size, mix, conv, True)
            for h in range(per_side)
        ]
    )


def attention_call(pieces, lengths, first, side, columns, mix, rows_held, bias, place, head_size):
    mine, mate = pieces
    k, (slots, width) = len(mine), mine[0].shape
    size = place.shape[1]
    heads = size // head_size
    rows = 2 * k * slots
    outs = [shape((slots, width), F32)] * k + [
        shape((k, slots, width), BF16),
        shape((rows, 4 * size), BF16),
        shape((2 * k, heads, slots, slots), F32),
        shape((rows, size), BF16),
    ]
    result = kernel_call(
        functools.partial(attention_kernel, k, first, head_size, rows_held),
        outs,
        list(mine) + list(mate) + [columns, mix, bias, place],
        scalars=(lengths, side),
        flops=2 * rows * width * size * 4 + 2 * k * heads * 10 * slots * slots * LANES,
    )
    return (result[:k], result[k]), result[k + 1 :]


def attention_back_kernel(k, head_size, rows_held, *refs):
    side_ref, refs = refs[0], refs[1:]
    mine, mate, refs = refs[:k], refs[k : 2 * k], refs[2 * k :]
    column_ref, mix_ref, place_ref, saved_ref, probs_ref, refs = (
        refs[0],
        refs[1],
        refs[2],
        refs[3],
        refs[4],
        refs[5:],
    )
    out_mine, out_mate, grad_ref, place_grad_ref, bias_ref = (
        refs[:k],
        refs[k],
        refs[k + 1],
        refs[k + 2],
        refs[k + 3],
    )
    slots, width = mine[0].shape
    size = place_ref.shape[1]
    mix = mix_rows(mix_ref, side_ref, width, size, rows_held)
    scale = head_size ** (-0.5)
    masks = head_masks(slots, head_size)
    flip = (
        lax.broadcasted_iota(jnp.int32, (slots, slots), 0)
        + lax.broadcasted_iota(jnp.int32, (slots, slots), 1)
        == slots - 1
    ).astype(F32).astype(BF16)
    bias_c = jnp.zeros((1, size), F32)
    bias_p = jnp.zeros((1, size), F32)
    for i in range(k):
        rows = jnp.concatenate([mine[i][...], mate[i][...]])
        grad_mixed_all = mm_nt(rows, mix).astype(BF16)
        at = pl.ds(2 * i * slots, 2 * slots)
        halves = []
        for j in range(2):
            b = 2 * i + j
            part = slice(j * slots, (j + 1) * slots)
            rows_at = pl.ds((2 * i + j) * slots, slots)
            grad_qc, grad_qp, grad_k, grad_v = [], [], [], []
            for lo in range(0, size, LANES):
                lanes = slice(lo, lo + LANES)
                grad_mixed = grad_mixed_all[part, lanes]
                query_c = saved_ref[rows_at, lo : lo + LANES]
                query_p = saved_ref[rows_at, size + lo : size + lo + LANES]
                key = saved_ref[rows_at, 2 * size + lo : 2 * size + lo + LANES]
                value = saved_ref[rows_at, 3 * size + lo : 3 * size + lo + LANES]
                place = place_ref[:, lanes]
                gqc = jnp.zeros((slots, LANES), F32)
                gqp, gk, gv = gqc, gqc, gqc
                place_grad = jnp.zeros(place.shape, F32)
                for h, mask in enumerate(masks):
                    probs = probs_ref[b, (lo // LANES) * len(masks) + h]
                    own = jnp.where(mask, grad_mixed, 0)
                    grad_probs = mm_nt(own, value)
                    gv = gv + mm_tn(probs.astype(BF16), own)
                    inner = jnp.sum(probs * grad_probs, axis=-1, keepdims=True)
                    grad = (probs * (grad_probs - inner)).astype(BF16) * scale
                    grad = grad.astype(BF16)
                    gqc = jnp.where(mask, mm(grad, key), gqc)
                    gk = gk + mm_tn(grad, jnp.where(mask, query_c, 0))
                    turned = mm(flip, grad)
                    wide = jnp.concatenate([turned, jnp.zeros_like(turned)], axis=1)
                    wide = pltpu.roll(wide, 0, 1, stride=1, stride_axis=0).astype(BF16)
                    wide = mm(flip, wide).astype(BF16)
                    gqp = jnp.where(mask, mm(wide, place), gqp)
                    place_grad = place_grad + mm_tn(wide, jnp.where(mask, query_p, 0))
                if i == 0 and j == 0:
                    place_grad_ref[:, lanes] = place_grad
                else:
                    place_grad_ref[:, lanes] = place_grad_ref[:, lanes] + place_grad
                grad_qc.append(gqc)
                grad_qp.append(gqp)
                grad_k.append(gk)
                grad_v.append(gv)

            def side_by_side(blocks):
                return jnp.concatenate(blocks, axis=1) if len(blocks) > 1 else blocks[0]

            gqc, gqp = side_by_side(grad_qc), side_by_side(grad_qp)
            bias_c = bias_c + jnp.sum(gqc, axis=0, keepdims=True)
            bias_p = bias_p + jnp.sum(gqp, axis=0, keepdims=True)
            halves.append(
                jnp.concatenate(
                    [gqc + gqp, side_by_side(grad_k), side_by_side(grad_v)], axis=1
                ).astype(BF16)
            )
        grad = jnp.concatenate(halves)
        grad_ref[at, :] = grad
        store_partial(out_mine, out_mate, i, slots, square_product_back(grad, column_ref, width, 0, 3 * size))
    bias_ref[...] = jnp.concatenate([bias_c, bias_p])


def attention_back_call(pieces, side, columns, mix, rows_held, place, saved, probs, head_size):
    mine, mate = pieces
    k, (slots, width) = len(mine), mine[0].shape
    size = place.shape[1]
    rows = 2 * k * slots
    outs = [shape((slots, width), F32)] * k + [
        shape((k, slots, width), BF16),
        shape((rows, 3 * size), BF16),
        shape(place.shape, F32),
        shape((2, size), F32),
    ]
    result = kernel_call(
        functools.partial(attention_back_kernel, k, head_size, rows_held),
        outs,
        list(mine) + list(mate) + [columns, mix, place, saved, probs],
        scalars=(side,),
        flops=2 * rows * width * size * 4 + 2 * k * 24 * slots * slots * size,
    )
    return (result[:k], result[k]), result[k + 1 :]


def place_kernel(table_ref, column_ref, out_ref):
    size = out_ref.shape[1]
    rows = square_product(table_ref[...], column_ref, 3 * size, 4 * size)
    out_ref[...] = rows.astype(BF16)


def item_reach(ends, row_at, slots):
    start = jnp.zeros_like(row_at)
    end = jnp.full_like(row_at, slots)
    for at in ends:
        start = jnp.where(row_at >= at, at, start)
    for at in reversed(ends):
        end = jnp.where(row_at < at, at, end)
    valid = (row_at < ends[-1]).astype(F32)
    return row_at - start, end - 1 - row_at, valid


def gate_kernel(k, first, tap_count, *refs):
    length_ref, refs = refs[0], refs[1:]
    mine, mate, refs = refs[:k], refs[k : 2 * k], refs[2 * k :]
    column_ref, tap_ref, gate_ref, conv_ref, stat_ref, pad_ref = refs
    slots, _ = mine[0].shape
    size = tap_ref.shape[1]
    reach = tap_count // 2
    row_at = lax.broadcasted_iota(jnp.int32, (slots, size), 0)
    pad_ref[...] = jnp.zeros_like(pad_ref)
    count = jnp.zeros((1, size), F32)
    total = jnp.zeros((1, size), F32)
    for i in range(k):
        rows = jnp.concatenate([mine[i][...], mate[i][...]])
        gates = square_product(rows, column_ref, 4 * size, 6 * size)
        gate_ref[pl.ds(2 * i * slots, 2 * slots), :] = gates
        glu = gates[:, :size] * sigmoid(gates[:, size:])
        for j in range(2):
            b = 2 * i + j
            before, behind, valid = item_reach(item_bounds(length_ref, first + b), row_at, slots)
            pad_ref[PAD : PAD + slots, :] = glu[j * slots : (j + 1) * slots] * valid
            conv = jnp.zeros((slots, size), F32)
            for tap in range(tap_count):
                o = tap - reach
                near = pad_ref[PAD + o : PAD + o + slots, :]
                if o < 0:
                    near = jnp.where(before >= -o, near, 0.0)
                elif o > 0:
                    near = jnp.where(behind >= o, near, 0.0)
                conv = conv + near * tap_ref[tap : tap + 1, :]
            conv_ref[pl.ds(b * slots, slots), :] = conv
            count = count + jnp.sum(valid, axis=0, keepdims=True)
            total = total + jnp.sum(conv * valid, axis=0, keepdims=True)
    mean = total / count
    spread = jnp.zeros((1, size), F32)
    for b in range(2 * k):
        valid = (row_at < item_bounds(length_ref, first + b)[-1]).astype(F32)
        gap = (conv_ref[pl.ds(b * slots, slots), :] - mean) * valid
        spread = spread + jnp.sum(gap * gap, axis=0, keepdims=True)
    stat_ref[...] = jnp.concatenate([count, mean, spread, jnp.zeros((5, size), F32)])


def gate_call(pieces, lengths, first, columns, taps, tap_count):
    mine, mate = pieces
    k, (slots, width) = len(mine), mine[0].shape
    size = taps.shape[1]
    rows = 2 * k * slots
    return kernel_call(
        functools.partial(gate_kernel, k, first, tap_count),
        [shape((rows, 2 * size), F32), shape((rows, size), F32), shape((8, size), F32)],
        list(mine) + list(mate) + [columns, taps],
        scalars=(lengths,),
        flops=4 * rows * width * size + 40 * tap_count * rows * size,
        scratch=[pltpu.VMEM((slots + 2 * PAD, size), F32)],
    )


def merge_kernel(left_ref, right_ref, out_ref):
    n_left, n_right = left_ref[0:1, :], right_ref[0:1, :]
    m_left, m_right = left_ref[1:2, :], right_ref[1:2, :]
    count = n_left + n_right
    gap = m_right - m_left
    mean = (n_left * m_left + n_right * m_right) / count
    spread = left_ref[2:3, :] + right_ref[2:3, :] + gap * gap * (n_left * n_right / count)
    size = left_ref.shape[1]
    out_ref[...] = jnp.concatenate([count, mean, spread, jnp.zeros((5, size), F32)])


def merge(left, right):
    return kernel_call(merge_kernel, [shape(left.shape, F32)], [left, right])[0]


def batch_unit(conv, stat_ref):
    inverse = lax.rsqrt(stat_ref[2:3, :] / stat_ref[0:1, :] + EPSILON)
    return (conv - stat_ref[1:2, :]) * inverse, inverse


def batch_kernel(k, rows_held, *refs):
    conv_ref, stat_ref, batch_ref, out_weight_ref, refs = (
        refs[0],
        refs[1],
        refs[2],
        refs[3],
        refs[4:],
    )
    out_mine, out_mate, active_ref = refs[:k], refs[k], refs[k + 1]
    slots, width = out_mine[0].shape
    weight = conv_rows(out_weight_ref, width, active_ref.shape[1], rows_held)
    for i in range(k):
        at = pl.ds(2 * i * slots, 2 * slots)
        unit, _ = batch_unit(conv_ref[at, :], stat_ref)
        value = unit * batch_ref[0:1, :] + batch_ref[1:2, :]
        active = (value * sigmoid(value)).astype(BF16)
        active_ref[at, :] = active
        store_partial(out_mine, out_mate, i, slots, mm(active, weight))


def conv_rows(ref, width, size, rows_held):
    _, mix, conv = rows_held
    return jnp.concatenate(
        [output_rows(ref, p, width, size, mix, conv, False) for p in range(ref.shape[0])]
    )


def batch_call(k, conv, stats, batch_rows, out_weight, rows_held, slots, width):
    size = conv.shape[1]
    outs = [shape((slots, width), F32)] * k + [
        shape((k, slots, width), BF16),
        shape(conv.shape, BF16),
    ]
    result = kernel_call(
        functools.partial(batch_kernel, k, rows_held),
        outs,
        [conv, stats, batch_rows, out_weight],
        flops=2 * conv.shape[0] * width * size,
    )
    return (result[:k], result[k]), result[k + 1]


def batch_back_kernel(k, first, rows_held, *refs):
    length_ref, refs = refs[0], refs[1:]
    mine, mate, refs = refs[:k], refs[k : 2 * k], refs[2 * k :]
    conv_ref, stat_ref, batch_ref, out_weight_ref, grad_ref, sum_ref = refs
    slots, width = mine[0].shape
    size = conv_ref.shape[1]
    weight = conv_rows(out_weight_ref, width, size, rows_held)
    row_at = lax.broadcasted_iota(jnp.int32, (slots, size), 0)
    sums = [jnp.zeros((1, size), F32)] * 4
    for i in range(k):
        rows = jnp.concatenate([mine[i][...], mate[i][...]])
        grad_active = mm_nt(rows, weight)
        for j in range(2):
            b = 2 * i + j
            at = pl.ds(b * slots, slots)
            unit, _ = batch_unit(conv_ref[at, :], stat_ref)
            value = unit * batch_ref[0:1, :] + batch_ref[1:2, :]
            grad = grad_active[j * slots : (j + 1) * slots] * swish_grad(value)
            valid = (row_at < item_bounds(length_ref, first + b)[-1]).astype(F32)
            grad_unit = grad * batch_ref[0:1, :]
            grad_ref[at, :] = grad_unit
            terms = (grad * unit, grad, grad_unit * valid, grad_unit * unit * valid)
            sums = [s + jnp.sum(t, axis=0, keepdims=True) for s, t in zip(sums, terms)]
    sum_ref[...] = jnp.concatenate(sums + [jnp.zeros((4, size), F32)])


def batch_back_call(pieces, lengths, first, conv, stats, batch_rows, out_weight, rows_held):
    mine, mate = pieces
    k, (slots, width) = len(mine), mine[0].shape
    size = conv.shape[1]
    return kernel_call(
        functools.partial(batch_back_kernel, k, first, rows_held),
        [shape(conv.shape, F32), shape((8, size), F32)],
        list(mine) + list(mate) + [conv, stats, batch_rows, out_weight],
        scalars=(lengths,),
        flops=2 * conv.shape[0] * width * size,
    )


def gate_back_kernel(k, first, tap_count, *refs):
    length_ref, refs = refs[0], refs[1:]
    grad_in_ref, conv_ref, gate_ref, stat_ref, sum_ref, column_ref, tap_ref, refs = (
        refs[0],
        refs[1],
        refs[2],
        refs[3],
        refs[4],
        refs[5],
        refs[6],
        refs[7:],
    )
    out_mine, out_mate, grad_ref, tap_grad_ref, glu_ref, conv_grad_ref = (
        refs[:k],
        refs[k],
        refs[k + 1],
        refs[k + 2],
        refs[k + 3],
        refs[k + 4],
    )
    slots, width = out_mine[0].shape
    size = tap_ref.shape[1]
    reach = tap_count // 2
    row_at = lax.broadcasted_iota(jnp.int32, (slots, size), 0)
    glu_ref[...] = jnp.zeros_like(glu_ref)
    conv_grad_ref[...] = jnp.zeros_like(conv_grad_ref)
    tap_grad_ref[...] = jnp.zeros_like(tap_grad_ref)
    frame_count = stat_ref[0:1, :]
    mean_grad = sum_ref[2:3, :] / frame_count
    mean_cross = sum_ref[3:4, :] / frame_count
    for i in range(k):
        halves = []
        for j in range(2):
            b = 2 * i + j
            at = pl.ds(b * slots, slots)
            before, behind, valid = item_reach(item_bounds(length_ref, first + b), row_at, slots)
            gate_a, gate_sig = gate_ref[at, :size], sigmoid(gate_ref[at, size:])
            glu_ref[PAD : PAD + slots, :] = gate_a * gate_sig * valid
            unit, inverse = batch_unit(conv_ref[at, :], stat_ref)
            conv_grad = valid * inverse * (grad_in_ref[at, :] - mean_grad - unit * mean_cross)
            conv_grad_ref[PAD : PAD + slots, :] = conv_grad
            grad_glu = jnp.zeros((slots, size), F32)
            for tap in range(tap_count):
                o = tap - reach
                near = glu_ref[PAD + o : PAD + o + slots, :]
                back = conv_grad_ref[PAD - o : PAD - o + slots, :]
                if o < 0:
                    near = jnp.where(before >= -o, near, 0.0)
                    back = jnp.where(behind >= -o, back, 0.0)
                elif o > 0:
                    near = jnp.where(behind >= o, near, 0.0)
                    back = jnp.where(before >= o, back, 0.0)
                grad_glu = grad_glu + back * tap_ref[tap : tap + 1, :]
                tap_grad_ref[tap : tap + 1, :] += jnp.sum(near * conv_grad, axis=0, keepdims=True)
            grad_glu = grad_glu * valid
            halves.append(
                jnp.concatenate(
                    [grad_glu * gate_sig, grad_glu * gate_a * gate_sig * (1.0 - gate_sig)], axis=1
                ).astype(BF16)
            )
        grad = jnp.concatenate(halves)
        grad_ref[pl.ds(2 * i * slots, 2 * slots), :] = grad
        store_partial(out_mine, out_mate, i, slots, square_product_back(grad, column_ref, width, 4 * size, 6 * size))


def gate_back_call(k, lengths, first, grad_unit, conv, gates, stats, sums, columns, taps, tap_count, slots, width):
    rows, size = conv.shape
    outs = [shape((slots, width), F32)] * k + [
        shape((k, slots, width), BF16),
        shape((rows, 2 * size), BF16),
        shape(taps.shape, F32),
    ]
    padded = pltpu.VMEM((slots + 2 * PAD, size), F32)
    result = kernel_call(
        functools.partial(gate_back_kernel, k, first, tap_count),
        outs,
        [grad_unit, conv, gates, stats, sums, columns, taps],
        scalars=(lengths,),
        flops=4 * rows * width * size + 80 * tap_count * rows * size,
        scratch=[padded, padded],
    )
    return (result[:k], result[k]), result[k + 1 :]


def join_kernel(count, coefficient, *refs):
    stream_ref, own_ref, mate_ref, refs = refs[0], refs[1], refs[2], refs[3:]
    far, norm_ref, stream_out, normed_ref = refs[:count], refs[count], refs[count + 1], refs[count + 2]
    branch = own_ref[...] + mate_ref[0].astype(F32)
    for ref in far:
        branch = branch + ref[...].astype(F32)
    stream = stream_ref[...].astype(F32) + coefficient * branch
    stream_out[...] = stream
    unit, _ = normalize(stream)
    normed_ref[...] = (unit * norm_ref[0:1, :] + norm_ref[1:2, :]).astype(BF16)


def join_call(stream, parts, coefficient, norm):
    own, mate, far = parts
    return kernel_call(
        functools.partial(join_kernel, len(far), coefficient),
        [shape(own.shape, F32), shape(own.shape, BF16)],
        [stream, own, mate] + list(far) + [norm],
    )


def turn_kernel(count, coefficient, *refs):
    length_ref, refs = refs[0], refs[1:]
    stream_ref, own_ref, mate_ref, refs = refs[0], refs[1], refs[2], refs[3:]
    far, norm_ref, cotangent_ref, refs = refs[:count], refs[count], refs[count + 1], refs[count + 2 :]
    output_ref, grad_out, low_out, norm_grad = refs
    branch = own_ref[...] + mate_ref[0].astype(F32)
    for ref in far:
        branch = branch + ref[...].astype(F32)
    stream = stream_ref[...] + coefficient * branch
    row_at = lax.broadcasted_iota(jnp.int32, (stream.shape[0], 1), 0)
    valid = (row_at < item_bounds(length_ref)[-1]).astype(F32)
    unit, scale = normalize(stream)
    output_ref[...] = ((unit * norm_ref[0:1, :] + norm_ref[1:2, :]) * valid).astype(BF16)
    norm_back(
        unit,
        scale,
        norm_ref,
        cotangent_ref[...].astype(F32) * valid,
        0.0,
        0.5,
        grad_out,
        low_out,
        norm_grad,
    )


def norm_back(unit, scale, norm_ref, grad, base, coefficient, grad_out, low_out, norm_grad):
    norm_grad[...] = jnp.concatenate(
        [jnp.sum(grad * unit, axis=0, keepdims=True), jnp.sum(grad, axis=0, keepdims=True)]
    )
    grad = grad * norm_ref[0:1, :]
    inner = jnp.mean(grad, axis=-1, keepdims=True)
    cross = jnp.mean(grad * unit, axis=-1, keepdims=True)
    grad = base + scale * (grad - inner - unit * cross)
    if grad_out is not None:
        grad_out[...] = grad
    low_out[...] = (coefficient * grad).astype(BF16)


def turn_call(stream, parts, coefficient, norm, cotangent, lengths):
    own, mate, far = parts
    return kernel_call(
        functools.partial(turn_kernel, len(far), coefficient),
        [
            shape(own.shape, BF16),
            shape(own.shape, F32),
            shape(own.shape, BF16),
            shape((2, own.shape[1]), F32),
        ],
        [stream, own, mate] + list(far) + [norm, cotangent],
        scalars=(lengths,),
    )


def join_back_kernel(count, coefficient, keep, *refs):
    stream_ref, grad_ref, own_ref, mate_ref, refs = refs[0], refs[1], refs[2], refs[3], refs[4:]
    far, norm_ref, refs = refs[:count], refs[count], refs[count + 1 :]
    grad_out, (low_out, norm_grad) = (refs[0] if keep else None), refs[-2:]
    grad = own_ref[...] + mate_ref[0].astype(F32)
    for ref in far:
        grad = grad + ref[...].astype(F32)
    unit, scale = normalize(stream_ref[...].astype(F32))
    norm_back(
        unit, scale, norm_ref, grad, grad_ref[...], coefficient, grad_out, low_out, norm_grad
    )


def join_back_call(stream, grad, parts, coefficient, norm, keep=True):
    own, mate, far = parts
    outs = [shape(own.shape, F32)] if keep else []
    return kernel_call(
        functools.partial(join_back_kernel, len(far), coefficient, keep),
        outs + [shape(own.shape, BF16), shape((2, own.shape[1]), F32)],
        [stream, grad, own, mate] + list(far) + [norm],
    )


def offset_table(slot_count, model_width):
    offsets = jnp.arange(2 * slot_count, dtype=F32) - (slot_count - 1)
    freqs = jnp.exp(-jnp.log(10000.0) * jnp.arange(0, model_width, 2, dtype=F32) / model_width)
    angles = offsets[:, None] * freqs[None, :]
    return jnp.concatenate([jnp.sin(angles), jnp.cos(angles)], axis=1)


def nesterov(weight, moment, average, grad_rows, rate, rate_scale):
    moment_new = MOMENTUM_DECAY * moment + grad_rows
    weight_new = weight - rate * rate_scale * (grad_rows + MOMENTUM_DECAY * moment_new)
    average_new = AVERAGE_DECAY * average + (1.0 - AVERAGE_DECAY) * weight_new
    return (moment_new, weight_new, average_new)


def head_lanes(member, i, sides, planes, size):
    side, rest = member % sides, member // sides
    plane = side * (planes // sides) + i
    return (plane * 4 + rest) * size


def split_down_kernel(weight_ref, first_ref, second_ref):
    hidden = first_ref.shape[1]
    rows = weight_ref.shape[1]
    for layer, out in enumerate((first_ref, second_ref)):
        for b in range(weight_ref.shape[2] // hidden):
            part = weight_ref[layer, :, b * hidden : (b + 1) * hidden]
            out[b * rows : (b + 1) * rows, :] = part.astype(BF16)


def split_up_kernel(weight_ref, first_ref, second_ref):
    team, _, hidden = first_ref.shape
    planes = weight_ref.shape[2] // (team * LANES)
    for layer, out in enumerate((first_ref, second_ref)):
        for t in range(team):
            for p in range(planes):
                at = (p * team + t) * LANES
                part = weight_ref[layer, :, at : at + LANES]
                out[t, :, p * LANES : (p + 1) * LANES] = part.astype(BF16)


def split_square_kernel(planes, sides, head_size, weight_ref, column_ref, mix_ref, conv_ref):
    team = column_ref.shape[0]
    width = weight_ref.shape[2]
    size = width // team
    for t in range(team):
        for i, matrix in enumerate((0, 1, 2, 4, 5, 6)):
            if i < 4:
                starts = [
                    head_lanes(t, h, sides, planes, head_size) for h in range(size // head_size)
                ]
                count = head_size
            else:
                count = size // planes
                starts = [(p * team + t) * count for p in range(planes)]
            parts = [weight_ref[matrix, :, at : at + count] for at in starts]
            column_ref[t, :, i * size : (i + 1) * size] = jnp.concatenate(parts, axis=1).astype(BF16)
    mix_ref[...] = weight_ref[3].astype(BF16)
    conv_ref[...] = weight_ref[7].astype(BF16)


def square_pack_kernel(side_ref, column_ref, own_ref, other_ref, conv_ref, out_ref):
    team, rows, lanes = column_ref.shape
    for b in range(lanes // BLOCK):
        for t in range(team):
            at = (b * team + t) * rows
            out_ref[at : at + rows, :] = column_ref[t, :, b * BLOCK : (b + 1) * BLOCK]
    base = (lanes // BLOCK) * team * rows
    low = side_ref[0] == 0
    for b in range(own_ref.shape[1] // BLOCK):
        lane = slice(b * BLOCK, (b + 1) * BLOCK)
        own, other = own_ref[:, lane].astype(F32), other_ref[:, lane].astype(F32)
        at = base + b * 3 * rows
        out_ref[at : at + rows, :] = jnp.where(low, own, other).astype(BF16)
        out_ref[at + rows : at + 2 * rows, :] = jnp.where(low, other, own).astype(BF16)
        out_ref[at + 2 * rows : at + 3 * rows, :] = conv_ref[:, lane]


def feed_pack_kernel(up_ref, down_ref, out_ref):
    team, rows, _ = up_ref.shape
    for t in range(team):
        out_ref[t * rows : (t + 1) * rows, :] = up_ref[t]
    out_ref[team * rows :, :] = down_ref[...]


def column_grad_kernel(mix_ref, conv_ref, out_ref):
    team, rows, lanes = out_ref.shape
    depth = team * rows
    for b in range(lanes // BLOCK):
        ref, at = (mix_ref, b) if b < 2 else (conv_ref, b - 2)
        for t in range(team):
            first = at * depth + t * rows
            out_ref[t, :, b * BLOCK : (b + 1) * BLOCK] = ref[first : first + rows, :]


def update(scale_ref, rate, index, grad, refs):
    weight_ref, moment_ref, average_ref, grad_out, moment_out, weight_out, average_out = refs
    moment = MOMENTUM_DECAY * moment_ref[index] + grad
    weight = weight_ref[index] - rate * scale_ref[0:1, 0:1] * (grad + MOMENTUM_DECAY * moment)
    grad_out[index] = grad
    moment_out[index] = moment
    weight_out[index] = weight
    average_out[index] = AVERAGE_DECAY * average_ref[index] + (1.0 - AVERAGE_DECAY) * weight


def update_up_kernel(scale_ref, first_ref, second_ref, *refs):
    team, _, hidden = first_ref.shape
    for layer, ref in enumerate((first_ref, second_ref)):
        parts = [
            ref[t, :, p * LANES : (p + 1) * LANES] for p in range(hidden // LANES) for t in range(team)
        ]
        update(scale_ref, RATE_UP, layer, jnp.concatenate(parts, axis=1).astype(F32), refs)


def update_down_kernel(scale_ref, first_ref, second_ref, *refs):
    rows, width = refs[0].shape[1:]
    hidden = first_ref.shape[1]
    for layer, ref in enumerate((first_ref, second_ref)):
        base = ref.shape[0] - rows * (width // hidden)
        parts = [
            ref[base + b * rows : base + (b + 1) * rows, :] for b in range(width // hidden)
        ]
        update(scale_ref, RATE_DOWN, layer, jnp.concatenate(parts, axis=1).astype(F32), refs)


def update_square_kernel(planes, sides, head_size, side_ref, *refs):
    scale_ref, column_ref, mix_ref, other_ref, conv_ref, refs = (
        refs[0],
        refs[1],
        refs[2],
        refs[3],
        refs[4],
        refs[5:],
    )
    team, rows, _ = column_ref.shape
    width = refs[0].shape[2]
    size = width // team
    per_side = planes // sides
    for i, matrix in enumerate((0, 1, 2, 4, 5, 6)):
        parts = []
        if i < 4:
            for head in range(width // head_size):
                plane, rest = head // 4, head % 4
                t = rest * sides + plane // per_side
                at = i * size + (plane % per_side) * head_size
                parts.append(column_ref[t, :, at : at + head_size])
        else:
            count = size // planes
            for p in range(planes):
                for t in range(team):
                    at = i * size + p * count
                    parts.append(column_ref[t, :, at : at + count])
        update(scale_ref, RATE_SQUARE, matrix, jnp.concatenate(parts, axis=1).astype(F32), refs)
    blocks = width // BLOCK
    head_rows = sides * rows
    base = mix_ref.shape[0] - blocks * head_rows
    parts = []
    for b in range(blocks):
        at = slice(base + b * head_rows, base + (b + 1) * head_rows)
        parts.append(mix_ref[at, :].astype(F32) + other_ref[at, :].astype(F32))
    whole = jnp.concatenate(parts, axis=1)
    update(scale_ref, RATE_SQUARE, 3, jnp.where(side_ref[0] == 0, whole[:rows], whole[rows:]), refs)
    base = conv_ref.shape[0] - blocks * rows
    parts = [conv_ref[base + b * rows : base + (b + 1) * rows, :] for b in range(blocks)]
    update(scale_ref, RATE_SQUARE, 7, jnp.concatenate(parts, axis=1).astype(F32), refs)


def update_call(body, scale, terms, weight, moment, average, scalars=()):
    return kernel_call(
        body,
        [shape(weight.shape, F32)] * 4,
        [scale] + list(terms) + [weight, moment, average],
        scalars=scalars,
    )


def feature_grad_kernel(planes, sides, *refs):
    member_ref, refs = refs[0], refs[1:]
    norms, near_ref, far_ref, out_ref = refs[:5], refs[5], refs[6], refs[7]
    team, _, size = out_ref.shape
    count = size // planes
    per_side = planes // sides
    head_size = sides * count
    bias = near_ref[...] + far_ref[...]
    rest, side = member_ref[0] // sides, member_ref[0] % sides
    rows = jnp.concatenate([n[0:1, :] for n in norms] + [n[1:2, :] for n in norms])
    for t in range(team):
        parts, own = [], []
        for p in range(planes):
            at = (p * team + t) * count
            parts.append(rows[:, at : at + count])
            at = (p % per_side) * head_size + (t % sides) * count
            held = (rest == t // sides) & (side == p // per_side)
            own.append(bias[:, at : at + count] * held.astype(jnp.int32).astype(F32))
        out_ref[t] = jnp.concatenate(
            [jnp.concatenate(parts, axis=1), jnp.concatenate(own, axis=1)]
        )


def channel_grad_kernel(taps, term_ref, near_ref, far_ref, sum_ref, out_ref):
    features = jnp.sum(term_ref[...], axis=0)
    out_ref[...] = jnp.concatenate(
        [near_ref[:taps] + far_ref[:taps], features[:10], sum_ref[0:2], features[10:12]]
    )


def make_step(planes, sides):
    wide_team = sides == 2
    team_axes = ("x", "c", "y") if wide_team else ("x", "c")
    team = 8 if wide_team else 4
    outer_bits = [("z", 1 << i) for i in range((planes - 1).bit_length())]
    if not wide_team:
        outer_bits += [("y", 1 << i) for i in range((sides - 1).bit_length())]
    head_aligned = wide_team and planes * 4 == HEADS

    def turn(values, first):
        pairs = []
        for x in range(2):
            for c in range(2):
                for y in range(2):
                    along_x = (c == 0) == first
                    to = (1 - x, c, y) if along_x else (x, c, 1 - y)
                    pairs.append((4 * x + 2 * c + y, 4 * to[0] + 2 * to[1] + to[2]))
        return lax.ppermute(values, team_axes, pairs)

    def gather(values):
        mate = swap(values, "c")
        if not wide_team:
            across = swap(values, "x")
            return ([values], [mate]), ([across], [swap(across, "c")])
        first, second = turn(values, True), turn(values, False)
        far = turn(first, False)
        near = ([values, first, second], [mate, swap(first, "c"), swap(second, "c")])
        return near, ([far], [swap(far, "c")])

    def scatter(near, far, fill=()):
        own_near, mate_near = near
        (own_far,), mate_far = far
        got_far = swap(mate_far, "c")
        got_near = swap(mate_near, "c")
        out_far = (own_far + got_far[0].astype(F32)).astype(BF16)
        if not wide_team:
            across, fill = lax.optimization_barrier((swap(out_far, "x"), fill))
            return (own_near[0], got_near, [across]), fill
        relay, fill = lax.optimization_barrier((turn(out_far, False), fill))
        second = (own_near[2] + got_near[2].astype(F32)).astype(BF16)
        from_second = turn(second, False)
        first = own_near[1] + got_near[1].astype(F32) + relay.astype(F32)
        from_first = turn(first.astype(BF16), True)
        return (own_near[0], got_near, [from_first, from_second]), fill

    def side_rows(rows):
        return rows if wide_team else lax.all_gather(rows, "y", axis=0, tiled=True)

    def side_scatter(rows):
        if wide_team:
            return rows
        return lax.psum_scatter(rows, "y", scatter_dimension=0, tiled=True)

    def split_hidden(rows):
        r, f = rows.shape
        return rows.reshape(r, planes, team, f // (planes * team)).transpose(2, 0, 1, 3).reshape(
            team, r, f // team
        )

    def join_hidden(blocks):
        _, r, f = blocks.shape
        return blocks.reshape(team, r, planes, f // planes).transpose(1, 2, 0, 3).reshape(
            r, team * f
        )

    def split_heads(rows):
        r, d = rows.shape
        if not head_aligned:
            return rows.reshape(r, team, d // team).transpose(1, 0, 2)
        size = d // HEADS
        rows = rows.reshape(r, sides, planes // sides, 2, 2, size)
        return rows.transpose(3, 4, 1, 0, 2, 5).reshape(team, r, d // team)

    def join_heads(blocks):
        _, r, f = blocks.shape
        if not head_aligned:
            return blocks.transpose(1, 0, 2).reshape(r, team * f)
        size = team * f // HEADS
        blocks = blocks.reshape(2, 2, sides, r, planes // sides, size)
        return blocks.transpose(3, 2, 4, 0, 1, 5).reshape(r, team * f)

    def team_swap(blocks):
        return lax.all_to_all(blocks, team_axes, split_axis=0, concat_axis=0, tiled=True)

    def plane_pieces(rows):
        return [rows] + [swap(rows, "z", d) for d in range(1, planes)]

    def plane_stack(ups, downs, plane):
        hidden = ups[0].shape[1]
        return kernel_call(
            functools.partial(stack_kernel, planes),
            [shape((planes, ups[0].shape[0] + downs[0].shape[0], hidden), BF16)],
            list(ups) + list(downs),
            scalars=(plane,),
        )[0]

    def plane_gather(rows):
        return lax.all_gather(rows, "z", axis=0, tiled=False)

    def plane_reduce(rows):
        return lax.psum_scatter(rows, "z", scatter_dimension=0, tiled=False)

    def to_blocks(rows, size):
        return jnp.concatenate([rows[:, i : i + size] for i in range(0, rows.shape[1], size)])

    def from_blocks(rows, count):
        return jnp.concatenate(jnp.split(rows, count), axis=1)

    def plane_scatter(pieces):
        total = pieces[0].astype(F32)
        for d in range(1, planes):
            total = total + swap(pieces[d], "z", d).astype(F32)
        return total

    def outer_sum(values):
        for axis, bit in outer_bits:
            values = values + swap(values, axis, bit)
        return values

    def step(
        frames,
        lengths,
        out_grad,
        up_weight,
        down_weight,
        square_weight,
        chan_weight,
        up_moment,
        down_moment,
        square_moment,
        chan_moment,
        up_average,
        down_average,
        square_average,
        chan_average,
    ):
        slots, width = frames.shape
        head_size = width // HEADS
        item_count = lengths.shape[1] - 1
        chan_rows = chan_weight.shape[0]
        tap_count = chan_rows - 14
        hidden = up_weight.shape[2]
        team_hidden = hidden // team
        team_width = width // team
        x_at, c_at, y_at = lax.axis_index("x"), lax.axis_index("c"), lax.axis_index("y")
        team_at = (x_at * 2 + c_at) * 2 + y_at if wide_team else x_at * 2 + c_at
        side = y_at.reshape(1).astype(jnp.int32)
        plane = lax.axis_index("z").reshape(1).astype(jnp.int32)

        chan_low = chan_weight.astype(BF16)
        if head_aligned:
            blocks = [shape((hidden // planes // team * (width // team_hidden), team_hidden), BF16)] * 2
            down_one, down_two = kernel_call(split_down_kernel, blocks, [down_weight])
            rows_in = up_weight.shape[1]
            blocks = [shape((team, rows_in, team_hidden), BF16)] * 2
            up_one, up_two = kernel_call(split_up_kernel, blocks, [up_weight])
            columns, mix, conv_out = kernel_call(
                functools.partial(split_square_kernel, planes, sides, head_size),
                [shape((team, rows_in, 6 * team_width), BF16)] + [shape((rows_in, width), BF16)] * 2,
                [square_weight],
            )
        else:
            up_low = up_weight.astype(BF16)
            down_low = down_weight.astype(BF16)
            square_low = square_weight.astype(BF16)
            down_one, down_two = [to_blocks(side_rows(down_low[i]), team_hidden) for i in (0, 1)]
            up_one, up_two = [split_hidden(side_rows(up_low[i])) for i in (0, 1)]
            columns = jnp.concatenate(
                [split_heads(side_rows(square_low[i])) for i in (0, 1, 2, 4)]
                + [split_hidden(side_rows(square_low[i])) for i in (5, 6)],
                axis=2,
            )
            mix, conv_out = square_low[3], side_rows(square_low[7])
        down_one = plane_pieces(down_one)
        up_one = team_swap(up_one).reshape(-1, team_hidden)
        near, far = gather(frames)

        if wide_team:
            lanes = jnp.pad(chan_low, ((0, LANES - chan_rows), (0, 0))).T
            carried = jnp.pad(
                lengths.astype(BF16), ((0, CARRY - 1), (0, LANES - lengths.shape[1]))
            )
            lanes = jnp.concatenate([lanes, carried])[None]
            for axis in ("y", "c", "x"):
                lanes = jnp.concatenate([lanes, swap(lanes, axis)])
            where_at = jnp.stack([plane[0], team_at, y_at, c_at]).astype(jnp.int32)
            norms = [shape((2, width), F32)] * 5
            params = kernel_call(
                functools.partial(channel_kernel, planes, sides, head_size),
                norms
                + [
                    shape((tap_count + 1, team_width), F32),
                    shape((2, team_width), F32),
                    shape((2, team_width), F32),
                    shape((team, lengths.shape[1]), jnp.int32),
                ],
                plane_pieces(lanes),
                scalars=(where_at,),
                scratch=[pltpu.VMEM((width, LANES), F32)],
            )
            norms, (taps, batch_rows, bias_rows, team_lengths) = params[:5], params[5:]
        else:
            team_lengths = jnp.concatenate(sum([chunk_order(p) for p in gather(lengths)], []))
            chan_float = lax.all_gather(chan_low, ALL, axis=1, tiled=True).astype(F32)

            def own_hidden(rows):
                rows = rows.reshape(rows.shape[0], planes, team, -1)
                rows = lax.dynamic_index_in_dim(rows, team_at, axis=2, keepdims=False)
                return rows.reshape(rows.shape[0], team_width)

            taps = own_hidden(chan_float[: tap_count + 1])
            batch_rows = own_hidden(chan_float[tap_count + 10 : tap_count + 12])
            bias_rows = lax.dynamic_index_in_dim(
                split_heads(chan_float[tap_count + 12 : tap_count + 14]), team_at, 0, False
            )
            norms = [
                jnp.stack([chan_float[tap_count + j], chan_float[tap_count + 5 + j]])
                for j in range(5)
            ]

        columns, up_two = team_swap(columns), team_swap(up_two)
        if head_aligned:
            head_rows = sides * rows_in
            per_side = planes // sides
            rows_held = (per_side, head_rows, rows_in)
            lines = 6 * team_width // BLOCK * team * rows_in + width // BLOCK * 3 * rows_in
            squares = kernel_call(
                square_pack_kernel,
                [shape((lines, BLOCK), BF16)],
                [columns, mix, swap(mix, "y"), conv_out],
                scalars=(side,),
            )[0]
            second = kernel_call(
                feed_pack_kernel,
                [shape((team * rows_in + down_two.shape[0], team_hidden), BF16)],
                [up_two, down_two],
            )[0]
        else:
            per_side = 0
            rows_held = (0, 0, conv_out.shape[0])
            mix = lax.all_gather(mix, ALL, axis=0, tiled=True)
            mix = lax.dynamic_slice_in_dim(mix, team_at * team_width, team_width, axis=0)
            columns = to_blocks(columns.reshape(-1, 6 * team_width), BLOCK)
            squares = jnp.concatenate([columns, to_blocks(conv_out, BLOCK)])
            second = jnp.concatenate([up_two.reshape(-1, team_hidden), down_two])
        table = offset_table(slots, width).astype(BF16)

        early = (near, far, norms, taps, team_lengths, down_one, table)
        up_one, early, squares, second, mix = lax.optimization_barrier(
            (up_one, early, squares, second, mix)
        )
        up_one = plane_pieces(up_one)
        up_one, early, squares, second, mix = lax.optimization_barrier(
            (up_one, early, squares, second, mix)
        )
        near, far, norms, taps, team_lengths, down_one, table = early
        squares = plane_gather(squares)
        if head_aligned:
            mix = squares
        pack_one = plane_stack(up_one, down_one, plane)

        part_near, (before_near, active_near, normed_near) = forward_call(near, pack_one, norms[0])
        part_far, (before_far, active_far, normed_far) = forward_call(far, pack_one, norms[0])
        saved_one = ([normed_near, normed_far], (before_near, before_far), [active_near, active_far])
        parts, _ = scatter(part_near, part_far)
        stream_one, normed = join_call(frames, parts, 0.5, norms[1])
        normed, second = lax.optimization_barrier((normed, second))
        pack_two = plane_gather(second)

        near, far = gather(normed)
        place = kernel_call(
            place_kernel,
            [shape((table.shape[0], team_width), BF16)],
            [table, squares],
            flops=2 * table.shape[0] * width * team_width,
        )[0]
        normed_two = chunk_order(near) + chunk_order(far)
        part_near, saved_near = attention_call(
            near, team_lengths, 0, side, squares, mix, rows_held, bias_rows, place, head_size
        )
        part_far, saved_far = attention_call(
            far, team_lengths, 2 * len(near[0]), side, squares, mix, rows_held, bias_rows, place, head_size
        )
        parts, _ = scatter(part_near, part_far)
        stream_two, normed = join_call(stream_one, parts, 1.0, norms[2])

        near, far = gather(normed)
        normed_three = chunk_order(near) + chunk_order(far)
        k_near, k_far = len(near[0]), len(far[0])
        gates_near, conv_near, stats_near = gate_call(
            near, team_lengths, 0, squares, taps, tap_count
        )
        gates_far, conv_far, stats_far = gate_call(
            far, team_lengths, 2 * k_near, squares, taps, tap_count
        )
        stats = merge(stats_near, stats_far)
        for axis, bit in outer_bits:
            stats = merge(stats, swap(stats, axis, bit))
        part_far, act_far = batch_call(
            k_far, conv_far, stats, batch_rows, squares, rows_held, slots, width
        )
        part_near, act_near = batch_call(
            k_near, conv_near, stats, batch_rows, squares, rows_held, slots, width
        )
        active_conv = [act_near, act_far]
        parts, _ = scatter(part_near, part_far)
        stream_three, normed = join_call(stream_two, parts, 1.0, norms[3])
        normed, pack_two = lax.optimization_barrier((normed, pack_two))

        near, far = gather(normed)
        part_near, (before_near, active_near) = forward_call(near, pack_two)
        part_far, (before_far, active_far) = forward_call(far, pack_two)
        saved_four = (
            chunk_order(near) + chunk_order(far),
            (before_near, before_far),
            [active_near, active_far],
        )
        parts, _ = scatter(part_near, part_far)
        output, grad_four, low, norm_four = turn_call(
            stream_three, parts, 0.5, norms[4], out_grad, lengths
        )

        def feed_backward(low, pack, saved, by_plane):
            normed, (before_near, before_far), active = saved
            near, far = gather(low)
            part_near, grad_near = backward_call(near, pack, before_near)
            part_far, grad_far = backward_call(far, pack, before_far)
            rows = chunk_order(near) + chunk_order(far)
            term = feed_weight_call(
                normed, [grad_near, grad_far], active, rows, plane, planes, by_plane
            )
            return scatter(part_near, part_far, term)

        parts, (second_term,) = feed_backward(low, pack_two, saved_four, True)
        grad_three, low, norm_three = join_back_call(stream_three, grad_four, parts, 1.0, norms[3])
        low, second_term = lax.optimization_barrier((low, second_term))
        second_term = plane_reduce(second_term)

        near, far = gather(low)
        grad_near, sums_near = batch_back_call(
            near, team_lengths, 0, conv_near, stats, batch_rows, squares, rows_held
        )
        grad_far, sums_far = batch_back_call(
            far, team_lengths, 2 * k_near, conv_far, stats, batch_rows, squares, rows_held
        )
        conv_grads = chunk_order(near) + chunk_order(far)
        local_sums = sums_near + sums_far
        sums = outer_sum(local_sums)
        part_far, (gate_grad_far, taps_far) = gate_back_call(
            k_far, team_lengths, 2 * k_near, grad_far, conv_far, gates_far, stats, sums, squares, taps,
            tap_count, slots, width,
        )
        part_near, (gate_grad_near, taps_near) = gate_back_call(
            k_near, team_lengths, 0, grad_near, conv_near, gates_near, stats, sums, squares, taps,
            tap_count, slots, width,
        )
        conv_term = conv_weight_call(
            normed_three, [gate_grad_near, gate_grad_far], active_conv, conv_grads, plane, planes
        )
        parts, conv_term = scatter(part_near, part_far, conv_term)
        grad_two, low, norm_two = join_back_call(stream_two, grad_three, parts, 1.0, norms[2])
        low, conv_term, second_term = lax.optimization_barrier((low, conv_term, second_term))
        conv_term = plane_reduce(conv_term)

        near, far = gather(low)
        part_near, (qkv_near, place_near, bias_near) = attention_back_call(
            near, side, squares, mix, rows_held, place, saved_near[0], saved_near[1], head_size
        )
        part_far, (qkv_far, place_far, bias_far) = attention_back_call(
            far, side, squares, mix, rows_held, place, saved_far[0], saved_far[1], head_size
        )
        mixed, rows = [saved_near[2], saved_far[2]], chunk_order(near) + chunk_order(far)
        mix_term = mix_weight_call(
            normed_two, [qkv_near, qkv_far], mixed, rows, [table, place_near, place_far], plane,
            side, planes, per_side,
        )
        parts, mix_term = scatter(part_near, part_far, mix_term)
        if not head_aligned:
            mix_own = mm_tn(jnp.concatenate(mixed), jnp.concatenate(rows)).astype(BF16)
            mix_own = lax.dynamic_update_slice_in_dim(
                jnp.zeros((width, width), BF16), mix_own, team_at * team_width, axis=0
            )
        grad_one, low, norm_one = join_back_call(stream_one, grad_two, parts, 0.5, norms[1])
        low, mix_term, conv_term = lax.optimization_barrier((low, mix_term, conv_term))
        mix_term = plane_reduce(mix_term)

        parts, first_term = feed_backward(low, pack_one, saved_one, False)
        first_term = plane_scatter(first_term)
        frames_grad, norm_zero = join_back_call(frames, grad_one, parts, 1.0, norms[0], keep=False)

        late = (second_term, conv_term, mix_term)
        frames_grad, late = lax.optimization_barrier((frames_grad, late))
        second_term, conv_term, mix_term = late
        depth = width // planes
        rate_scale = lax.rsqrt(stats[0:1])

        def from_team(rows, columns):
            return team_swap(rows.astype(BF16).reshape(team, -1, columns))

        def finish_channels(chan_term):
            chan_term = outer_sum(chan_term).reshape(chan_rows, planes, -1)
            chan_term = lax.dynamic_index_in_dim(chan_term, lax.axis_index("z"), 1, keepdims=False)
            if not wide_team:
                chan_term = lax.dynamic_index_in_dim(
                    chan_term.reshape(chan_rows, sides, -1), y_at, 1, keepdims=False
                )
            return chan_term

        norm_terms = [norm_zero, norm_one, norm_two, norm_three, norm_four]
        if head_aligned:
            second_up = from_team(second_term[:depth], team_hidden)
            features = kernel_call(
                functools.partial(feature_grad_kernel, planes, sides),
                [shape((team, 12, team_width), F32)],
                norm_terms + [bias_near, bias_far],
                scalars=(team_at.reshape(1).astype(jnp.int32),),
            )[0]
            chan_term = kernel_call(
                functools.partial(channel_grad_kernel, tap_count),
                [shape((chan_rows, team_width), F32)],
                [team_swap(features), taps_near, taps_far, local_sums],
            )[0]
            chan_grad = finish_channels(chan_term)
            blocks = kernel_call(
                column_grad_kernel,
                [shape((team, rows_in, 6 * team_width), BF16)],
                [mix_term, conv_term],
            )[0]
            square_all = update_call(
                functools.partial(update_square_kernel, planes, sides, head_size),
                rate_scale,
                [team_swap(blocks), mix_term, swap(mix_term, "y"), conv_term],
                square_weight,
                square_moment,
                square_average,
                scalars=(side,),
            )
            first_term, square_all, chan_grad, second_up = lax.optimization_barrier(
                (first_term, square_all, chan_grad, second_up)
            )
            first_term = first_term.astype(BF16)
            down_all = update_call(
                update_down_kernel,
                rate_scale,
                [first_term, second_term],
                down_weight,
                down_moment,
                down_average,
            )
            up_all = update_call(
                update_up_kernel,
                rate_scale,
                [from_team(first_term[:depth], team_hidden), second_up],
                up_weight,
                up_moment,
                up_average,
            )
            up_grad, up_new = up_all[0], up_all[1:]
            down_grad, down_new = down_all[0], down_all[1:]
            square_grad, square_new = square_all[0], square_all[1:]
            rate_scale = rate_scale[0, 0]
        else:
            column_blocks = 4 * team_width // BLOCK
            qkv_term = from_blocks(mix_term[: column_blocks * depth], column_blocks)
            gate_blocks = 2 * team_width // BLOCK
            gate_term = from_blocks(conv_term[: gate_blocks * depth], gate_blocks)
            conv_out_term = from_blocks(conv_term[gate_blocks * depth :], width // BLOCK)
            mix_grad = lax.psum_scatter(mix_own, ALL, scatter_dimension=0, tiled=True).astype(F32)
            blocks = from_team(jnp.concatenate([qkv_term, gate_term], axis=1), 6 * team_width)

            def block(i):
                return blocks[:, :, i * team_width : (i + 1) * team_width]

            square_grad = jnp.stack(
                [side_scatter(join_heads(block(i))).astype(F32) for i in range(3)]
                + [mix_grad, side_scatter(join_heads(block(3))).astype(F32)]
                + [side_scatter(join_hidden(block(i))).astype(F32) for i in (4, 5)]
                + [side_scatter(conv_out_term).astype(F32)]
            )
            bias_terms = join_heads(
                lax.dynamic_update_slice_in_dim(
                    jnp.zeros((team, 2, team_width), F32), (bias_near + bias_far)[None], team_at, 0
                )
            )
            features = jnp.concatenate(
                [t[0:1] for t in norm_terms] + [t[1:2] for t in norm_terms] + [bias_terms]
            )
            features = jnp.sum(team_swap(split_hidden(features)), axis=0)
            chan_grad = finish_channels(
                jnp.concatenate(
                    [
                        (taps_near + taps_far)[:tap_count],
                        features[:10],
                        local_sums[:2],
                        features[10:],
                    ]
                )
            )
            feed_terms = (first_term.astype(BF16), second_term)
            up_grad = jnp.stack(
                [
                    side_scatter(join_hidden(from_team(rows[:depth], team_hidden))).astype(F32)
                    for rows in feed_terms
                ]
            )
            down_grad = jnp.stack(
                [
                    side_scatter(from_blocks(rows[depth:], width // team_hidden)).astype(F32)
                    for rows in feed_terms
                ]
            )
            rate_scale = rate_scale[0, 0]
            up_new = nesterov(up_weight, up_moment, up_average, up_grad, RATE_UP, rate_scale)
            down_new = nesterov(
                down_weight, down_moment, down_average, down_grad, RATE_DOWN, rate_scale
            )
            square_new = nesterov(
                square_weight, square_moment, square_average, square_grad, RATE_SQUARE, rate_scale
            )
        chan_new = nesterov(
            chan_weight, chan_moment, chan_average, chan_grad, RATE_CHANNEL, rate_scale
        )
        bias_grad = chan_grad[tap_count + 12 : tap_count + 14]
        return (
            output,
            frames_grad,
            up_grad,
            down_grad,
            square_grad,
            chan_grad,
            up_new[0],
            down_new[0],
            square_new[0],
            chan_new[0],
            up_new[1],
            down_new[1],
            square_new[1],
            chan_new[1],
            up_new[2],
            down_new[2],
            square_new[2],
            chan_new[2],
            bias_grad,
        )

    return step


def solution(mesh):
    wide, narrow = mesh.shape["wide"], mesh.shape["narrow"]
    planes = wide // 4
    inner = Mesh(mesh.devices.reshape(planes, 2, 2, narrow), ALL)
    token = P(ALL, None)
    matrix = P(None, ALL, None)
    vector = P(None, ALL)
    group = (matrix, matrix, matrix, vector)
    return jax.shard_map(
        make_step(planes, narrow),
        mesh=inner,
        in_specs=(token, token, token) + group * 3,
        out_specs=(token, token) + group * 4 + (vector,),
        check_vma=False,
    )
```

```python
import functools

import jax
import jax.numpy as jnp
from jax import lax
from jax.experimental import pallas as pl
from jax.experimental.pallas import tpu as pltpu
from jax.sharding import Mesh
from jax.sharding import PartitionSpec as P

HEADS = 16
EPSILON = 1e-05
MOMENTUM_DECAY = 0.9
AVERAGE_DECAY = 0.9
RATE_UP = 0.05
RATE_DOWN = 0.026
RATE_SQUARE = 0.05
RATE_CHANNEL = 0.5
MASKED_SCORE = -1e30
BF16 = jnp.bfloat16
F32 = jnp.float32
ALL = ("z", "x", "c", "y")
LANES = 128
PAD = 16
BLOCK = 256
CARRY = 16
ROOM = 6 << 20


def mm(left, right):
    return jnp.dot(left, right, preferred_element_type=F32)


def mm_tn(left, right):
    return lax.dot_general(left, right, (((0,), (0,)), ((), ())), preferred_element_type=F32)


def mm_nt(left, right):
    return lax.dot_general(left, right, (((1,), (1,)), ((), ())), preferred_element_type=F32)


def swap(values, axis, bit=1):
    size = lax.axis_size(axis)
    return lax.ppermute(values, axis, [(i, i ^ bit) for i in range(size)])


def sigmoid(values):
    return 1.0 / (1.0 + jnp.exp(-values))


def swish_grad(values):
    sig = sigmoid(values)
    return sig * (1.0 + values * (1.0 - sig))


def normalize(values):
    centre = values - jnp.mean(values, axis=-1, keepdims=True)
    scale = lax.rsqrt(jnp.mean(centre * centre, axis=-1, keepdims=True) + EPSILON)
    return centre * scale, scale


def shape(dims, dtype):
    return jax.ShapeDtypeStruct(tuple(dims), dtype)


def size_of(item):
    total = 1
    for n in item.shape:
        total *= n
    return total * item.dtype.itemsize


def kernel_call(body, outs, args, scalars=(), flops=0, scratch=()):
    moved = sum(size_of(a) for a in args) + sum(size_of(o) for o in outs)
    return pl.pallas_call(
        body,
        out_shape=tuple(outs),
        in_specs=[pl.BlockSpec(memory_space=pltpu.SMEM)] * len(scalars)
        + [pl.BlockSpec(memory_space=pltpu.VMEM)] * len(args),
        out_specs=tuple(pl.BlockSpec(memory_space=pltpu.VMEM) for _ in outs),
        scratch_shapes=list(scratch),
        compiler_params=pltpu.CompilerParams(vmem_limit_bytes=moved + ROOM),
        cost_estimate=pl.CostEstimate(flops=int(flops), bytes_accessed=moved, transcendentals=0),
    )(*scalars, *args)


def store_partial(mine_refs, mate_ref, i, slots, value):
    mine_refs[i][...] = value[:slots]
    mate_ref[i] = value[slots:].astype(BF16)


def up_product(rows, ref):
    planes = ref.shape[0]
    depth = rows.shape[1] // planes
    total = mm(rows[:, :depth], ref[0, :depth, :])
    for p in range(1, planes):
        total = total + mm(rows[:, p * depth : (p + 1) * depth], ref[p, :depth, :])
    return total


def up_product_back(rows, ref, width):
    planes = ref.shape[0]
    depth = width // planes
    return jnp.concatenate([mm_nt(rows, ref[p, :depth, :]) for p in range(planes)], axis=1)


def down_blocks(ref, width):
    planes, hidden = ref.shape[0], ref.shape[2]
    depth, rows = width // planes, hidden // planes
    return [
        jnp.concatenate(
            [ref[p, depth + b * rows : depth + (b + 1) * rows, :] for p in range(planes)]
        )
        for b in range(width // hidden)
    ]


def down_product(rows, blocks):
    return jnp.concatenate([mm(rows, block) for block in blocks], axis=1)


def down_product_back(rows, blocks):
    size = blocks[0].shape[1]
    total = mm_nt(rows[:, :size], blocks[0])
    for b in range(1, len(blocks)):
        total = total + mm_nt(rows[:, b * size : (b + 1) * size], blocks[b])
    return total


def square_columns(ref, p, depth, first, last):
    parts = []
    while first < last:
        block = first // BLOCK
        stop = min(last, (block + 1) * BLOCK)
        lanes = slice(first - block * BLOCK, stop - block * BLOCK)
        parts.append(ref[p, block * depth : (block + 1) * depth, lanes])
        first = stop
    return jnp.concatenate(parts, axis=1) if len(parts) > 1 else parts[0]


def square_product(rows, ref, first, last):
    planes = ref.shape[0]
    depth = rows.shape[1] // planes
    total = None
    for p in range(planes):
        term = mm(rows[:, p * depth : (p + 1) * depth], square_columns(ref, p, depth, first, last))
        total = term if total is None else total + term
    return total


def square_product_back(rows, ref, width, first, last):
    planes = ref.shape[0]
    depth = width // planes
    return jnp.concatenate(
        [mm_nt(rows, square_columns(ref, p, depth, first, last)) for p in range(planes)], axis=1
    )


def output_rows(ref, p, width, size, mix, conv, want_mix):
    base = (6 * size // BLOCK) * (width // ref.shape[0])
    parts = []
    for b in range(width // BLOCK):
        at = base + b * (mix + conv) + (0 if want_mix else mix)
        rows = ref[pl.ds(p, 1), at : at + (mix if want_mix else conv), :]
        parts.append(rows.reshape(rows.shape[1:]))
    return jnp.concatenate(parts, axis=1)


def forward_kernel(k, with_norm, *refs):
    mine, mate, refs = refs[:k], refs[k : 2 * k], refs[2 * k :]
    if with_norm:
        norm_ref, refs = refs[0], refs[1:]
    pack_ref, refs = refs[0], refs[1:]
    out_mine, out_mate, before_ref, active_ref = refs[:k], refs[k], refs[k + 1], refs[k + 2]
    slots, width = mine[0].shape
    blocks = down_blocks(pack_ref, width)
    for i in range(k):
        rows = jnp.concatenate([mine[i][...], mate[i][...]])
        at = pl.ds(2 * i * slots, 2 * slots)
        if with_norm:
            unit, _ = normalize(rows.astype(F32))
            rows = (unit * norm_ref[0:1, :] + norm_ref[1:2, :]).astype(BF16)
            refs[k + 3][at, :] = rows
        before = up_product(rows, pack_ref)
        before_ref[at, :] = before
        active = (before * sigmoid(before)).astype(BF16)
        active_ref[at, :] = active
        store_partial(out_mine, out_mate, i, slots, down_product(active, blocks))


def forward_call(pieces, pack, norm=None):
    mine, mate = pieces
    k, (slots, width) = len(mine), mine[0].shape
    hidden = pack.shape[2]
    rows = 2 * k * slots
    outs = [shape((slots, width), F32)] * k + [
        shape((k, slots, width), BF16),
        shape((rows, hidden), F32),
        shape((rows, hidden), BF16),
    ]
    args = list(mine) + list(mate)
    if norm is not None:
        outs.append(shape((rows, width), BF16))
        args.append(norm)
    result = kernel_call(
        functools.partial(forward_kernel, k, norm is not None),
        outs,
        args + [pack],
        flops=4 * rows * width * hidden,
    )
    return (result[:k], result[k]), result[k + 1 :]


def backward_kernel(k, *refs):
    mine, mate, refs = refs[:k], refs[k : 2 * k], refs[2 * k :]
    pack_ref, before_ref, refs = refs[0], refs[1], refs[2:]
    out_mine, out_mate, grad_ref = refs[:k], refs[k], refs[k + 1]
    slots, width = mine[0].shape
    blocks = down_blocks(pack_ref, width)
    for i in range(k):
        at = pl.ds(2 * i * slots, 2 * slots)
        rows = jnp.concatenate([mine[i][...], mate[i][...]])
        grad = down_product_back(rows, blocks) * swish_grad(before_ref[at, :])
        grad = grad.astype(BF16)
        grad_ref[at, :] = grad
        store_partial(out_mine, out_mate, i, slots, up_product_back(grad, pack_ref, width))


def backward_call(pieces, pack, before):
    mine, mate = pieces
    k, (slots, width) = len(mine), mine[0].shape
    rows, hidden = before.shape
    outs = [shape((slots, width), F32)] * k + [
        shape((k, slots, width), BF16),
        shape((rows, hidden), BF16),
    ]
    result = kernel_call(
        functools.partial(backward_kernel, k),
        outs,
        list(mine) + list(mate) + [pack, before],
        flops=4 * rows * width * hidden,
    )
    return (result[:k], result[k]), result[k + 1]


def joined(refs):
    return jnp.concatenate([r[...] for r in refs])


def take(refs, counts):
    groups, at = [], 0
    for n in counts:
        groups.append(refs[at : at + n])
        at += n
    return groups + [refs[at:]]


def put(out_ref, planes, write):
    for p in range(planes):
        write(out_ref.at[p], p)


def rows_at(ref, p, rows, lanes=slice(None)):
    return ref[pl.ds(pl.multiple_of(p * rows, rows), rows), lanes]


def feed_weight_kernel(counts, planes, *refs):
    normed, grads, active, rows, refs = take(refs, counts)
    out_ref, up_ref, down_ref = refs
    width, hidden = up_ref.shape
    depth, below = width // planes, hidden // planes
    down_ref[...] = mm_tn(joined(active), joined(rows))
    up_ref[...] = mm_tn(joined(normed), joined(grads))

    def write(out, p):
        out[:depth, :] = rows_at(up_ref, p, depth).astype(BF16)
        for b in range(width // hidden):
            at = depth + b * below
            lanes = slice(b * hidden, (b + 1) * hidden)
            out[at : at + below, :] = rows_at(down_ref, p, below, lanes).astype(BF16)

    put(out_ref, planes, write)


def feed_weight_call(normed, grads, active, rows, planes):
    width, hidden = normed[0].shape[1], grads[0].shape[1]
    lines = width // planes + (hidden // planes) * (width // hidden)
    groups = (normed, grads, active, rows)
    tokens = sum(a.shape[0] for a in grads)
    return kernel_call(
        functools.partial(feed_weight_kernel, [len(g) for g in groups], planes),
        [shape((planes, lines, hidden), BF16)],
        [a for g in groups for a in g],
        flops=4 * width * hidden * tokens,
        scratch=[pltpu.VMEM((width, hidden), F32), pltpu.VMEM((hidden, width), F32)],
    )[0]


def write_columns(out, total_ref, p, depth):
    for b in range(total_ref.shape[1] // BLOCK):
        lanes = slice(b * BLOCK, (b + 1) * BLOCK)
        out[b * depth : (b + 1) * depth, :] = rows_at(total_ref, p, depth, lanes).astype(BF16)


def write_output_rows(out, base, rows):
    count = rows.shape[0]
    for b in range(rows.shape[1] // BLOCK):
        at = base + b * count
        out[at : at + count, :] = rows[:, b * BLOCK : (b + 1) * BLOCK].astype(BF16)


def conv_weight_kernel(counts, planes, *refs):
    normed, grads, active, rows, refs = take(refs, counts)
    out_ref, gate_ref, row_ref = refs
    depth = gate_ref.shape[0] // planes
    below = row_ref.shape[0] // planes
    base = (gate_ref.shape[1] // BLOCK) * depth
    gate_ref[...] = mm_tn(joined(normed), joined(grads))
    row_ref[...] = mm_tn(joined(active), joined(rows))

    def write(out, p):
        write_columns(out, gate_ref, p, depth)
        write_output_rows(out, base, rows_at(row_ref, p, below))

    put(out_ref, planes, write)


def conv_weight_call(normed, grads, active, rows, planes):
    width, gates, size = normed[0].shape[1], grads[0].shape[1], active[0].shape[1]
    lines = (gates // BLOCK) * (width // planes) + (width // BLOCK) * (size // planes)
    groups = (normed, grads, active, rows)
    tokens = sum(a.shape[0] for a in grads)
    return kernel_call(
        functools.partial(conv_weight_kernel, [len(g) for g in groups], planes),
        [shape((planes, lines, BLOCK), BF16)],
        [a for g in groups for a in g],
        flops=2 * width * (gates + size) * tokens,
        scratch=[pltpu.VMEM((width, gates), F32), pltpu.VMEM((size, width), F32)],
    )[0]


def mix_weight_kernel(counts, planes, per_side, *refs):
    side_ref, refs = refs[0], refs[1:]
    normed, grads, mixed, rows, place, refs = take(refs, counts)
    table_ref, place = place[0], place[1:]
    out_ref, total_ref, row_ref = refs
    depth = total_ref.shape[0] // planes
    base = (total_ref.shape[1] // BLOCK) * depth
    right = joined(grads)
    qkv = right.shape[1]
    total_ref[:, :qkv] = mm_tn(joined(normed), right)
    position = sum(ref[...] for ref in place)
    total_ref[:, qkv:] = mm_tn(table_ref[...], position.astype(BF16))
    if per_side:
        row_ref[...] = mm_tn(joined(mixed), joined(rows))

    def write(out, p):
        write_columns(out, total_ref, p, depth)
        if per_side:
            below = row_ref.shape[0] // per_side
            place = p - side_ref[0] * per_side
            held = (place >= 0) & (place < per_side)
            share = held.astype(jnp.int32).astype(F32)
            head = rows_at(row_ref, jnp.where(held, place, 0), below) * share
            write_output_rows(out, base, head)

    put(out_ref, planes, write)


def mix_weight_call(normed, grads, mixed, rows, place, side, planes, per_side):
    width, qkv, size = normed[0].shape[1], grads[0].shape[1], mixed[0].shape[1]
    total = qkv + size
    lines = (total // BLOCK) * (width // planes)
    if per_side:
        lines += (width // BLOCK) * (size // per_side)
    groups = (normed, grads, mixed, rows, place)
    tokens = sum(a.shape[0] for a in grads)
    return kernel_call(
        functools.partial(mix_weight_kernel, [len(g) for g in groups], planes, per_side),
        [shape((planes, lines, BLOCK), BF16)],
        [a for g in groups for a in g],
        scalars=(side,),
        flops=2 * width * (total + size) * tokens,
        scratch=[pltpu.VMEM((width, total), F32), pltpu.VMEM((size, width), F32)],
    )[0]


def channel_kernel(planes, sides, head_size, *refs):
    at_ref, pieces, refs = refs[0], refs[1 : 1 + planes], refs[1 + planes :]
    norm_refs, (tap_ref, batch_ref, bias_ref, length_ref, wide_ref) = refs[:5], refs[5:]
    plane, member, side, core = at_ref[0], at_ref[1], at_ref[2], at_ref[3]
    team, rows = pieces[0].shape[0], pieces[0].shape[1] - CARRY
    size = tap_ref.shape[1]
    listed = [pieces[0][m, rows : rows + 1, :].astype(F32) for m in range(team)]
    one = jnp.concatenate([listed[4], listed[3]])
    two = jnp.concatenate([listed[1], listed[6]])
    table = [
        listed[0],
        listed[2],
        jnp.where(core == 0, one, two),
        jnp.where(core == 0, two, one),
        listed[5],
        listed[7],
    ]
    length_ref[...] = jnp.concatenate(table).astype(jnp.int32)[:, : length_ref.shape[1]]
    for d in range(planes):
        for m in range(team):
            at = ((plane ^ d) * team + (member ^ m)) * rows
            wide_ref[pl.ds(pl.multiple_of(at, rows), rows), :] = pieces[d][m, :rows, :].astype(F32)
    every = wide_ref[...].T
    taps = tap_ref.shape[0] - 1
    for j in range(5):
        first = every[taps + j : taps + j + 1]
        norm_refs[j][...] = jnp.concatenate([first, every[taps + 5 + j : taps + 6 + j]])
    own = [
        wide_ref[pl.ds(pl.multiple_of((p * team + member) * rows, rows), rows), :]
        for p in range(planes)
    ]
    own = jnp.concatenate(own).T
    tap_ref[...] = own[: taps + 1]
    batch_ref[...] = own[taps + 10 : taps + 12]
    heads = size // head_size
    own = [
        wide_ref[
            pl.ds(
                pl.multiple_of(
                    (side * heads + h) * team * rows + (member // sides) * head_size, head_size
                ),
                head_size,
            ),
            :,
        ]
        for h in range(heads)
    ]
    own = jnp.concatenate(own).T
    bias_ref[...] = own[taps + 12 : taps + 14]


def chunk_order(groups):
    return [chunk for group in groups for pair in zip(*group) for chunk in pair]


def add_kernel(count, *refs):
    own_ref, mate_ref, out_ref = refs[0], refs[1], refs[-1]
    total = own_ref[...] + mate_ref[count].astype(F32)
    for ref in refs[2:-1]:
        total = total + ref[...].astype(F32)
    out_ref[...] = total.astype(BF16)


def add_call(own, mate, index, *more):
    return kernel_call(
        functools.partial(add_kernel, index), [shape(own.shape, BF16)], [own, mate] + list(more)
    )[0]


def item_bounds(length_ref, b=0):
    ends = [length_ref[b, 0]]
    for j in range(1, length_ref.shape[1] - 1):
        ends.append(ends[-1] + length_ref[b, j])
    return ends


def item_index(ends, where_at):
    total = (where_at >= ends[0]).astype(jnp.int32)
    for end in ends[1:]:
        total = total + (where_at >= end).astype(jnp.int32)
    return total


def head_masks(slots, head_size):
    lane = lax.broadcasted_iota(jnp.int32, (slots, LANES), 1)
    return [
        (lane >= h * head_size) & (lane < (h + 1) * head_size) for h in range(LANES // head_size)
    ]


def attention_kernel(k, first, head_size, rows_held, *refs):
    length_ref, side_ref, refs = refs[0], refs[1], refs[2:]
    mine, mate, refs = refs[:k], refs[k : 2 * k], refs[2 * k :]
    column_ref, mix_ref, bias_ref, place_ref, refs = refs[0], refs[1], refs[2], refs[3], refs[4:]
    out_mine, out_mate, saved_ref, probs_ref, mixed_ref = (
        refs[:k],
        refs[k],
        refs[k + 1],
        refs[k + 2],
        refs[k + 3],
    )
    slots, width = mine[0].shape
    size = place_ref.shape[1]
    mix = mix_rows(mix_ref, side_ref, width, size, rows_held)
    scale = head_size ** (-0.5)
    row_at = lax.broadcasted_iota(jnp.int32, (slots, slots), 0)
    column_at = lax.broadcasted_iota(jnp.int32, (slots, slots), 1)
    masks = head_masks(slots, head_size)
    for i in range(k):
        rows = jnp.concatenate([mine[i][...], mate[i][...]])
        qkv = square_product(rows, column_ref, 0, 3 * size)
        query = qkv[:, :size]
        query_c = (query + bias_ref[0:1, :]).astype(BF16)
        query_p = (query + bias_ref[1:2, :]).astype(BF16)
        key = qkv[:, size : 2 * size].astype(BF16)
        value = qkv[:, 2 * size :].astype(BF16)
        at = pl.ds(2 * i * slots, 2 * slots)
        saved_ref[at, 0:size] = query_c
        saved_ref[at, size : 2 * size] = query_p
        saved_ref[at, 2 * size : 3 * size] = key
        saved_ref[at, 3 * size : 4 * size] = value
        halves = []
        for j in range(2):
            b = 2 * i + j
            part = slice(j * slots, (j + 1) * slots)
            ends = item_bounds(length_ref, first + b)
            same = item_index(ends, row_at) == item_index(ends, column_at)
            blocks = []
            for lo in range(0, size, LANES):
                lanes = slice(lo, lo + LANES)
                mixed = jnp.zeros((slots, LANES), F32)
                for h, mask in enumerate(masks):
                    qc = jnp.where(mask, query_c[part, lanes], 0)
                    qp = jnp.where(mask, query_p[part, lanes], 0)
                    wide = mm_nt(qp, place_ref[:, lanes])
                    moved = pltpu.roll(wide, slots + 1, 1, stride=1, stride_axis=0)
                    scores = (mm_nt(qc, key[part, lanes]) + moved[:, :slots]) * scale
                    scores = jnp.where(same, scores, MASKED_SCORE)
                    top = jnp.max(scores, axis=-1, keepdims=True)
                    weights = jnp.exp(scores - top)
                    probs = weights / jnp.sum(weights, axis=-1, keepdims=True)
                    probs_ref[b, (lo // LANES) * len(masks) + h] = probs
                    mixed = jnp.where(mask, mm(probs.astype(BF16), value[part, lanes]), mixed)
                blocks.append(mixed)
            halves.append(jnp.concatenate(blocks, axis=1) if len(blocks) > 1 else blocks[0])
        mixed = jnp.concatenate(halves).astype(BF16)
        mixed_ref[at, :] = mixed
        store_partial(out_mine, out_mate, i, slots, mm(mixed, mix))


def mix_rows(mix_ref, side_ref, width, size, rows_held):
    per_side, mix, conv = rows_held
    if not per_side:
        return mix_ref[...]
    return jnp.concatenate(
        [
            output_rows(mix_ref, side_ref[0] * per_side + h, width, size, mix, conv, True)
            for h in range(per_side)
        ]
    )


def attention_call(pieces, lengths, first, side, columns, mix, rows_held, bias, place, head_size):
    mine, mate = pieces
    k, (slots, width) = len(mine), mine[0].shape
    size = place.shape[1]
    heads = size // head_size
    rows = 2 * k * slots
    outs = [shape((slots, width), F32)] * k + [
        shape((k, slots, width), BF16),
        shape((rows, 4 * size), BF16),
        shape((2 * k, heads, slots, slots), F32),
        shape((rows, size), BF16),
    ]
    result = kernel_call(
        functools.partial(attention_kernel, k, first, head_size, rows_held),
        outs,
        list(mine) + list(mate) + [columns, mix, bias, place],
        scalars=(lengths, side),
        flops=2 * rows * width * size * 4 + 2 * k * heads * 10 * slots * slots * LANES,
    )
    return (result[:k], result[k]), result[k + 1 :]


def attention_back_kernel(k, head_size, rows_held, *refs):
    side_ref, refs = refs[0], refs[1:]
    mine, mate, refs = refs[:k], refs[k : 2 * k], refs[2 * k :]
    column_ref, mix_ref, place_ref, saved_ref, probs_ref, refs = (
        refs[0],
        refs[1],
        refs[2],
        refs[3],
        refs[4],
        refs[5:],
    )
    out_mine, out_mate, grad_ref, place_grad_ref, bias_ref = (
        refs[:k],
        refs[k],
        refs[k + 1],
        refs[k + 2],
        refs[k + 3],
    )
    slots, width = mine[0].shape
    size = place_ref.shape[1]
    mix = mix_rows(mix_ref, side_ref, width, size, rows_held)
    scale = head_size ** (-0.5)
    masks = head_masks(slots, head_size)
    flip = (
        lax.broadcasted_iota(jnp.int32, (slots, slots), 0)
        + lax.broadcasted_iota(jnp.int32, (slots, slots), 1)
        == slots - 1
    ).astype(F32).astype(BF16)
    bias_c = jnp.zeros((1, size), F32)
    bias_p = jnp.zeros((1, size), F32)
    for i in range(k):
        rows = jnp.concatenate([mine[i][...], mate[i][...]])
        grad_mixed_all = mm_nt(rows, mix).astype(BF16)
        at = pl.ds(2 * i * slots, 2 * slots)
        halves = []
        for j in range(2):
            b = 2 * i + j
            part = slice(j * slots, (j + 1) * slots)
            rows_at = pl.ds((2 * i + j) * slots, slots)
            grad_qc, grad_qp, grad_k, grad_v = [], [], [], []
            for lo in range(0, size, LANES):
                lanes = slice(lo, lo + LANES)
                grad_mixed = grad_mixed_all[part, lanes]
                query_c = saved_ref[rows_at, lo : lo + LANES]
                query_p = saved_ref[rows_at, size + lo : size + lo + LANES]
                key = saved_ref[rows_at, 2 * size + lo : 2 * size + lo + LANES]
                value = saved_ref[rows_at, 3 * size + lo : 3 * size + lo + LANES]
                place = place_ref[:, lanes]
                gqc = jnp.zeros((slots, LANES), F32)
                gqp, gk, gv = gqc, gqc, gqc
                place_grad = jnp.zeros(place.shape, F32)
                for h, mask in enumerate(masks):
                    probs = probs_ref[b, (lo // LANES) * len(masks) + h]
                    own = jnp.where(mask, grad_mixed, 0)
                    grad_probs = mm_nt(own, value)
                    gv = gv + mm_tn(probs.astype(BF16), own)
                    inner = jnp.sum(probs * grad_probs, axis=-1, keepdims=True)
                    grad = (probs * (grad_probs - inner)).astype(BF16) * scale
                    grad = grad.astype(BF16)
                    gqc = jnp.where(mask, mm(grad, key), gqc)
                    gk = gk + mm_tn(grad, jnp.where(mask, query_c, 0))
                    turned = mm(flip, grad)
                    wide = jnp.concatenate([turned, jnp.zeros_like(turned)], axis=1)
                    wide = pltpu.roll(wide, 0, 1, stride=1, stride_axis=0).astype(BF16)
                    wide = mm(flip, wide).astype(BF16)
                    gqp = jnp.where(mask, mm(wide, place), gqp)
                    place_grad = place_grad + mm_tn(wide, jnp.where(mask, query_p, 0))
                if i == 0 and j == 0:
                    place_grad_ref[:, lanes] = place_grad
                else:
                    place_grad_ref[:, lanes] = place_grad_ref[:, lanes] + place_grad
                grad_qc.append(gqc)
                grad_qp.append(gqp)
                grad_k.append(gk)
                grad_v.append(gv)

            def side_by_side(blocks):
                return jnp.concatenate(blocks, axis=1) if len(blocks) > 1 else blocks[0]

            gqc, gqp = side_by_side(grad_qc), side_by_side(grad_qp)
            bias_c = bias_c + jnp.sum(gqc, axis=0, keepdims=True)
            bias_p = bias_p + jnp.sum(gqp, axis=0, keepdims=True)
            halves.append(
                jnp.concatenate(
                    [gqc + gqp, side_by_side(grad_k), side_by_side(grad_v)], axis=1
                ).astype(BF16)
            )
        grad = jnp.concatenate(halves)
        grad_ref[at, :] = grad
        store_partial(out_mine, out_mate, i, slots, square_product_back(grad, column_ref, width, 0, 3 * size))
    bias_ref[...] = jnp.concatenate([bias_c, bias_p])


def attention_back_call(pieces, side, columns, mix, rows_held, place, saved, probs, head_size):
    mine, mate = pieces
    k, (slots, width) = len(mine), mine[0].shape
    size = place.shape[1]
    rows = 2 * k * slots
    outs = [shape((slots, width), F32)] * k + [
        shape((k, slots, width), BF16),
        shape((rows, 3 * size), BF16),
        shape(place.shape, F32),
        shape((2, size), F32),
    ]
    result = kernel_call(
        functools.partial(attention_back_kernel, k, head_size, rows_held),
        outs,
        list(mine) + list(mate) + [columns, mix, place, saved, probs],
        scalars=(side,),
        flops=2 * rows * width * size * 4 + 2 * k * 24 * slots * slots * size,
    )
    return (result[:k], result[k]), result[k + 1 :]


def place_kernel(table_ref, column_ref, out_ref):
    size = out_ref.shape[1]
    rows = square_product(table_ref[...], column_ref, 3 * size, 4 * size)
    out_ref[...] = rows.astype(BF16)


def item_reach(ends, row_at, slots):
    start = jnp.zeros_like(row_at)
    end = jnp.full_like(row_at, slots)
    for at in ends:
        start = jnp.where(row_at >= at, at, start)
    for at in reversed(ends):
        end = jnp.where(row_at < at, at, end)
    valid = (row_at < ends[-1]).astype(F32)
    return row_at - start, end - 1 - row_at, valid


def gate_kernel(k, first, tap_count, *refs):
    length_ref, refs = refs[0], refs[1:]
    mine, mate, refs = refs[:k], refs[k : 2 * k], refs[2 * k :]
    column_ref, tap_ref, gate_ref, conv_ref, stat_ref, pad_ref = refs
    slots, _ = mine[0].shape
    size = tap_ref.shape[1]
    reach = tap_count // 2
    row_at = lax.broadcasted_iota(jnp.int32, (slots, size), 0)
    pad_ref[...] = jnp.zeros_like(pad_ref)
    count = jnp.zeros((1, size), F32)
    total = jnp.zeros((1, size), F32)
    for i in range(k):
        rows = jnp.concatenate([mine[i][...], mate[i][...]])
        gates = square_product(rows, column_ref, 4 * size, 6 * size)
        gate_ref[pl.ds(2 * i * slots, 2 * slots), :] = gates
        glu = gates[:, :size] * sigmoid(gates[:, size:])
        for j in range(2):
            b = 2 * i + j
            before, behind, valid = item_reach(item_bounds(length_ref, first + b), row_at, slots)
            pad_ref[PAD : PAD + slots, :] = glu[j * slots : (j + 1) * slots] * valid
            conv = jnp.zeros((slots, size), F32)
            for tap in range(tap_count):
                o = tap - reach
                near = pad_ref[PAD + o : PAD + o + slots, :]
                if o < 0:
                    near = jnp.where(before >= -o, near, 0.0)
                elif o > 0:
                    near = jnp.where(behind >= o, near, 0.0)
                conv = conv + near * tap_ref[tap : tap + 1, :]
            conv_ref[pl.ds(b * slots, slots), :] = conv
            count = count + jnp.sum(valid, axis=0, keepdims=True)
            total = total + jnp.sum(conv * valid, axis=0, keepdims=True)
    mean = total / count
    spread = jnp.zeros((1, size), F32)
    for b in range(2 * k):
        valid = (row_at < item_bounds(length_ref, first + b)[-1]).astype(F32)
        gap = (conv_ref[pl.ds(b * slots, slots), :] - mean) * valid
        spread = spread + jnp.sum(gap * gap, axis=0, keepdims=True)
    stat_ref[...] = jnp.concatenate([count, mean, spread, jnp.zeros((5, size), F32)])


def gate_call(pieces, lengths, first, columns, taps, tap_count):
    mine, mate = pieces
    k, (slots, width) = len(mine), mine[0].shape
    size = taps.shape[1]
    rows = 2 * k * slots
    return kernel_call(
        functools.partial(gate_kernel, k, first, tap_count),
        [shape((rows, 2 * size), F32), shape((rows, size), F32), shape((8, size), F32)],
        list(mine) + list(mate) + [columns, taps],
        scalars=(lengths,),
        flops=4 * rows * width * size + 40 * tap_count * rows * size,
        scratch=[pltpu.VMEM((slots + 2 * PAD, size), F32)],
    )


def merge_kernel(left_ref, right_ref, out_ref):
    n_left, n_right = left_ref[0:1, :], right_ref[0:1, :]
    m_left, m_right = left_ref[1:2, :], right_ref[1:2, :]
    count = n_left + n_right
    gap = m_right - m_left
    mean = (n_left * m_left + n_right * m_right) / count
    spread = left_ref[2:3, :] + right_ref[2:3, :] + gap * gap * (n_left * n_right / count)
    size = left_ref.shape[1]
    out_ref[...] = jnp.concatenate([count, mean, spread, jnp.zeros((5, size), F32)])


def merge(left, right):
    return kernel_call(merge_kernel, [shape(left.shape, F32)], [left, right])[0]


def batch_unit(conv, stat_ref):
    inverse = lax.rsqrt(stat_ref[2:3, :] / stat_ref[0:1, :] + EPSILON)
    return (conv - stat_ref[1:2, :]) * inverse, inverse


def batch_kernel(k, rows_held, *refs):
    conv_ref, stat_ref, batch_ref, out_weight_ref, refs = (
        refs[0],
        refs[1],
        refs[2],
        refs[3],
        refs[4:],
    )
    out_mine, out_mate, active_ref = refs[:k], refs[k], refs[k + 1]
    slots, width = out_mine[0].shape
    weight = conv_rows(out_weight_ref, width, active_ref.shape[1], rows_held)
    for i in range(k):
        at = pl.ds(2 * i * slots, 2 * slots)
        unit, _ = batch_unit(conv_ref[at, :], stat_ref)
        value = unit * batch_ref[0:1, :] + batch_ref[1:2, :]
        active = (value * sigmoid(value)).astype(BF16)
        active_ref[at, :] = active
        store_partial(out_mine, out_mate, i, slots, mm(active, weight))


def conv_rows(ref, width, size, rows_held):
    _, mix, conv = rows_held
    return jnp.concatenate(
        [output_rows(ref, p, width, size, mix, conv, False) for p in range(ref.shape[0])]
    )


def batch_call(k, conv, stats, batch_rows, out_weight, rows_held, slots, width):
    size = conv.shape[1]
    outs = [shape((slots, width), F32)] * k + [
        shape((k, slots, width), BF16),
        shape(conv.shape, BF16),
    ]
    result = kernel_call(
        functools.partial(batch_kernel, k, rows_held),
        outs,
        [conv, stats, batch_rows, out_weight],
        flops=2 * conv.shape[0] * width * size,
    )
    return (result[:k], result[k]), result[k + 1]


def batch_back_kernel(k, first, rows_held, *refs):
    length_ref, refs = refs[0], refs[1:]
    mine, mate, refs = refs[:k], refs[k : 2 * k], refs[2 * k :]
    conv_ref, stat_ref, batch_ref, out_weight_ref, grad_ref, sum_ref = refs
    slots, width = mine[0].shape
    size = conv_ref.shape[1]
    weight = conv_rows(out_weight_ref, width, size, rows_held)
    row_at = lax.broadcasted_iota(jnp.int32, (slots, size), 0)
    sums = [jnp.zeros((1, size), F32)] * 4
    for i in range(k):
        rows = jnp.concatenate([mine[i][...], mate[i][...]])
        grad_active = mm_nt(rows, weight)
        for j in range(2):
            b = 2 * i + j
            at = pl.ds(b * slots, slots)
            unit, _ = batch_unit(conv_ref[at, :], stat_ref)
            value = unit * batch_ref[0:1, :] + batch_ref[1:2, :]
            grad = grad_active[j * slots : (j + 1) * slots] * swish_grad(value)
            valid = (row_at < item_bounds(length_ref, first + b)[-1]).astype(F32)
            grad_unit = grad * batch_ref[0:1, :]
            grad_ref[at, :] = grad_unit
            terms = (grad * unit, grad, grad_unit * valid, grad_unit * unit * valid)
            sums = [s + jnp.sum(t, axis=0, keepdims=True) for s, t in zip(sums, terms)]
    sum_ref[...] = jnp.concatenate(sums + [jnp.zeros((4, size), F32)])


def batch_back_call(pieces, lengths, first, conv, stats, batch_rows, out_weight, rows_held):
    mine, mate = pieces
    k, (slots, width) = len(mine), mine[0].shape
    size = conv.shape[1]
    return kernel_call(
        functools.partial(batch_back_kernel, k, first, rows_held),
        [shape(conv.shape, F32), shape((8, size), F32)],
        list(mine) + list(mate) + [conv, stats, batch_rows, out_weight],
        scalars=(lengths,),
        flops=2 * conv.shape[0] * width * size,
    )


def gate_back_kernel(k, first, tap_count, *refs):
    length_ref, refs = refs[0], refs[1:]
    grad_in_ref, conv_ref, gate_ref, stat_ref, sum_ref, column_ref, tap_ref, refs = (
        refs[0],
        refs[1],
        refs[2],
        refs[3],
        refs[4],
        refs[5],
        refs[6],
        refs[7:],
    )
    out_mine, out_mate, grad_ref, tap_grad_ref, glu_ref, conv_grad_ref = (
        refs[:k],
        refs[k],
        refs[k + 1],
        refs[k + 2],
        refs[k + 3],
        refs[k + 4],
    )
    slots, width = out_mine[0].shape
    size = tap_ref.shape[1]
    reach = tap_count // 2
    row_at = lax.broadcasted_iota(jnp.int32, (slots, size), 0)
    glu_ref[...] = jnp.zeros_like(glu_ref)
    conv_grad_ref[...] = jnp.zeros_like(conv_grad_ref)
    tap_grad_ref[...] = jnp.zeros_like(tap_grad_ref)
    frame_count = stat_ref[0:1, :]
    mean_grad = sum_ref[2:3, :] / frame_count
    mean_cross = sum_ref[3:4, :] / frame_count
    for i in range(k):
        halves = []
        for j in range(2):
            b = 2 * i + j
            at = pl.ds(b * slots, slots)
            before, behind, valid = item_reach(item_bounds(length_ref, first + b), row_at, slots)
            gate_a, gate_sig = gate_ref[at, :size], sigmoid(gate_ref[at, size:])
            glu_ref[PAD : PAD + slots, :] = gate_a * gate_sig * valid
            unit, inverse = batch_unit(conv_ref[at, :], stat_ref)
            conv_grad = valid * inverse * (grad_in_ref[at, :] - mean_grad - unit * mean_cross)
            conv_grad_ref[PAD : PAD + slots, :] = conv_grad
            grad_glu = jnp.zeros((slots, size), F32)
            for tap in range(tap_count):
                o = tap - reach
                near = glu_ref[PAD + o : PAD + o + slots, :]
                back = conv_grad_ref[PAD - o : PAD - o + slots, :]
                if o < 0:
                    near = jnp.where(before >= -o, near, 0.0)
                    back = jnp.where(behind >= -o, back, 0.0)
                elif o > 0:
                    near = jnp.where(behind >= o, near, 0.0)
                    back = jnp.where(before >= o, back, 0.0)
                grad_glu = grad_glu + back * tap_ref[tap : tap + 1, :]
                tap_grad_ref[tap : tap + 1, :] += jnp.sum(near * conv_grad, axis=0, keepdims=True)
            grad_glu = grad_glu * valid
            halves.append(
                jnp.concatenate(
                    [grad_glu * gate_sig, grad_glu * gate_a * gate_sig * (1.0 - gate_sig)], axis=1
                ).astype(BF16)
            )
        grad = jnp.concatenate(halves)
        grad_ref[pl.ds(2 * i * slots, 2 * slots), :] = grad
        store_partial(out_mine, out_mate, i, slots, square_product_back(grad, column_ref, width, 4 * size, 6 * size))


def gate_back_call(k, lengths, first, grad_unit, conv, gates, stats, sums, columns, taps, tap_count, slots, width):
    rows, size = conv.shape
    outs = [shape((slots, width), F32)] * k + [
        shape((k, slots, width), BF16),
        shape((rows, 2 * size), BF16),
        shape(taps.shape, F32),
    ]
    padded = pltpu.VMEM((slots + 2 * PAD, size), F32)
    result = kernel_call(
        functools.partial(gate_back_kernel, k, first, tap_count),
        outs,
        [grad_unit, conv, gates, stats, sums, columns, taps],
        scalars=(lengths,),
        flops=4 * rows * width * size + 80 * tap_count * rows * size,
        scratch=[padded, padded],
    )
    return (result[:k], result[k]), result[k + 1 :]


def join_kernel(count, coefficient, *refs):
    stream_ref, own_ref, mate_ref, refs = refs[0], refs[1], refs[2], refs[3:]
    far, norm_ref, stream_out, normed_ref = refs[:count], refs[count], refs[count + 1], refs[count + 2]
    branch = own_ref[...] + mate_ref[0].astype(F32)
    for ref in far:
        branch = branch + ref[...].astype(F32)
    stream = stream_ref[...].astype(F32) + coefficient * branch
    stream_out[...] = stream
    unit, _ = normalize(stream)
    normed_ref[...] = (unit * norm_ref[0:1, :] + norm_ref[1:2, :]).astype(BF16)


def join_call(stream, parts, coefficient, norm):
    own, mate, far = parts
    return kernel_call(
        functools.partial(join_kernel, len(far), coefficient),
        [shape(own.shape, F32), shape(own.shape, BF16)],
        [stream, own, mate] + list(far) + [norm],
    )


def turn_kernel(count, coefficient, *refs):
    length_ref, refs = refs[0], refs[1:]
    stream_ref, own_ref, mate_ref, refs = refs[0], refs[1], refs[2], refs[3:]
    far, norm_ref, cotangent_ref, refs = refs[:count], refs[count], refs[count + 1], refs[count + 2 :]
    output_ref, grad_out, low_out, norm_grad = refs
    branch = own_ref[...] + mate_ref[0].astype(F32)
    for ref in far:
        branch = branch + ref[...].astype(F32)
    stream = stream_ref[...] + coefficient * branch
    row_at = lax.broadcasted_iota(jnp.int32, (stream.shape[0], 1), 0)
    valid = (row_at < item_bounds(length_ref)[-1]).astype(F32)
    unit, scale = normalize(stream)
    output_ref[...] = ((unit * norm_ref[0:1, :] + norm_ref[1:2, :]) * valid).astype(BF16)
    norm_back(
        unit,
        scale,
        norm_ref,
        cotangent_ref[...].astype(F32) * valid,
        0.0,
        0.5,
        grad_out,
        low_out,
        norm_grad,
    )


def norm_back(unit, scale, norm_ref, grad, base, coefficient, grad_out, low_out, norm_grad):
    norm_grad[...] = jnp.concatenate(
        [jnp.sum(grad * unit, axis=0, keepdims=True), jnp.sum(grad, axis=0, keepdims=True)]
    )
    grad = grad * norm_ref[0:1, :]
    inner = jnp.mean(grad, axis=-1, keepdims=True)
    cross = jnp.mean(grad * unit, axis=-1, keepdims=True)
    grad = base + scale * (grad - inner - unit * cross)
    if grad_out is not None:
        grad_out[...] = grad
    low_out[...] = (coefficient * grad).astype(BF16)


def turn_call(stream, parts, coefficient, norm, cotangent, lengths):
    own, mate, far = parts
    return kernel_call(
        functools.partial(turn_kernel, len(far), coefficient),
        [
            shape(own.shape, BF16),
            shape(own.shape, F32),
            shape(own.shape, BF16),
            shape((2, own.shape[1]), F32),
        ],
        [stream, own, mate] + list(far) + [norm, cotangent],
        scalars=(lengths,),
    )


def join_back_kernel(count, coefficient, keep, *refs):
    stream_ref, grad_ref, own_ref, mate_ref, refs = refs[0], refs[1], refs[2], refs[3], refs[4:]
    far, norm_ref, refs = refs[:count], refs[count], refs[count + 1 :]
    grad_out, (low_out, norm_grad) = (refs[0] if keep else None), refs[-2:]
    grad = own_ref[...] + mate_ref[0].astype(F32)
    for ref in far:
        grad = grad + ref[...].astype(F32)
    unit, scale = normalize(stream_ref[...].astype(F32))
    norm_back(
        unit, scale, norm_ref, grad, grad_ref[...], coefficient, grad_out, low_out, norm_grad
    )


def join_back_call(stream, grad, parts, coefficient, norm, keep=True):
    own, mate, far = parts
    outs = [shape(own.shape, F32)] if keep else []
    return kernel_call(
        functools.partial(join_back_kernel, len(far), coefficient, keep),
        outs + [shape(own.shape, BF16), shape((2, own.shape[1]), F32)],
        [stream, grad, own, mate] + list(far) + [norm],
    )


def offset_table(slot_count, model_width):
    offsets = jnp.arange(2 * slot_count, dtype=F32) - (slot_count - 1)
    freqs = jnp.exp(-jnp.log(10000.0) * jnp.arange(0, model_width, 2, dtype=F32) / model_width)
    angles = offsets[:, None] * freqs[None, :]
    return jnp.concatenate([jnp.sin(angles), jnp.cos(angles)], axis=1)


def nesterov(weight, moment, average, grad_rows, rate, rate_scale):
    moment_new = MOMENTUM_DECAY * moment + grad_rows
    weight_new = weight - rate * rate_scale * (grad_rows + MOMENTUM_DECAY * moment_new)
    average_new = AVERAGE_DECAY * average + (1.0 - AVERAGE_DECAY) * weight_new
    return (moment_new, weight_new, average_new)


def head_lanes(member, i, sides, planes, size):
    side, rest = member % sides, member // sides
    plane = side * (planes // sides) + i
    return (plane * 4 + rest) * size


def split_down_kernel(weight_ref, first_ref, second_ref):
    hidden = first_ref.shape[1]
    rows = weight_ref.shape[1]
    for layer, out in enumerate((first_ref, second_ref)):
        for b in range(weight_ref.shape[2] // hidden):
            part = weight_ref[layer, :, b * hidden : (b + 1) * hidden]
            out[b * rows : (b + 1) * rows, :] = part.astype(BF16)


def split_up_kernel(weight_ref, first_ref, second_ref):
    team, _, hidden = first_ref.shape
    planes = weight_ref.shape[2] // (team * LANES)
    for layer, out in enumerate((first_ref, second_ref)):
        for t in range(team):
            for p in range(planes):
                at = (p * team + t) * LANES
                part = weight_ref[layer, :, at : at + LANES]
                out[t, :, p * LANES : (p + 1) * LANES] = part.astype(BF16)


def split_square_kernel(planes, sides, head_size, weight_ref, column_ref, mix_ref, conv_ref):
    team = column_ref.shape[0]
    width = weight_ref.shape[2]
    size = width // team
    for t in range(team):
        for i, matrix in enumerate((0, 1, 2, 4, 5, 6)):
            if i < 4:
                starts = [
                    head_lanes(t, h, sides, planes, head_size) for h in range(size // head_size)
                ]
                count = head_size
            else:
                count = size // planes
                starts = [(p * team + t) * count for p in range(planes)]
            parts = [weight_ref[matrix, :, at : at + count] for at in starts]
            column_ref[t, :, i * size : (i + 1) * size] = jnp.concatenate(parts, axis=1).astype(BF16)
    mix_ref[...] = weight_ref[3].astype(BF16)
    conv_ref[...] = weight_ref[7].astype(BF16)


def square_pack_kernel(side_ref, column_ref, own_ref, other_ref, conv_ref, out_ref):
    team, rows, lanes = column_ref.shape
    for b in range(lanes // BLOCK):
        for t in range(team):
            at = (b * team + t) * rows
            out_ref[at : at + rows, :] = column_ref[t, :, b * BLOCK : (b + 1) * BLOCK]
    base = (lanes // BLOCK) * team * rows
    low = side_ref[0] == 0
    for b in range(own_ref.shape[1] // BLOCK):
        lane = slice(b * BLOCK, (b + 1) * BLOCK)
        own, other = own_ref[:, lane].astype(F32), other_ref[:, lane].astype(F32)
        at = base + b * 3 * rows
        out_ref[at : at + rows, :] = jnp.where(low, own, other).astype(BF16)
        out_ref[at + rows : at + 2 * rows, :] = jnp.where(low, other, own).astype(BF16)
        out_ref[at + 2 * rows : at + 3 * rows, :] = conv_ref[:, lane]


def feed_pack_kernel(up_ref, down_ref, out_ref):
    team, rows, _ = up_ref.shape
    for t in range(team):
        out_ref[t * rows : (t + 1) * rows, :] = up_ref[t]
    out_ref[team * rows :, :] = down_ref[...]


def column_grad_kernel(mix_ref, conv_ref, out_ref):
    team, rows, lanes = out_ref.shape
    depth = team * rows
    for b in range(lanes // BLOCK):
        ref, at = (mix_ref, b) if b < 2 else (conv_ref, b - 2)
        for t in range(team):
            first = at * depth + t * rows
            out_ref[t, :, b * BLOCK : (b + 1) * BLOCK] = ref[first : first + rows, :]


def update(scale_ref, rate, index, grad, refs):
    weight_ref, moment_ref, average_ref, grad_out, moment_out, weight_out, average_out = refs
    moment = MOMENTUM_DECAY * moment_ref[index] + grad
    weight = weight_ref[index] - rate * scale_ref[0:1, 0:1] * (grad + MOMENTUM_DECAY * moment)
    grad_out[index] = grad
    moment_out[index] = moment
    weight_out[index] = weight
    average_out[index] = AVERAGE_DECAY * average_ref[index] + (1.0 - AVERAGE_DECAY) * weight


def update_up_kernel(scale_ref, first_ref, second_ref, *refs):
    team, _, hidden = first_ref.shape
    for layer, ref in enumerate((first_ref, second_ref)):
        parts = [
            ref[t, :, p * LANES : (p + 1) * LANES] for p in range(hidden // LANES) for t in range(team)
        ]
        update(scale_ref, RATE_UP, layer, jnp.concatenate(parts, axis=1).astype(F32), refs)


def update_down_kernel(scale_ref, first_ref, second_ref, *refs):
    rows, width = refs[0].shape[1:]
    hidden = first_ref.shape[1]
    for layer, ref in enumerate((first_ref, second_ref)):
        base = ref.shape[0] - rows * (width // hidden)
        parts = [
            ref[base + b * rows : base + (b + 1) * rows, :] for b in range(width // hidden)
        ]
        update(scale_ref, RATE_DOWN, layer, jnp.concatenate(parts, axis=1).astype(F32), refs)


def update_square_kernel(planes, sides, head_size, side_ref, *refs):
    scale_ref, column_ref, mix_ref, other_ref, conv_ref, refs = (
        refs[0],
        refs[1],
        refs[2],
        refs[3],
        refs[4],
        refs[5:],
    )
    team, rows, _ = column_ref.shape
    width = refs[0].shape[2]
    size = width // team
    per_side = planes // sides
    for i, matrix in enumerate((0, 1, 2, 4, 5, 6)):
        parts = []
        if i < 4:
            for head in range(width // head_size):
                plane, rest = head // 4, head % 4
                t = rest * sides + plane // per_side
                at = i * size + (plane % per_side) * head_size
                parts.append(column_ref[t, :, at : at + head_size])
        else:
            count = size // planes
            for p in range(planes):
                for t in range(team):
                    at = i * size + p * count
                    parts.append(column_ref[t, :, at : at + count])
        update(scale_ref, RATE_SQUARE, matrix, jnp.concatenate(parts, axis=1).astype(F32), refs)
    blocks = width // BLOCK
    head_rows = sides * rows
    base = mix_ref.shape[0] - blocks * head_rows
    parts = []
    for b in range(blocks):
        at = slice(base + b * head_rows, base + (b + 1) * head_rows)
        parts.append(mix_ref[at, :].astype(F32) + other_ref[at, :].astype(F32))
    whole = jnp.concatenate(parts, axis=1)
    update(scale_ref, RATE_SQUARE, 3, jnp.where(side_ref[0] == 0, whole[:rows], whole[rows:]), refs)
    base = conv_ref.shape[0] - blocks * rows
    parts = [conv_ref[base + b * rows : base + (b + 1) * rows, :] for b in range(blocks)]
    update(scale_ref, RATE_SQUARE, 7, jnp.concatenate(parts, axis=1).astype(F32), refs)


def update_call(body, scale, terms, weight, moment, average, scalars=()):
    return kernel_call(
        body,
        [shape(weight.shape, F32)] * 4,
        [scale] + list(terms) + [weight, moment, average],
        scalars=scalars,
    )


def feature_grad_kernel(planes, sides, *refs):
    member_ref, refs = refs[0], refs[1:]
    norms, biases, out_ref = refs[:5], refs[5:-1], refs[-1]
    team, _, size = out_ref.shape
    count = size // planes
    per_side = planes // sides
    head_size = sides * count
    bias = sum(ref[...] for ref in biases)
    rest, side = member_ref[0] // sides, member_ref[0] % sides
    rows = jnp.concatenate([n[0:1, :] for n in norms] + [n[1:2, :] for n in norms])
    for t in range(team):
        parts, own = [], []
        for p in range(planes):
            at = (p * team + t) * count
            parts.append(rows[:, at : at + count])
            at = (p % per_side) * head_size + (t % sides) * count
            held = (rest == t // sides) & (side == p // per_side)
            own.append(bias[:, at : at + count] * held.astype(jnp.int32).astype(F32))
        out_ref[t] = jnp.concatenate(
            [jnp.concatenate(parts, axis=1), jnp.concatenate(own, axis=1)]
        )


def channel_grad_kernel(taps, term_ref, sum_ref, *refs):
    tap_refs, out_ref = refs[:-1], refs[-1]
    features = jnp.sum(term_ref[...], axis=0)
    out_ref[...] = jnp.concatenate(
        [
            sum(ref[:taps] for ref in tap_refs),
            features[:10],
            sum_ref[0:2],
            features[10:12],
        ]
    )


def make_step(planes, sides):
    wide_team = sides == 2
    team_axes = ("x", "c", "y") if wide_team else ("x", "c")
    team = 8 if wide_team else 4
    outer_bits = [("z", 1 << i) for i in range((planes - 1).bit_length())]
    if not wide_team:
        outer_bits += [("y", 1 << i) for i in range((sides - 1).bit_length())]
    head_aligned = wide_team and planes * 4 == HEADS

    def turn(values, first):
        pairs = []
        for x in range(2):
            for c in range(2):
                for y in range(2):
                    along_x = (c == 0) == first
                    to = (1 - x, c, y) if along_x else (x, c, 1 - y)
                    pairs.append((4 * x + 2 * c + y, 4 * to[0] + 2 * to[1] + to[2]))
        return lax.ppermute(values, team_axes, pairs)

    def gather(values):
        return spread(values, None)[0]

    def spread(values, run):
        groups, results = [([values], [swap(values, "c")])], []

        def work(*travelling):
            if run is not None:
                result = run(len(results), groups[-1])
                travelling, result = lax.optimization_barrier((travelling, result))
                results.append(result)
            return travelling

        if not wide_team:
            (far,) = work(swap(values, "x"))
        else:
            first, second = work(turn(values, True), turn(values, False))
            far = turn(first, False)
            groups.append(([first, second], [swap(first, "c"), swap(second, "c")]))
            (far,) = work(far)
        groups.append(([far], [swap(far, "c")]))
        if run is not None:
            results.append(run(len(results), groups[-1]))
        return groups, results

    def scatter(parts, fill=()):
        (own,), own_mate = parts[0]
        (far,), far_mate = parts[-1]
        out_far = add_call(far, swap(far_mate, "c"), 0)
        got_own = swap(own_mate, "c")
        if not wide_team:
            across, fill = lax.optimization_barrier((swap(out_far, "x"), fill))
            return (own, got_own, [across]), fill
        (first, second), side_mate = parts[1]
        got_side = swap(side_mate, "c")
        relay = turn(out_far, False)
        from_second = turn(add_call(second, got_side, 1), False)
        relay, fill = lax.optimization_barrier((relay, fill))
        from_first = turn(add_call(first, got_side, 0, relay), True)
        return (own, got_own, [from_first, from_second]), fill

    def side_rows(rows):
        return rows if wide_team else lax.all_gather(rows, "y", axis=0, tiled=True)

    def side_scatter(rows):
        if wide_team:
            return rows
        return lax.psum_scatter(rows, "y", scatter_dimension=0, tiled=True)

    def split_hidden(rows):
        r, f = rows.shape
        return rows.reshape(r, planes, team, f // (planes * team)).transpose(2, 0, 1, 3).reshape(
            team, r, f // team
        )

    def join_hidden(blocks):
        _, r, f = blocks.shape
        return blocks.reshape(team, r, planes, f // planes).transpose(1, 2, 0, 3).reshape(
            r, team * f
        )

    def split_heads(rows):
        r, d = rows.shape
        if not head_aligned:
            return rows.reshape(r, team, d // team).transpose(1, 0, 2)
        size = d // HEADS
        rows = rows.reshape(r, sides, planes // sides, 2, 2, size)
        return rows.transpose(3, 4, 1, 0, 2, 5).reshape(team, r, d // team)

    def join_heads(blocks):
        _, r, f = blocks.shape
        if not head_aligned:
            return blocks.transpose(1, 0, 2).reshape(r, team * f)
        size = team * f // HEADS
        blocks = blocks.reshape(2, 2, sides, r, planes // sides, size)
        return blocks.transpose(3, 2, 4, 0, 1, 5).reshape(r, team * f)

    def team_swap(blocks):
        return lax.all_to_all(blocks, team_axes, split_axis=0, concat_axis=0, tiled=True)

    def plane_pieces(rows):
        return [rows] + [swap(rows, "z", d) for d in range(1, planes)]

    def plane_gather(rows):
        return lax.all_gather(rows, "z", axis=0, tiled=False)

    def plane_reduce(rows):
        return lax.psum_scatter(rows, "z", scatter_dimension=0, tiled=False)

    def to_blocks(rows, size):
        return jnp.concatenate([rows[:, i : i + size] for i in range(0, rows.shape[1], size)])

    def from_blocks(rows, count):
        return jnp.concatenate(jnp.split(rows, count), axis=1)

    def outer_sum(values):
        for axis, bit in outer_bits:
            values = values + swap(values, axis, bit)
        return values

    def step(
        frames,
        lengths,
        out_grad,
        up_weight,
        down_weight,
        square_weight,
        chan_weight,
        up_moment,
        down_moment,
        square_moment,
        chan_moment,
        up_average,
        down_average,
        square_average,
        chan_average,
    ):
        slots, width = frames.shape
        head_size = width // HEADS
        item_count = lengths.shape[1] - 1
        chan_rows = chan_weight.shape[0]
        tap_count = chan_rows - 14
        hidden = up_weight.shape[2]
        team_hidden = hidden // team
        team_width = width // team
        x_at, c_at, y_at = lax.axis_index("x"), lax.axis_index("c"), lax.axis_index("y")
        team_at = (x_at * 2 + c_at) * 2 + y_at if wide_team else x_at * 2 + c_at
        side = y_at.reshape(1).astype(jnp.int32)
        plane = lax.axis_index("z").reshape(1).astype(jnp.int32)

        chan_low = chan_weight.astype(BF16)
        if head_aligned:
            blocks = [shape((hidden // planes // team * (width // team_hidden), team_hidden), BF16)] * 2
            down_one, down_two = kernel_call(split_down_kernel, blocks, [down_weight])
            rows_in = up_weight.shape[1]
            blocks = [shape((team, rows_in, team_hidden), BF16)] * 2
            up_one, up_two = kernel_call(split_up_kernel, blocks, [up_weight])
            columns, mix, conv_out = kernel_call(
                functools.partial(split_square_kernel, planes, sides, head_size),
                [shape((team, rows_in, 6 * team_width), BF16)] + [shape((rows_in, width), BF16)] * 2,
                [square_weight],
            )
        else:
            up_low = up_weight.astype(BF16)
            down_low = down_weight.astype(BF16)
            square_low = square_weight.astype(BF16)
            down_one, down_two = [to_blocks(side_rows(down_low[i]), team_hidden) for i in (0, 1)]
            up_one, up_two = [split_hidden(side_rows(up_low[i])) for i in (0, 1)]
            columns = jnp.concatenate(
                [split_heads(side_rows(square_low[i])) for i in (0, 1, 2, 4)]
                + [split_hidden(side_rows(square_low[i])) for i in (5, 6)],
                axis=2,
            )
            mix, conv_out = square_low[3], side_rows(square_low[7])
        up_one = team_swap(up_one)
        up_one, frames, chan_low, lengths, columns, up_two, mix = lax.optimization_barrier(
            (up_one, frames, chan_low, lengths, columns, up_two, mix)
        )
        if head_aligned:
            first = kernel_call(
                feed_pack_kernel,
                [shape((team * rows_in + down_one.shape[0], team_hidden), BF16)],
                [up_one, down_one],
            )[0]
        else:
            first = jnp.concatenate([up_one.reshape(-1, team_hidden), down_one])
        pack_one = plane_gather(first)
        groups = gather(frames)

        if wide_team:
            lanes = jnp.pad(chan_low, ((0, LANES - chan_rows), (0, 0))).T
            carried = jnp.pad(
                lengths.astype(BF16), ((0, CARRY - 1), (0, LANES - lengths.shape[1]))
            )
            lanes = jnp.concatenate([lanes, carried])[None]
            for axis in ("y", "c", "x"):
                lanes = jnp.concatenate([lanes, swap(lanes, axis)])
            where_at = jnp.stack([plane[0], team_at, y_at, c_at]).astype(jnp.int32)
            norms = [shape((2, width), F32)] * 5
            params = kernel_call(
                functools.partial(channel_kernel, planes, sides, head_size),
                norms
                + [
                    shape((tap_count + 1, team_width), F32),
                    shape((2, team_width), F32),
                    shape((2, team_width), F32),
                    shape((team, lengths.shape[1]), jnp.int32),
                ],
                plane_pieces(lanes),
                scalars=(where_at,),
                scratch=[pltpu.VMEM((width, LANES), F32)],
            )
            norms, (taps, batch_rows, bias_rows, team_lengths) = params[:5], params[5:]
        else:
            team_lengths = jnp.concatenate(chunk_order(gather(lengths)))
            chan_float = lax.all_gather(chan_low, ALL, axis=1, tiled=True).astype(F32)

            def own_hidden(rows):
                rows = rows.reshape(rows.shape[0], planes, team, -1)
                rows = lax.dynamic_index_in_dim(rows, team_at, axis=2, keepdims=False)
                return rows.reshape(rows.shape[0], team_width)

            taps = own_hidden(chan_float[: tap_count + 1])
            batch_rows = own_hidden(chan_float[tap_count + 10 : tap_count + 12])
            bias_rows = lax.dynamic_index_in_dim(
                split_heads(chan_float[tap_count + 12 : tap_count + 14]), team_at, 0, False
            )
            norms = [
                jnp.stack([chan_float[tap_count + j], chan_float[tap_count + 5 + j]])
                for j in range(5)
            ]

        columns, up_two = team_swap(columns), team_swap(up_two)
        if head_aligned:
            head_rows = sides * rows_in
            per_side = planes // sides
            rows_held = (per_side, head_rows, rows_in)
            lines = 6 * team_width // BLOCK * team * rows_in + width // BLOCK * 3 * rows_in
            squares = kernel_call(
                square_pack_kernel,
                [shape((lines, BLOCK), BF16)],
                [columns, mix, swap(mix, "y"), conv_out],
                scalars=(side,),
            )[0]
            second = kernel_call(
                feed_pack_kernel,
                [shape((team * rows_in + down_two.shape[0], team_hidden), BF16)],
                [up_two, down_two],
            )[0]
        else:
            per_side = 0
            rows_held = (0, 0, conv_out.shape[0])
            mix = lax.all_gather(mix, ALL, axis=0, tiled=True)
            mix = lax.dynamic_slice_in_dim(mix, team_at * team_width, team_width, axis=0)
            columns = to_blocks(columns.reshape(-1, 6 * team_width), BLOCK)
            squares = jnp.concatenate([columns, to_blocks(conv_out, BLOCK)])
            second = jnp.concatenate([up_two.reshape(-1, team_hidden), down_two])
        table = offset_table(slots, width).astype(BF16)

        ready = (pack_one, groups, norms, taps, team_lengths, table)
        ready, squares, second, mix = lax.optimization_barrier((ready, squares, second, mix))
        pack_one, groups, norms, taps, team_lengths, table = ready
        squares = plane_gather(squares)
        if head_aligned:
            mix = squares

        def columns_of(results, i):
            return [result[i] for result in results]

        at = [0]
        for group in groups:
            at.append(at[-1] + 2 * len(group[0]))

        results = [forward_call(group, pack_one, norms[0]) for group in groups]
        saved_one = [columns_of(columns_of(results, 1), i) for i in (2, 0, 1)]
        parts, _ = scatter(columns_of(results, 0))
        stream_one, normed = join_call(frames, parts, 0.5, norms[1])
        normed, second = lax.optimization_barrier((normed, second))
        pack_two = plane_gather(second)

        place = kernel_call(
            place_kernel,
            [shape((table.shape[0], team_width), BF16)],
            [table, squares],
            flops=2 * table.shape[0] * width * team_width,
        )[0]

        def attention(i, group):
            return attention_call(
                group, team_lengths, at[i], side, squares, mix, rows_held, bias_rows, place, head_size
            )

        groups, results = spread(normed, attention)
        normed_two = chunk_order(groups)
        saved_two = columns_of(results, 1)
        parts, _ = scatter(columns_of(results, 0))
        stream_two, normed = join_call(stream_one, parts, 1.0, norms[2])

        def gates(i, group):
            return gate_call(group, team_lengths, at[i], squares, taps, tap_count)

        groups, saved_three = spread(normed, gates)
        normed_three = chunk_order(groups)
        stats = saved_three[0][2]
        for saved in saved_three[1:]:
            stats = merge(stats, saved[2])
        for axis, bit in outer_bits:
            stats = merge(stats, swap(stats, axis, bit))
        results = [
            batch_call(
                len(group[0]), saved[1], stats, batch_rows, squares, rows_held, slots, width
            )
            for group, saved in reversed(list(zip(groups, saved_three)))
        ][::-1]
        active_conv = columns_of(results, 1)
        parts, _ = scatter(columns_of(results, 0))
        stream_three, normed = join_call(stream_two, parts, 1.0, norms[3])
        normed, pack_two = lax.optimization_barrier((normed, pack_two))

        groups, results = spread(normed, lambda i, group: forward_call(group, pack_two))
        saved_four = [chunk_order(groups)] + [columns_of(columns_of(results, 1), i) for i in (0, 1)]
        parts, _ = scatter(columns_of(results, 0))
        output, grad_four, low, norm_four = turn_call(
            stream_three, parts, 0.5, norms[4], out_grad, lengths
        )

        def feed_backward(low, pack, saved):
            normed, before, active = saved
            groups, results = spread(
                low, lambda i, group: backward_call(group, pack, before[i])
            )
            term = feed_weight_call(
                normed, columns_of(results, 1), active, chunk_order(groups), planes
            )
            return scatter(columns_of(results, 0), term)

        parts, second_term = feed_backward(low, pack_two, saved_four)
        grad_three, low, norm_three = join_back_call(stream_three, grad_four, parts, 1.0, norms[3])
        low, second_term = lax.optimization_barrier((low, second_term))
        second_term = plane_reduce(second_term)

        def batch_back(i, group):
            return batch_back_call(
                group, team_lengths, at[i], saved_three[i][1], stats, batch_rows, squares, rows_held
            )

        groups, grads = spread(low, batch_back)
        local_sums = sum(columns_of(grads, 1))
        sums = outer_sum(local_sums)
        results = [
            gate_back_call(
                len(groups[i][0]), team_lengths, at[i], grads[i][0], saved_three[i][1],
                saved_three[i][0], stats, sums, squares, taps, tap_count, slots, width,
            )
            for i in reversed(range(len(groups)))
        ][::-1]
        tap_terms = columns_of(columns_of(results, 1), 1)
        conv_term = conv_weight_call(
            normed_three, columns_of(columns_of(results, 1), 0), active_conv, chunk_order(groups),
            planes,
        )
        parts, conv_term = scatter(columns_of(results, 0), conv_term)
        grad_two, low, norm_two = join_back_call(stream_two, grad_three, parts, 1.0, norms[2])
        low, conv_term, second_term = lax.optimization_barrier((low, conv_term, second_term))
        conv_term = plane_reduce(conv_term)

        def attention_back(i, group):
            return attention_back_call(
                group, side, squares, mix, rows_held, place, saved_two[i][0], saved_two[i][1],
                head_size,
            )

        groups, results = spread(low, attention_back)
        mixed, rows = columns_of(saved_two, 2), chunk_order(groups)
        grads = columns_of(results, 1)
        bias_terms = columns_of(grads, 2)
        mix_term = mix_weight_call(
            normed_two, columns_of(grads, 0), mixed, rows, [table] + columns_of(grads, 1), side,
            planes, per_side,
        )
        parts, mix_term = scatter(columns_of(results, 0), mix_term)
        if not head_aligned:
            mix_own = mm_tn(jnp.concatenate(mixed), jnp.concatenate(rows)).astype(BF16)
            mix_own = lax.dynamic_update_slice_in_dim(
                jnp.zeros((width, width), BF16), mix_own, team_at * team_width, axis=0
            )
        grad_one, low, norm_one = join_back_call(stream_one, grad_two, parts, 0.5, norms[1])
        low, mix_term, conv_term = lax.optimization_barrier((low, mix_term, conv_term))
        mix_term = plane_reduce(mix_term)

        parts, first_term = feed_backward(low, pack_one, saved_one)
        first_term = plane_reduce(first_term)
        frames_grad, norm_zero = join_back_call(frames, grad_one, parts, 1.0, norms[0], keep=False)

        late = (second_term, conv_term, mix_term)
        frames_grad, late = lax.optimization_barrier((frames_grad, late))
        second_term, conv_term, mix_term = late
        depth = width // planes
        rate_scale = lax.rsqrt(stats[0:1])

        def from_team(rows, columns):
            return team_swap(rows.astype(BF16).reshape(team, -1, columns))

        def finish_channels(chan_term):
            chan_term = outer_sum(chan_term).reshape(chan_rows, planes, -1)
            chan_term = lax.dynamic_index_in_dim(chan_term, lax.axis_index("z"), 1, keepdims=False)
            if not wide_team:
                chan_term = lax.dynamic_index_in_dim(
                    chan_term.reshape(chan_rows, sides, -1), y_at, 1, keepdims=False
                )
            return chan_term

        norm_terms = [norm_zero, norm_one, norm_two, norm_three, norm_four]
        if head_aligned:
            second_up = from_team(second_term[:depth], team_hidden)
            features = kernel_call(
                functools.partial(feature_grad_kernel, planes, sides),
                [shape((team, 12, team_width), F32)],
                norm_terms + bias_terms,
                scalars=(team_at.reshape(1).astype(jnp.int32),),
            )[0]
            chan_term = kernel_call(
                functools.partial(channel_grad_kernel, tap_count),
                [shape((chan_rows, team_width), F32)],
                [team_swap(features), local_sums] + tap_terms,
            )[0]
            chan_grad = finish_channels(chan_term)
            blocks = kernel_call(
                column_grad_kernel,
                [shape((team, rows_in, 6 * team_width), BF16)],
                [mix_term, conv_term],
            )[0]
            square_all = update_call(
                functools.partial(update_square_kernel, planes, sides, head_size),
                rate_scale,
                [team_swap(blocks), mix_term, swap(mix_term, "y"), conv_term],
                square_weight,
                square_moment,
                square_average,
                scalars=(side,),
            )
            first_term, square_all, second_up = lax.optimization_barrier(
                (first_term, square_all, second_up)
            )
            down_all = update_call(
                update_down_kernel,
                rate_scale,
                [first_term, second_term],
                down_weight,
                down_moment,
                down_average,
            )
            up_all = update_call(
                update_up_kernel,
                rate_scale,
                [from_team(first_term[:depth], team_hidden), second_up],
                up_weight,
                up_moment,
                up_average,
            )
            up_grad, up_new = up_all[0], up_all[1:]
            down_grad, down_new = down_all[0], down_all[1:]
            square_grad, square_new = square_all[0], square_all[1:]
            rate_scale = rate_scale[0, 0]
        else:
            column_blocks = 4 * team_width // BLOCK
            qkv_term = from_blocks(mix_term[: column_blocks * depth], column_blocks)
            gate_blocks = 2 * team_width // BLOCK
            gate_term = from_blocks(conv_term[: gate_blocks * depth], gate_blocks)
            conv_out_term = from_blocks(conv_term[gate_blocks * depth :], width // BLOCK)
            mix_grad = lax.psum_scatter(mix_own, ALL, scatter_dimension=0, tiled=True).astype(F32)
            blocks = from_team(jnp.concatenate([qkv_term, gate_term], axis=1), 6 * team_width)

            def block(i):
                return blocks[:, :, i * team_width : (i + 1) * team_width]

            square_grad = jnp.stack(
                [side_scatter(join_heads(block(i))).astype(F32) for i in range(3)]
                + [mix_grad, side_scatter(join_heads(block(3))).astype(F32)]
                + [side_scatter(join_hidden(block(i))).astype(F32) for i in (4, 5)]
                + [side_scatter(conv_out_term).astype(F32)]
            )
            bias_rows = join_heads(
                lax.dynamic_update_slice_in_dim(
                    jnp.zeros((team, 2, team_width), F32), sum(bias_terms)[None], team_at, 0
                )
            )
            features = jnp.concatenate(
                [t[0:1] for t in norm_terms] + [t[1:2] for t in norm_terms] + [bias_rows]
            )
            features = jnp.sum(team_swap(split_hidden(features)), axis=0)
            chan_grad = finish_channels(
                jnp.concatenate(
                    [
                        sum(tap_terms)[:tap_count],
                        features[:10],
                        local_sums[:2],
                        features[10:],
                    ]
                )
            )
            feed_terms = (first_term, second_term)
            up_grad = jnp.stack(
                [
                    side_scatter(join_hidden(from_team(rows[:depth], team_hidden))).astype(F32)
                    for rows in feed_terms
                ]
            )
            down_grad = jnp.stack(
                [
                    side_scatter(from_blocks(rows[depth:], width // team_hidden)).astype(F32)
                    for rows in feed_terms
                ]
            )
            rate_scale = rate_scale[0, 0]
            up_new = nesterov(up_weight, up_moment, up_average, up_grad, RATE_UP, rate_scale)
            down_new = nesterov(
                down_weight, down_moment, down_average, down_grad, RATE_DOWN, rate_scale
            )
            square_new = nesterov(
                square_weight, square_moment, square_average, square_grad, RATE_SQUARE, rate_scale
            )
        chan_new = nesterov(
            chan_weight, chan_moment, chan_average, chan_grad, RATE_CHANNEL, rate_scale
        )
        bias_grad = chan_grad[tap_count + 12 : tap_count + 14]
        return (
            output,
            frames_grad,
            up_grad,
            down_grad,
            square_grad,
            chan_grad,
            up_new[0],
            down_new[0],
            square_new[0],
            chan_new[0],
            up_new[1],
            down_new[1],
            square_new[1],
            chan_new[1],
            up_new[2],
            down_new[2],
            square_new[2],
            chan_new[2],
            bias_grad,
        )

    return step


def solution(mesh):
    wide, narrow = mesh.shape["wide"], mesh.shape["narrow"]
    planes = wide // 4
    inner = Mesh(mesh.devices.reshape(planes, 2, 2, narrow), ALL)
    token = P(ALL, None)
    matrix = P(None, ALL, None)
    vector = P(None, ALL)
    group = (matrix, matrix, matrix, vector)
    return jax.shard_map(
        make_step(planes, narrow),
        mesh=inner,
        in_specs=(token, token, token) + group * 3,
        out_specs=(token, token) + group * 4 + (vector,),
        check_vma=False,
    )
```

```python
import functools

import jax
import jax.numpy as jnp
from jax import lax
from jax.experimental import pallas as pl
from jax.experimental.pallas import tpu as pltpu
from jax.sharding import Mesh
from jax.sharding import PartitionSpec as P

HEADS = 16
EPSILON = 1e-05
MOMENTUM_DECAY = 0.9
AVERAGE_DECAY = 0.9
RATE_UP = 0.05
RATE_DOWN = 0.026
RATE_SQUARE = 0.05
RATE_CHANNEL = 0.5
MASKED_SCORE = -1e30
BF16 = jnp.bfloat16
F32 = jnp.float32
ALL = ("z", "x", "c", "y")
LANES = 128
PAD = 16
BLOCK = 256
CARRY = 16
ROOM = 6 << 20


def mm(left, right):
    return jnp.dot(left, right, preferred_element_type=F32)


def mm_tn(left, right):
    return lax.dot_general(left, right, (((0,), (0,)), ((), ())), preferred_element_type=F32)


def mm_nt(left, right):
    return lax.dot_general(left, right, (((1,), (1,)), ((), ())), preferred_element_type=F32)


def swap(values, axis, bit=1):
    size = lax.axis_size(axis)
    return lax.ppermute(values, axis, [(i, i ^ bit) for i in range(size)])


def sigmoid(values):
    return 1.0 / (1.0 + jnp.exp(-values))


def swish_grad(values):
    sig = sigmoid(values)
    return sig * (1.0 + values * (1.0 - sig))


def normalize(values):
    centre = values - jnp.mean(values, axis=-1, keepdims=True)
    scale = lax.rsqrt(jnp.mean(centre * centre, axis=-1, keepdims=True) + EPSILON)
    return centre * scale, scale


def shape(dims, dtype):
    return jax.ShapeDtypeStruct(tuple(dims), dtype)


def size_of(item):
    total = 1
    for n in item.shape:
        total *= n
    return total * item.dtype.itemsize


def kernel_call(body, outs, args, scalars=(), flops=0, scratch=()):
    moved = sum(size_of(a) for a in args) + sum(size_of(o) for o in outs)
    return pl.pallas_call(
        body,
        out_shape=tuple(outs),
        in_specs=[pl.BlockSpec(memory_space=pltpu.SMEM)] * len(scalars)
        + [pl.BlockSpec(memory_space=pltpu.VMEM)] * len(args),
        out_specs=tuple(pl.BlockSpec(memory_space=pltpu.VMEM) for _ in outs),
        scratch_shapes=list(scratch),
        compiler_params=pltpu.CompilerParams(vmem_limit_bytes=moved + ROOM),
        cost_estimate=pl.CostEstimate(flops=int(flops), bytes_accessed=moved, transcendentals=0),
    )(*scalars, *args)


def store_partial(mine_refs, mate_ref, i, slots, value):
    mine_refs[i][...] = value[:slots]
    mate_ref[i] = value[slots:].astype(BF16)


def up_product(rows, ref):
    planes = ref.shape[0]
    depth = rows.shape[1] // planes
    total = mm(rows[:, :depth], ref[0, :depth, :])
    for p in range(1, planes):
        total = total + mm(rows[:, p * depth : (p + 1) * depth], ref[p, :depth, :])
    return total


def up_product_back(rows, ref, width):
    planes = ref.shape[0]
    depth = width // planes
    return jnp.concatenate([mm_nt(rows, ref[p, :depth, :]) for p in range(planes)], axis=1)


def down_blocks(ref, width):
    planes, hidden = ref.shape[0], ref.shape[2]
    rows = hidden // planes
    depth = ref.shape[1] - rows * (width // hidden)
    return [
        jnp.concatenate(
            [ref[p, depth + b * rows : depth + (b + 1) * rows, :] for p in range(planes)]
        )
        for b in range(width // hidden)
    ]


def down_product(rows, blocks):
    return jnp.concatenate([mm(rows, block) for block in blocks], axis=1)


def down_product_back(rows, blocks):
    size = blocks[0].shape[1]
    total = mm_nt(rows[:, :size], blocks[0])
    for b in range(1, len(blocks)):
        total = total + mm_nt(rows[:, b * size : (b + 1) * size], blocks[b])
    return total


def square_columns(ref, p, depth, first, last):
    parts = []
    while first < last:
        block = first // BLOCK
        stop = min(last, (block + 1) * BLOCK)
        lanes = slice(first - block * BLOCK, stop - block * BLOCK)
        parts.append(ref[p, block * depth : (block + 1) * depth, lanes])
        first = stop
    return jnp.concatenate(parts, axis=1) if len(parts) > 1 else parts[0]


def square_product(rows, ref, first, last):
    planes = ref.shape[0]
    depth = rows.shape[1] // planes
    total = None
    for p in range(planes):
        term = mm(rows[:, p * depth : (p + 1) * depth], square_columns(ref, p, depth, first, last))
        total = term if total is None else total + term
    return total


def square_product_back(rows, ref, width, first, last):
    planes = ref.shape[0]
    depth = width // planes
    return jnp.concatenate(
        [mm_nt(rows, square_columns(ref, p, depth, first, last)) for p in range(planes)], axis=1
    )


def output_rows(ref, p, width, base):
    blocks = width // BLOCK
    rows = (ref.shape[1] - base) // blocks
    parts = []
    for b in range(blocks):
        at = base + b * rows
        part = ref[pl.ds(p, 1), at : at + rows, :]
        parts.append(part.reshape(part.shape[1:]))
    return jnp.concatenate(parts, axis=1)


def forward_kernel(k, packs, with_norm, *refs):
    mine, mate, refs = refs[:k], refs[k : 2 * k], refs[2 * k :]
    if with_norm:
        norm_ref, refs = refs[0], refs[1:]
    up_ref, down_ref, refs = refs[0], refs[packs - 1], refs[packs:]
    out_mine, out_mate, before_ref = refs[:k], refs[k], refs[k + 1]
    slots, width = mine[0].shape
    blocks = down_blocks(down_ref, width)
    for i in range(k):
        rows = jnp.concatenate([mine[i][...], mate[i][...]])
        at = pl.ds(2 * i * slots, 2 * slots)
        if with_norm:
            unit, _ = normalize(rows.astype(F32))
            rows = (unit * norm_ref[0:1, :] + norm_ref[1:2, :]).astype(BF16)
            refs[k + 2][at, :] = rows
        before = up_product(rows, up_ref)
        before_ref[at, :] = before
        active = (before * sigmoid(before)).astype(BF16)
        store_partial(out_mine, out_mate, i, slots, down_product(active, blocks))


def forward_call(group, packs, norm=None):
    mine, mate = group
    k, (slots, width) = len(mine), mine[0].shape
    hidden = packs[0].shape[2]
    rows = 2 * k * slots
    outs = [shape((slots, width), F32)] * k + [
        shape((k, slots, width), BF16),
        shape((rows, hidden), F32),
    ]
    args = list(mine) + list(mate)
    if norm is not None:
        outs.append(shape((rows, width), BF16))
        args.append(norm)
    result = kernel_call(
        functools.partial(forward_kernel, k, len(packs), norm is not None),
        outs,
        args + list(packs),
        flops=4 * rows * width * hidden,
    )
    return (result[:k], result[k]), result[k + 1 :]


def backward_kernel(k, packs, *refs):
    mine, mate, refs = refs[:k], refs[k : 2 * k], refs[2 * k :]
    up_ref, down_ref, before_ref, refs = refs[0], refs[packs - 1], refs[packs], refs[packs + 1 :]
    out_mine, out_mate, grad_ref, active_ref = refs[:k], refs[k], refs[k + 1], refs[k + 2]
    slots, width = mine[0].shape
    blocks = down_blocks(down_ref, width)
    for i in range(k):
        at = pl.ds(2 * i * slots, 2 * slots)
        rows = jnp.concatenate([mine[i][...], mate[i][...]])
        before = before_ref[at, :]
        sig = sigmoid(before)
        active_ref[at, :] = (before * sig).astype(BF16)
        grad = down_product_back(rows, blocks) * (sig * (1.0 + before * (1.0 - sig)))
        grad = grad.astype(BF16)
        grad_ref[at, :] = grad
        store_partial(out_mine, out_mate, i, slots, up_product_back(grad, up_ref, width))


def backward_call(group, packs, before):
    mine, mate = group
    k, (slots, width) = len(mine), mine[0].shape
    rows, hidden = before.shape
    outs = [shape((slots, width), F32)] * k + [
        shape((k, slots, width), BF16),
        shape((rows, hidden), BF16),
        shape((rows, hidden), BF16),
    ]
    result = kernel_call(
        functools.partial(backward_kernel, k, len(packs)),
        outs,
        list(mine) + list(mate) + list(packs) + [before],
        flops=4 * rows * width * hidden,
    )
    return (result[:k], result[k]), result[k + 1 :]


def joined(refs, first=0, last=None):
    return jnp.concatenate([r[:, first:last] for r in refs])


def take(refs, counts):
    groups, at = [], 0
    for n in counts:
        groups.append(refs[at : at + n])
        at += n
    return groups + [refs[at:]]


def put(out_ref, planes, write):
    for p in range(planes):
        write(out_ref.at[p], p)


def rows_at(ref, p, rows, lanes=slice(None)):
    return ref[pl.ds(pl.multiple_of(p * rows, rows), rows), lanes]


def feed_weight_kernel(counts, planes, *refs):
    normed, grads, active, rows, refs = take(refs, counts)
    out_ref, up_ref, down_ref = refs
    width, hidden = up_ref.shape
    depth, below = width // planes, hidden // planes
    down_ref[...] = mm_tn(joined(active), joined(rows))
    up_ref[...] = mm_tn(joined(normed), joined(grads))

    def write(out, p):
        out[:depth, :] = rows_at(up_ref, p, depth).astype(BF16)
        for b in range(width // hidden):
            at = depth + b * below
            lanes = slice(b * hidden, (b + 1) * hidden)
            out[at : at + below, :] = rows_at(down_ref, p, below, lanes).astype(BF16)

    put(out_ref, planes, write)


def feed_weight_call(normed, grads, active, rows, planes):
    width, hidden = normed[0].shape[1], grads[0].shape[1]
    lines = width // planes + (hidden // planes) * (width // hidden)
    groups = (normed, grads, active, rows)
    tokens = sum(a.shape[0] for a in grads)
    return kernel_call(
        functools.partial(feed_weight_kernel, [len(g) for g in groups], planes),
        [shape((planes, lines, hidden), BF16)],
        [a for g in groups for a in g],
        flops=4 * width * hidden * tokens,
        scratch=[pltpu.VMEM((width, hidden), F32), pltpu.VMEM((hidden, width), F32)],
    )[0]


def write_columns(out, total_ref, p, depth):
    for b in range(total_ref.shape[1] // BLOCK):
        lanes = slice(b * BLOCK, (b + 1) * BLOCK)
        out[b * depth : (b + 1) * depth, :] = rows_at(total_ref, p, depth, lanes).astype(BF16)


def write_output_rows(out, base, rows):
    count = rows.shape[0]
    for b in range(rows.shape[1] // BLOCK):
        at = base + b * count
        out[at : at + count, :] = rows[:, b * BLOCK : (b + 1) * BLOCK].astype(BF16)


def conv_weight_kernel(counts, planes, *refs):
    normed, grads, active, rows, refs = take(refs, counts)
    out_ref, gate_ref, row_ref = refs
    depth = gate_ref.shape[0] // planes
    below = row_ref.shape[0] // planes
    base = (gate_ref.shape[1] // BLOCK) * depth
    gate_ref[...] = mm_tn(joined(normed), joined(grads))
    row_ref[...] = mm_tn(joined(active), joined(rows))

    def write(out, p):
        write_columns(out, gate_ref, p, depth)
        write_output_rows(out, base, rows_at(row_ref, p, below))

    put(out_ref, planes, write)


def conv_weight_call(normed, grads, active, rows, planes):
    width, gates, size = normed[0].shape[1], grads[0].shape[1], active[0].shape[1]
    lines = (gates // BLOCK) * (width // planes) + (width // BLOCK) * (size // planes)
    groups = (normed, grads, active, rows)
    tokens = sum(a.shape[0] for a in grads)
    return kernel_call(
        functools.partial(conv_weight_kernel, [len(g) for g in groups], planes),
        [shape((planes, lines, BLOCK), BF16)],
        [a for g in groups for a in g],
        flops=2 * width * (gates + size) * tokens,
        scratch=[pltpu.VMEM((width, gates), F32), pltpu.VMEM((size, width), F32)],
    )[0]


def mix_weight_kernel(counts, planes, per_side, *refs):
    side_ref, refs = refs[0], refs[1:]
    saved, grads, rows, place, refs = take(refs, counts)
    table_ref, place = place[0], place[1:]
    out_ref, total_ref, row_ref = refs
    size = row_ref.shape[0]
    depth = total_ref.shape[0] // planes
    base = (total_ref.shape[1] // BLOCK) * depth
    right = joined(grads)
    qkv = right.shape[1]
    total_ref[:, :qkv] = mm_tn(joined(saved, 0, total_ref.shape[0]), right)
    position = sum(ref[...] for ref in place)
    total_ref[:, qkv:] = mm_tn(table_ref[...], position.astype(BF16))
    if per_side:
        last = saved[0].shape[1]
        row_ref[...] = mm_tn(joined(saved, last - size, last), joined(rows))

    def write(out, p):
        write_columns(out, total_ref, p, depth)
        if per_side:
            below = row_ref.shape[0] // per_side
            place = p - side_ref[0] * per_side
            held = (place >= 0) & (place < per_side)
            share = held.astype(jnp.int32).astype(F32)
            head = rows_at(row_ref, jnp.where(held, place, 0), below) * share
            write_output_rows(out, base, head)

    put(out_ref, planes, write)


def mix_weight_call(saved, grads, rows, place, side, planes, per_side):
    width, qkv, size = rows[0].shape[1], grads[0].shape[1], grads[0].shape[1] // 3
    total = qkv + size
    lines = (total // BLOCK) * (width // planes)
    if per_side:
        lines += (width // BLOCK) * (size // per_side)
    groups = (saved, grads, rows, place)
    tokens = sum(a.shape[0] for a in grads)
    return kernel_call(
        functools.partial(mix_weight_kernel, [len(g) for g in groups], planes, per_side),
        [shape((planes, lines, BLOCK), BF16)],
        [a for g in groups for a in g],
        scalars=(side,),
        flops=2 * width * (total + size) * tokens,
        scratch=[pltpu.VMEM((width, total), F32), pltpu.VMEM((size, width), F32)],
    )[0]


def channel_kernel(planes, sides, head_size, *refs):
    at_ref, pieces, refs = refs[0], refs[1 : 1 + planes], refs[1 + planes :]
    norm_refs, (tap_ref, batch_ref, bias_ref, length_ref, wide_ref) = refs[:5], refs[5:]
    plane, member, side, core = at_ref[0], at_ref[1], at_ref[2], at_ref[3]
    team, rows = pieces[0].shape[0], pieces[0].shape[1] - CARRY
    size = tap_ref.shape[1]
    listed = [pieces[0][m, rows : rows + 1, :].astype(F32) for m in range(team)]
    one = jnp.concatenate([listed[4], listed[3]])
    two = jnp.concatenate([listed[1], listed[6]])
    table = [
        listed[0],
        listed[2],
        jnp.where(core == 0, one, two),
        jnp.where(core == 0, two, one),
        listed[5],
        listed[7],
    ]
    length_ref[...] = jnp.concatenate(table).astype(jnp.int32)[:, : length_ref.shape[1]]
    for d in range(planes):
        for m in range(team):
            at = ((plane ^ d) * team + (member ^ m)) * rows
            wide_ref[pl.ds(pl.multiple_of(at, rows), rows), :] = pieces[d][m, :rows, :].astype(F32)
    every = wide_ref[...].T
    taps = tap_ref.shape[0] - 1
    for j in range(5):
        first = every[taps + j : taps + j + 1]
        norm_refs[j][...] = jnp.concatenate([first, every[taps + 5 + j : taps + 6 + j]])
    own = [
        wide_ref[pl.ds(pl.multiple_of((p * team + member) * rows, rows), rows), :]
        for p in range(planes)
    ]
    own = jnp.concatenate(own).T
    tap_ref[...] = own[: taps + 1]
    batch_ref[...] = own[taps + 10 : taps + 12]
    heads = size // head_size
    own = [
        wide_ref[
            pl.ds(
                pl.multiple_of(
                    (side * heads + h) * team * rows + (member // sides) * head_size, head_size
                ),
                head_size,
            ),
            :,
        ]
        for h in range(heads)
    ]
    own = jnp.concatenate(own).T
    bias_ref[...] = own[taps + 12 : taps + 14]


def chunk_order(groups):
    return [chunk for group in groups for pair in zip(*group) for chunk in pair]


def add_kernel(count, *refs):
    own_ref, mate_ref, out_ref = refs[0], refs[1], refs[-1]
    total = own_ref[...] + mate_ref[count].astype(F32)
    for ref in refs[2:-1]:
        total = total + ref[...].astype(F32)
    out_ref[...] = total.astype(BF16)


def add_call(own, mate, index, *more):
    return kernel_call(
        functools.partial(add_kernel, index), [shape(own.shape, BF16)], [own, mate] + list(more)
    )[0]


def item_bounds(length_ref, b=0):
    ends = [length_ref[b, 0]]
    for j in range(1, length_ref.shape[1] - 1):
        ends.append(ends[-1] + length_ref[b, j])
    return ends


def item_index(ends, where_at):
    total = (where_at >= ends[0]).astype(jnp.int32)
    for end in ends[1:]:
        total = total + (where_at >= end).astype(jnp.int32)
    return total


def head_masks(slots, head_size):
    lane = lax.broadcasted_iota(jnp.int32, (slots, LANES), 1)
    return [
        (lane >= h * head_size) & (lane < (h + 1) * head_size) for h in range(LANES // head_size)
    ]


def saved_lanes(width, size, heads, slots):
    ends = [width]
    for lanes in [size] * 4 + [slots] * heads + [size]:
        ends.append(ends[-1] + lanes)
    return ends


def attention_kernel(k, first, head_size, per_side, *refs):
    length_ref, side_ref, refs = refs[0], refs[1], refs[2:]
    mine, mate, refs = refs[:k], refs[k : 2 * k], refs[2 * k :]
    bias_ref, place_ref, pack_ref = refs[:3]
    mix_ref, refs = (None, refs[3:]) if per_side else (refs[3], refs[4:])
    out_mine, out_mate, saved_ref = refs[:k], refs[k], refs[k + 1]
    slots, width = mine[0].shape
    size = place_ref.shape[1]
    ends = saved_lanes(width, size, size // head_size, slots)
    mix = mix_rows(pack_ref, mix_ref, side_ref, width, size, per_side)
    scale = head_size ** (-0.5)
    row_at = lax.broadcasted_iota(jnp.int32, (slots, slots), 0)
    column_at = lax.broadcasted_iota(jnp.int32, (slots, slots), 1)
    masks = head_masks(slots, head_size)
    for i in range(k):
        rows = jnp.concatenate([mine[i][...], mate[i][...]])
        qkv = square_product(rows, pack_ref, 0, 3 * size)
        query = qkv[:, :size]
        query_c = (query + bias_ref[0:1, :]).astype(BF16)
        query_p = (query + bias_ref[1:2, :]).astype(BF16)
        key = qkv[:, size : 2 * size].astype(BF16)
        value = qkv[:, 2 * size :].astype(BF16)
        at = pl.ds(2 * i * slots, 2 * slots)
        saved_ref[at, : ends[0]] = rows
        for n, part in enumerate((query_c, query_p, key, value)):
            saved_ref[at, ends[n] : ends[n + 1]] = part
        halves = []
        for j in range(2):
            b = 2 * i + j
            part = slice(j * slots, (j + 1) * slots)
            rows_of = pl.ds(b * slots, slots)
            edges = item_bounds(length_ref, first + b)
            same = item_index(edges, row_at) == item_index(edges, column_at)
            blocks = []
            for lo in range(0, size, LANES):
                lanes = slice(lo, lo + LANES)
                mixed = jnp.zeros((slots, LANES), F32)
                for h, mask in enumerate(masks):
                    qc = jnp.where(mask, query_c[part, lanes], 0)
                    qp = jnp.where(mask, query_p[part, lanes], 0)
                    wide = mm_nt(qp, place_ref[:, lanes])
                    moved = pltpu.roll(wide, slots + 1, 1, stride=1, stride_axis=0)
                    scores = (mm_nt(qc, key[part, lanes]) + moved[:, :slots]) * scale
                    scores = jnp.where(same, scores, MASKED_SCORE)
                    top = jnp.max(scores, axis=-1, keepdims=True)
                    weights = jnp.exp(scores - top)
                    probs = weights / jnp.sum(weights, axis=-1, keepdims=True)
                    probs = probs.astype(BF16)
                    n = 4 + (lo // LANES) * len(masks) + h
                    saved_ref[rows_of, ends[n] : ends[n + 1]] = probs
                    mixed = jnp.where(mask, mm(probs, value[part, lanes]), mixed)
                blocks.append(mixed)
            halves.append(jnp.concatenate(blocks, axis=1) if len(blocks) > 1 else blocks[0])
        mixed = jnp.concatenate(halves).astype(BF16)
        saved_ref[at, ends[-2] : ends[-1]] = mixed
        store_partial(out_mine, out_mate, i, slots, mm(mixed, mix))


def mix_rows(pack_ref, mix_ref, side_ref, width, size, per_side):
    if not per_side:
        return mix_ref[...]
    base = (4 * size // BLOCK) * (width // pack_ref.shape[0])
    return jnp.concatenate(
        [output_rows(pack_ref, side_ref[0] * per_side + h, width, base) for h in range(per_side)]
    )


def attention_call(group, lengths, first, side, packs, per_side, bias, place, head_size):
    mine, mate = group
    k, (slots, width) = len(mine), mine[0].shape
    size = place.shape[1]
    heads = size // head_size
    rows = 2 * k * slots
    outs = [shape((slots, width), F32)] * k + [
        shape((k, slots, width), BF16),
        shape((rows, saved_lanes(width, size, heads, slots)[-1]), BF16),
    ]
    result = kernel_call(
        functools.partial(attention_kernel, k, first, head_size, per_side),
        outs,
        list(mine) + list(mate) + [bias, place] + list(packs),
        scalars=(lengths, side),
        flops=2 * rows * width * size * 4 + 2 * k * heads * 10 * slots * slots * LANES,
    )
    return (result[:k], result[k]), result[k + 1]


def attention_back_kernel(k, head_size, per_side, *refs):
    side_ref, refs = refs[0], refs[1:]
    mine, mate, refs = refs[:k], refs[k : 2 * k], refs[2 * k :]
    place_ref, saved_ref, pack_ref = refs[:3]
    mix_ref, refs = (None, refs[3:]) if per_side else (refs[3], refs[4:])
    out_mine, out_mate, grad_ref, place_grad_ref, bias_ref = (
        refs[:k],
        refs[k],
        refs[k + 1],
        refs[k + 2],
        refs[k + 3],
    )
    slots, width = mine[0].shape
    size = place_ref.shape[1]
    mix = mix_rows(pack_ref, mix_ref, side_ref, width, size, per_side)
    ends = saved_lanes(width, size, size // head_size, slots)
    scale = head_size ** (-0.5)
    masks = head_masks(slots, head_size)
    flip = (
        lax.broadcasted_iota(jnp.int32, (slots, slots), 0)
        + lax.broadcasted_iota(jnp.int32, (slots, slots), 1)
        == slots - 1
    ).astype(F32).astype(BF16)
    bias_c = jnp.zeros((1, size), F32)
    bias_p = jnp.zeros((1, size), F32)
    for i in range(k):
        rows = jnp.concatenate([mine[i][...], mate[i][...]])
        grad_mixed_all = mm_nt(rows, mix).astype(BF16)
        at = pl.ds(2 * i * slots, 2 * slots)
        halves = []
        for j in range(2):
            b = 2 * i + j
            part = slice(j * slots, (j + 1) * slots)
            rows_at = pl.ds((2 * i + j) * slots, slots)
            grad_qc, grad_qp, grad_k, grad_v = [], [], [], []
            for lo in range(0, size, LANES):
                lanes = slice(lo, lo + LANES)
                grad_mixed = grad_mixed_all[part, lanes]
                query_c, query_p, key, value = [
                    saved_ref[rows_at, ends[n] + lo : ends[n] + lo + LANES] for n in range(4)
                ]
                place = place_ref[:, lanes]
                gqc = jnp.zeros((slots, LANES), F32)
                gqp, gk, gv = gqc, gqc, gqc
                place_grad = jnp.zeros(place.shape, F32)
                for h, mask in enumerate(masks):
                    n = 4 + (lo // LANES) * len(masks) + h
                    probs = saved_ref[rows_at, ends[n] : ends[n + 1]]
                    own = jnp.where(mask, grad_mixed, 0)
                    grad_probs = mm_nt(own, value)
                    gv = gv + mm_tn(probs, own)
                    probs = probs.astype(F32)
                    inner = jnp.sum(probs * grad_probs, axis=-1, keepdims=True)
                    grad = (probs * (grad_probs - inner)).astype(BF16) * scale
                    grad = grad.astype(BF16)
                    gqc = jnp.where(mask, mm(grad, key), gqc)
                    gk = gk + mm_tn(grad, jnp.where(mask, query_c, 0))
                    turned = mm(flip, grad)
                    wide = jnp.concatenate([turned, jnp.zeros_like(turned)], axis=1)
                    wide = pltpu.roll(wide, 0, 1, stride=1, stride_axis=0).astype(BF16)
                    wide = mm(flip, wide).astype(BF16)
                    gqp = jnp.where(mask, mm(wide, place), gqp)
                    place_grad = place_grad + mm_tn(wide, jnp.where(mask, query_p, 0))
                if i == 0 and j == 0:
                    place_grad_ref[:, lanes] = place_grad
                else:
                    place_grad_ref[:, lanes] = place_grad_ref[:, lanes] + place_grad
                grad_qc.append(gqc)
                grad_qp.append(gqp)
                grad_k.append(gk)
                grad_v.append(gv)

            def side_by_side(blocks):
                return jnp.concatenate(blocks, axis=1) if len(blocks) > 1 else blocks[0]

            gqc, gqp = side_by_side(grad_qc), side_by_side(grad_qp)
            bias_c = bias_c + jnp.sum(gqc, axis=0, keepdims=True)
            bias_p = bias_p + jnp.sum(gqp, axis=0, keepdims=True)
            halves.append(
                jnp.concatenate(
                    [gqc + gqp, side_by_side(grad_k), side_by_side(grad_v)], axis=1
                ).astype(BF16)
            )
        grad = jnp.concatenate(halves)
        grad_ref[at, :] = grad
        store_partial(out_mine, out_mate, i, slots, square_product_back(grad, pack_ref, width, 0, 3 * size))
    bias_ref[...] = jnp.concatenate([bias_c, bias_p])


def attention_back_call(group, side, packs, per_side, place, saved, head_size):
    mine, mate = group
    k, (slots, width) = len(mine), mine[0].shape
    size = place.shape[1]
    rows = 2 * k * slots
    outs = [shape((slots, width), F32)] * k + [
        shape((k, slots, width), BF16),
        shape((rows, 3 * size), BF16),
        shape(place.shape, F32),
        shape((2, size), F32),
    ]
    result = kernel_call(
        functools.partial(attention_back_kernel, k, head_size, per_side),
        outs,
        list(mine) + list(mate) + [place, saved] + list(packs),
        scalars=(side,),
        flops=2 * rows * width * size * 4 + 2 * k * 24 * slots * slots * size,
    )
    return (result[:k], result[k]), result[k + 1 :]


def place_kernel(table_ref, column_ref, out_ref):
    size = out_ref.shape[1]
    rows = square_product(table_ref[...], column_ref, 3 * size, 4 * size)
    out_ref[...] = rows.astype(BF16)


def item_reach(ends, row_at, slots):
    start = jnp.zeros_like(row_at)
    end = jnp.full_like(row_at, slots)
    for at in ends:
        start = jnp.where(row_at >= at, at, start)
    for at in reversed(ends):
        end = jnp.where(row_at < at, at, end)
    valid = (row_at < ends[-1]).astype(F32)
    return row_at - start, end - 1 - row_at, valid


def gate_kernel(k, first, tap_count, *refs):
    length_ref, refs = refs[0], refs[1:]
    mine, mate, refs = refs[:k], refs[k : 2 * k], refs[2 * k :]
    pack_ref, tap_ref, gate_ref, normed_ref, stat_ref, pad_ref = refs
    slots, _ = mine[0].shape
    size = tap_ref.shape[1]
    reach = tap_count // 2
    row_at = lax.broadcasted_iota(jnp.int32, (slots, size), 0)
    pad_ref[...] = jnp.zeros_like(pad_ref)
    count = jnp.zeros((1, size), F32)
    total = jnp.zeros((1, size), F32)
    for i in range(k):
        rows = jnp.concatenate([mine[i][...], mate[i][...]])
        gates = square_product(rows, pack_ref, 0, 2 * size)
        gate_ref[pl.ds(2 * i * slots, 2 * slots), : 2 * size] = gates
        normed_ref[pl.ds(2 * i * slots, 2 * slots), :] = rows
        glu = gates[:, :size] * sigmoid(gates[:, size:])
        for j in range(2):
            b = 2 * i + j
            before, behind, valid = item_reach(item_bounds(length_ref, first + b), row_at, slots)
            pad_ref[PAD : PAD + slots, :] = glu[j * slots : (j + 1) * slots] * valid
            conv = jnp.zeros((slots, size), F32)
            for tap in range(tap_count):
                o = tap - reach
                near = pad_ref[PAD + o : PAD + o + slots, :]
                if o < 0:
                    near = jnp.where(before >= -o, near, 0.0)
                elif o > 0:
                    near = jnp.where(behind >= o, near, 0.0)
                conv = conv + near * tap_ref[tap : tap + 1, :]
            gate_ref[pl.ds(b * slots, slots), 2 * size :] = conv
            count = count + jnp.sum(valid, axis=0, keepdims=True)
            total = total + jnp.sum(conv * valid, axis=0, keepdims=True)
    mean = total / count
    spread = jnp.zeros((1, size), F32)
    for b in range(2 * k):
        valid = (row_at < item_bounds(length_ref, first + b)[-1]).astype(F32)
        gap = (gate_ref[pl.ds(b * slots, slots), 2 * size :] - mean) * valid
        spread = spread + jnp.sum(gap * gap, axis=0, keepdims=True)
    stat_ref[...] = jnp.concatenate([count, mean, spread, jnp.zeros((5, size), F32)])


def gate_call(group, lengths, first, pack, taps, tap_count):
    mine, mate = group
    k, (slots, width) = len(mine), mine[0].shape
    size = taps.shape[1]
    rows = 2 * k * slots
    return kernel_call(
        functools.partial(gate_kernel, k, first, tap_count),
        [shape((rows, 3 * size), F32), shape((rows, width), BF16), shape((8, size), F32)],
        list(mine) + list(mate) + [pack, taps],
        scalars=(lengths,),
        flops=4 * rows * width * size + 40 * tap_count * rows * size,
        scratch=[pltpu.VMEM((slots + 2 * PAD, size), F32)],
    )


def merge_kernel(*refs):
    out_ref = refs[-1]
    count, mean, spread = refs[0][0:1, :], refs[0][1:2, :], refs[0][2:3, :]
    for ref in refs[1:-1]:
        more = ref[0:1, :]
        total = count + more
        gap = ref[1:2, :] - mean
        spread = spread + ref[2:3, :] + gap * gap * (count * more / total)
        mean = (count * mean + more * ref[1:2, :]) / total
        count = total
    out_ref[...] = jnp.concatenate([count, mean, spread, jnp.zeros((5, mean.shape[1]), F32)])


def merge(parts):
    return kernel_call(merge_kernel, [shape(parts[0].shape, F32)], parts)[0]


def sum_kernel(*refs):
    refs[-1][...] = sum(ref[...] for ref in refs[:-1])


def sum_call(parts):
    return kernel_call(sum_kernel, [shape(parts[0].shape, F32)], parts)[0]


def batch_unit(conv, stat_ref):
    inverse = lax.rsqrt(stat_ref[2:3, :] / stat_ref[0:1, :] + EPSILON)
    return (conv - stat_ref[1:2, :]) * inverse, inverse


def batch_kernel(k, *refs):
    gate_ref, stat_ref, batch_ref, pack_ref, refs = refs[0], refs[1], refs[2], refs[3], refs[4:]
    out_mine, out_mate = refs[:k], refs[k]
    slots, width = out_mine[0].shape
    size = batch_ref.shape[1]
    weight = conv_rows(pack_ref, width, size)
    for i in range(k):
        at = pl.ds(2 * i * slots, 2 * slots)
        unit, _ = batch_unit(gate_ref[at, 2 * size :], stat_ref)
        value = unit * batch_ref[0:1, :] + batch_ref[1:2, :]
        active = (value * sigmoid(value)).astype(BF16)
        store_partial(out_mine, out_mate, i, slots, mm(active, weight))


def conv_rows(pack_ref, width, size):
    planes = pack_ref.shape[0]
    base = (2 * size // BLOCK) * (width // planes)
    rows = size // planes
    parts = []
    for p in range(planes):
        blocks = [
            pack_ref[p, base + b * rows : base + (b + 1) * rows, :] for b in range(width // BLOCK)
        ]
        parts.append(jnp.concatenate(blocks, axis=1))
    return jnp.concatenate(parts)


def batch_call(k, gates, stats, batch_rows, pack, slots, width):
    rows, size = gates.shape[0], batch_rows.shape[1]
    outs = [shape((slots, width), F32)] * k + [shape((k, slots, width), BF16)]
    result = kernel_call(
        functools.partial(batch_kernel, k),
        outs,
        [gates, stats, batch_rows, pack],
        flops=2 * rows * width * size,
    )
    return result[:k], result[k]


def batch_back_kernel(k, first, *refs):
    length_ref, refs = refs[0], refs[1:]
    mine, mate, refs = refs[:k], refs[k : 2 * k], refs[2 * k :]
    gate_ref, stat_ref, batch_ref, pack_ref, grad_ref, active_ref, sum_ref = refs
    slots, width = mine[0].shape
    size = batch_ref.shape[1]
    weight = conv_rows(pack_ref, width, size)
    row_at = lax.broadcasted_iota(jnp.int32, (slots, size), 0)
    sums = [jnp.zeros((1, size), F32)] * 4
    for i in range(k):
        rows = jnp.concatenate([mine[i][...], mate[i][...]])
        grad_active = mm_nt(rows, weight)
        for j in range(2):
            b = 2 * i + j
            at = pl.ds(b * slots, slots)
            unit, _ = batch_unit(gate_ref[at, 2 * size :], stat_ref)
            value = unit * batch_ref[0:1, :] + batch_ref[1:2, :]
            sig = sigmoid(value)
            active_ref[at, :] = (value * sig).astype(BF16)
            grad = grad_active[j * slots : (j + 1) * slots] * (sig * (1.0 + value * (1.0 - sig)))
            valid = (row_at < item_bounds(length_ref, first + b)[-1]).astype(F32)
            grad_unit = grad * batch_ref[0:1, :]
            grad_ref[at, :] = grad_unit
            terms = (grad * unit, grad, grad_unit * valid, grad_unit * unit * valid)
            sums = [s + jnp.sum(t, axis=0, keepdims=True) for s, t in zip(sums, terms)]
    sum_ref[...] = jnp.concatenate(sums + [jnp.zeros((4, size), F32)])


def batch_back_call(group, lengths, first, gates, stats, batch_rows, pack):
    mine, mate = group
    k, (slots, width) = len(mine), mine[0].shape
    rows, size = gates.shape[0], batch_rows.shape[1]
    return kernel_call(
        functools.partial(batch_back_kernel, k, first),
        [shape((rows, size), F32), shape((rows, size), BF16), shape((8, size), F32)],
        list(mine) + list(mate) + [gates, stats, batch_rows, pack],
        scalars=(lengths,),
        flops=2 * rows * width * size,
    )


def gate_back_kernel(k, first, tap_count, *refs):
    length_ref, refs = refs[0], refs[1:]
    grad_in_ref, gate_ref, stat_ref, sum_ref, pack_ref, tap_ref, refs = (
        refs[0],
        refs[1],
        refs[2],
        refs[3],
        refs[4],
        refs[5],
        refs[6:],
    )
    out_mine, out_mate, grad_ref, tap_grad_ref, glu_ref, conv_grad_ref = (
        refs[:k],
        refs[k],
        refs[k + 1],
        refs[k + 2],
        refs[k + 3],
        refs[k + 4],
    )
    slots, width = out_mine[0].shape
    size = tap_ref.shape[1]
    reach = tap_count // 2
    row_at = lax.broadcasted_iota(jnp.int32, (slots, size), 0)
    glu_ref[...] = jnp.zeros_like(glu_ref)
    conv_grad_ref[...] = jnp.zeros_like(conv_grad_ref)
    tap_grad_ref[...] = jnp.zeros_like(tap_grad_ref)
    frame_count = stat_ref[0:1, :]
    mean_grad = sum_ref[2:3, :] / frame_count
    mean_cross = sum_ref[3:4, :] / frame_count
    for i in range(k):
        halves = []
        for j in range(2):
            b = 2 * i + j
            at = pl.ds(b * slots, slots)
            before, behind, valid = item_reach(item_bounds(length_ref, first + b), row_at, slots)
            gate_a, gate_sig = gate_ref[at, :size], sigmoid(gate_ref[at, size : 2 * size])
            glu_ref[PAD : PAD + slots, :] = gate_a * gate_sig * valid
            unit, inverse = batch_unit(gate_ref[at, 2 * size :], stat_ref)
            conv_grad = valid * inverse * (grad_in_ref[at, :] - mean_grad - unit * mean_cross)
            conv_grad_ref[PAD : PAD + slots, :] = conv_grad
            grad_glu = jnp.zeros((slots, size), F32)
            for tap in range(tap_count):
                o = tap - reach
                near = glu_ref[PAD + o : PAD + o + slots, :]
                back = conv_grad_ref[PAD - o : PAD - o + slots, :]
                if o < 0:
                    near = jnp.where(before >= -o, near, 0.0)
                    back = jnp.where(behind >= -o, back, 0.0)
                elif o > 0:
                    near = jnp.where(behind >= o, near, 0.0)
                    back = jnp.where(before >= o, back, 0.0)
                grad_glu = grad_glu + back * tap_ref[tap : tap + 1, :]
                tap_grad_ref[tap : tap + 1, :] += jnp.sum(near * conv_grad, axis=0, keepdims=True)
            grad_glu = grad_glu * valid
            halves.append(
                jnp.concatenate(
                    [grad_glu * gate_sig, grad_glu * gate_a * gate_sig * (1.0 - gate_sig)], axis=1
                ).astype(BF16)
            )
        grad = jnp.concatenate(halves)
        grad_ref[pl.ds(2 * i * slots, 2 * slots), :] = grad
        store_partial(out_mine, out_mate, i, slots, square_product_back(grad, pack_ref, width, 0, 2 * size))


def gate_back_call(k, lengths, first, grads, gates, stats, sums, pack, taps, tap_count, slots, width):
    rows, size = grads.shape
    outs = [shape((slots, width), F32)] * k + [
        shape((k, slots, width), BF16),
        shape((rows, 2 * size), BF16),
        shape(taps.shape, F32),
    ]
    padded = pltpu.VMEM((slots + 2 * PAD, size), F32)
    result = kernel_call(
        functools.partial(gate_back_kernel, k, first, tap_count),
        outs,
        [grads, gates, stats, sums, pack, taps],
        scalars=(lengths,),
        flops=4 * rows * width * size + 80 * tap_count * rows * size,
        scratch=[padded, padded],
    )
    return (result[:k], result[k]), result[k + 1 :]


def join_kernel(count, coefficient, *refs):
    stream_ref, own_ref, mate_ref, refs = refs[0], refs[1], refs[2], refs[3:]
    far, norm_ref, stream_out, normed_ref = refs[:count], refs[count], refs[count + 1], refs[count + 2]
    branch = own_ref[...] + mate_ref[0].astype(F32)
    for ref in far:
        branch = branch + ref[...].astype(F32)
    stream = stream_ref[...].astype(F32) + coefficient * branch
    stream_out[...] = stream
    unit, _ = normalize(stream)
    normed_ref[...] = (unit * norm_ref[0:1, :] + norm_ref[1:2, :]).astype(BF16)


def join_call(stream, parts, coefficient, norm):
    own, mate, far = parts
    return kernel_call(
        functools.partial(join_kernel, len(far), coefficient),
        [shape(own.shape, F32), shape(own.shape, BF16)],
        [stream, own, mate] + list(far) + [norm],
    )


def turn_kernel(count, coefficient, *refs):
    length_ref, refs = refs[0], refs[1:]
    stream_ref, own_ref, mate_ref, refs = refs[0], refs[1], refs[2], refs[3:]
    far, norm_ref, cotangent_ref, refs = refs[:count], refs[count], refs[count + 1], refs[count + 2 :]
    output_ref, grad_out, low_out, norm_grad = refs
    branch = own_ref[...] + mate_ref[0].astype(F32)
    for ref in far:
        branch = branch + ref[...].astype(F32)
    stream = stream_ref[...] + coefficient * branch
    row_at = lax.broadcasted_iota(jnp.int32, (stream.shape[0], 1), 0)
    valid = (row_at < item_bounds(length_ref)[-1]).astype(F32)
    unit, scale = normalize(stream)
    output_ref[...] = ((unit * norm_ref[0:1, :] + norm_ref[1:2, :]) * valid).astype(BF16)
    norm_back(
        unit,
        scale,
        norm_ref,
        cotangent_ref[...].astype(F32) * valid,
        0.0,
        0.5,
        grad_out,
        low_out,
        norm_grad,
    )


def norm_back(unit, scale, norm_ref, grad, base, coefficient, grad_out, low_out, norm_grad):
    norm_grad[...] = jnp.concatenate(
        [jnp.sum(grad * unit, axis=0, keepdims=True), jnp.sum(grad, axis=0, keepdims=True)]
    )
    grad = grad * norm_ref[0:1, :]
    inner = jnp.mean(grad, axis=-1, keepdims=True)
    cross = jnp.mean(grad * unit, axis=-1, keepdims=True)
    grad = base + scale * (grad - inner - unit * cross)
    if grad_out is not None:
        grad_out[...] = grad
    low_out[...] = (coefficient * grad).astype(BF16)


def turn_call(stream, parts, coefficient, norm, cotangent, lengths):
    own, mate, far = parts
    return kernel_call(
        functools.partial(turn_kernel, len(far), coefficient),
        [
            shape(own.shape, BF16),
            shape(own.shape, F32),
            shape(own.shape, BF16),
            shape((2, own.shape[1]), F32),
        ],
        [stream, own, mate] + list(far) + [norm, cotangent],
        scalars=(lengths,),
    )


def join_back_kernel(count, coefficient, keep, *refs):
    stream_ref, grad_ref, own_ref, mate_ref, refs = refs[0], refs[1], refs[2], refs[3], refs[4:]
    far, norm_ref, refs = refs[:count], refs[count], refs[count + 1 :]
    grad_out, (low_out, norm_grad) = (refs[0] if keep else None), refs[-2:]
    grad = own_ref[...] + mate_ref[0].astype(F32)
    for ref in far:
        grad = grad + ref[...].astype(F32)
    unit, scale = normalize(stream_ref[...].astype(F32))
    norm_back(
        unit, scale, norm_ref, grad, grad_ref[...], coefficient, grad_out, low_out, norm_grad
    )


def join_back_call(stream, grad, parts, coefficient, norm, keep=True):
    own, mate, far = parts
    outs = [shape(own.shape, F32)] if keep else []
    return kernel_call(
        functools.partial(join_back_kernel, len(far), coefficient, keep),
        outs + [shape(own.shape, BF16), shape((2, own.shape[1]), F32)],
        [stream, grad, own, mate] + list(far) + [norm],
    )


def offset_table(slot_count, model_width):
    offsets = jnp.arange(2 * slot_count, dtype=F32) - (slot_count - 1)
    freqs = jnp.exp(-jnp.log(10000.0) * jnp.arange(0, model_width, 2, dtype=F32) / model_width)
    angles = offsets[:, None] * freqs[None, :]
    return jnp.concatenate([jnp.sin(angles), jnp.cos(angles)], axis=1)


def nesterov(weight, moment, average, grad_rows, rate, rate_scale):
    moment_new = MOMENTUM_DECAY * moment + grad_rows
    weight_new = weight - rate * rate_scale * (grad_rows + MOMENTUM_DECAY * moment_new)
    average_new = AVERAGE_DECAY * average + (1.0 - AVERAGE_DECAY) * weight_new
    return (moment_new, weight_new, average_new)


def head_lanes(member, i, sides, planes, size):
    side, rest = member % sides, member // sides
    plane = side * (planes // sides) + i
    return (plane * 4 + rest) * size


def split_down_kernel(weight_ref, first_ref, second_ref):
    hidden = first_ref.shape[1]
    rows = weight_ref.shape[1]
    for layer, out in enumerate((first_ref, second_ref)):
        for b in range(weight_ref.shape[2] // hidden):
            part = weight_ref[layer, :, b * hidden : (b + 1) * hidden]
            out[b * rows : (b + 1) * rows, :] = part.astype(BF16)


def split_up_kernel(weight_ref, first_ref, second_ref):
    team, _, hidden = first_ref.shape
    planes = weight_ref.shape[2] // (team * LANES)
    for layer, out in enumerate((first_ref, second_ref)):
        for t in range(team):
            for p in range(planes):
                at = (p * team + t) * LANES
                part = weight_ref[layer, :, at : at + LANES]
                out[t, :, p * LANES : (p + 1) * LANES] = part.astype(BF16)


def split_square_kernel(planes, sides, head_size, weight_ref, column_ref, mix_ref, conv_ref):
    team = column_ref.shape[0]
    width = weight_ref.shape[2]
    size = width // team
    for t in range(team):
        for i, matrix in enumerate((0, 1, 2, 4, 5, 6)):
            if i < 4:
                starts = [
                    head_lanes(t, h, sides, planes, head_size) for h in range(size // head_size)
                ]
                count = head_size
            else:
                count = size // planes
                starts = [(p * team + t) * count for p in range(planes)]
            parts = [weight_ref[matrix, :, at : at + count] for at in starts]
            column_ref[t, :, i * size : (i + 1) * size] = jnp.concatenate(parts, axis=1).astype(BF16)
    mix_ref[...] = weight_ref[3].astype(BF16)
    conv_ref[...] = weight_ref[7].astype(BF16)


def square_pack_kernel(side_ref, column_ref, own_ref, other_ref, conv_ref, mix_out, conv_out):
    team, rows, lanes = column_ref.shape
    depth = team * rows
    for b in range(lanes // BLOCK):
        out, at = (mix_out, b * depth) if b < 2 else (conv_out, (b - 2) * depth)
        for t in range(team):
            first = at + t * rows
            out[first : first + rows, :] = column_ref[t, :, b * BLOCK : (b + 1) * BLOCK]
    low = side_ref[0] == 0
    for b in range(own_ref.shape[1] // BLOCK):
        lane = slice(b * BLOCK, (b + 1) * BLOCK)
        own, other = own_ref[:, lane].astype(F32), other_ref[:, lane].astype(F32)
        at = 2 * depth + b * 2 * rows
        mix_out[at : at + rows, :] = jnp.where(low, own, other).astype(BF16)
        mix_out[at + rows : at + 2 * rows, :] = jnp.where(low, other, own).astype(BF16)
        at = depth + b * rows
        conv_out[at : at + rows, :] = conv_ref[:, lane]
    at = depth + (own_ref.shape[1] // BLOCK) * rows
    conv_out[at:, :] = jnp.zeros((conv_out.shape[0] - at, BLOCK), BF16)


def feed_pack_kernel(up_ref, down_ref, out_ref):
    team, rows, _ = up_ref.shape
    for t in range(team):
        out_ref[t * rows : (t + 1) * rows, :] = up_ref[t]
    out_ref[team * rows :, :] = down_ref[...]


def column_grad_kernel(mix_ref, conv_ref, out_ref):
    team, rows, lanes = out_ref.shape
    depth = team * rows
    for b in range(lanes // BLOCK):
        ref, at = (mix_ref, b) if b < 2 else (conv_ref, b - 2)
        for t in range(team):
            first = at * depth + t * rows
            out_ref[t, :, b * BLOCK : (b + 1) * BLOCK] = ref[first : first + rows, :]


def update(scale_ref, rate, index, grad, refs):
    weight_ref, moment_ref, average_ref, grad_out, moment_out, weight_out, average_out = refs
    moment = MOMENTUM_DECAY * moment_ref[index] + grad
    weight = weight_ref[index] - rate * scale_ref[0:1, 0:1] * (grad + MOMENTUM_DECAY * moment)
    grad_out[index] = grad
    moment_out[index] = moment
    weight_out[index] = weight
    average_out[index] = AVERAGE_DECAY * average_ref[index] + (1.0 - AVERAGE_DECAY) * weight


def update_up_kernel(scale_ref, first_ref, second_ref, *refs):
    team, _, hidden = first_ref.shape
    for layer, ref in enumerate((first_ref, second_ref)):
        parts = [
            ref[t, :, p * LANES : (p + 1) * LANES] for p in range(hidden // LANES) for t in range(team)
        ]
        update(scale_ref, RATE_UP, layer, jnp.concatenate(parts, axis=1).astype(F32), refs)


def update_down_kernel(scale_ref, first_ref, second_ref, *refs):
    rows, width = refs[0].shape[1:]
    hidden = first_ref.shape[1]
    for layer, ref in enumerate((first_ref, second_ref)):
        base = ref.shape[0] - rows * (width // hidden)
        parts = [
            ref[base + b * rows : base + (b + 1) * rows, :] for b in range(width // hidden)
        ]
        update(scale_ref, RATE_DOWN, layer, jnp.concatenate(parts, axis=1).astype(F32), refs)


def update_square_kernel(planes, sides, head_size, side_ref, *refs):
    scale_ref, column_ref, mix_ref, other_ref, conv_ref, refs = (
        refs[0],
        refs[1],
        refs[2],
        refs[3],
        refs[4],
        refs[5:],
    )
    team, rows, _ = column_ref.shape
    width = refs[0].shape[2]
    size = width // team
    per_side = planes // sides
    for i, matrix in enumerate((0, 1, 2, 4, 5, 6)):
        parts = []
        if i < 4:
            for head in range(width // head_size):
                plane, rest = head // 4, head % 4
                t = rest * sides + plane // per_side
                at = i * size + (plane % per_side) * head_size
                parts.append(column_ref[t, :, at : at + head_size])
        else:
            count = size // planes
            for p in range(planes):
                for t in range(team):
                    at = i * size + p * count
                    parts.append(column_ref[t, :, at : at + count])
        update(scale_ref, RATE_SQUARE, matrix, jnp.concatenate(parts, axis=1).astype(F32), refs)
    blocks = width // BLOCK
    head_rows = sides * rows
    base = mix_ref.shape[0] - blocks * head_rows
    parts = []
    for b in range(blocks):
        at = slice(base + b * head_rows, base + (b + 1) * head_rows)
        parts.append(mix_ref[at, :].astype(F32) + other_ref[at, :].astype(F32))
    whole = jnp.concatenate(parts, axis=1)
    update(scale_ref, RATE_SQUARE, 3, jnp.where(side_ref[0] == 0, whole[:rows], whole[rows:]), refs)
    base = conv_ref.shape[0] - blocks * rows
    parts = [conv_ref[base + b * rows : base + (b + 1) * rows, :] for b in range(blocks)]
    update(scale_ref, RATE_SQUARE, 7, jnp.concatenate(parts, axis=1).astype(F32), refs)


def update_call(body, scale, terms, weight, moment, average, scalars=()):
    return kernel_call(
        body,
        [shape(weight.shape, F32)] * 4,
        [scale] + list(terms) + [weight, moment, average],
        scalars=scalars,
    )


def feature_grad_kernel(planes, sides, *refs):
    member_ref, refs = refs[0], refs[1:]
    norms, biases, out_ref = refs[:5], refs[5:-1], refs[-1]
    team, _, size = out_ref.shape
    count = size // planes
    per_side = planes // sides
    head_size = sides * count
    bias = sum(ref[...] for ref in biases)
    rest, side = member_ref[0] // sides, member_ref[0] % sides
    rows = jnp.concatenate([n[0:1, :] for n in norms] + [n[1:2, :] for n in norms])
    for t in range(team):
        parts, own = [], []
        for p in range(planes):
            at = (p * team + t) * count
            parts.append(rows[:, at : at + count])
            at = (p % per_side) * head_size + (t % sides) * count
            held = (rest == t // sides) & (side == p // per_side)
            own.append(bias[:, at : at + count] * held.astype(jnp.int32).astype(F32))
        out_ref[t] = jnp.concatenate(
            [jnp.concatenate(parts, axis=1), jnp.concatenate(own, axis=1)]
        )


def channel_grad_kernel(taps, term_ref, sum_ref, *refs):
    tap_refs, out_ref = refs[:-1], refs[-1]
    features = jnp.sum(term_ref[...], axis=0)
    out_ref[...] = jnp.concatenate(
        [
            sum(ref[:taps] for ref in tap_refs),
            features[:10],
            sum_ref[0:2],
            features[10:12],
        ]
    )


def make_step(planes, sides):
    wide_team = sides == 2
    team_axes = ("x", "c", "y") if wide_team else ("x", "c")
    team = 8 if wide_team else 4
    outer_bits = [("z", 1 << i) for i in range((planes - 1).bit_length())]
    if not wide_team:
        outer_bits += [("y", 1 << i) for i in range((sides - 1).bit_length())]
    head_aligned = wide_team and planes * 4 == HEADS

    def turn(values, first):
        pairs = []
        for x in range(2):
            for c in range(2):
                for y in range(2):
                    along_x = (c == 0) == first
                    to = (1 - x, c, y) if along_x else (x, c, 1 - y)
                    pairs.append((4 * x + 2 * c + y, 4 * to[0] + 2 * to[1] + to[2]))
        return lax.ppermute(values, team_axes, pairs)

    def gather(values):
        return spread(values, None)[0]

    def spread(values, run):
        groups, results = [([values], [swap(values, "c")])], []

        def work(*travelling):
            if run is not None:
                result = run(len(results), groups[-1])
                travelling, result = lax.optimization_barrier((travelling, result))
                results.append(result)
            return travelling

        if not wide_team:
            (far,) = work(swap(values, "x"))
        else:
            first, second = work(turn(values, True), turn(values, False))
            far = turn(first, False)
            groups.append(([first, second], [swap(first, "c"), swap(second, "c")]))
            (far,) = work(far)
        groups.append(([far], [swap(far, "c")]))
        if run is not None:
            results.append(run(len(results), groups[-1]))
        return groups, results

    def scatter(parts, fill=()):
        (own,), own_mate = parts[0]
        (far,), far_mate = parts[-1]
        out_far = add_call(far, swap(far_mate, "c"), 0)
        got_own = swap(own_mate, "c")
        if not wide_team:
            across, fill = lax.optimization_barrier((swap(out_far, "x"), fill))
            return (own, got_own, [across]), fill
        (first, second), side_mate = parts[1]
        got_side = swap(side_mate, "c")
        relay = turn(out_far, False)
        from_second = turn(add_call(second, got_side, 1), False)
        relay, fill = lax.optimization_barrier((relay, fill))
        from_first = turn(add_call(first, got_side, 0, relay), True)
        return (own, got_own, [from_first, from_second]), fill

    def side_rows(rows):
        return rows if wide_team else lax.all_gather(rows, "y", axis=0, tiled=True)

    def side_scatter(rows):
        if wide_team:
            return rows
        return lax.psum_scatter(rows, "y", scatter_dimension=0, tiled=True)

    def split_hidden(rows):
        r, f = rows.shape
        return rows.reshape(r, planes, team, f // (planes * team)).transpose(2, 0, 1, 3).reshape(
            team, r, f // team
        )

    def join_hidden(blocks):
        _, r, f = blocks.shape
        return blocks.reshape(team, r, planes, f // planes).transpose(1, 2, 0, 3).reshape(
            r, team * f
        )

    def split_heads(rows):
        r, d = rows.shape
        if not head_aligned:
            return rows.reshape(r, team, d // team).transpose(1, 0, 2)
        size = d // HEADS
        rows = rows.reshape(r, sides, planes // sides, 2, 2, size)
        return rows.transpose(3, 4, 1, 0, 2, 5).reshape(team, r, d // team)

    def join_heads(blocks):
        _, r, f = blocks.shape
        if not head_aligned:
            return blocks.transpose(1, 0, 2).reshape(r, team * f)
        size = team * f // HEADS
        blocks = blocks.reshape(2, 2, sides, r, planes // sides, size)
        return blocks.transpose(3, 2, 4, 0, 1, 5).reshape(r, team * f)

    def team_swap(blocks):
        return lax.all_to_all(blocks, team_axes, split_axis=0, concat_axis=0, tiled=True)

    def plane_pieces(rows):
        return [rows] + [swap(rows, "z", d) for d in range(1, planes)]

    def plane_gather(rows):
        return lax.all_gather(rows, "z", axis=0, tiled=False)

    def plane_reduce(rows):
        return lax.psum_scatter(rows, "z", scatter_dimension=0, tiled=False)

    def to_blocks(rows, size):
        return jnp.concatenate([rows[:, i : i + size] for i in range(0, rows.shape[1], size)])

    def from_blocks(rows, count):
        return jnp.concatenate(jnp.split(rows, count), axis=1)

    def outer_merge(values, combine):
        if wide_team:
            return combine([values] + [swap(values, "z", d) for d in range(1, planes)])
        for axis, bit in outer_bits:
            values = combine([values, swap(values, axis, bit)])
        return values

    def step(
        frames,
        lengths,
        out_grad,
        up_weight,
        down_weight,
        square_weight,
        chan_weight,
        up_moment,
        down_moment,
        square_moment,
        chan_moment,
        up_average,
        down_average,
        square_average,
        chan_average,
    ):
        slots, width = frames.shape
        head_size = width // HEADS
        item_count = lengths.shape[1] - 1
        chan_rows = chan_weight.shape[0]
        tap_count = chan_rows - 14
        hidden = up_weight.shape[2]
        team_hidden = hidden // team
        team_width = width // team
        x_at, c_at, y_at = lax.axis_index("x"), lax.axis_index("c"), lax.axis_index("y")
        team_at = (x_at * 2 + c_at) * 2 + y_at if wide_team else x_at * 2 + c_at
        side = y_at.reshape(1).astype(jnp.int32)
        plane = lax.axis_index("z").reshape(1).astype(jnp.int32)

        chan_low = chan_weight.astype(BF16)
        if head_aligned:
            blocks = [shape((hidden // planes // team * (width // team_hidden), team_hidden), BF16)] * 2
            down_one, down_two = kernel_call(split_down_kernel, blocks, [down_weight])
            rows_in = up_weight.shape[1]
            blocks = [shape((team, rows_in, team_hidden), BF16)] * 2
            up_one, up_two = kernel_call(split_up_kernel, blocks, [up_weight])
            columns, mix, conv_out = kernel_call(
                functools.partial(split_square_kernel, planes, sides, head_size),
                [shape((team, rows_in, 6 * team_width), BF16)] + [shape((rows_in, width), BF16)] * 2,
                [square_weight],
            )
        else:
            up_low = up_weight.astype(BF16)
            down_low = down_weight.astype(BF16)
            square_low = square_weight.astype(BF16)
            down_one, down_two = [to_blocks(side_rows(down_low[i]), team_hidden) for i in (0, 1)]
            up_one, up_two = [split_hidden(side_rows(up_low[i])) for i in (0, 1)]
            columns = jnp.concatenate(
                [split_heads(side_rows(square_low[i])) for i in (0, 1, 2, 4)]
                + [split_hidden(side_rows(square_low[i])) for i in (5, 6)],
                axis=2,
            )
            mix, conv_out = square_low[3], side_rows(square_low[7])
        down_one = plane_gather(down_one)
        up_one = team_swap(up_one)
        up_one, frames, chan_low, lengths, columns, up_two, mix = lax.optimization_barrier(
            (up_one, frames, chan_low, lengths, columns, up_two, mix)
        )
        packs_one = (plane_gather(up_one.reshape(-1, team_hidden)), down_one)
        groups = gather(frames)

        if wide_team:
            lanes = jnp.pad(chan_low, ((0, LANES - chan_rows), (0, 0))).T
            carried = jnp.pad(
                lengths.astype(BF16), ((0, CARRY - 1), (0, LANES - lengths.shape[1]))
            )
            lanes = jnp.concatenate([lanes, carried])[None]
            for axis in ("y", "c", "x"):
                lanes = jnp.concatenate([lanes, swap(lanes, axis)])
            where_at = jnp.stack([plane[0], team_at, y_at, c_at]).astype(jnp.int32)
            norms = [shape((2, width), F32)] * 5
            params = kernel_call(
                functools.partial(channel_kernel, planes, sides, head_size),
                norms
                + [
                    shape((tap_count + 1, team_width), F32),
                    shape((2, team_width), F32),
                    shape((2, team_width), F32),
                    shape((team, lengths.shape[1]), jnp.int32),
                ],
                plane_pieces(lanes),
                scalars=(where_at,),
                scratch=[pltpu.VMEM((width, LANES), F32)],
            )
            norms, (taps, batch_rows, bias_rows, team_lengths) = params[:5], params[5:]
        else:
            team_lengths = jnp.concatenate(chunk_order(gather(lengths)))
            chan_float = lax.all_gather(chan_low, ALL, axis=1, tiled=True).astype(F32)

            def own_hidden(rows):
                rows = rows.reshape(rows.shape[0], planes, team, -1)
                rows = lax.dynamic_index_in_dim(rows, team_at, axis=2, keepdims=False)
                return rows.reshape(rows.shape[0], team_width)

            taps = own_hidden(chan_float[: tap_count + 1])
            batch_rows = own_hidden(chan_float[tap_count + 10 : tap_count + 12])
            bias_rows = lax.dynamic_index_in_dim(
                split_heads(chan_float[tap_count + 12 : tap_count + 14]), team_at, 0, False
            )
            norms = [
                jnp.stack([chan_float[tap_count + j], chan_float[tap_count + 5 + j]])
                for j in range(5)
            ]

        columns, up_two = team_swap(columns), team_swap(up_two)
        if head_aligned:
            head_rows = sides * rows_in
            per_side = planes // sides
            depth = team * rows_in
            lines = [2 * depth + width // BLOCK * head_rows, 2 * depth]
            mix_pack, conv_pack = kernel_call(
                square_pack_kernel,
                [shape((n, BLOCK), BF16) for n in lines],
                [columns, mix, swap(mix, "y"), conv_out],
                scalars=(side,),
            )
            second = kernel_call(
                feed_pack_kernel,
                [shape((depth + down_two.shape[0], team_hidden), BF16)],
                [up_two, down_two],
            )[0]
        else:
            per_side = 0
            mix = lax.all_gather(mix, ALL, axis=0, tiled=True)
            mix = lax.dynamic_slice_in_dim(mix, team_at * team_width, team_width, axis=0)
            columns = columns.reshape(-1, 6 * team_width)
            mix_pack = to_blocks(columns[:, : 4 * team_width], BLOCK)
            conv_pack = jnp.concatenate(
                [to_blocks(columns[:, 4 * team_width :], BLOCK), to_blocks(conv_out, BLOCK)]
            )
            second = jnp.concatenate([up_two.reshape(-1, team_hidden), down_two])
        table = offset_table(slots, width).astype(BF16)

        ready = (packs_one, groups, norms, taps, team_lengths, table)
        ready, mix_pack, conv_pack, second, mix = lax.optimization_barrier(
            (ready, mix_pack, conv_pack, second, mix)
        )
        packs_one, groups, norms, taps, team_lengths, table = ready
        mix_pack = plane_gather(mix_pack)
        mix_packs = (mix_pack,) if head_aligned else (mix_pack, mix)

        def columns_of(results, i):
            return [result[i] for result in results]

        at = [0]
        for group in groups:
            at.append(at[-1] + 2 * len(group[0]))

        results = [forward_call(group, packs_one, norms[0]) for group in groups]
        saved_one = [columns_of(columns_of(results, 1), i) for i in (1, 0)]
        parts, _ = scatter(columns_of(results, 0))
        stream_one, normed = join_call(frames, parts, 0.5, norms[1])
        normed, conv_pack, second = lax.optimization_barrier((normed, conv_pack, second))
        conv_pack = plane_gather(conv_pack)
        pack_two = plane_gather(second)

        place = kernel_call(
            place_kernel,
            [shape((table.shape[0], team_width), BF16)],
            [table, mix_pack],
            flops=2 * table.shape[0] * width * team_width,
        )[0]

        def attention(i, group):
            return attention_call(
                group, team_lengths, at[i], side, mix_packs, per_side, bias_rows, place, head_size
            )

        groups, results = spread(normed, attention)
        saved_two = columns_of(results, 1)
        parts, _ = scatter(columns_of(results, 0))
        stream_two, normed = join_call(stream_one, parts, 1.0, norms[2])

        def gates(i, group):
            return gate_call(group, team_lengths, at[i], conv_pack, taps, tap_count)

        groups, saved_three = spread(normed, gates)
        stats = outer_merge(merge(columns_of(saved_three, 2)), merge)
        results = [
            batch_call(len(group[0]), saved[0], stats, batch_rows, conv_pack, slots, width)
            for group, saved in reversed(list(zip(groups, saved_three)))
        ][::-1]
        parts, _ = scatter(results)
        stream_three, normed = join_call(stream_two, parts, 1.0, norms[3])
        normed, pack_two = lax.optimization_barrier((normed, pack_two))

        groups, results = spread(normed, lambda i, group: forward_call(group, (pack_two,)))
        saved_four = [chunk_order(groups), columns_of(columns_of(results, 1), 0)]
        parts, _ = scatter(columns_of(results, 0))
        output, grad_four, low, norm_four = turn_call(
            stream_three, parts, 0.5, norms[4], out_grad, lengths
        )

        def feed_backward(low, packs, saved):
            normed, before = saved
            groups, results = spread(
                low, lambda i, group: backward_call(group, packs, before[i])
            )
            grads, active = [columns_of(columns_of(results, 1), i) for i in (0, 1)]
            term = feed_weight_call(normed, grads, active, chunk_order(groups), planes)
            return scatter(columns_of(results, 0), term)

        parts, second_term = feed_backward(low, (pack_two,), saved_four)
        grad_three, low, norm_three = join_back_call(stream_three, grad_four, parts, 1.0, norms[3])
        low, second_term = lax.optimization_barrier((low, second_term))
        second_term = plane_reduce(second_term)

        def batch_back(i, group):
            return batch_back_call(
                group, team_lengths, at[i], saved_three[i][0], stats, batch_rows, conv_pack
            )

        groups, grads = spread(low, batch_back)
        local_sums = sum_call(columns_of(grads, 2))
        sums = outer_merge(local_sums, sum_call)
        results = [
            gate_back_call(
                len(groups[i][0]), team_lengths, at[i], grads[i][0], saved_three[i][0], stats, sums,
                conv_pack, taps, tap_count, slots, width,
            )
            for i in reversed(range(len(groups)))
        ][::-1]
        tap_terms = columns_of(columns_of(results, 1), 1)
        conv_term = conv_weight_call(
            columns_of(saved_three, 1), columns_of(columns_of(results, 1), 0), columns_of(grads, 1),
            chunk_order(groups), planes,
        )
        parts, conv_term = scatter(columns_of(results, 0), conv_term)
        grad_two, low, norm_two = join_back_call(stream_two, grad_three, parts, 1.0, norms[2])
        low, conv_term, second_term = lax.optimization_barrier((low, conv_term, second_term))
        conv_term = plane_reduce(conv_term)

        def attention_back(i, group):
            return attention_back_call(
                group, side, mix_packs, per_side, place, saved_two[i], head_size
            )

        groups, results = spread(low, attention_back)
        rows = chunk_order(groups)
        grads = columns_of(results, 1)
        bias_terms = columns_of(grads, 2)
        mix_term = mix_weight_call(
            saved_two, columns_of(grads, 0), rows, [table] + columns_of(grads, 1), side, planes,
            per_side,
        )
        parts, mix_term = scatter(columns_of(results, 0), mix_term)
        if not head_aligned:
            mixed = jnp.concatenate([saved[:, -team_width:] for saved in saved_two])
            mix_own = mm_tn(mixed, jnp.concatenate(rows)).astype(BF16)
            mix_own = lax.dynamic_update_slice_in_dim(
                jnp.zeros((width, width), BF16), mix_own, team_at * team_width, axis=0
            )
        grad_one, low, norm_one = join_back_call(stream_one, grad_two, parts, 0.5, norms[1])
        low, conv_term = lax.optimization_barrier((low, conv_term))
        mix_term = plane_reduce(mix_term)

        parts, first_term = feed_backward(low, packs_one, saved_one)
        first_term = plane_reduce(first_term)
        frames_grad, norm_zero = join_back_call(frames, grad_one, parts, 1.0, norms[0], keep=False)

        late = (second_term, conv_term, mix_term)
        frames_grad, late = lax.optimization_barrier((frames_grad, late))
        second_term, conv_term, mix_term = late
        depth = width // planes
        rate_scale = lax.rsqrt(stats[0:1])

        def from_team(rows, columns):
            return team_swap(rows.astype(BF16).reshape(team, -1, columns))

        def finish_channels(chan_term):
            chan_term = outer_merge(chan_term, sum_call).reshape(chan_rows, planes, -1)
            chan_term = lax.dynamic_index_in_dim(chan_term, lax.axis_index("z"), 1, keepdims=False)
            if not wide_team:
                chan_term = lax.dynamic_index_in_dim(
                    chan_term.reshape(chan_rows, sides, -1), y_at, 1, keepdims=False
                )
            return chan_term

        norm_terms = [norm_zero, norm_one, norm_two, norm_three, norm_four]
        if head_aligned:
            second_up = from_team(second_term[:depth], team_hidden)
            features = kernel_call(
                functools.partial(feature_grad_kernel, planes, sides),
                [shape((team, 12, team_width), F32)],
                norm_terms + bias_terms,
                scalars=(team_at.reshape(1).astype(jnp.int32),),
            )[0]
            chan_term = kernel_call(
                functools.partial(channel_grad_kernel, tap_count),
                [shape((chan_rows, team_width), F32)],
                [team_swap(features), local_sums] + tap_terms,
            )[0]
            chan_grad = finish_channels(chan_term)
            blocks = kernel_call(
                column_grad_kernel,
                [shape((team, rows_in, 6 * team_width), BF16)],
                [mix_term, conv_term],
            )[0]
            square_all = update_call(
                functools.partial(update_square_kernel, planes, sides, head_size),
                rate_scale,
                [team_swap(blocks), mix_term, swap(mix_term, "y"), conv_term],
                square_weight,
                square_moment,
                square_average,
                scalars=(side,),
            )
            first_term, square_all, second_up = lax.optimization_barrier(
                (first_term, square_all, second_up)
            )
            down_all = update_call(
                update_down_kernel,
                rate_scale,
                [first_term, second_term],
                down_weight,
                down_moment,
                down_average,
            )
            up_all = update_call(
                update_up_kernel,
                rate_scale,
                [from_team(first_term[:depth], team_hidden), second_up],
                up_weight,
                up_moment,
                up_average,
            )
            up_grad, up_new = up_all[0], up_all[1:]
            down_grad, down_new = down_all[0], down_all[1:]
            square_grad, square_new = square_all[0], square_all[1:]
            rate_scale = rate_scale[0, 0]
        else:
            column_blocks = 4 * team_width // BLOCK
            qkv_term = from_blocks(mix_term[: column_blocks * depth], column_blocks)
            gate_blocks = 2 * team_width // BLOCK
            gate_term = from_blocks(conv_term[: gate_blocks * depth], gate_blocks)
            conv_out_term = from_blocks(conv_term[gate_blocks * depth :], width // BLOCK)
            mix_grad = lax.psum_scatter(mix_own, ALL, scatter_dimension=0, tiled=True).astype(F32)
            blocks = from_team(jnp.concatenate([qkv_term, gate_term], axis=1), 6 * team_width)

            def block(i):
                return blocks[:, :, i * team_width : (i + 1) * team_width]

            square_grad = jnp.stack(
                [side_scatter(join_heads(block(i))).astype(F32) for i in range(3)]
                + [mix_grad, side_scatter(join_heads(block(3))).astype(F32)]
                + [side_scatter(join_hidden(block(i))).astype(F32) for i in (4, 5)]
                + [side_scatter(conv_out_term).astype(F32)]
            )
            bias_rows = join_heads(
                lax.dynamic_update_slice_in_dim(
                    jnp.zeros((team, 2, team_width), F32), sum(bias_terms)[None], team_at, 0
                )
            )
            features = jnp.concatenate(
                [t[0:1] for t in norm_terms] + [t[1:2] for t in norm_terms] + [bias_rows]
            )
            features = jnp.sum(team_swap(split_hidden(features)), axis=0)
            chan_grad = finish_channels(
                jnp.concatenate(
                    [
                        sum(tap_terms)[:tap_count],
                        features[:10],
                        local_sums[:2],
                        features[10:],
                    ]
                )
            )
            feed_terms = (first_term, second_term)
            up_grad = jnp.stack(
                [
                    side_scatter(join_hidden(from_team(rows[:depth], team_hidden))).astype(F32)
                    for rows in feed_terms
                ]
            )
            down_grad = jnp.stack(
                [
                    side_scatter(from_blocks(rows[depth:], width // team_hidden)).astype(F32)
                    for rows in feed_terms
                ]
            )
            rate_scale = rate_scale[0, 0]
            up_new = nesterov(up_weight, up_moment, up_average, up_grad, RATE_UP, rate_scale)
            down_new = nesterov(
                down_weight, down_moment, down_average, down_grad, RATE_DOWN, rate_scale
            )
            square_new = nesterov(
                square_weight, square_moment, square_average, square_grad, RATE_SQUARE, rate_scale
            )
        chan_new = nesterov(
            chan_weight, chan_moment, chan_average, chan_grad, RATE_CHANNEL, rate_scale
        )
        bias_grad = chan_grad[tap_count + 12 : tap_count + 14]
        return (
            output,
            frames_grad,
            up_grad,
            down_grad,
            square_grad,
            chan_grad,
            up_new[0],
            down_new[0],
            square_new[0],
            chan_new[0],
            up_new[1],
            down_new[1],
            square_new[1],
            chan_new[1],
            up_new[2],
            down_new[2],
            square_new[2],
            chan_new[2],
            bias_grad,
        )

    return step


def solution(mesh):
    wide, narrow = mesh.shape["wide"], mesh.shape["narrow"]
    planes = wide // 4
    inner = Mesh(mesh.devices.reshape(planes, 2, 2, narrow), ALL)
    token = P(ALL, None)
    matrix = P(None, ALL, None)
    vector = P(None, ALL)
    group = (matrix, matrix, matrix, vector)
    return jax.shard_map(
        make_step(planes, narrow),
        mesh=inner,
        in_specs=(token, token, token) + group * 3,
        out_specs=(token, token) + group * 4 + (vector,),
        check_vma=False,
    )
```

```python
import functools

import jax
import jax.numpy as jnp
from jax import lax
from jax.experimental import pallas as pl
from jax.experimental.pallas import tpu as pltpu
from jax.sharding import Mesh
from jax.sharding import PartitionSpec as P

HEADS = 16
EPSILON = 1e-05
MOMENTUM_DECAY = 0.9
AVERAGE_DECAY = 0.9
RATE_UP = 0.05
RATE_DOWN = 0.026
RATE_SQUARE = 0.05
RATE_CHANNEL = 0.5
MASKED_SCORE = -1e30
BF16 = jnp.bfloat16
F32 = jnp.float32
ALL = ("z", "x", "c", "y")
LANES = 128
PAD = 16
BLOCK = 256
CARRY = 16
ROOM = 6 << 20


def mm(left, right):
    return jnp.dot(left, right, preferred_element_type=F32)


def mm_tn(left, right):
    return lax.dot_general(left, right, (((0,), (0,)), ((), ())), preferred_element_type=F32)


def mm_nt(left, right):
    return lax.dot_general(left, right, (((1,), (1,)), ((), ())), preferred_element_type=F32)


def swap(values, axis, bit=1):
    size = lax.axis_size(axis)
    return lax.ppermute(values, axis, [(i, i ^ bit) for i in range(size)])


def sigmoid(values):
    return 1.0 / (1.0 + jnp.exp(-values))


def swish_grad(values):
    sig = sigmoid(values)
    return sig * (1.0 + values * (1.0 - sig))


def normalize(values):
    centre = values - jnp.mean(values, axis=-1, keepdims=True)
    scale = lax.rsqrt(jnp.mean(centre * centre, axis=-1, keepdims=True) + EPSILON)
    return centre * scale, scale


def shape(dims, dtype):
    return jax.ShapeDtypeStruct(tuple(dims), dtype)


def size_of(item):
    total = 1
    for n in item.shape:
        total *= n
    return total * item.dtype.itemsize


def kernel_call(body, outs, args, scalars=(), flops=0, scratch=()):
    moved = sum(size_of(a) for a in args) + sum(size_of(o) for o in outs)
    return pl.pallas_call(
        body,
        out_shape=tuple(outs),
        in_specs=[pl.BlockSpec(memory_space=pltpu.SMEM)] * len(scalars)
        + [pl.BlockSpec(memory_space=pltpu.VMEM)] * len(args),
        out_specs=tuple(pl.BlockSpec(memory_space=pltpu.VMEM) for _ in outs),
        scratch_shapes=list(scratch),
        compiler_params=pltpu.CompilerParams(vmem_limit_bytes=moved + ROOM),
        cost_estimate=pl.CostEstimate(flops=int(flops), bytes_accessed=moved, transcendentals=0),
    )(*scalars, *args)


def stay(values):
    return pltpu.with_memory_space_constraint(values, pltpu.HBM)


def store_partial(mine_refs, mate_ref, i, slots, value):
    mine_refs[i][...] = value[:slots]
    mate_ref[i] = value[slots:].astype(BF16)


def up_product(rows, ref):
    planes = ref.shape[0]
    depth = rows.shape[1] // planes
    total = mm(rows[:, :depth], ref[0, :depth, :])
    for p in range(1, planes):
        total = total + mm(rows[:, p * depth : (p + 1) * depth], ref[p, :depth, :])
    return total


def up_product_back(rows, ref, width):
    planes = ref.shape[0]
    depth = width // planes
    return jnp.concatenate([mm_nt(rows, ref[p, :depth, :]) for p in range(planes)], axis=1)


def down_blocks(ref, width):
    planes, hidden = ref.shape[0], ref.shape[2]
    rows = hidden // planes
    depth = ref.shape[1] - rows * (width // hidden)
    return [
        jnp.concatenate(
            [ref[p, depth + b * rows : depth + (b + 1) * rows, :] for p in range(planes)]
        )
        for b in range(width // hidden)
    ]


def down_product(rows, blocks):
    return jnp.concatenate([mm(rows, block) for block in blocks], axis=1)


def down_product_back(rows, blocks):
    size = blocks[0].shape[1]
    total = mm_nt(rows[:, :size], blocks[0])
    for b in range(1, len(blocks)):
        total = total + mm_nt(rows[:, b * size : (b + 1) * size], blocks[b])
    return total


def square_columns(ref, p, depth, first, last):
    parts = []
    while first < last:
        block = first // BLOCK
        stop = min(last, (block + 1) * BLOCK)
        lanes = slice(first - block * BLOCK, stop - block * BLOCK)
        parts.append(ref[p, block * depth : (block + 1) * depth, lanes])
        first = stop
    return jnp.concatenate(parts, axis=1) if len(parts) > 1 else parts[0]


def square_product(rows, ref, first, last):
    planes = ref.shape[0]
    depth = rows.shape[1] // planes
    total = None
    for p in range(planes):
        term = mm(rows[:, p * depth : (p + 1) * depth], square_columns(ref, p, depth, first, last))
        total = term if total is None else total + term
    return total


def square_product_back(rows, ref, width, first, last):
    planes = ref.shape[0]
    depth = width // planes
    return jnp.concatenate(
        [mm_nt(rows, square_columns(ref, p, depth, first, last)) for p in range(planes)], axis=1
    )


def output_rows(ref, p, width, base):
    blocks = width // BLOCK
    rows = (ref.shape[1] - base) // blocks
    parts = []
    for b in range(blocks):
        at = base + b * rows
        part = ref[pl.ds(p, 1), at : at + rows, :]
        parts.append(part.reshape(part.shape[1:]))
    return jnp.concatenate(parts, axis=1)


def forward_kernel(k, packs, with_norm, *refs):
    mine, mate, refs = refs[:k], refs[k : 2 * k], refs[2 * k :]
    if with_norm:
        norm_ref, refs = refs[0], refs[1:]
    up_ref, down_ref, refs = refs[0], refs[packs - 1], refs[packs:]
    out_mine, out_mate, before_ref = refs[:k], refs[k], refs[k + 1]
    slots, width = mine[0].shape
    blocks = down_blocks(down_ref, width)
    for i in range(k):
        rows = jnp.concatenate([mine[i][...], mate[i][...]])
        at = pl.ds(2 * i * slots, 2 * slots)
        if with_norm:
            unit, _ = normalize(rows.astype(F32))
            rows = (unit * norm_ref[0:1, :] + norm_ref[1:2, :]).astype(BF16)
            refs[k + 2][at, :] = rows
        before = up_product(rows, up_ref)
        before_ref[at, :] = before
        active = (before * sigmoid(before)).astype(BF16)
        store_partial(out_mine, out_mate, i, slots, down_product(active, blocks))


def forward_call(group, packs, norm=None):
    mine, mate = group
    k, (slots, width) = len(mine), mine[0].shape
    hidden = packs[0].shape[2]
    rows = 2 * k * slots
    outs = [shape((slots, width), F32)] * k + [
        shape((k, slots, width), BF16),
        shape((rows, hidden), F32),
    ]
    args = list(mine) + list(mate)
    if norm is not None:
        outs.append(shape((rows, width), BF16))
        args.append(norm)
    result = kernel_call(
        functools.partial(forward_kernel, k, len(packs), norm is not None),
        outs,
        args + list(packs),
        flops=4 * rows * width * hidden,
    )
    return (result[:k], result[k]), result[k + 1 :]


def backward_kernel(k, packs, *refs):
    mine, mate, refs = refs[:k], refs[k : 2 * k], refs[2 * k :]
    up_ref, down_ref, before_ref, refs = refs[0], refs[packs - 1], refs[packs], refs[packs + 1 :]
    out_mine, out_mate, grad_ref, active_ref = refs[:k], refs[k], refs[k + 1], refs[k + 2]
    slots, width = mine[0].shape
    blocks = down_blocks(down_ref, width)
    for i in range(k):
        at = pl.ds(2 * i * slots, 2 * slots)
        rows = jnp.concatenate([mine[i][...], mate[i][...]])
        before = before_ref[at, :]
        sig = sigmoid(before)
        active_ref[at, :] = (before * sig).astype(BF16)
        grad = down_product_back(rows, blocks) * (sig * (1.0 + before * (1.0 - sig)))
        grad = grad.astype(BF16)
        grad_ref[at, :] = grad
        store_partial(out_mine, out_mate, i, slots, up_product_back(grad, up_ref, width))


def backward_call(group, packs, before):
    mine, mate = group
    k, (slots, width) = len(mine), mine[0].shape
    rows, hidden = before.shape
    outs = [shape((slots, width), F32)] * k + [
        shape((k, slots, width), BF16),
        shape((rows, hidden), BF16),
        shape((rows, hidden), BF16),
    ]
    result = kernel_call(
        functools.partial(backward_kernel, k, len(packs)),
        outs,
        list(mine) + list(mate) + list(packs) + [before],
        flops=4 * rows * width * hidden,
    )
    return (result[:k], result[k]), result[k + 1 :]


def joined(refs, first=0, last=None):
    return jnp.concatenate([r[:, first:last] for r in refs])


def take(refs, counts):
    groups, at = [], 0
    for n in counts:
        groups.append(refs[at : at + n])
        at += n
    return groups + [refs[at:]]


def put(out_ref, planes, write):
    for p in range(planes):
        write(out_ref.at[p], p)


def rows_at(ref, p, rows, lanes=slice(None)):
    return ref[pl.ds(pl.multiple_of(p * rows, rows), rows), lanes]


def feed_weight_kernel(counts, planes, *refs):
    normed, grads, active, rows, refs = take(refs, counts)
    out_ref, up_ref, down_ref = refs
    width, hidden = up_ref.shape
    depth, below = width // planes, hidden // planes
    down_ref[...] = mm_tn(joined(active), joined(rows))
    up_ref[...] = mm_tn(joined(normed), joined(grads))

    def write(out, p):
        out[:depth, :] = rows_at(up_ref, p, depth).astype(BF16)
        for b in range(width // hidden):
            at = depth + b * below
            lanes = slice(b * hidden, (b + 1) * hidden)
            out[at : at + below, :] = rows_at(down_ref, p, below, lanes).astype(BF16)

    put(out_ref, planes, write)


def feed_weight_call(normed, grads, active, rows, planes):
    width, hidden = normed[0].shape[1], grads[0].shape[1]
    lines = width // planes + (hidden // planes) * (width // hidden)
    groups = (normed, grads, active, rows)
    tokens = sum(a.shape[0] for a in grads)
    return kernel_call(
        functools.partial(feed_weight_kernel, [len(g) for g in groups], planes),
        [shape((planes, lines, hidden), BF16)],
        [a for g in groups for a in g],
        flops=4 * width * hidden * tokens,
        scratch=[pltpu.VMEM((width, hidden), F32), pltpu.VMEM((hidden, width), F32)],
    )[0]


def write_columns(out, total_ref, p, depth):
    for b in range(total_ref.shape[1] // BLOCK):
        lanes = slice(b * BLOCK, (b + 1) * BLOCK)
        out[b * depth : (b + 1) * depth, :] = rows_at(total_ref, p, depth, lanes).astype(BF16)


def write_output_rows(out, base, rows):
    count = rows.shape[0]
    for b in range(rows.shape[1] // BLOCK):
        at = base + b * count
        out[at : at + count, :] = rows[:, b * BLOCK : (b + 1) * BLOCK].astype(BF16)


def conv_weight_kernel(counts, planes, *refs):
    normed, grads, active, rows, refs = take(refs, counts)
    out_ref, gate_ref, row_ref = refs
    depth = gate_ref.shape[0] // planes
    below = row_ref.shape[0] // planes
    base = (gate_ref.shape[1] // BLOCK) * depth
    gate_ref[...] = mm_tn(joined(normed), joined(grads))
    row_ref[...] = mm_tn(joined(active), joined(rows))

    def write(out, p):
        write_columns(out, gate_ref, p, depth)
        write_output_rows(out, base, rows_at(row_ref, p, below))

    put(out_ref, planes, write)


def conv_weight_call(normed, grads, active, rows, planes):
    width, gates, size = normed[0].shape[1], grads[0].shape[1], active[0].shape[1]
    lines = (gates // BLOCK) * (width // planes) + (width // BLOCK) * (size // planes)
    groups = (normed, grads, active, rows)
    tokens = sum(a.shape[0] for a in grads)
    return kernel_call(
        functools.partial(conv_weight_kernel, [len(g) for g in groups], planes),
        [shape((planes, lines, BLOCK), BF16)],
        [a for g in groups for a in g],
        flops=2 * width * (gates + size) * tokens,
        scratch=[pltpu.VMEM((width, gates), F32), pltpu.VMEM((size, width), F32)],
    )[0]


def mix_weight_kernel(counts, planes, per_side, *refs):
    side_ref, refs = refs[0], refs[1:]
    saved, grads, rows, place, refs = take(refs, counts)
    table_ref, place = place[0], place[1:]
    out_ref, total_ref, row_ref = refs
    size = row_ref.shape[0]
    depth = total_ref.shape[0] // planes
    base = (total_ref.shape[1] // BLOCK) * depth
    right = joined(grads)
    qkv = right.shape[1]
    total_ref[:, :qkv] = mm_tn(joined(saved, 0, total_ref.shape[0]), right)
    position = sum(ref[...] for ref in place)
    total_ref[:, qkv:] = mm_tn(table_ref[...], position.astype(BF16))
    if per_side:
        last = saved[0].shape[1]
        row_ref[...] = mm_tn(joined(saved, last - size, last), joined(rows))

    def write(out, p):
        write_columns(out, total_ref, p, depth)
        if per_side:
            below = row_ref.shape[0] // per_side
            place = p - side_ref[0] * per_side
            held = (place >= 0) & (place < per_side)
            share = held.astype(jnp.int32).astype(F32)
            head = rows_at(row_ref, jnp.where(held, place, 0), below) * share
            write_output_rows(out, base, head)

    put(out_ref, planes, write)


def mix_weight_call(saved, grads, rows, place, side, planes, per_side):
    width, qkv, size = rows[0].shape[1], grads[0].shape[1], grads[0].shape[1] // 3
    total = qkv + size
    lines = (total // BLOCK) * (width // planes)
    if per_side:
        lines += (width // BLOCK) * (size // per_side)
    groups = (saved, grads, rows, place)
    tokens = sum(a.shape[0] for a in grads)
    return kernel_call(
        functools.partial(mix_weight_kernel, [len(g) for g in groups], planes, per_side),
        [shape((planes, lines, BLOCK), BF16)],
        [a for g in groups for a in g],
        scalars=(side,),
        flops=2 * width * (total + size) * tokens,
        scratch=[pltpu.VMEM((width, total), F32), pltpu.VMEM((size, width), F32)],
    )[0]


def channel_kernel(planes, sides, head_size, *refs):
    at_ref, pieces, refs = refs[0], refs[1 : 1 + planes], refs[1 + planes :]
    norm_refs, (tap_ref, batch_ref, bias_ref, length_ref, wide_ref) = refs[:5], refs[5:]
    plane, member, side, core = at_ref[0], at_ref[1], at_ref[2], at_ref[3]
    team, rows = pieces[0].shape[0], pieces[0].shape[1] - CARRY
    size = tap_ref.shape[1]
    listed = [pieces[0][m, rows : rows + 1, :].astype(F32) for m in range(team)]
    one = jnp.concatenate([listed[4], listed[3]])
    two = jnp.concatenate([listed[1], listed[6]])
    table = [
        listed[0],
        listed[2],
        jnp.where(core == 0, one, two),
        jnp.where(core == 0, two, one),
        listed[5],
        listed[7],
    ]
    length_ref[...] = jnp.concatenate(table).astype(jnp.int32)[:, : length_ref.shape[1]]
    for d in range(planes):
        for m in range(team):
            at = ((plane ^ d) * team + (member ^ m)) * rows
            wide_ref[pl.ds(pl.multiple_of(at, rows), rows), :] = pieces[d][m, :rows, :].astype(F32)
    every = wide_ref[...].T
    taps = tap_ref.shape[0] - 1
    for j in range(5):
        first = every[taps + j : taps + j + 1]
        norm_refs[j][...] = jnp.concatenate([first, every[taps + 5 + j : taps + 6 + j]])
    own = [
        wide_ref[pl.ds(pl.multiple_of((p * team + member) * rows, rows), rows), :]
        for p in range(planes)
    ]
    own = jnp.concatenate(own).T
    tap_ref[...] = own[: taps + 1]
    batch_ref[...] = own[taps + 10 : taps + 12]
    heads = size // head_size
    own = [
        wide_ref[
            pl.ds(
                pl.multiple_of(
                    (side * heads + h) * team * rows + (member // sides) * head_size, head_size
                ),
                head_size,
            ),
            :,
        ]
        for h in range(heads)
    ]
    own = jnp.concatenate(own).T
    bias_ref[...] = own[taps + 12 : taps + 14]


def chunk_order(groups):
    return [chunk for group in groups for pair in zip(*group) for chunk in pair]


def add_kernel(count, *refs):
    own_ref, mate_ref, out_ref = refs[0], refs[1], refs[-1]
    total = own_ref[...] + mate_ref[count].astype(F32)
    for ref in refs[2:-1]:
        total = total + ref[...].astype(F32)
    out_ref[...] = total.astype(BF16)


def add_call(own, mate, index, *more):
    return kernel_call(
        functools.partial(add_kernel, index), [shape(own.shape, BF16)], [own, mate] + list(more)
    )[0]


def item_bounds(length_ref, b=0):
    ends = [length_ref[b, 0]]
    for j in range(1, length_ref.shape[1] - 1):
        ends.append(ends[-1] + length_ref[b, j])
    return ends


def item_index(ends, where_at):
    total = (where_at >= ends[0]).astype(jnp.int32)
    for end in ends[1:]:
        total = total + (where_at >= end).astype(jnp.int32)
    return total


def head_masks(slots, head_size):
    lane = lax.broadcasted_iota(jnp.int32, (slots, LANES), 1)
    return [
        (lane >= h * head_size) & (lane < (h + 1) * head_size) for h in range(LANES // head_size)
    ]


def saved_lanes(width, size, heads, slots):
    ends = [width]
    for lanes in [size] * 4 + [slots] * heads + [size]:
        ends.append(ends[-1] + lanes)
    return ends


def attention_kernel(k, first, head_size, per_side, *refs):
    length_ref, side_ref, refs = refs[0], refs[1], refs[2:]
    mine, mate, refs = refs[:k], refs[k : 2 * k], refs[2 * k :]
    bias_ref, place_ref, pack_ref = refs[:3]
    mix_ref, refs = (None, refs[3:]) if per_side else (refs[3], refs[4:])
    out_mine, out_mate, saved_ref = refs[:k], refs[k], refs[k + 1]
    slots, width = mine[0].shape
    size = place_ref.shape[1]
    ends = saved_lanes(width, size, size // head_size, slots)
    mix = mix_rows(pack_ref, mix_ref, side_ref, width, size, per_side)
    scale = head_size ** (-0.5)
    row_at = lax.broadcasted_iota(jnp.int32, (slots, slots), 0)
    column_at = lax.broadcasted_iota(jnp.int32, (slots, slots), 1)
    masks = head_masks(slots, head_size)
    for i in range(k):
        rows = jnp.concatenate([mine[i][...], mate[i][...]])
        qkv = square_product(rows, pack_ref, 0, 3 * size)
        query = qkv[:, :size]
        query_c = (query + bias_ref[0:1, :]).astype(BF16)
        query_p = (query + bias_ref[1:2, :]).astype(BF16)
        key = qkv[:, size : 2 * size].astype(BF16)
        value = qkv[:, 2 * size :].astype(BF16)
        at = pl.ds(2 * i * slots, 2 * slots)
        saved_ref[at, : ends[0]] = rows
        for n, part in enumerate((query_c, query_p, key, value)):
            saved_ref[at, ends[n] : ends[n + 1]] = part
        halves = []
        for j in range(2):
            b = 2 * i + j
            part = slice(j * slots, (j + 1) * slots)
            rows_of = pl.ds(b * slots, slots)
            edges = item_bounds(length_ref, first + b)
            same = item_index(edges, row_at) == item_index(edges, column_at)
            blocks = []
            for lo in range(0, size, LANES):
                lanes = slice(lo, lo + LANES)
                mixed = jnp.zeros((slots, LANES), F32)
                for h, mask in enumerate(masks):
                    qc = jnp.where(mask, query_c[part, lanes], 0)
                    qp = jnp.where(mask, query_p[part, lanes], 0)
                    wide = mm_nt(qp, place_ref[:, lanes])
                    moved = pltpu.roll(wide, slots + 1, 1, stride=1, stride_axis=0)
                    scores = (mm_nt(qc, key[part, lanes]) + moved[:, :slots]) * scale
                    scores = jnp.where(same, scores, MASKED_SCORE)
                    top = jnp.max(scores, axis=-1, keepdims=True)
                    weights = jnp.exp(scores - top)
                    probs = weights / jnp.sum(weights, axis=-1, keepdims=True)
                    probs = probs.astype(BF16)
                    n = 4 + (lo // LANES) * len(masks) + h
                    saved_ref[rows_of, ends[n] : ends[n + 1]] = probs
                    mixed = jnp.where(mask, mm(probs, value[part, lanes]), mixed)
                blocks.append(mixed)
            halves.append(jnp.concatenate(blocks, axis=1) if len(blocks) > 1 else blocks[0])
        mixed = jnp.concatenate(halves).astype(BF16)
        saved_ref[at, ends[-2] : ends[-1]] = mixed
        store_partial(out_mine, out_mate, i, slots, mm(mixed, mix))


def mix_rows(pack_ref, mix_ref, side_ref, width, size, per_side):
    if not per_side:
        return mix_ref[...]
    base = (4 * size // BLOCK) * (width // pack_ref.shape[0])
    return jnp.concatenate(
        [output_rows(pack_ref, side_ref[0] * per_side + h, width, base) for h in range(per_side)]
    )


def attention_call(group, lengths, first, side, packs, per_side, bias, place, head_size):
    mine, mate = group
    k, (slots, width) = len(mine), mine[0].shape
    size = place.shape[1]
    heads = size // head_size
    rows = 2 * k * slots
    outs = [shape((slots, width), F32)] * k + [
        shape((k, slots, width), BF16),
        shape((rows, saved_lanes(width, size, heads, slots)[-1]), BF16),
    ]
    result = kernel_call(
        functools.partial(attention_kernel, k, first, head_size, per_side),
        outs,
        list(mine) + list(mate) + [bias, place] + list(packs),
        scalars=(lengths, side),
        flops=2 * rows * width * size * 4 + 2 * k * heads * 10 * slots * slots * LANES,
    )
    return (result[:k], result[k]), result[k + 1]


def attention_back_kernel(k, head_size, per_side, *refs):
    side_ref, refs = refs[0], refs[1:]
    mine, mate, refs = refs[:k], refs[k : 2 * k], refs[2 * k :]
    place_ref, saved_ref, pack_ref = refs[:3]
    mix_ref, refs = (None, refs[3:]) if per_side else (refs[3], refs[4:])
    out_mine, out_mate, grad_ref, place_grad_ref, bias_ref = (
        refs[:k],
        refs[k],
        refs[k + 1],
        refs[k + 2],
        refs[k + 3],
    )
    slots, width = mine[0].shape
    size = place_ref.shape[1]
    mix = mix_rows(pack_ref, mix_ref, side_ref, width, size, per_side)
    ends = saved_lanes(width, size, size // head_size, slots)
    scale = head_size ** (-0.5)
    masks = head_masks(slots, head_size)
    flip = (
        lax.broadcasted_iota(jnp.int32, (slots, slots), 0)
        + lax.broadcasted_iota(jnp.int32, (slots, slots), 1)
        == slots - 1
    ).astype(F32).astype(BF16)
    bias_c = jnp.zeros((1, size), F32)
    bias_p = jnp.zeros((1, size), F32)
    for i in range(k):
        rows = jnp.concatenate([mine[i][...], mate[i][...]])
        grad_mixed_all = mm_nt(rows, mix).astype(BF16)
        at = pl.ds(2 * i * slots, 2 * slots)
        halves = []
        for j in range(2):
            b = 2 * i + j
            part = slice(j * slots, (j + 1) * slots)
            rows_at = pl.ds((2 * i + j) * slots, slots)
            grad_qc, grad_qp, grad_k, grad_v = [], [], [], []
            for lo in range(0, size, LANES):
                lanes = slice(lo, lo + LANES)
                grad_mixed = grad_mixed_all[part, lanes]
                query_c, query_p, key, value = [
                    saved_ref[rows_at, ends[n] + lo : ends[n] + lo + LANES] for n in range(4)
                ]
                place = place_ref[:, lanes]
                gqc = jnp.zeros((slots, LANES), F32)
                gqp, gk, gv = gqc, gqc, gqc
                place_grad = jnp.zeros(place.shape, F32)
                for h, mask in enumerate(masks):
                    n = 4 + (lo // LANES) * len(masks) + h
                    probs = saved_ref[rows_at, ends[n] : ends[n + 1]]
                    own = jnp.where(mask, grad_mixed, 0)
                    grad_probs = mm_nt(own, value)
                    gv = gv + mm_tn(probs, own)
                    probs = probs.astype(F32)
                    inner = jnp.sum(probs * grad_probs, axis=-1, keepdims=True)
                    grad = (probs * (grad_probs - inner)).astype(BF16) * scale
                    grad = grad.astype(BF16)
                    gqc = jnp.where(mask, mm(grad, key), gqc)
                    gk = gk + mm_tn(grad, jnp.where(mask, query_c, 0))
                    turned = mm(flip, grad)
                    wide = jnp.concatenate([turned, jnp.zeros_like(turned)], axis=1)
                    wide = pltpu.roll(wide, 0, 1, stride=1, stride_axis=0).astype(BF16)
                    wide = mm(flip, wide).astype(BF16)
                    gqp = jnp.where(mask, mm(wide, place), gqp)
                    place_grad = place_grad + mm_tn(wide, jnp.where(mask, query_p, 0))
                if i == 0 and j == 0:
                    place_grad_ref[:, lanes] = place_grad
                else:
                    place_grad_ref[:, lanes] = place_grad_ref[:, lanes] + place_grad
                grad_qc.append(gqc)
                grad_qp.append(gqp)
                grad_k.append(gk)
                grad_v.append(gv)

            def side_by_side(blocks):
                return jnp.concatenate(blocks, axis=1) if len(blocks) > 1 else blocks[0]

            gqc, gqp = side_by_side(grad_qc), side_by_side(grad_qp)
            bias_c = bias_c + jnp.sum(gqc, axis=0, keepdims=True)
            bias_p = bias_p + jnp.sum(gqp, axis=0, keepdims=True)
            halves.append(
                jnp.concatenate(
                    [gqc + gqp, side_by_side(grad_k), side_by_side(grad_v)], axis=1
                ).astype(BF16)
            )
        grad = jnp.concatenate(halves)
        grad_ref[at, :] = grad
        store_partial(out_mine, out_mate, i, slots, square_product_back(grad, pack_ref, width, 0, 3 * size))
    bias_ref[...] = jnp.concatenate([bias_c, bias_p])


def attention_back_call(group, side, packs, per_side, place, saved, head_size):
    mine, mate = group
    k, (slots, width) = len(mine), mine[0].shape
    size = place.shape[1]
    rows = 2 * k * slots
    outs = [shape((slots, width), F32)] * k + [
        shape((k, slots, width), BF16),
        shape((rows, 3 * size), BF16),
        shape(place.shape, F32),
        shape((2, size), F32),
    ]
    result = kernel_call(
        functools.partial(attention_back_kernel, k, head_size, per_side),
        outs,
        list(mine) + list(mate) + [place, saved] + list(packs),
        scalars=(side,),
        flops=2 * rows * width * size * 4 + 2 * k * 24 * slots * slots * size,
    )
    return (result[:k], result[k]), result[k + 1 :]


def place_kernel(table_ref, column_ref, out_ref):
    size = out_ref.shape[1]
    rows = square_product(table_ref[...], column_ref, 3 * size, 4 * size)
    out_ref[...] = rows.astype(BF16)


def item_reach(ends, row_at, slots):
    start = jnp.zeros_like(row_at)
    end = jnp.full_like(row_at, slots)
    for at in ends:
        start = jnp.where(row_at >= at, at, start)
    for at in reversed(ends):
        end = jnp.where(row_at < at, at, end)
    valid = (row_at < ends[-1]).astype(F32)
    return row_at - start, end - 1 - row_at, valid


def gate_kernel(k, first, tap_count, *refs):
    length_ref, refs = refs[0], refs[1:]
    mine, mate, refs = refs[:k], refs[k : 2 * k], refs[2 * k :]
    pack_ref, tap_ref, gate_ref, normed_ref, stat_ref, pad_ref = refs
    slots, _ = mine[0].shape
    size = tap_ref.shape[1]
    reach = tap_count // 2
    row_at = lax.broadcasted_iota(jnp.int32, (slots, size), 0)
    pad_ref[...] = jnp.zeros_like(pad_ref)
    count = jnp.zeros((1, size), F32)
    total = jnp.zeros((1, size), F32)
    for i in range(k):
        rows = jnp.concatenate([mine[i][...], mate[i][...]])
        gates = square_product(rows, pack_ref, 0, 2 * size)
        gate_ref[pl.ds(2 * i * slots, 2 * slots), : 2 * size] = gates
        normed_ref[pl.ds(2 * i * slots, 2 * slots), :] = rows
        glu = gates[:, :size] * sigmoid(gates[:, size:])
        for j in range(2):
            b = 2 * i + j
            before, behind, valid = item_reach(item_bounds(length_ref, first + b), row_at, slots)
            pad_ref[PAD : PAD + slots, :] = glu[j * slots : (j + 1) * slots] * valid
            conv = jnp.zeros((slots, size), F32)
            for tap in range(tap_count):
                o = tap - reach
                near = pad_ref[PAD + o : PAD + o + slots, :]
                if o < 0:
                    near = jnp.where(before >= -o, near, 0.0)
                elif o > 0:
                    near = jnp.where(behind >= o, near, 0.0)
                conv = conv + near * tap_ref[tap : tap + 1, :]
            gate_ref[pl.ds(b * slots, slots), 2 * size :] = conv
            count = count + jnp.sum(valid, axis=0, keepdims=True)
            total = total + jnp.sum(conv * valid, axis=0, keepdims=True)
    mean = total / count
    spread = jnp.zeros((1, size), F32)
    for b in range(2 * k):
        valid = (row_at < item_bounds(length_ref, first + b)[-1]).astype(F32)
        gap = (gate_ref[pl.ds(b * slots, slots), 2 * size :] - mean) * valid
        spread = spread + jnp.sum(gap * gap, axis=0, keepdims=True)
    stat_ref[...] = jnp.concatenate([count, mean, spread, jnp.zeros((5, size), F32)])


def gate_call(group, lengths, first, pack, taps, tap_count):
    mine, mate = group
    k, (slots, width) = len(mine), mine[0].shape
    size = taps.shape[1]
    rows = 2 * k * slots
    return kernel_call(
        functools.partial(gate_kernel, k, first, tap_count),
        [shape((rows, 3 * size), F32), shape((rows, width), BF16), shape((8, size), F32)],
        list(mine) + list(mate) + [pack, taps],
        scalars=(lengths,),
        flops=4 * rows * width * size + 40 * tap_count * rows * size,
        scratch=[pltpu.VMEM((slots + 2 * PAD, size), F32)],
    )


def merge_kernel(*refs):
    out_ref = refs[-1]
    count, mean, spread = refs[0][0:1, :], refs[0][1:2, :], refs[0][2:3, :]
    for ref in refs[1:-1]:
        more = ref[0:1, :]
        total = count + more
        gap = ref[1:2, :] - mean
        spread = spread + ref[2:3, :] + gap * gap * (count * more / total)
        mean = (count * mean + more * ref[1:2, :]) / total
        count = total
    out_ref[...] = jnp.concatenate([count, mean, spread, jnp.zeros((5, mean.shape[1]), F32)])


def merge(parts):
    return kernel_call(merge_kernel, [shape(parts[0].shape, F32)], parts)[0]


def sum_kernel(*refs):
    refs[-1][...] = sum(ref[...] for ref in refs[:-1])


def sum_call(parts):
    return kernel_call(sum_kernel, [shape(parts[0].shape, F32)], parts)[0]


def batch_unit(conv, stat_ref):
    inverse = lax.rsqrt(stat_ref[2:3, :] / stat_ref[0:1, :] + EPSILON)
    return (conv - stat_ref[1:2, :]) * inverse, inverse


def batch_kernel(k, *refs):
    gate_ref, stat_ref, batch_ref, pack_ref, refs = refs[0], refs[1], refs[2], refs[3], refs[4:]
    out_mine, out_mate = refs[:k], refs[k]
    slots, width = out_mine[0].shape
    size = batch_ref.shape[1]
    weight = conv_rows(pack_ref, width, size)
    for i in range(k):
        at = pl.ds(2 * i * slots, 2 * slots)
        unit, _ = batch_unit(gate_ref[at, 2 * size :], stat_ref)
        value = unit * batch_ref[0:1, :] + batch_ref[1:2, :]
        active = (value * sigmoid(value)).astype(BF16)
        store_partial(out_mine, out_mate, i, slots, mm(active, weight))


def conv_rows(pack_ref, width, size):
    planes = pack_ref.shape[0]
    base = (2 * size // BLOCK) * (width // planes)
    rows = size // planes
    parts = []
    for p in range(planes):
        blocks = [
            pack_ref[p, base + b * rows : base + (b + 1) * rows, :] for b in range(width // BLOCK)
        ]
        parts.append(jnp.concatenate(blocks, axis=1))
    return jnp.concatenate(parts)


def batch_call(k, gates, stats, batch_rows, pack, slots, width):
    rows, size = gates.shape[0], batch_rows.shape[1]
    outs = [shape((slots, width), F32)] * k + [shape((k, slots, width), BF16)]
    result = kernel_call(
        functools.partial(batch_kernel, k),
        outs,
        [gates, stats, batch_rows, pack],
        flops=2 * rows * width * size,
    )
    return result[:k], result[k]


def batch_back_kernel(k, first, *refs):
    length_ref, refs = refs[0], refs[1:]
    mine, mate, refs = refs[:k], refs[k : 2 * k], refs[2 * k :]
    gate_ref, stat_ref, batch_ref, pack_ref, grad_ref, active_ref, sum_ref = refs
    slots, width = mine[0].shape
    size = batch_ref.shape[1]
    weight = conv_rows(pack_ref, width, size)
    row_at = lax.broadcasted_iota(jnp.int32, (slots, size), 0)
    sums = [jnp.zeros((1, size), F32)] * 4
    for i in range(k):
        rows = jnp.concatenate([mine[i][...], mate[i][...]])
        grad_active = mm_nt(rows, weight)
        for j in range(2):
            b = 2 * i + j
            at = pl.ds(b * slots, slots)
            unit, _ = batch_unit(gate_ref[at, 2 * size :], stat_ref)
            value = unit * batch_ref[0:1, :] + batch_ref[1:2, :]
            sig = sigmoid(value)
            active_ref[at, :] = (value * sig).astype(BF16)
            grad = grad_active[j * slots : (j + 1) * slots] * (sig * (1.0 + value * (1.0 - sig)))
            valid = (row_at < item_bounds(length_ref, first + b)[-1]).astype(F32)
            grad_unit = grad * batch_ref[0:1, :]
            grad_ref[at, :] = grad_unit
            terms = (grad * unit, grad, grad_unit * valid, grad_unit * unit * valid)
            sums = [s + jnp.sum(t, axis=0, keepdims=True) for s, t in zip(sums, terms)]
    sum_ref[...] = jnp.concatenate(sums + [jnp.zeros((4, size), F32)])


def batch_back_call(group, lengths, first, gates, stats, batch_rows, pack):
    mine, mate = group
    k, (slots, width) = len(mine), mine[0].shape
    rows, size = gates.shape[0], batch_rows.shape[1]
    return kernel_call(
        functools.partial(batch_back_kernel, k, first),
        [shape((rows, size), F32), shape((rows, size), BF16), shape((8, size), F32)],
        list(mine) + list(mate) + [gates, stats, batch_rows, pack],
        scalars=(lengths,),
        flops=2 * rows * width * size,
    )


def gate_back_kernel(k, first, tap_count, *refs):
    length_ref, refs = refs[0], refs[1:]
    grad_in_ref, gate_ref, stat_ref, sum_ref, pack_ref, tap_ref, refs = (
        refs[0],
        refs[1],
        refs[2],
        refs[3],
        refs[4],
        refs[5],
        refs[6:],
    )
    out_mine, out_mate, grad_ref, tap_grad_ref, glu_ref, conv_grad_ref = (
        refs[:k],
        refs[k],
        refs[k + 1],
        refs[k + 2],
        refs[k + 3],
        refs[k + 4],
    )
    slots, width = out_mine[0].shape
    size = tap_ref.shape[1]
    reach = tap_count // 2
    row_at = lax.broadcasted_iota(jnp.int32, (slots, size), 0)
    glu_ref[...] = jnp.zeros_like(glu_ref)
    conv_grad_ref[...] = jnp.zeros_like(conv_grad_ref)
    tap_grad_ref[...] = jnp.zeros_like(tap_grad_ref)
    frame_count = stat_ref[0:1, :]
    mean_grad = sum_ref[2:3, :] / frame_count
    mean_cross = sum_ref[3:4, :] / frame_count
    for i in range(k):
        halves = []
        for j in range(2):
            b = 2 * i + j
            at = pl.ds(b * slots, slots)
            before, behind, valid = item_reach(item_bounds(length_ref, first + b), row_at, slots)
            gate_a, gate_sig = gate_ref[at, :size], sigmoid(gate_ref[at, size : 2 * size])
            glu_ref[PAD : PAD + slots, :] = gate_a * gate_sig * valid
            unit, inverse = batch_unit(gate_ref[at, 2 * size :], stat_ref)
            conv_grad = valid * inverse * (grad_in_ref[at, :] - mean_grad - unit * mean_cross)
            conv_grad_ref[PAD : PAD + slots, :] = conv_grad
            grad_glu = jnp.zeros((slots, size), F32)
            for tap in range(tap_count):
                o = tap - reach
                near = glu_ref[PAD + o : PAD + o + slots, :]
                back = conv_grad_ref[PAD - o : PAD - o + slots, :]
                if o < 0:
                    near = jnp.where(before >= -o, near, 0.0)
                    back = jnp.where(behind >= -o, back, 0.0)
                elif o > 0:
                    near = jnp.where(behind >= o, near, 0.0)
                    back = jnp.where(before >= o, back, 0.0)
                grad_glu = grad_glu + back * tap_ref[tap : tap + 1, :]
                tap_grad_ref[tap : tap + 1, :] += jnp.sum(near * conv_grad, axis=0, keepdims=True)
            grad_glu = grad_glu * valid
            halves.append(
                jnp.concatenate(
                    [grad_glu * gate_sig, grad_glu * gate_a * gate_sig * (1.0 - gate_sig)], axis=1
                ).astype(BF16)
            )
        grad = jnp.concatenate(halves)
        grad_ref[pl.ds(2 * i * slots, 2 * slots), :] = grad
        store_partial(out_mine, out_mate, i, slots, square_product_back(grad, pack_ref, width, 0, 2 * size))


def gate_back_call(k, lengths, first, grads, gates, stats, sums, pack, taps, tap_count, slots, width):
    rows, size = grads.shape
    outs = [shape((slots, width), F32)] * k + [
        shape((k, slots, width), BF16),
        shape((rows, 2 * size), BF16),
        shape(taps.shape, F32),
    ]
    padded = pltpu.VMEM((slots + 2 * PAD, size), F32)
    result = kernel_call(
        functools.partial(gate_back_kernel, k, first, tap_count),
        outs,
        [grads, gates, stats, sums, pack, taps],
        scalars=(lengths,),
        flops=4 * rows * width * size + 80 * tap_count * rows * size,
        scratch=[padded, padded],
    )
    return (result[:k], result[k]), result[k + 1 :]


def join_kernel(count, coefficient, *refs):
    stream_ref, own_ref, mate_ref, refs = refs[0], refs[1], refs[2], refs[3:]
    far, norm_ref, stream_out, normed_ref = refs[:count], refs[count], refs[count + 1], refs[count + 2]
    branch = own_ref[...] + mate_ref[0].astype(F32)
    for ref in far:
        branch = branch + ref[...].astype(F32)
    stream = stream_ref[...].astype(F32) + coefficient * branch
    stream_out[...] = stream
    unit, _ = normalize(stream)
    normed_ref[...] = (unit * norm_ref[0:1, :] + norm_ref[1:2, :]).astype(BF16)


def join_call(stream, parts, coefficient, norm):
    own, mate, far = parts
    return kernel_call(
        functools.partial(join_kernel, len(far), coefficient),
        [shape(own.shape, F32), shape(own.shape, BF16)],
        [stay(stream), own, mate] + list(far) + [norm],
    )


def turn_kernel(count, coefficient, *refs):
    length_ref, refs = refs[0], refs[1:]
    stream_ref, own_ref, mate_ref, refs = refs[0], refs[1], refs[2], refs[3:]
    far, norm_ref, cotangent_ref, refs = refs[:count], refs[count], refs[count + 1], refs[count + 2 :]
    output_ref, grad_out, low_out, norm_grad = refs
    branch = own_ref[...] + mate_ref[0].astype(F32)
    for ref in far:
        branch = branch + ref[...].astype(F32)
    stream = stream_ref[...] + coefficient * branch
    row_at = lax.broadcasted_iota(jnp.int32, (stream.shape[0], 1), 0)
    valid = (row_at < item_bounds(length_ref)[-1]).astype(F32)
    unit, scale = normalize(stream)
    output_ref[...] = ((unit * norm_ref[0:1, :] + norm_ref[1:2, :]) * valid).astype(BF16)
    norm_back(
        unit,
        scale,
        norm_ref,
        cotangent_ref[...].astype(F32) * valid,
        0.0,
        0.5,
        grad_out,
        low_out,
        norm_grad,
    )


def norm_back(unit, scale, norm_ref, grad, base, coefficient, grad_out, low_out, norm_grad):
    norm_grad[...] = jnp.concatenate(
        [jnp.sum(grad * unit, axis=0, keepdims=True), jnp.sum(grad, axis=0, keepdims=True)]
    )
    grad = grad * norm_ref[0:1, :]
    inner = jnp.mean(grad, axis=-1, keepdims=True)
    cross = jnp.mean(grad * unit, axis=-1, keepdims=True)
    grad = base + scale * (grad - inner - unit * cross)
    if grad_out is not None:
        grad_out[...] = grad
    low_out[...] = (coefficient * grad).astype(BF16)


def turn_call(stream, parts, coefficient, norm, cotangent, lengths):
    own, mate, far = parts
    return kernel_call(
        functools.partial(turn_kernel, len(far), coefficient),
        [
            shape(own.shape, BF16),
            shape(own.shape, F32),
            shape(own.shape, BF16),
            shape((2, own.shape[1]), F32),
        ],
        [stay(stream), own, mate] + list(far) + [norm, stay(cotangent)],
        scalars=(lengths,),
    )


def join_back_kernel(count, coefficient, keep, *refs):
    stream_ref, grad_ref, own_ref, mate_ref, refs = refs[0], refs[1], refs[2], refs[3], refs[4:]
    far, norm_ref, refs = refs[:count], refs[count], refs[count + 1 :]
    grad_out, (low_out, norm_grad) = (refs[0] if keep else None), refs[-2:]
    grad = own_ref[...] + mate_ref[0].astype(F32)
    for ref in far:
        grad = grad + ref[...].astype(F32)
    unit, scale = normalize(stream_ref[...].astype(F32))
    norm_back(
        unit, scale, norm_ref, grad, grad_ref[...], coefficient, grad_out, low_out, norm_grad
    )


def join_back_call(stream, grad, parts, coefficient, norm, keep=True):
    own, mate, far = parts
    outs = [shape(own.shape, F32)] if keep else []
    return kernel_call(
        functools.partial(join_back_kernel, len(far), coefficient, keep),
        outs + [shape(own.shape, BF16), shape((2, own.shape[1]), F32)],
        [stay(stream), stay(grad), own, mate] + list(far) + [norm],
    )


def offset_table(slot_count, model_width):
    offsets = jnp.arange(2 * slot_count, dtype=F32) - (slot_count - 1)
    freqs = jnp.exp(-jnp.log(10000.0) * jnp.arange(0, model_width, 2, dtype=F32) / model_width)
    angles = offsets[:, None] * freqs[None, :]
    return jnp.concatenate([jnp.sin(angles), jnp.cos(angles)], axis=1)


def nesterov(weight, moment, average, grad_rows, rate, rate_scale):
    moment_new = MOMENTUM_DECAY * moment + grad_rows
    weight_new = weight - rate * rate_scale * (grad_rows + MOMENTUM_DECAY * moment_new)
    average_new = AVERAGE_DECAY * average + (1.0 - AVERAGE_DECAY) * weight_new
    return (moment_new, weight_new, average_new)


def head_lanes(member, i, sides, planes, size):
    side, rest = member % sides, member // sides
    plane = side * (planes // sides) + i
    return (plane * 4 + rest) * size


def split_down_kernel(weight_ref, first_ref, second_ref):
    hidden = first_ref.shape[1]
    rows = weight_ref.shape[1]
    for layer, out in enumerate((first_ref, second_ref)):
        for b in range(weight_ref.shape[2] // hidden):
            part = weight_ref[layer, :, b * hidden : (b + 1) * hidden]
            out[b * rows : (b + 1) * rows, :] = part.astype(BF16)


def split_up_kernel(weight_ref, first_ref, second_ref):
    team, _, hidden = first_ref.shape
    planes = weight_ref.shape[2] // (team * LANES)
    for layer, out in enumerate((first_ref, second_ref)):
        for t in range(team):
            for p in range(planes):
                at = (p * team + t) * LANES
                part = weight_ref[layer, :, at : at + LANES]
                out[t, :, p * LANES : (p + 1) * LANES] = part.astype(BF16)


def split_square_kernel(planes, sides, head_size, weight_ref, column_ref, mix_ref, conv_ref):
    team = column_ref.shape[0]
    width = weight_ref.shape[2]
    size = width // team
    for t in range(team):
        for i, matrix in enumerate((0, 1, 2, 4, 5, 6)):
            if i < 4:
                starts = [
                    head_lanes(t, h, sides, planes, head_size) for h in range(size // head_size)
                ]
                count = head_size
            else:
                count = size // planes
                starts = [(p * team + t) * count for p in range(planes)]
            parts = [weight_ref[matrix, :, at : at + count] for at in starts]
            column_ref[t, :, i * size : (i + 1) * size] = jnp.concatenate(parts, axis=1).astype(BF16)
    mix_ref[...] = weight_ref[3].astype(BF16)
    conv_ref[...] = weight_ref[7].astype(BF16)


def square_pack_kernel(side_ref, column_ref, own_ref, other_ref, conv_ref, mix_out, conv_out):
    team, rows, lanes = column_ref.shape
    depth = team * rows
    for b in range(lanes // BLOCK):
        out, at = (mix_out, b * depth) if b < 2 else (conv_out, (b - 2) * depth)
        for t in range(team):
            first = at + t * rows
            out[first : first + rows, :] = column_ref[t, :, b * BLOCK : (b + 1) * BLOCK]
    low = side_ref[0] == 0
    for b in range(own_ref.shape[1] // BLOCK):
        lane = slice(b * BLOCK, (b + 1) * BLOCK)
        own, other = own_ref[:, lane].astype(F32), other_ref[:, lane].astype(F32)
        at = 2 * depth + b * 2 * rows
        mix_out[at : at + rows, :] = jnp.where(low, own, other).astype(BF16)
        mix_out[at + rows : at + 2 * rows, :] = jnp.where(low, other, own).astype(BF16)
        at = depth + b * rows
        conv_out[at : at + rows, :] = conv_ref[:, lane]
    at = depth + (own_ref.shape[1] // BLOCK) * rows
    conv_out[at:, :] = jnp.zeros((conv_out.shape[0] - at, BLOCK), BF16)


def feed_pack_kernel(up_ref, down_ref, out_ref):
    team, rows, _ = up_ref.shape
    for t in range(team):
        out_ref[t * rows : (t + 1) * rows, :] = up_ref[t]
    out_ref[team * rows :, :] = down_ref[...]


def column_grad_kernel(mix_ref, conv_ref, out_ref):
    team, rows, lanes = out_ref.shape
    depth = team * rows
    for b in range(lanes // BLOCK):
        ref, at = (mix_ref, b) if b < 2 else (conv_ref, b - 2)
        for t in range(team):
            first = at * depth + t * rows
            out_ref[t, :, b * BLOCK : (b + 1) * BLOCK] = ref[first : first + rows, :]


def update(scale_ref, rate, index, grad, refs):
    weight_ref, moment_ref, average_ref, grad_out, moment_out, weight_out, average_out = refs
    moment = MOMENTUM_DECAY * moment_ref[index] + grad
    weight = weight_ref[index] - rate * scale_ref[0:1, 0:1] * (grad + MOMENTUM_DECAY * moment)
    grad_out[index] = grad
    moment_out[index] = moment
    weight_out[index] = weight
    average_out[index] = AVERAGE_DECAY * average_ref[index] + (1.0 - AVERAGE_DECAY) * weight


def update_up_kernel(scale_ref, first_ref, second_ref, *refs):
    team, _, hidden = first_ref.shape
    for layer, ref in enumerate((first_ref, second_ref)):
        parts = [
            ref[t, :, p * LANES : (p + 1) * LANES] for p in range(hidden // LANES) for t in range(team)
        ]
        update(scale_ref, RATE_UP, layer, jnp.concatenate(parts, axis=1).astype(F32), refs)


def update_down_kernel(scale_ref, first_ref, second_ref, *refs):
    rows, width = refs[0].shape[1:]
    hidden = first_ref.shape[1]
    for layer, ref in enumerate((first_ref, second_ref)):
        base = ref.shape[0] - rows * (width // hidden)
        parts = [
            ref[base + b * rows : base + (b + 1) * rows, :] for b in range(width // hidden)
        ]
        update(scale_ref, RATE_DOWN, layer, jnp.concatenate(parts, axis=1).astype(F32), refs)


def update_square_kernel(planes, sides, head_size, side_ref, *refs):
    scale_ref, column_ref, mix_ref, other_ref, conv_ref, refs = (
        refs[0],
        refs[1],
        refs[2],
        refs[3],
        refs[4],
        refs[5:],
    )
    team, rows, _ = column_ref.shape
    width = refs[0].shape[2]
    size = width // team
    per_side = planes // sides
    for i, matrix in enumerate((0, 1, 2, 4, 5, 6)):
        parts = []
        if i < 4:
            for head in range(width // head_size):
                plane, rest = head // 4, head % 4
                t = rest * sides + plane // per_side
                at = i * size + (plane % per_side) * head_size
                parts.append(column_ref[t, :, at : at + head_size])
        else:
            count = size // planes
            for p in range(planes):
                for t in range(team):
                    at = i * size + p * count
                    parts.append(column_ref[t, :, at : at + count])
        update(scale_ref, RATE_SQUARE, matrix, jnp.concatenate(parts, axis=1).astype(F32), refs)
    blocks = width // BLOCK
    head_rows = sides * rows
    base = mix_ref.shape[0] - blocks * head_rows
    parts = []
    for b in range(blocks):
        at = slice(base + b * head_rows, base + (b + 1) * head_rows)
        parts.append(mix_ref[at, :].astype(F32) + other_ref[at, :].astype(F32))
    whole = jnp.concatenate(parts, axis=1)
    update(scale_ref, RATE_SQUARE, 3, jnp.where(side_ref[0] == 0, whole[:rows], whole[rows:]), refs)
    base = conv_ref.shape[0] - blocks * rows
    parts = [conv_ref[base + b * rows : base + (b + 1) * rows, :] for b in range(blocks)]
    update(scale_ref, RATE_SQUARE, 7, jnp.concatenate(parts, axis=1).astype(F32), refs)


def update_call(body, scale, terms, weight, moment, average, scalars=()):
    return kernel_call(
        body,
        [shape(weight.shape, F32)] * 4,
        [scale]
        + list(terms)
        + [stay(x) for x in (weight, moment, average)],
        scalars=scalars,
    )


def feature_grad_kernel(planes, sides, *refs):
    member_ref, refs = refs[0], refs[1:]
    norms, biases, out_ref = refs[:5], refs[5:-1], refs[-1]
    team, _, size = out_ref.shape
    count = size // planes
    per_side = planes // sides
    head_size = sides * count
    bias = sum(ref[...] for ref in biases)
    rest, side = member_ref[0] // sides, member_ref[0] % sides
    rows = jnp.concatenate([n[0:1, :] for n in norms] + [n[1:2, :] for n in norms])
    for t in range(team):
        parts, own = [], []
        for p in range(planes):
            at = (p * team + t) * count
            parts.append(rows[:, at : at + count])
            at = (p % per_side) * head_size + (t % sides) * count
            held = (rest == t // sides) & (side == p // per_side)
            own.append(bias[:, at : at + count] * held.astype(jnp.int32).astype(F32))
        out_ref[t] = jnp.concatenate(
            [jnp.concatenate(parts, axis=1), jnp.concatenate(own, axis=1)]
        )


def channel_grad_kernel(taps, term_ref, sum_ref, *refs):
    tap_refs, out_ref = refs[:-1], refs[-1]
    features = jnp.sum(term_ref[...], axis=0)
    out_ref[...] = jnp.concatenate(
        [
            sum(ref[:taps] for ref in tap_refs),
            features[:10],
            sum_ref[0:2],
            features[10:12],
        ]
    )


def make_step(planes, sides):
    wide_team = sides == 2
    team_axes = ("x", "c", "y") if wide_team else ("x", "c")
    team = 8 if wide_team else 4
    outer_bits = [("z", 1 << i) for i in range((planes - 1).bit_length())]
    if not wide_team:
        outer_bits += [("y", 1 << i) for i in range((sides - 1).bit_length())]
    head_aligned = wide_team and planes * 4 == HEADS

    def turn(values, first):
        pairs = []
        for x in range(2):
            for c in range(2):
                for y in range(2):
                    along_x = (c == 0) == first
                    to = (1 - x, c, y) if along_x else (x, c, 1 - y)
                    pairs.append((4 * x + 2 * c + y, 4 * to[0] + 2 * to[1] + to[2]))
        return lax.ppermute(values, team_axes, pairs)

    def gather(values):
        return spread(values, None)[0]

    def spread(values, run):
        groups, results = [([values], [swap(values, "c")])], []

        def work(*travelling):
            if run is not None:
                result = run(len(results), groups[-1])
                travelling, result = lax.optimization_barrier((travelling, result))
                results.append(result)
            return travelling

        if not wide_team:
            (far,) = work(swap(values, "x"))
        else:
            first, second = work(turn(values, True), turn(values, False))
            far = turn(first, False)
            groups.append(([first, second], [swap(first, "c"), swap(second, "c")]))
            (far,) = work(far)
        groups.append(([far], [swap(far, "c")]))
        if run is not None:
            results.append(run(len(results), groups[-1]))
        return groups, results

    def scatter(parts, fill=(), near=None):
        (far,), far_mate = parts[-1]
        out_far = add_call(far, swap(far_mate, "c"), 0)
        if near is not None:
            argument, run = near
            out_far, argument = lax.optimization_barrier((out_far, argument))
            parts = run(argument)
        (own,), own_mate = parts[0]
        got_own = swap(own_mate, "c")
        if not wide_team:
            across, fill = lax.optimization_barrier((swap(out_far, "x"), fill))
            return (own, got_own, [across]), fill
        (first, second), side_mate = parts[1]
        got_side = swap(side_mate, "c")
        relay = turn(out_far, False)
        from_second = turn(add_call(second, got_side, 1), False)
        relay, fill = lax.optimization_barrier((relay, fill))
        from_first = turn(add_call(first, got_side, 0, relay), True)
        return (own, got_own, [from_first, from_second]), fill

    def side_rows(rows):
        return rows if wide_team else lax.all_gather(rows, "y", axis=0, tiled=True)

    def side_scatter(rows):
        if wide_team:
            return rows
        return lax.psum_scatter(rows, "y", scatter_dimension=0, tiled=True)

    def split_hidden(rows):
        r, f = rows.shape
        return rows.reshape(r, planes, team, f // (planes * team)).transpose(2, 0, 1, 3).reshape(
            team, r, f // team
        )

    def join_hidden(blocks):
        _, r, f = blocks.shape
        return blocks.reshape(team, r, planes, f // planes).transpose(1, 2, 0, 3).reshape(
            r, team * f
        )

    def split_heads(rows):
        r, d = rows.shape
        if not head_aligned:
            return rows.reshape(r, team, d // team).transpose(1, 0, 2)
        size = d // HEADS
        rows = rows.reshape(r, sides, planes // sides, 2, 2, size)
        return rows.transpose(3, 4, 1, 0, 2, 5).reshape(team, r, d // team)

    def join_heads(blocks):
        _, r, f = blocks.shape
        if not head_aligned:
            return blocks.transpose(1, 0, 2).reshape(r, team * f)
        size = team * f // HEADS
        blocks = blocks.reshape(2, 2, sides, r, planes // sides, size)
        return blocks.transpose(3, 2, 4, 0, 1, 5).reshape(r, team * f)

    def team_swap(blocks):
        return lax.all_to_all(blocks, team_axes, split_axis=0, concat_axis=0, tiled=True)

    def plane_pieces(rows):
        return [rows] + [swap(rows, "z", d) for d in range(1, planes)]

    def plane_gather(rows):
        return lax.all_gather(rows, "z", axis=0, tiled=False)

    def plane_reduce(rows):
        return lax.psum_scatter(rows, "z", scatter_dimension=0, tiled=False)

    def to_blocks(rows, size):
        return jnp.concatenate([rows[:, i : i + size] for i in range(0, rows.shape[1], size)])

    def from_blocks(rows, count):
        return jnp.concatenate(jnp.split(rows, count), axis=1)

    def outer_merge(values, combine):
        if wide_team:
            return combine([values] + [swap(values, "z", d) for d in range(1, planes)])
        for axis, bit in outer_bits:
            values = combine([values, swap(values, axis, bit)])
        return values

    def step(
        frames,
        lengths,
        out_grad,
        up_weight,
        down_weight,
        square_weight,
        chan_weight,
        up_moment,
        down_moment,
        square_moment,
        chan_moment,
        up_average,
        down_average,
        square_average,
        chan_average,
    ):
        slots, width = frames.shape
        head_size = width // HEADS
        item_count = lengths.shape[1] - 1
        chan_rows = chan_weight.shape[0]
        tap_count = chan_rows - 14
        hidden = up_weight.shape[2]
        team_hidden = hidden // team
        team_width = width // team
        x_at, c_at, y_at = lax.axis_index("x"), lax.axis_index("c"), lax.axis_index("y")
        team_at = (x_at * 2 + c_at) * 2 + y_at if wide_team else x_at * 2 + c_at
        side = y_at.reshape(1).astype(jnp.int32)
        plane = lax.axis_index("z").reshape(1).astype(jnp.int32)

        chan_low = chan_weight.astype(BF16)
        if head_aligned:
            blocks = [shape((hidden // planes // team * (width // team_hidden), team_hidden), BF16)] * 2
            down_one, down_two = kernel_call(split_down_kernel, blocks, [stay(down_weight)])
            rows_in = up_weight.shape[1]
            blocks = [shape((team, rows_in, team_hidden), BF16)] * 2
            up_one, up_two = kernel_call(split_up_kernel, blocks, [stay(up_weight)])
            columns, mix, conv_out = kernel_call(
                functools.partial(split_square_kernel, planes, sides, head_size),
                [shape((team, rows_in, 6 * team_width), BF16)] + [shape((rows_in, width), BF16)] * 2,
                [stay(square_weight)],
            )
        else:
            up_low = up_weight.astype(BF16)
            down_low = down_weight.astype(BF16)
            square_low = square_weight.astype(BF16)
            down_one, down_two = [to_blocks(side_rows(down_low[i]), team_hidden) for i in (0, 1)]
            up_one, up_two = [split_hidden(side_rows(up_low[i])) for i in (0, 1)]
            columns = jnp.concatenate(
                [split_heads(side_rows(square_low[i])) for i in (0, 1, 2, 4)]
                + [split_hidden(side_rows(square_low[i])) for i in (5, 6)],
                axis=2,
            )
            mix, conv_out = square_low[3], side_rows(square_low[7])
        down_one = plane_gather(down_one)
        up_one = team_swap(up_one)
        up_one, frames, chan_low, lengths, columns, up_two, mix = lax.optimization_barrier(
            (up_one, frames, chan_low, lengths, columns, up_two, mix)
        )
        packs_one = (plane_gather(up_one.reshape(-1, team_hidden)), down_one)
        groups = gather(frames)

        if wide_team:
            lanes = jnp.pad(chan_low, ((0, LANES - chan_rows), (0, 0))).T
            carried = jnp.pad(
                lengths.astype(BF16), ((0, CARRY - 1), (0, LANES - lengths.shape[1]))
            )
            lanes = jnp.concatenate([lanes, carried])[None]
            for axis in ("y", "c", "x"):
                lanes = jnp.concatenate([lanes, swap(lanes, axis)])
            where_at = jnp.stack([plane[0], team_at, y_at, c_at]).astype(jnp.int32)
            norms = [shape((2, width), F32)] * 5
            params = kernel_call(
                functools.partial(channel_kernel, planes, sides, head_size),
                norms
                + [
                    shape((tap_count + 1, team_width), F32),
                    shape((2, team_width), F32),
                    shape((2, team_width), F32),
                    shape((team, lengths.shape[1]), jnp.int32),
                ],
                plane_pieces(lanes),
                scalars=(where_at,),
                scratch=[pltpu.VMEM((width, LANES), F32)],
            )
            norms, (taps, batch_rows, bias_rows, team_lengths) = params[:5], params[5:]
        else:
            team_lengths = jnp.concatenate(chunk_order(gather(lengths)))
            chan_float = lax.all_gather(chan_low, ALL, axis=1, tiled=True).astype(F32)

            def own_hidden(rows):
                rows = rows.reshape(rows.shape[0], planes, team, -1)
                rows = lax.dynamic_index_in_dim(rows, team_at, axis=2, keepdims=False)
                return rows.reshape(rows.shape[0], team_width)

            taps = own_hidden(chan_float[: tap_count + 1])
            batch_rows = own_hidden(chan_float[tap_count + 10 : tap_count + 12])
            bias_rows = lax.dynamic_index_in_dim(
                split_heads(chan_float[tap_count + 12 : tap_count + 14]), team_at, 0, False
            )
            norms = [
                jnp.stack([chan_float[tap_count + j], chan_float[tap_count + 5 + j]])
                for j in range(5)
            ]

        columns, up_two = team_swap(columns), team_swap(up_two)
        if head_aligned:
            head_rows = sides * rows_in
            per_side = planes // sides
            depth = team * rows_in
            lines = [2 * depth + width // BLOCK * head_rows, 2 * depth]
            mix_pack, conv_pack = kernel_call(
                square_pack_kernel,
                [shape((n, BLOCK), BF16) for n in lines],
                [columns, mix, swap(mix, "y"), conv_out],
                scalars=(side,),
            )
            second = kernel_call(
                feed_pack_kernel,
                [shape((depth + down_two.shape[0], team_hidden), BF16)],
                [up_two, down_two],
            )[0]
        else:
            per_side = 0
            mix = lax.all_gather(mix, ALL, axis=0, tiled=True)
            mix = lax.dynamic_slice_in_dim(mix, team_at * team_width, team_width, axis=0)
            columns = columns.reshape(-1, 6 * team_width)
            mix_pack = to_blocks(columns[:, : 4 * team_width], BLOCK)
            conv_pack = jnp.concatenate(
                [to_blocks(columns[:, 4 * team_width :], BLOCK), to_blocks(conv_out, BLOCK)]
            )
            second = jnp.concatenate([up_two.reshape(-1, team_hidden), down_two])
        table = offset_table(slots, width).astype(BF16)

        ready = (packs_one, groups, norms, taps, team_lengths, table)
        ready, mix_pack, conv_pack, second, mix = lax.optimization_barrier(
            (ready, mix_pack, conv_pack, second, mix)
        )
        packs_one, groups, norms, taps, team_lengths, table = ready
        mix_pack = plane_gather(mix_pack)
        mix_packs = (mix_pack,) if head_aligned else (mix_pack, mix)

        def columns_of(results, i):
            return [result[i] for result in results]

        at = [0]
        for group in groups:
            at.append(at[-1] + 2 * len(group[0]))

        results = [forward_call(group, packs_one, norms[0]) for group in groups]
        saved_one = [columns_of(columns_of(results, 1), i) for i in (1, 0)]
        parts, _ = scatter(columns_of(results, 0))
        stream_one, normed = join_call(frames, parts, 0.5, norms[1])
        normed, conv_pack, second = lax.optimization_barrier((normed, conv_pack, second))
        conv_pack = plane_gather(conv_pack)
        pack_two = plane_gather(second)

        place = kernel_call(
            place_kernel,
            [shape((table.shape[0], team_width), BF16)],
            [table, mix_pack],
            flops=2 * table.shape[0] * width * team_width,
        )[0]

        def attention(i, group):
            return attention_call(
                group, team_lengths, at[i], side, mix_packs, per_side, bias_rows, place, head_size
            )

        groups, results = spread(normed, attention)
        saved_two = columns_of(results, 1)
        parts, _ = scatter(columns_of(results, 0))
        stream_two, normed = join_call(stream_one, parts, 1.0, norms[2])

        def gates(i, group):
            return gate_call(group, team_lengths, at[i], conv_pack, taps, tap_count)

        groups, saved_three = spread(normed, gates)
        stats = outer_merge(merge(columns_of(saved_three, 2)), merge)
        results = [
            batch_call(len(group[0]), saved[0], stats, batch_rows, conv_pack, slots, width)
            for group, saved in reversed(list(zip(groups, saved_three)))
        ][::-1]
        parts, _ = scatter(results)
        stream_three, normed = join_call(stream_two, parts, 1.0, norms[3])
        normed, pack_two = lax.optimization_barrier((normed, pack_two))

        groups, results = spread(normed, lambda i, group: forward_call(group, (pack_two,)))
        saved_four = [chunk_order(groups), columns_of(columns_of(results, 1), 0)]
        parts, _ = scatter(columns_of(results, 0))
        output, grad_four, low, norm_four = turn_call(
            stream_three, parts, 0.5, norms[4], out_grad, lengths
        )

        def feed_backward(low, packs, saved):
            normed, before = saved
            groups, results = spread(
                low, lambda i, group: backward_call(group, packs, before[i])
            )
            grads, active = [columns_of(columns_of(results, 1), i) for i in (0, 1)]
            term = feed_weight_call(normed, grads, active, chunk_order(groups), planes)
            return scatter(columns_of(results, 0), term)

        parts, second_term = feed_backward(low, (pack_two,), saved_four)
        grad_three, low, norm_three = join_back_call(stream_three, grad_four, parts, 1.0, norms[3])
        low, second_term = lax.optimization_barrier((low, second_term))
        second_term = plane_reduce(second_term)

        def batch_back(i, group):
            return batch_back_call(
                group, team_lengths, at[i], saved_three[i][0], stats, batch_rows, conv_pack
            )

        groups, grads = spread(low, batch_back)
        local_sums = sum_call(columns_of(grads, 2))
        sums = outer_merge(local_sums, sum_call)
        def gate_back(sums, numbers):
            return [
                gate_back_call(
                    len(groups[i][0]), team_lengths, at[i], grads[i][0], saved_three[i][0], stats,
                    sums, conv_pack, taps, tap_count, slots, width,
                )
                for i in numbers
            ]

        results = gate_back(sums, [len(groups) - 1])

        def gate_back_near(sums):
            results[:0] = gate_back(sums, range(len(groups) - 1))
            return columns_of(results, 0)

        parts, _ = scatter(columns_of(results, 0), near=(sums, gate_back_near))
        tap_terms = columns_of(columns_of(results, 1), 1)
        conv_term = conv_weight_call(
            columns_of(saved_three, 1), columns_of(columns_of(results, 1), 0), columns_of(grads, 1),
            chunk_order(groups), planes,
        )
        parts, conv_term = lax.optimization_barrier((parts, conv_term))
        grad_two, low, norm_two = join_back_call(stream_two, grad_three, parts, 1.0, norms[2])
        low, conv_term, second_term = lax.optimization_barrier((low, conv_term, second_term))
        conv_term = plane_reduce(conv_term)

        def attention_back(i, group):
            return attention_back_call(
                group, side, mix_packs, per_side, place, saved_two[i], head_size
            )

        groups, results = spread(low, attention_back)
        rows = chunk_order(groups)
        grads = columns_of(results, 1)
        bias_terms = columns_of(grads, 2)
        mix_term = mix_weight_call(
            saved_two, columns_of(grads, 0), rows, [table] + columns_of(grads, 1), side, planes,
            per_side,
        )
        parts, mix_term = scatter(columns_of(results, 0), mix_term)
        if not head_aligned:
            mixed = jnp.concatenate([saved[:, -team_width:] for saved in saved_two])
            mix_own = mm_tn(mixed, jnp.concatenate(rows)).astype(BF16)
            mix_own = lax.dynamic_update_slice_in_dim(
                jnp.zeros((width, width), BF16), mix_own, team_at * team_width, axis=0
            )
        grad_one, low, norm_one = join_back_call(stream_one, grad_two, parts, 0.5, norms[1])
        low, conv_term = lax.optimization_barrier((low, conv_term))
        mix_term = plane_reduce(mix_term)

        parts, first_term = feed_backward(low, packs_one, saved_one)
        first_term = plane_reduce(first_term)
        frames_grad, norm_zero = join_back_call(frames, grad_one, parts, 1.0, norms[0], keep=False)

        late = (second_term, conv_term, mix_term)
        frames_grad, late = lax.optimization_barrier((frames_grad, late))
        second_term, conv_term, mix_term = late
        depth = width // planes
        rate_scale = lax.rsqrt(stats[0:1])

        def from_team(rows, columns):
            return team_swap(rows.astype(BF16).reshape(team, -1, columns))

        def finish_channels(chan_term):
            chan_term = outer_merge(chan_term, sum_call).reshape(chan_rows, planes, -1)
            chan_term = lax.dynamic_index_in_dim(chan_term, lax.axis_index("z"), 1, keepdims=False)
            if not wide_team:
                chan_term = lax.dynamic_index_in_dim(
                    chan_term.reshape(chan_rows, sides, -1), y_at, 1, keepdims=False
                )
            return chan_term

        norm_terms = [norm_zero, norm_one, norm_two, norm_three, norm_four]
        if head_aligned:
            second_up = from_team(second_term[:depth], team_hidden)
            features = kernel_call(
                functools.partial(feature_grad_kernel, planes, sides),
                [shape((team, 12, team_width), F32)],
                norm_terms + bias_terms,
                scalars=(team_at.reshape(1).astype(jnp.int32),),
            )[0]
            chan_term = kernel_call(
                functools.partial(channel_grad_kernel, tap_count),
                [shape((chan_rows, team_width), F32)],
                [team_swap(features), local_sums] + tap_terms,
            )[0]
            chan_grad = finish_channels(chan_term)
            blocks = kernel_call(
                column_grad_kernel,
                [shape((team, rows_in, 6 * team_width), BF16)],
                [mix_term, conv_term],
            )[0]
            square_all = update_call(
                functools.partial(update_square_kernel, planes, sides, head_size),
                rate_scale,
                [team_swap(blocks), mix_term, swap(mix_term, "y"), conv_term],
                square_weight,
                square_moment,
                square_average,
                scalars=(side,),
            )
            first_term, square_all, second_up = lax.optimization_barrier(
                (first_term, square_all, second_up)
            )
            down_all = update_call(
                update_down_kernel,
                rate_scale,
                [first_term, second_term],
                down_weight,
                down_moment,
                down_average,
            )
            up_all = update_call(
                update_up_kernel,
                rate_scale,
                [from_team(first_term[:depth], team_hidden), second_up],
                up_weight,
                up_moment,
                up_average,
            )
            up_grad, up_new = up_all[0], up_all[1:]
            down_grad, down_new = down_all[0], down_all[1:]
            square_grad, square_new = square_all[0], square_all[1:]
            rate_scale = rate_scale[0, 0]
        else:
            column_blocks = 4 * team_width // BLOCK
            qkv_term = from_blocks(mix_term[: column_blocks * depth], column_blocks)
            gate_blocks = 2 * team_width // BLOCK
            gate_term = from_blocks(conv_term[: gate_blocks * depth], gate_blocks)
            conv_out_term = from_blocks(conv_term[gate_blocks * depth :], width // BLOCK)
            mix_grad = lax.psum_scatter(mix_own, ALL, scatter_dimension=0, tiled=True).astype(F32)
            blocks = from_team(jnp.concatenate([qkv_term, gate_term], axis=1), 6 * team_width)

            def block(i):
                return blocks[:, :, i * team_width : (i + 1) * team_width]

            square_grad = jnp.stack(
                [side_scatter(join_heads(block(i))).astype(F32) for i in range(3)]
                + [mix_grad, side_scatter(join_heads(block(3))).astype(F32)]
                + [side_scatter(join_hidden(block(i))).astype(F32) for i in (4, 5)]
                + [side_scatter(conv_out_term).astype(F32)]
            )
            bias_rows = join_heads(
                lax.dynamic_update_slice_in_dim(
                    jnp.zeros((team, 2, team_width), F32), sum(bias_terms)[None], team_at, 0
                )
            )
            features = jnp.concatenate(
                [t[0:1] for t in norm_terms] + [t[1:2] for t in norm_terms] + [bias_rows]
            )
            features = jnp.sum(team_swap(split_hidden(features)), axis=0)
            chan_grad = finish_channels(
                jnp.concatenate(
                    [
                        sum(tap_terms)[:tap_count],
                        features[:10],
                        local_sums[:2],
                        features[10:],
                    ]
                )
            )
            feed_terms = (first_term, second_term)
            up_grad = jnp.stack(
                [
                    side_scatter(join_hidden(from_team(rows[:depth], team_hidden))).astype(F32)
                    for rows in feed_terms
                ]
            )
            down_grad = jnp.stack(
                [
                    side_scatter(from_blocks(rows[depth:], width // team_hidden)).astype(F32)
                    for rows in feed_terms
                ]
            )
            rate_scale = rate_scale[0, 0]
            up_new = nesterov(up_weight, up_moment, up_average, up_grad, RATE_UP, rate_scale)
            down_new = nesterov(
                down_weight, down_moment, down_average, down_grad, RATE_DOWN, rate_scale
            )
            square_new = nesterov(
                square_weight, square_moment, square_average, square_grad, RATE_SQUARE, rate_scale
            )
        chan_new = nesterov(
            chan_weight, chan_moment, chan_average, chan_grad, RATE_CHANNEL, rate_scale
        )
        bias_grad = chan_grad[tap_count + 12 : tap_count + 14]
        return (
            output,
            frames_grad,
            up_grad,
            down_grad,
            square_grad,
            chan_grad,
            up_new[0],
            down_new[0],
            square_new[0],
            chan_new[0],
            up_new[1],
            down_new[1],
            square_new[1],
            chan_new[1],
            up_new[2],
            down_new[2],
            square_new[2],
            chan_new[2],
            bias_grad,
        )

    return step


def solution(mesh):
    wide, narrow = mesh.shape["wide"], mesh.shape["narrow"]
    planes = wide // 4
    inner = Mesh(mesh.devices.reshape(planes, 2, 2, narrow), ALL)
    token = P(ALL, None)
    matrix = P(None, ALL, None)
    vector = P(None, ALL)
    group = (matrix, matrix, matrix, vector)
    return jax.shard_map(
        make_step(planes, narrow),
        mesh=inner,
        in_specs=(token, token, token) + group * 3,
        out_specs=(token, token) + group * 4 + (vector,),
        check_vma=False,
    )
```

```python
import functools

import jax
import jax.numpy as jnp
from jax import lax
from jax.experimental import pallas as pl
from jax.experimental.pallas import tpu as pltpu
from jax.sharding import Mesh
from jax.sharding import PartitionSpec as P

HEADS = 16
EPSILON = 1e-05
MOMENTUM_DECAY = 0.9
AVERAGE_DECAY = 0.9
RATE_UP = 0.05
RATE_DOWN = 0.026
RATE_SQUARE = 0.05
RATE_CHANNEL = 0.5
MASKED_SCORE = -1e30
BF16 = jnp.bfloat16
F32 = jnp.float32
ALL = ("z", "x", "c", "y")
LANES = 128
PAD = 16
BLOCK = 256
CARRY = 16
ROOM = 6 << 20


def mm(left, right):
    return jnp.dot(left, right, preferred_element_type=F32)


def mm_tn(left, right):
    return lax.dot_general(left, right, (((0,), (0,)), ((), ())), preferred_element_type=F32)


def mm_nt(left, right):
    return lax.dot_general(left, right, (((1,), (1,)), ((), ())), preferred_element_type=F32)


def swap(values, axis, bit=1):
    size = lax.axis_size(axis)
    return lax.ppermute(values, axis, [(i, i ^ bit) for i in range(size)])


def sigmoid(values):
    return 1.0 / (1.0 + jnp.exp(-values))


def swish_grad(values):
    sig = sigmoid(values)
    return sig * (1.0 + values * (1.0 - sig))


def normalize(values):
    centre = values - jnp.mean(values, axis=-1, keepdims=True)
    scale = lax.rsqrt(jnp.mean(centre * centre, axis=-1, keepdims=True) + EPSILON)
    return centre * scale, scale


def shape(dims, dtype):
    return jax.ShapeDtypeStruct(tuple(dims), dtype)


def size_of(item):
    total = 1
    for n in item.shape:
        total *= n
    return total * item.dtype.itemsize


def kernel_call(body, outs, args, scalars=(), flops=0, scratch=()):
    moved = sum(size_of(a) for a in args) + sum(size_of(o) for o in outs)
    return pl.pallas_call(
        body,
        out_shape=tuple(outs),
        in_specs=[pl.BlockSpec(memory_space=pltpu.SMEM)] * len(scalars)
        + [pl.BlockSpec(memory_space=pltpu.VMEM)] * len(args),
        out_specs=tuple(pl.BlockSpec(memory_space=pltpu.VMEM) for _ in outs),
        scratch_shapes=list(scratch),
        compiler_params=pltpu.CompilerParams(vmem_limit_bytes=moved + ROOM),
        cost_estimate=pl.CostEstimate(flops=int(flops), bytes_accessed=moved, transcendentals=0),
    )(*scalars, *args)


def stay(values):
    return pltpu.with_memory_space_constraint(values, pltpu.HBM)


def store_partial(mine_refs, mate_ref, i, slots, value):
    mine_refs[i][...] = value[:slots]
    mate_ref[i] = value[slots:].astype(BF16)


def up_product(rows, ref):
    planes = ref.shape[0]
    depth = rows.shape[1] // planes
    total = mm(rows[:, :depth], ref[0, :depth, :])
    for p in range(1, planes):
        total = total + mm(rows[:, p * depth : (p + 1) * depth], ref[p, :depth, :])
    return total


def up_product_back(rows, ref, width):
    planes = ref.shape[0]
    depth = width // planes
    return jnp.concatenate([mm_nt(rows, ref[p, :depth, :]) for p in range(planes)], axis=1)


def down_blocks(ref, width):
    planes, hidden = ref.shape[0], ref.shape[2]
    rows = hidden // planes
    depth = ref.shape[1] - rows * (width // hidden)
    return [
        jnp.concatenate(
            [ref[p, depth + b * rows : depth + (b + 1) * rows, :] for p in range(planes)]
        )
        for b in range(width // hidden)
    ]


def down_product(rows, blocks):
    return jnp.concatenate([mm(rows, block) for block in blocks], axis=1)


def down_product_back(rows, blocks):
    size = blocks[0].shape[1]
    total = mm_nt(rows[:, :size], blocks[0])
    for b in range(1, len(blocks)):
        total = total + mm_nt(rows[:, b * size : (b + 1) * size], blocks[b])
    return total


def square_columns(ref, p, depth, first, last):
    parts = []
    while first < last:
        block = first // BLOCK
        stop = min(last, (block + 1) * BLOCK)
        lanes = slice(first - block * BLOCK, stop - block * BLOCK)
        parts.append(ref[p, block * depth : (block + 1) * depth, lanes])
        first = stop
    return jnp.concatenate(parts, axis=1) if len(parts) > 1 else parts[0]


def square_product(rows, ref, first, last):
    planes = ref.shape[0]
    depth = rows.shape[1] // planes
    total = None
    for p in range(planes):
        term = mm(rows[:, p * depth : (p + 1) * depth], square_columns(ref, p, depth, first, last))
        total = term if total is None else total + term
    return total


def square_product_back(rows, ref, width, first, last):
    planes = ref.shape[0]
    depth = width // planes
    return jnp.concatenate(
        [mm_nt(rows, square_columns(ref, p, depth, first, last)) for p in range(planes)], axis=1
    )


def output_rows(ref, p, width, base):
    blocks = width // BLOCK
    rows = (ref.shape[1] - base) // blocks
    parts = []
    for b in range(blocks):
        at = base + b * rows
        part = ref[pl.ds(p, 1), at : at + rows, :]
        parts.append(part.reshape(part.shape[1:]))
    return jnp.concatenate(parts, axis=1)


def forward_kernel(k, packs, with_norm, *refs):
    mine, mate, refs = refs[:k], refs[k : 2 * k], refs[2 * k :]
    if with_norm:
        norm_ref, refs = refs[0], refs[1:]
    up_ref, down_ref, refs = refs[0], refs[packs - 1], refs[packs:]
    out_mine, out_mate, before_ref = refs[:k], refs[k], refs[k + 1]
    slots, width = mine[0].shape
    blocks = down_blocks(down_ref, width)
    for i in range(k):
        rows = jnp.concatenate([mine[i][...], mate[i][...]])
        at = pl.ds(2 * i * slots, 2 * slots)
        if with_norm:
            unit, _ = normalize(rows.astype(F32))
            rows = (unit * norm_ref[0:1, :] + norm_ref[1:2, :]).astype(BF16)
            refs[k + 2][at, :] = rows
        before = up_product(rows, up_ref)
        before_ref[at, :] = before
        active = (before * sigmoid(before)).astype(BF16)
        store_partial(out_mine, out_mate, i, slots, down_product(active, blocks))


def forward_call(group, packs, norm=None):
    mine, mate = group
    k, (slots, width) = len(mine), mine[0].shape
    hidden = packs[0].shape[2]
    rows = 2 * k * slots
    outs = [shape((slots, width), F32)] * k + [
        shape((k, slots, width), BF16),
        shape((rows, hidden), F32),
    ]
    args = list(mine) + list(mate)
    if norm is not None:
        outs.append(shape((rows, width), BF16))
        args.append(norm)
    result = kernel_call(
        functools.partial(forward_kernel, k, len(packs), norm is not None),
        outs,
        args + list(packs),
        flops=4 * rows * width * hidden,
    )
    return (result[:k], result[k]), result[k + 1 :]


def backward_kernel(k, packs, *refs):
    mine, mate, refs = refs[:k], refs[k : 2 * k], refs[2 * k :]
    up_ref, down_ref, before_ref, refs = refs[0], refs[packs - 1], refs[packs], refs[packs + 1 :]
    out_mine, out_mate, grad_ref, active_ref = refs[:k], refs[k], refs[k + 1], refs[k + 2]
    slots, width = mine[0].shape
    blocks = down_blocks(down_ref, width)
    for i in range(k):
        at = pl.ds(2 * i * slots, 2 * slots)
        rows = jnp.concatenate([mine[i][...], mate[i][...]])
        before = before_ref[at, :]
        sig = sigmoid(before)
        active_ref[at, :] = (before * sig).astype(BF16)
        grad = down_product_back(rows, blocks) * (sig * (1.0 + before * (1.0 - sig)))
        grad = grad.astype(BF16)
        grad_ref[at, :] = grad
        store_partial(out_mine, out_mate, i, slots, up_product_back(grad, up_ref, width))


def backward_call(group, packs, before):
    mine, mate = group
    k, (slots, width) = len(mine), mine[0].shape
    rows, hidden = before.shape
    outs = [shape((slots, width), F32)] * k + [
        shape((k, slots, width), BF16),
        shape((rows, hidden), BF16),
        shape((rows, hidden), BF16),
    ]
    result = kernel_call(
        functools.partial(backward_kernel, k, len(packs)),
        outs,
        list(mine) + list(mate) + list(packs) + [before],
        flops=4 * rows * width * hidden,
    )
    return (result[:k], result[k]), result[k + 1 :]


def joined(refs, first=0, last=None):
    return jnp.concatenate([r[:, first:last] for r in refs])


def take(refs, counts):
    groups, at = [], 0
    for n in counts:
        groups.append(refs[at : at + n])
        at += n
    return groups + [refs[at:]]


def put(out_ref, planes, write):
    for p in range(planes):
        write(out_ref.at[p], p)


def rows_at(ref, p, rows, lanes=slice(None)):
    return ref[pl.ds(pl.multiple_of(p * rows, rows), rows), lanes]


def feed_weight_kernel(counts, planes, *refs):
    normed, grads, active, rows, refs = take(refs, counts)
    out_ref, up_ref, down_ref = refs
    width, hidden = up_ref.shape
    depth, below = width // planes, hidden // planes
    down_ref[...] = mm_tn(joined(active), joined(rows))
    up_ref[...] = mm_tn(joined(normed), joined(grads))

    def write(out, p):
        out[:depth, :] = rows_at(up_ref, p, depth).astype(BF16)
        for b in range(width // hidden):
            at = depth + b * below
            lanes = slice(b * hidden, (b + 1) * hidden)
            out[at : at + below, :] = rows_at(down_ref, p, below, lanes).astype(BF16)

    put(out_ref, planes, write)


def feed_weight_call(normed, grads, active, rows, planes):
    width, hidden = normed[0].shape[1], grads[0].shape[1]
    lines = width // planes + (hidden // planes) * (width // hidden)
    groups = (normed, grads, active, rows)
    tokens = sum(a.shape[0] for a in grads)
    return kernel_call(
        functools.partial(feed_weight_kernel, [len(g) for g in groups], planes),
        [shape((planes, lines, hidden), BF16)],
        [a for g in groups for a in g],
        flops=4 * width * hidden * tokens,
        scratch=[pltpu.VMEM((width, hidden), F32), pltpu.VMEM((hidden, width), F32)],
    )[0]


def write_columns(out, total_ref, p, depth):
    for b in range(total_ref.shape[1] // BLOCK):
        lanes = slice(b * BLOCK, (b + 1) * BLOCK)
        out[b * depth : (b + 1) * depth, :] = rows_at(total_ref, p, depth, lanes).astype(BF16)


def write_output_rows(out, base, rows):
    count = rows.shape[0]
    for b in range(rows.shape[1] // BLOCK):
        at = base + b * count
        out[at : at + count, :] = rows[:, b * BLOCK : (b + 1) * BLOCK].astype(BF16)


def conv_weight_kernel(counts, planes, *refs):
    normed, grads, active, rows, refs = take(refs, counts)
    out_ref, gate_ref, row_ref = refs
    depth = gate_ref.shape[0] // planes
    below = row_ref.shape[0] // planes
    base = (gate_ref.shape[1] // BLOCK) * depth
    gate_ref[...] = mm_tn(joined(normed), joined(grads))
    row_ref[...] = mm_tn(joined(active), joined(rows))

    def write(out, p):
        write_columns(out, gate_ref, p, depth)
        write_output_rows(out, base, rows_at(row_ref, p, below))

    put(out_ref, planes, write)


def conv_weight_call(normed, grads, active, rows, planes):
    width, gates, size = normed[0].shape[1], grads[0].shape[1], active[0].shape[1]
    lines = (gates // BLOCK) * (width // planes) + (width // BLOCK) * (size // planes)
    groups = (normed, grads, active, rows)
    tokens = sum(a.shape[0] for a in grads)
    return kernel_call(
        functools.partial(conv_weight_kernel, [len(g) for g in groups], planes),
        [shape((planes, lines, BLOCK), BF16)],
        [a for g in groups for a in g],
        flops=2 * width * (gates + size) * tokens,
        scratch=[pltpu.VMEM((width, gates), F32), pltpu.VMEM((size, width), F32)],
    )[0]


def mix_weight_kernel(counts, planes, per_side, *refs):
    side_ref, refs = refs[0], refs[1:]
    saved, grads, rows, place, refs = take(refs, counts)
    table_ref, place = place[0], place[1:]
    out_ref, total_ref, row_ref = refs
    size = row_ref.shape[0]
    depth = total_ref.shape[0] // planes
    base = (total_ref.shape[1] // BLOCK) * depth
    right = joined(grads)
    qkv = right.shape[1]
    total_ref[:, :qkv] = mm_tn(joined(saved, 0, total_ref.shape[0]), right)
    position = sum(ref[...] for ref in place)
    total_ref[:, qkv:] = mm_tn(table_ref[...], position.astype(BF16))
    if per_side:
        last = saved[0].shape[1]
        row_ref[...] = mm_tn(joined(saved, last - size, last), joined(rows))

    def write(out, p):
        write_columns(out, total_ref, p, depth)
        if per_side:
            below = row_ref.shape[0] // per_side
            place = p - side_ref[0] * per_side
            held = (place >= 0) & (place < per_side)
            share = held.astype(jnp.int32).astype(F32)
            head = rows_at(row_ref, jnp.where(held, place, 0), below) * share
            write_output_rows(out, base, head)

    put(out_ref, planes, write)


def mix_weight_call(saved, grads, rows, place, side, planes, per_side):
    width, qkv, size = rows[0].shape[1], grads[0].shape[1], grads[0].shape[1] // 3
    total = qkv + size
    lines = (total // BLOCK) * (width // planes)
    if per_side:
        lines += (width // BLOCK) * (size // per_side)
    groups = (saved, grads, rows, place)
    tokens = sum(a.shape[0] for a in grads)
    return kernel_call(
        functools.partial(mix_weight_kernel, [len(g) for g in groups], planes, per_side),
        [shape((planes, lines, BLOCK), BF16)],
        [a for g in groups for a in g],
        scalars=(side,),
        flops=2 * width * (total + size) * tokens,
        scratch=[pltpu.VMEM((width, total), F32), pltpu.VMEM((size, width), F32)],
    )[0]


def channel_kernel(planes, sides, head_size, *refs):
    at_ref, pieces, refs = refs[0], refs[1 : 1 + planes], refs[1 + planes :]
    norm_refs, (tap_ref, batch_ref, bias_ref, length_ref, wide_ref) = refs[:5], refs[5:]
    plane, member, side, core = at_ref[0], at_ref[1], at_ref[2], at_ref[3]
    team, rows = pieces[0].shape[0], pieces[0].shape[1] - CARRY
    size = tap_ref.shape[1]
    listed = [pieces[0][m, rows : rows + 1, :].astype(F32) for m in range(team)]
    one = jnp.concatenate([listed[4], listed[3]])
    two = jnp.concatenate([listed[1], listed[6]])
    table = [
        listed[0],
        listed[2],
        jnp.where(core == 0, one, two),
        jnp.where(core == 0, two, one),
        listed[5],
        listed[7],
    ]
    length_ref[...] = jnp.concatenate(table).astype(jnp.int32)[:, : length_ref.shape[1]]
    for d in range(planes):
        for m in range(team):
            at = ((plane ^ d) * team + (member ^ m)) * rows
            wide_ref[pl.ds(pl.multiple_of(at, rows), rows), :] = pieces[d][m, :rows, :].astype(F32)
    every = wide_ref[...].T
    taps = tap_ref.shape[0] - 1
    for j in range(5):
        first = every[taps + j : taps + j + 1]
        norm_refs[j][...] = jnp.concatenate([first, every[taps + 5 + j : taps + 6 + j]])
    own = [
        wide_ref[pl.ds(pl.multiple_of((p * team + member) * rows, rows), rows), :]
        for p in range(planes)
    ]
    own = jnp.concatenate(own).T
    tap_ref[...] = own[: taps + 1]
    batch_ref[...] = own[taps + 10 : taps + 12]
    heads = size // head_size
    own = [
        wide_ref[
            pl.ds(
                pl.multiple_of(
                    (side * heads + h) * team * rows + (member // sides) * head_size, head_size
                ),
                head_size,
            ),
            :,
        ]
        for h in range(heads)
    ]
    own = jnp.concatenate(own).T
    bias_ref[...] = own[taps + 12 : taps + 14]


def chunk_order(groups):
    return [chunk for group in groups for pair in zip(*group) for chunk in pair]


def add_kernel(count, *refs):
    own_ref, mate_ref, out_ref = refs[0], refs[1], refs[-1]
    total = own_ref[...] + mate_ref[count].astype(F32)
    for ref in refs[2:-1]:
        total = total + ref[...].astype(F32)
    out_ref[...] = total.astype(BF16)


def add_call(own, mate, index, *more):
    return kernel_call(
        functools.partial(add_kernel, index), [shape(own.shape, BF16)], [own, mate] + list(more)
    )[0]


def item_bounds(length_ref, b=0):
    ends = [length_ref[b, 0]]
    for j in range(1, length_ref.shape[1] - 1):
        ends.append(ends[-1] + length_ref[b, j])
    return ends


def item_index(ends, where_at):
    total = (where_at >= ends[0]).astype(jnp.int32)
    for end in ends[1:]:
        total = total + (where_at >= end).astype(jnp.int32)
    return total


def head_masks(slots, head_size):
    lane = lax.broadcasted_iota(jnp.int32, (slots, LANES), 1)
    return [
        (lane >= h * head_size) & (lane < (h + 1) * head_size) for h in range(LANES // head_size)
    ]


def saved_lanes(width, size, heads, slots):
    ends = [width]
    for lanes in [size] * 4 + [slots] * heads + [size]:
        ends.append(ends[-1] + lanes)
    return ends


def attention_kernel(k, first, head_size, per_side, *refs):
    length_ref, side_ref, refs = refs[0], refs[1], refs[2:]
    mine, mate, refs = refs[:k], refs[k : 2 * k], refs[2 * k :]
    bias_ref, place_ref, pack_ref = refs[:3]
    mix_ref, refs = (None, refs[3:]) if per_side else (refs[3], refs[4:])
    out_mine, out_mate, saved_ref = refs[:k], refs[k], refs[k + 1]
    slots, width = mine[0].shape
    size = place_ref.shape[1]
    ends = saved_lanes(width, size, size // head_size, slots)
    mix = mix_rows(pack_ref, mix_ref, side_ref, width, size, per_side)
    scale = head_size ** (-0.5)
    row_at = lax.broadcasted_iota(jnp.int32, (slots, slots), 0)
    column_at = lax.broadcasted_iota(jnp.int32, (slots, slots), 1)
    masks = head_masks(slots, head_size)
    for i in range(k):
        rows = jnp.concatenate([mine[i][...], mate[i][...]])
        qkv = square_product(rows, pack_ref, 0, 3 * size)
        query = qkv[:, :size]
        query_c = (query + bias_ref[0:1, :]).astype(BF16)
        query_p = (query + bias_ref[1:2, :]).astype(BF16)
        key = qkv[:, size : 2 * size].astype(BF16)
        value = qkv[:, 2 * size :].astype(BF16)
        at = pl.ds(2 * i * slots, 2 * slots)
        saved_ref[at, : ends[0]] = rows
        for n, part in enumerate((query_c, query_p, key, value)):
            saved_ref[at, ends[n] : ends[n + 1]] = part
        halves = []
        for j in range(2):
            b = 2 * i + j
            part = slice(j * slots, (j + 1) * slots)
            rows_of = pl.ds(b * slots, slots)
            edges = item_bounds(length_ref, first + b)
            same = item_index(edges, row_at) == item_index(edges, column_at)
            blocks = []
            for lo in range(0, size, LANES):
                lanes = slice(lo, lo + LANES)
                mixed = jnp.zeros((slots, LANES), F32)
                for h, mask in enumerate(masks):
                    qc = jnp.where(mask, query_c[part, lanes], 0)
                    qp = jnp.where(mask, query_p[part, lanes], 0)
                    wide = mm_nt(qp, place_ref[:, lanes])
                    moved = pltpu.roll(wide, slots + 1, 1, stride=1, stride_axis=0)
                    scores = (mm_nt(qc, key[part, lanes]) + moved[:, :slots]) * scale
                    scores = jnp.where(same, scores, MASKED_SCORE)
                    top = jnp.max(scores, axis=-1, keepdims=True)
                    weights = jnp.exp(scores - top)
                    probs = weights / jnp.sum(weights, axis=-1, keepdims=True)
                    probs = probs.astype(BF16)
                    n = 4 + (lo // LANES) * len(masks) + h
                    saved_ref[rows_of, ends[n] : ends[n + 1]] = probs
                    mixed = jnp.where(mask, mm(probs, value[part, lanes]), mixed)
                blocks.append(mixed)
            halves.append(jnp.concatenate(blocks, axis=1) if len(blocks) > 1 else blocks[0])
        mixed = jnp.concatenate(halves).astype(BF16)
        saved_ref[at, ends[-2] : ends[-1]] = mixed
        store_partial(out_mine, out_mate, i, slots, mm(mixed, mix))


def mix_rows(pack_ref, mix_ref, side_ref, width, size, per_side):
    if not per_side:
        return mix_ref[...]
    base = (4 * size // BLOCK) * (width // pack_ref.shape[0])
    return jnp.concatenate(
        [output_rows(pack_ref, side_ref[0] * per_side + h, width, base) for h in range(per_side)]
    )


def attention_call(group, lengths, first, side, packs, per_side, bias, place, head_size):
    mine, mate = group
    k, (slots, width) = len(mine), mine[0].shape
    size = place.shape[1]
    heads = size // head_size
    rows = 2 * k * slots
    outs = [shape((slots, width), F32)] * k + [
        shape((k, slots, width), BF16),
        shape((rows, saved_lanes(width, size, heads, slots)[-1]), BF16),
    ]
    result = kernel_call(
        functools.partial(attention_kernel, k, first, head_size, per_side),
        outs,
        list(mine) + list(mate) + [bias, place] + list(packs),
        scalars=(lengths, side),
        flops=2 * rows * width * size * 4 + 2 * k * heads * 10 * slots * slots * LANES,
    )
    return (result[:k], result[k]), result[k + 1]


def attention_back_kernel(k, head_size, per_side, *refs):
    side_ref, refs = refs[0], refs[1:]
    mine, mate, refs = refs[:k], refs[k : 2 * k], refs[2 * k :]
    place_ref, saved_ref, pack_ref = refs[:3]
    mix_ref, refs = (None, refs[3:]) if per_side else (refs[3], refs[4:])
    out_mine, out_mate, grad_ref, place_grad_ref, bias_ref = (
        refs[:k],
        refs[k],
        refs[k + 1],
        refs[k + 2],
        refs[k + 3],
    )
    slots, width = mine[0].shape
    size = place_ref.shape[1]
    mix = mix_rows(pack_ref, mix_ref, side_ref, width, size, per_side)
    ends = saved_lanes(width, size, size // head_size, slots)
    scale = head_size ** (-0.5)
    masks = head_masks(slots, head_size)
    flip = (
        lax.broadcasted_iota(jnp.int32, (slots, slots), 0)
        + lax.broadcasted_iota(jnp.int32, (slots, slots), 1)
        == slots - 1
    ).astype(F32).astype(BF16)
    bias_c = jnp.zeros((1, size), F32)
    bias_p = jnp.zeros((1, size), F32)
    for i in range(k):
        rows = jnp.concatenate([mine[i][...], mate[i][...]])
        grad_mixed_all = mm_nt(rows, mix).astype(BF16)
        at = pl.ds(2 * i * slots, 2 * slots)
        halves = []
        for j in range(2):
            b = 2 * i + j
            part = slice(j * slots, (j + 1) * slots)
            rows_at = pl.ds((2 * i + j) * slots, slots)
            grad_qc, grad_qp, grad_k, grad_v = [], [], [], []
            for lo in range(0, size, LANES):
                lanes = slice(lo, lo + LANES)
                grad_mixed = grad_mixed_all[part, lanes]
                query_c, query_p, key, value = [
                    saved_ref[rows_at, ends[n] + lo : ends[n] + lo + LANES] for n in range(4)
                ]
                place = place_ref[:, lanes]
                gqc = jnp.zeros((slots, LANES), F32)
                gqp, gk, gv = gqc, gqc, gqc
                place_grad = jnp.zeros(place.shape, F32)
                for h, mask in enumerate(masks):
                    n = 4 + (lo // LANES) * len(masks) + h
                    probs = saved_ref[rows_at, ends[n] : ends[n + 1]]
                    own = jnp.where(mask, grad_mixed, 0)
                    grad_probs = mm_nt(own, value)
                    gv = gv + mm_tn(probs, own)
                    probs = probs.astype(F32)
                    inner = jnp.sum(probs * grad_probs, axis=-1, keepdims=True)
                    grad = (probs * (grad_probs - inner)).astype(BF16) * scale
                    grad = grad.astype(BF16)
                    gqc = jnp.where(mask, mm(grad, key), gqc)
                    gk = gk + mm_tn(grad, jnp.where(mask, query_c, 0))
                    turned = mm(flip, grad)
                    wide = jnp.concatenate([turned, jnp.zeros_like(turned)], axis=1)
                    wide = pltpu.roll(wide, 0, 1, stride=1, stride_axis=0).astype(BF16)
                    wide = mm(flip, wide).astype(BF16)
                    gqp = jnp.where(mask, mm(wide, place), gqp)
                    place_grad = place_grad + mm_tn(wide, jnp.where(mask, query_p, 0))
                if i == 0 and j == 0:
                    place_grad_ref[:, lanes] = place_grad
                else:
                    place_grad_ref[:, lanes] = place_grad_ref[:, lanes] + place_grad
                grad_qc.append(gqc)
                grad_qp.append(gqp)
                grad_k.append(gk)
                grad_v.append(gv)

            def side_by_side(blocks):
                return jnp.concatenate(blocks, axis=1) if len(blocks) > 1 else blocks[0]

            gqc, gqp = side_by_side(grad_qc), side_by_side(grad_qp)
            bias_c = bias_c + jnp.sum(gqc, axis=0, keepdims=True)
            bias_p = bias_p + jnp.sum(gqp, axis=0, keepdims=True)
            halves.append(
                jnp.concatenate(
                    [gqc + gqp, side_by_side(grad_k), side_by_side(grad_v)], axis=1
                ).astype(BF16)
            )
        grad = jnp.concatenate(halves)
        grad_ref[at, :] = grad
        store_partial(out_mine, out_mate, i, slots, square_product_back(grad, pack_ref, width, 0, 3 * size))
    bias_ref[...] = jnp.concatenate([bias_c, bias_p])


def attention_back_call(group, side, packs, per_side, place, saved, head_size):
    mine, mate = group
    k, (slots, width) = len(mine), mine[0].shape
    size = place.shape[1]
    rows = 2 * k * slots
    outs = [shape((slots, width), F32)] * k + [
        shape((k, slots, width), BF16),
        shape((rows, 3 * size), BF16),
        shape(place.shape, F32),
        shape((2, size), F32),
    ]
    result = kernel_call(
        functools.partial(attention_back_kernel, k, head_size, per_side),
        outs,
        list(mine) + list(mate) + [place, saved] + list(packs),
        scalars=(side,),
        flops=2 * rows * width * size * 4 + 2 * k * 24 * slots * slots * size,
    )
    return (result[:k], result[k]), result[k + 1 :]


def place_kernel(table_ref, column_ref, out_ref):
    size = out_ref.shape[1]
    rows = square_product(table_ref[...], column_ref, 3 * size, 4 * size)
    out_ref[...] = rows.astype(BF16)


def item_reach(ends, row_at, slots):
    start = jnp.zeros_like(row_at)
    end = jnp.full_like(row_at, slots)
    for at in ends:
        start = jnp.where(row_at >= at, at, start)
    for at in reversed(ends):
        end = jnp.where(row_at < at, at, end)
    valid = (row_at < ends[-1]).astype(F32)
    return row_at - start, end - 1 - row_at, valid


def gate_kernel(k, first, tap_count, *refs):
    length_ref, refs = refs[0], refs[1:]
    mine, mate, refs = refs[:k], refs[k : 2 * k], refs[2 * k :]
    pack_ref, tap_ref, gate_ref, normed_ref, stat_ref, pad_ref = refs
    slots, _ = mine[0].shape
    size = tap_ref.shape[1]
    reach = tap_count // 2
    row_at = lax.broadcasted_iota(jnp.int32, (slots, size), 0)
    pad_ref[...] = jnp.zeros_like(pad_ref)
    count = jnp.zeros((1, size), F32)
    total = jnp.zeros((1, size), F32)
    for i in range(k):
        rows = jnp.concatenate([mine[i][...], mate[i][...]])
        gates = square_product(rows, pack_ref, 0, 2 * size)
        gate_ref[pl.ds(2 * i * slots, 2 * slots), : 2 * size] = gates
        normed_ref[pl.ds(2 * i * slots, 2 * slots), :] = rows
        glu = gates[:, :size] * sigmoid(gates[:, size:])
        for j in range(2):
            b = 2 * i + j
            before, behind, valid = item_reach(item_bounds(length_ref, first + b), row_at, slots)
            pad_ref[PAD : PAD + slots, :] = glu[j * slots : (j + 1) * slots] * valid
            conv = jnp.zeros((slots, size), F32)
            for tap in range(tap_count):
                o = tap - reach
                near = pad_ref[PAD + o : PAD + o + slots, :]
                if o < 0:
                    near = jnp.where(before >= -o, near, 0.0)
                elif o > 0:
                    near = jnp.where(behind >= o, near, 0.0)
                conv = conv + near * tap_ref[tap : tap + 1, :]
            gate_ref[pl.ds(b * slots, slots), 2 * size :] = conv
            count = count + jnp.sum(valid, axis=0, keepdims=True)
            total = total + jnp.sum(conv * valid, axis=0, keepdims=True)
    mean = total / count
    spread = jnp.zeros((1, size), F32)
    for b in range(2 * k):
        valid = (row_at < item_bounds(length_ref, first + b)[-1]).astype(F32)
        gap = (gate_ref[pl.ds(b * slots, slots), 2 * size :] - mean) * valid
        spread = spread + jnp.sum(gap * gap, axis=0, keepdims=True)
    stat_ref[...] = jnp.concatenate([count, mean, spread, jnp.zeros((5, size), F32)])


def gate_call(group, lengths, first, pack, taps, tap_count):
    mine, mate = group
    k, (slots, width) = len(mine), mine[0].shape
    size = taps.shape[1]
    rows = 2 * k * slots
    return kernel_call(
        functools.partial(gate_kernel, k, first, tap_count),
        [shape((rows, 3 * size), F32), shape((rows, width), BF16), shape((8, size), F32)],
        list(mine) + list(mate) + [pack, taps],
        scalars=(lengths,),
        flops=4 * rows * width * size + 40 * tap_count * rows * size,
        scratch=[pltpu.VMEM((slots + 2 * PAD, size), F32)],
    )


def merge_kernel(*refs):
    out_ref = refs[-1]
    count, mean, spread = refs[0][0:1, :], refs[0][1:2, :], refs[0][2:3, :]
    for ref in refs[1:-1]:
        more = ref[0:1, :]
        total = count + more
        gap = ref[1:2, :] - mean
        spread = spread + ref[2:3, :] + gap * gap * (count * more / total)
        mean = (count * mean + more * ref[1:2, :]) / total
        count = total
    out_ref[...] = jnp.concatenate([count, mean, spread, jnp.zeros((5, mean.shape[1]), F32)])


def merge(parts):
    return kernel_call(merge_kernel, [shape(parts[0].shape, F32)], parts)[0]


def sum_kernel(*refs):
    refs[-1][...] = sum(ref[...] for ref in refs[:-1])


def sum_call(parts):
    return kernel_call(sum_kernel, [shape(parts[0].shape, F32)], parts)[0]


def batch_unit(conv, stat_ref):
    inverse = lax.rsqrt(stat_ref[2:3, :] / stat_ref[0:1, :] + EPSILON)
    return (conv - stat_ref[1:2, :]) * inverse, inverse


def batch_kernel(k, *refs):
    gate_ref, stat_ref, batch_ref, pack_ref, refs = refs[0], refs[1], refs[2], refs[3], refs[4:]
    out_mine, out_mate = refs[:k], refs[k]
    slots, width = out_mine[0].shape
    size = batch_ref.shape[1]
    weight = conv_rows(pack_ref, width, size)
    for i in range(k):
        at = pl.ds(2 * i * slots, 2 * slots)
        unit, _ = batch_unit(gate_ref[at, 2 * size :], stat_ref)
        value = unit * batch_ref[0:1, :] + batch_ref[1:2, :]
        active = (value * sigmoid(value)).astype(BF16)
        store_partial(out_mine, out_mate, i, slots, mm(active, weight))


def conv_rows(pack_ref, width, size):
    planes = pack_ref.shape[0]
    base = (2 * size // BLOCK) * (width // planes)
    rows = size // planes
    parts = []
    for p in range(planes):
        blocks = [
            pack_ref[p, base + b * rows : base + (b + 1) * rows, :] for b in range(width // BLOCK)
        ]
        parts.append(jnp.concatenate(blocks, axis=1))
    return jnp.concatenate(parts)


def batch_call(k, gates, stats, batch_rows, pack, slots, width):
    rows, size = gates.shape[0], batch_rows.shape[1]
    outs = [shape((slots, width), F32)] * k + [shape((k, slots, width), BF16)]
    result = kernel_call(
        functools.partial(batch_kernel, k),
        outs,
        [gates, stats, batch_rows, pack],
        flops=2 * rows * width * size,
    )
    return result[:k], result[k]


def batch_back_kernel(k, first, *refs):
    length_ref, refs = refs[0], refs[1:]
    mine, mate, refs = refs[:k], refs[k : 2 * k], refs[2 * k :]
    gate_ref, stat_ref, batch_ref, pack_ref, grad_ref, active_ref, sum_ref = refs
    slots, width = mine[0].shape
    size = batch_ref.shape[1]
    weight = conv_rows(pack_ref, width, size)
    row_at = lax.broadcasted_iota(jnp.int32, (slots, size), 0)
    sums = [jnp.zeros((1, size), F32)] * 4
    for i in range(k):
        rows = jnp.concatenate([mine[i][...], mate[i][...]])
        grad_active = mm_nt(rows, weight)
        for j in range(2):
            b = 2 * i + j
            at = pl.ds(b * slots, slots)
            unit, _ = batch_unit(gate_ref[at, 2 * size :], stat_ref)
            value = unit * batch_ref[0:1, :] + batch_ref[1:2, :]
            sig = sigmoid(value)
            active_ref[at, :] = (value * sig).astype(BF16)
            grad = grad_active[j * slots : (j + 1) * slots] * (sig * (1.0 + value * (1.0 - sig)))
            valid = (row_at < item_bounds(length_ref, first + b)[-1]).astype(F32)
            grad_unit = grad * batch_ref[0:1, :]
            grad_ref[at, :] = grad_unit
            terms = (grad * unit, grad, grad_unit * valid, grad_unit * unit * valid)
            sums = [s + jnp.sum(t, axis=0, keepdims=True) for s, t in zip(sums, terms)]
    sum_ref[...] = jnp.concatenate(sums + [jnp.zeros((4, size), F32)])


def batch_back_call(group, lengths, first, gates, stats, batch_rows, pack):
    mine, mate = group
    k, (slots, width) = len(mine), mine[0].shape
    rows, size = gates.shape[0], batch_rows.shape[1]
    return kernel_call(
        functools.partial(batch_back_kernel, k, first),
        [shape((rows, size), F32), shape((rows, size), BF16), shape((8, size), F32)],
        list(mine) + list(mate) + [gates, stats, batch_rows, pack],
        scalars=(lengths,),
        flops=2 * rows * width * size,
    )


def gate_back_kernel(k, first, tap_count, *refs):
    length_ref, refs = refs[0], refs[1:]
    grad_in_ref, gate_ref, stat_ref, sum_ref, pack_ref, tap_ref, refs = (
        refs[0],
        refs[1],
        refs[2],
        refs[3],
        refs[4],
        refs[5],
        refs[6:],
    )
    out_mine, out_mate, grad_ref, tap_grad_ref, glu_ref, conv_grad_ref = (
        refs[:k],
        refs[k],
        refs[k + 1],
        refs[k + 2],
        refs[k + 3],
        refs[k + 4],
    )
    slots, width = out_mine[0].shape
    size = tap_ref.shape[1]
    reach = tap_count // 2
    row_at = lax.broadcasted_iota(jnp.int32, (slots, size), 0)
    glu_ref[...] = jnp.zeros_like(glu_ref)
    conv_grad_ref[...] = jnp.zeros_like(conv_grad_ref)
    tap_grad_ref[...] = jnp.zeros_like(tap_grad_ref)
    frame_count = stat_ref[0:1, :]
    mean_grad = sum_ref[2:3, :] / frame_count
    mean_cross = sum_ref[3:4, :] / frame_count
    for i in range(k):
        halves = []
        for j in range(2):
            b = 2 * i + j
            at = pl.ds(b * slots, slots)
            before, behind, valid = item_reach(item_bounds(length_ref, first + b), row_at, slots)
            gate_a, gate_sig = gate_ref[at, :size], sigmoid(gate_ref[at, size : 2 * size])
            glu_ref[PAD : PAD + slots, :] = gate_a * gate_sig * valid
            unit, inverse = batch_unit(gate_ref[at, 2 * size :], stat_ref)
            conv_grad = valid * inverse * (grad_in_ref[at, :] - mean_grad - unit * mean_cross)
            conv_grad_ref[PAD : PAD + slots, :] = conv_grad
            grad_glu = jnp.zeros((slots, size), F32)
            for tap in range(tap_count):
                o = tap - reach
                near = glu_ref[PAD + o : PAD + o + slots, :]
                back = conv_grad_ref[PAD - o : PAD - o + slots, :]
                if o < 0:
                    near = jnp.where(before >= -o, near, 0.0)
                    back = jnp.where(behind >= -o, back, 0.0)
                elif o > 0:
                    near = jnp.where(behind >= o, near, 0.0)
                    back = jnp.where(before >= o, back, 0.0)
                grad_glu = grad_glu + back * tap_ref[tap : tap + 1, :]
                tap_grad_ref[tap : tap + 1, :] += jnp.sum(near * conv_grad, axis=0, keepdims=True)
            grad_glu = grad_glu * valid
            halves.append(
                jnp.concatenate(
                    [grad_glu * gate_sig, grad_glu * gate_a * gate_sig * (1.0 - gate_sig)], axis=1
                ).astype(BF16)
            )
        grad = jnp.concatenate(halves)
        grad_ref[pl.ds(2 * i * slots, 2 * slots), :] = grad
        store_partial(out_mine, out_mate, i, slots, square_product_back(grad, pack_ref, width, 0, 2 * size))


def gate_back_call(k, lengths, first, grads, gates, stats, sums, pack, taps, tap_count, slots, width):
    rows, size = grads.shape
    outs = [shape((slots, width), F32)] * k + [
        shape((k, slots, width), BF16),
        shape((rows, 2 * size), BF16),
        shape(taps.shape, F32),
    ]
    padded = pltpu.VMEM((slots + 2 * PAD, size), F32)
    result = kernel_call(
        functools.partial(gate_back_kernel, k, first, tap_count),
        outs,
        [grads, gates, stats, sums, pack, taps],
        scalars=(lengths,),
        flops=4 * rows * width * size + 80 * tap_count * rows * size,
        scratch=[padded, padded],
    )
    return (result[:k], result[k]), result[k + 1 :]


def join_kernel(count, coefficient, *refs):
    stream_ref, own_ref, mate_ref, refs = refs[0], refs[1], refs[2], refs[3:]
    far, norm_ref, stream_out, normed_ref = refs[:count], refs[count], refs[count + 1], refs[count + 2]
    branch = own_ref[...] + mate_ref[0].astype(F32)
    for ref in far:
        branch = branch + ref[...].astype(F32)
    stream = stream_ref[...].astype(F32) + coefficient * branch
    stream_out[...] = stream
    unit, _ = normalize(stream)
    normed_ref[...] = (unit * norm_ref[0:1, :] + norm_ref[1:2, :]).astype(BF16)


def join_call(stream, parts, coefficient, norm):
    own, mate, far = parts
    return kernel_call(
        functools.partial(join_kernel, len(far), coefficient),
        [shape(own.shape, F32), shape(own.shape, BF16)],
        [stay(stream), own, mate] + list(far) + [norm],
    )


def turn_kernel(count, coefficient, *refs):
    length_ref, refs = refs[0], refs[1:]
    stream_ref, own_ref, mate_ref, refs = refs[0], refs[1], refs[2], refs[3:]
    far, norm_ref, cotangent_ref, refs = refs[:count], refs[count], refs[count + 1], refs[count + 2 :]
    output_ref, grad_out, low_out, norm_grad = refs
    branch = own_ref[...] + mate_ref[0].astype(F32)
    for ref in far:
        branch = branch + ref[...].astype(F32)
    stream = stream_ref[...] + coefficient * branch
    row_at = lax.broadcasted_iota(jnp.int32, (stream.shape[0], 1), 0)
    valid = (row_at < item_bounds(length_ref)[-1]).astype(F32)
    unit, scale = normalize(stream)
    output_ref[...] = ((unit * norm_ref[0:1, :] + norm_ref[1:2, :]) * valid).astype(BF16)
    norm_back(
        unit,
        scale,
        norm_ref,
        cotangent_ref[...].astype(F32) * valid,
        0.0,
        0.5,
        grad_out,
        low_out,
        norm_grad,
    )


def norm_back(unit, scale, norm_ref, grad, base, coefficient, grad_out, low_out, norm_grad):
    norm_grad[...] = jnp.concatenate(
        [jnp.sum(grad * unit, axis=0, keepdims=True), jnp.sum(grad, axis=0, keepdims=True)]
    )
    grad = grad * norm_ref[0:1, :]
    inner = jnp.mean(grad, axis=-1, keepdims=True)
    cross = jnp.mean(grad * unit, axis=-1, keepdims=True)
    grad = base + scale * (grad - inner - unit * cross)
    if grad_out is not None:
        grad_out[...] = grad
    low_out[...] = (coefficient * grad).astype(BF16)


def turn_call(stream, parts, coefficient, norm, cotangent, lengths):
    own, mate, far = parts
    return kernel_call(
        functools.partial(turn_kernel, len(far), coefficient),
        [
            shape(own.shape, BF16),
            shape(own.shape, F32),
            shape(own.shape, BF16),
            shape((2, own.shape[1]), F32),
        ],
        [stay(stream), own, mate] + list(far) + [norm, stay(cotangent)],
        scalars=(lengths,),
    )


def join_back_kernel(count, coefficient, keep, *refs):
    stream_ref, grad_ref, own_ref, mate_ref, refs = refs[0], refs[1], refs[2], refs[3], refs[4:]
    far, norm_ref, refs = refs[:count], refs[count], refs[count + 1 :]
    grad_out, (low_out, norm_grad) = (refs[0] if keep else None), refs[-2:]
    grad = own_ref[...] + mate_ref[0].astype(F32)
    for ref in far:
        grad = grad + ref[...].astype(F32)
    unit, scale = normalize(stream_ref[...].astype(F32))
    norm_back(
        unit, scale, norm_ref, grad, grad_ref[...], coefficient, grad_out, low_out, norm_grad
    )


def join_back_call(stream, grad, parts, coefficient, norm, keep=True):
    own, mate, far = parts
    outs = [shape(own.shape, F32)] if keep else []
    return kernel_call(
        functools.partial(join_back_kernel, len(far), coefficient, keep),
        outs + [shape(own.shape, BF16), shape((2, own.shape[1]), F32)],
        [stay(stream), stay(grad), own, mate] + list(far) + [norm],
    )


def offset_table(slot_count, model_width):
    offsets = jnp.arange(2 * slot_count, dtype=F32) - (slot_count - 1)
    freqs = jnp.exp(-jnp.log(10000.0) * jnp.arange(0, model_width, 2, dtype=F32) / model_width)
    angles = offsets[:, None] * freqs[None, :]
    return jnp.concatenate([jnp.sin(angles), jnp.cos(angles)], axis=1)


def nesterov(weight, moment, average, grad_rows, rate, rate_scale):
    moment_new = MOMENTUM_DECAY * moment + grad_rows
    weight_new = weight - rate * rate_scale * (grad_rows + MOMENTUM_DECAY * moment_new)
    average_new = AVERAGE_DECAY * average + (1.0 - AVERAGE_DECAY) * weight_new
    return (moment_new, weight_new, average_new)


def head_lanes(member, i, sides, planes, size):
    side, rest = member % sides, member // sides
    plane = side * (planes // sides) + i
    return (plane * 4 + rest) * size


def split_down_kernel(weight_ref, first_ref, second_ref):
    hidden = first_ref.shape[1]
    rows = weight_ref.shape[1]
    for layer, out in enumerate((first_ref, second_ref)):
        for b in range(weight_ref.shape[2] // hidden):
            part = weight_ref[layer, :, b * hidden : (b + 1) * hidden]
            out[b * rows : (b + 1) * rows, :] = part.astype(BF16)


def split_up_kernel(weight_ref, first_ref, second_ref):
    team, _, hidden = first_ref.shape
    planes = weight_ref.shape[2] // (team * LANES)
    for layer, out in enumerate((first_ref, second_ref)):
        for t in range(team):
            for p in range(planes):
                at = (p * team + t) * LANES
                part = weight_ref[layer, :, at : at + LANES]
                out[t, :, p * LANES : (p + 1) * LANES] = part.astype(BF16)


def split_square_kernel(planes, sides, head_size, weight_ref, column_ref, mix_ref, conv_ref):
    team = column_ref.shape[0]
    width = weight_ref.shape[2]
    size = width // team
    for t in range(team):
        for i, matrix in enumerate((0, 1, 2, 4, 5, 6)):
            if i < 4:
                starts = [
                    head_lanes(t, h, sides, planes, head_size) for h in range(size // head_size)
                ]
                count = head_size
            else:
                count = size // planes
                starts = [(p * team + t) * count for p in range(planes)]
            parts = [weight_ref[matrix, :, at : at + count] for at in starts]
            column_ref[t, :, i * size : (i + 1) * size] = jnp.concatenate(parts, axis=1).astype(BF16)
    mix_ref[...] = weight_ref[3].astype(BF16)
    conv_ref[...] = weight_ref[7].astype(BF16)


def square_pack_kernel(side_ref, column_ref, own_ref, other_ref, conv_ref, mix_out, conv_out):
    team, rows, lanes = column_ref.shape
    depth = team * rows
    for b in range(lanes // BLOCK):
        out, at = (mix_out, b * depth) if b < 2 else (conv_out, (b - 2) * depth)
        for t in range(team):
            first = at + t * rows
            out[first : first + rows, :] = column_ref[t, :, b * BLOCK : (b + 1) * BLOCK]
    low = side_ref[0] == 0
    for b in range(own_ref.shape[1] // BLOCK):
        lane = slice(b * BLOCK, (b + 1) * BLOCK)
        own, other = own_ref[:, lane].astype(F32), other_ref[:, lane].astype(F32)
        at = 2 * depth + b * 2 * rows
        mix_out[at : at + rows, :] = jnp.where(low, own, other).astype(BF16)
        mix_out[at + rows : at + 2 * rows, :] = jnp.where(low, other, own).astype(BF16)
        at = depth + b * rows
        conv_out[at : at + rows, :] = conv_ref[:, lane]
    at = depth + (own_ref.shape[1] // BLOCK) * rows
    conv_out[at:, :] = jnp.zeros((conv_out.shape[0] - at, BLOCK), BF16)


def feed_pack_kernel(up_ref, down_ref, out_ref):
    team, rows, _ = up_ref.shape
    for t in range(team):
        out_ref[t * rows : (t + 1) * rows, :] = up_ref[t]
    out_ref[team * rows :, :] = down_ref[...]


def column_grad_kernel(mix_ref, conv_ref, out_ref):
    team, rows, lanes = out_ref.shape
    depth = team * rows
    for b in range(lanes // BLOCK):
        ref, at = (mix_ref, b) if b < 2 else (conv_ref, b - 2)
        for t in range(team):
            first = at * depth + t * rows
            out_ref[t, :, b * BLOCK : (b + 1) * BLOCK] = ref[first : first + rows, :]


def update(scale_ref, rate, index, grad, refs):
    weight_ref, moment_ref, average_ref, grad_out, moment_out, weight_out, average_out = refs
    moment = MOMENTUM_DECAY * moment_ref[index] + grad
    weight = weight_ref[index] - rate * scale_ref[0:1, 0:1] * (grad + MOMENTUM_DECAY * moment)
    grad_out[index] = grad
    moment_out[index] = moment
    weight_out[index] = weight
    average_out[index] = AVERAGE_DECAY * average_ref[index] + (1.0 - AVERAGE_DECAY) * weight


def update_up_kernel(scale_ref, first_ref, second_ref, *refs):
    team, _, hidden = first_ref.shape
    for layer, ref in enumerate((first_ref, second_ref)):
        parts = [
            ref[t, :, p * LANES : (p + 1) * LANES] for p in range(hidden // LANES) for t in range(team)
        ]
        update(scale_ref, RATE_UP, layer, jnp.concatenate(parts, axis=1).astype(F32), refs)


def update_down_kernel(scale_ref, first_ref, second_ref, *refs):
    rows, width = refs[0].shape[1:]
    hidden = first_ref.shape[1]
    for layer, ref in enumerate((first_ref, second_ref)):
        base = ref.shape[0] - rows * (width // hidden)
        parts = [
            ref[base + b * rows : base + (b + 1) * rows, :] for b in range(width // hidden)
        ]
        update(scale_ref, RATE_DOWN, layer, jnp.concatenate(parts, axis=1).astype(F32), refs)


def update_square_kernel(planes, sides, head_size, side_ref, *refs):
    scale_ref, column_ref, mix_ref, other_ref, conv_ref, refs = (
        refs[0],
        refs[1],
        refs[2],
        refs[3],
        refs[4],
        refs[5:],
    )
    team, rows, _ = column_ref.shape
    width = refs[0].shape[2]
    size = width // team
    per_side = planes // sides
    for i, matrix in enumerate((0, 1, 2, 4, 5, 6)):
        parts = []
        if i < 4:
            for head in range(width // head_size):
                plane, rest = head // 4, head % 4
                t = rest * sides + plane // per_side
                at = i * size + (plane % per_side) * head_size
                parts.append(column_ref[t, :, at : at + head_size])
        else:
            count = size // planes
            for p in range(planes):
                for t in range(team):
                    at = i * size + p * count
                    parts.append(column_ref[t, :, at : at + count])
        update(scale_ref, RATE_SQUARE, matrix, jnp.concatenate(parts, axis=1).astype(F32), refs)
    blocks = width // BLOCK
    head_rows = sides * rows
    base = mix_ref.shape[0] - blocks * head_rows
    parts = []
    for b in range(blocks):
        at = slice(base + b * head_rows, base + (b + 1) * head_rows)
        other_at = slice(b * head_rows, (b + 1) * head_rows)
        parts.append(mix_ref[at, :].astype(F32) + other_ref[other_at, :].astype(F32))
    whole = jnp.concatenate(parts, axis=1)
    update(scale_ref, RATE_SQUARE, 3, jnp.where(side_ref[0] == 0, whole[:rows], whole[rows:]), refs)
    base = conv_ref.shape[0] - blocks * rows
    parts = [conv_ref[base + b * rows : base + (b + 1) * rows, :] for b in range(blocks)]
    update(scale_ref, RATE_SQUARE, 7, jnp.concatenate(parts, axis=1).astype(F32), refs)


def update_call(body, scale, terms, weight, moment, average, scalars=()):
    return kernel_call(
        body,
        [shape(weight.shape, F32)] * 4,
        [scale]
        + list(terms)
        + [stay(x) for x in (weight, moment, average)],
        scalars=scalars,
    )


def feature_grad_kernel(planes, sides, *refs):
    member_ref, refs = refs[0], refs[1:]
    norms, biases, out_ref = refs[:5], refs[5:-1], refs[-1]
    team, _, size = out_ref.shape
    count = size // planes
    per_side = planes // sides
    head_size = sides * count
    bias = sum(ref[...] for ref in biases)
    rest, side = member_ref[0] // sides, member_ref[0] % sides
    rows = jnp.concatenate([n[0:1, :] for n in norms] + [n[1:2, :] for n in norms])
    for t in range(team):
        parts, own = [], []
        for p in range(planes):
            at = (p * team + t) * count
            parts.append(rows[:, at : at + count])
            at = (p % per_side) * head_size + (t % sides) * count
            held = (rest == t // sides) & (side == p // per_side)
            own.append(bias[:, at : at + count] * held.astype(jnp.int32).astype(F32))
        out_ref[t] = jnp.concatenate(
            [jnp.concatenate(parts, axis=1), jnp.concatenate(own, axis=1)]
        )


def channel_grad_kernel(taps, term_ref, sum_ref, *refs):
    tap_refs, out_ref = refs[:-1], refs[-1]
    features = jnp.sum(term_ref[...], axis=0)
    out_ref[...] = jnp.concatenate(
        [
            sum(ref[:taps] for ref in tap_refs),
            features[:10],
            sum_ref[0:2],
            features[10:12],
        ]
    )


def make_step(planes, sides):
    wide_team = sides == 2
    team_axes = ("x", "c", "y") if wide_team else ("x", "c")
    team = 8 if wide_team else 4
    outer_bits = [("z", 1 << i) for i in range((planes - 1).bit_length())]
    if not wide_team:
        outer_bits += [("y", 1 << i) for i in range((sides - 1).bit_length())]
    head_aligned = wide_team and planes * 4 == HEADS

    def turn(values, first):
        pairs = []
        for x in range(2):
            for c in range(2):
                for y in range(2):
                    along_x = (c == 0) == first
                    to = (1 - x, c, y) if along_x else (x, c, 1 - y)
                    pairs.append((4 * x + 2 * c + y, 4 * to[0] + 2 * to[1] + to[2]))
        return lax.ppermute(values, team_axes, pairs)

    def gather(values):
        return spread(values, None)[0]

    def spread(values, run):
        groups, results = [([values], [swap(values, "c")])], []

        def work(*travelling):
            if run is not None:
                result = run(len(results), groups[-1])
                travelling, result = lax.optimization_barrier((travelling, result))
                results.append(result)
            return travelling

        if not wide_team:
            (far,) = work(swap(values, "x"))
        else:
            first, second = work(turn(values, True), turn(values, False))
            far = turn(first, False)
            groups.append(([first, second], [swap(first, "c"), swap(second, "c")]))
            (far,) = work(far)
        groups.append(([far], [swap(far, "c")]))
        if run is not None:
            results.append(run(len(results), groups[-1]))
        return groups, results

    def scatter(parts, fill=(), near=None):
        (far,), far_mate = parts[-1]
        out_far = add_call(far, swap(far_mate, "c"), 0)
        if near is not None:
            argument, run = near
            out_far, argument = lax.optimization_barrier((out_far, argument))
            parts = run(argument)
        (own,), own_mate = parts[0]
        got_own = swap(own_mate, "c")
        if not wide_team:
            across, fill = lax.optimization_barrier((swap(out_far, "x"), fill))
            return (own, got_own, [across]), fill
        (first, second), side_mate = parts[1]
        got_side = swap(side_mate, "c")
        relay = turn(out_far, False)
        from_second = turn(add_call(second, got_side, 1), False)
        relay, fill = lax.optimization_barrier((relay, fill))
        from_first = turn(add_call(first, got_side, 0, relay), True)
        return (own, got_own, [from_first, from_second]), fill

    def side_rows(rows):
        return rows if wide_team else lax.all_gather(rows, "y", axis=0, tiled=True)

    def side_scatter(rows):
        if wide_team:
            return rows
        return lax.psum_scatter(rows, "y", scatter_dimension=0, tiled=True)

    def split_hidden(rows):
        r, f = rows.shape
        return rows.reshape(r, planes, team, f // (planes * team)).transpose(2, 0, 1, 3).reshape(
            team, r, f // team
        )

    def join_hidden(blocks):
        _, r, f = blocks.shape
        return blocks.reshape(team, r, planes, f // planes).transpose(1, 2, 0, 3).reshape(
            r, team * f
        )

    def split_heads(rows):
        r, d = rows.shape
        if not head_aligned:
            return rows.reshape(r, team, d // team).transpose(1, 0, 2)
        size = d // HEADS
        rows = rows.reshape(r, sides, planes // sides, 2, 2, size)
        return rows.transpose(3, 4, 1, 0, 2, 5).reshape(team, r, d // team)

    def join_heads(blocks):
        _, r, f = blocks.shape
        if not head_aligned:
            return blocks.transpose(1, 0, 2).reshape(r, team * f)
        size = team * f // HEADS
        blocks = blocks.reshape(2, 2, sides, r, planes // sides, size)
        return blocks.transpose(3, 2, 4, 0, 1, 5).reshape(r, team * f)

    def team_swap(blocks):
        return lax.all_to_all(blocks, team_axes, split_axis=0, concat_axis=0, tiled=True)

    def plane_pieces(rows):
        return [rows] + [swap(rows, "z", d) for d in range(1, planes)]

    def plane_gather(rows):
        return lax.all_gather(rows, "z", axis=0, tiled=False)

    def plane_reduce(rows):
        return lax.psum_scatter(rows, "z", scatter_dimension=0, tiled=False)

    def to_blocks(rows, size):
        return jnp.concatenate([rows[:, i : i + size] for i in range(0, rows.shape[1], size)])

    def from_blocks(rows, count):
        return jnp.concatenate(jnp.split(rows, count), axis=1)

    def outer_merge(values, combine):
        if wide_team:
            return combine([values] + [swap(values, "z", d) for d in range(1, planes)])
        for axis, bit in outer_bits:
            values = combine([values, swap(values, axis, bit)])
        return values

    def step(
        frames,
        lengths,
        out_grad,
        up_weight,
        down_weight,
        square_weight,
        chan_weight,
        up_moment,
        down_moment,
        square_moment,
        chan_moment,
        up_average,
        down_average,
        square_average,
        chan_average,
    ):
        slots, width = frames.shape
        head_size = width // HEADS
        item_count = lengths.shape[1] - 1
        chan_rows = chan_weight.shape[0]
        tap_count = chan_rows - 14
        hidden = up_weight.shape[2]
        team_hidden = hidden // team
        team_width = width // team
        x_at, c_at, y_at = lax.axis_index("x"), lax.axis_index("c"), lax.axis_index("y")
        team_at = (x_at * 2 + c_at) * 2 + y_at if wide_team else x_at * 2 + c_at
        side = y_at.reshape(1).astype(jnp.int32)
        plane = lax.axis_index("z").reshape(1).astype(jnp.int32)

        chan_low = chan_weight.astype(BF16)
        if head_aligned:
            blocks = [shape((hidden // planes // team * (width // team_hidden), team_hidden), BF16)] * 2
            down_one, down_two = kernel_call(split_down_kernel, blocks, [stay(down_weight)])
            rows_in = up_weight.shape[1]
            blocks = [shape((team, rows_in, team_hidden), BF16)] * 2
            up_one, up_two = kernel_call(split_up_kernel, blocks, [stay(up_weight)])
            columns, mix, conv_out = kernel_call(
                functools.partial(split_square_kernel, planes, sides, head_size),
                [shape((team, rows_in, 6 * team_width), BF16)] + [shape((rows_in, width), BF16)] * 2,
                [stay(square_weight)],
            )
        else:
            up_low = up_weight.astype(BF16)
            down_low = down_weight.astype(BF16)
            square_low = square_weight.astype(BF16)
            down_one, down_two = [to_blocks(side_rows(down_low[i]), team_hidden) for i in (0, 1)]
            up_one, up_two = [split_hidden(side_rows(up_low[i])) for i in (0, 1)]
            columns = jnp.concatenate(
                [split_heads(side_rows(square_low[i])) for i in (0, 1, 2, 4)]
                + [split_hidden(side_rows(square_low[i])) for i in (5, 6)],
                axis=2,
            )
            mix, conv_out = square_low[3], side_rows(square_low[7])
        down_one = plane_gather(down_one)
        up_one = team_swap(up_one)
        up_one, frames, chan_low, lengths, columns, up_two, mix = lax.optimization_barrier(
            (up_one, frames, chan_low, lengths, columns, up_two, mix)
        )
        packs_one = (plane_gather(up_one.reshape(-1, team_hidden)), down_one)
        groups = gather(frames)

        if wide_team:
            lanes = jnp.pad(chan_low, ((0, LANES - chan_rows), (0, 0))).T
            carried = jnp.pad(
                lengths.astype(BF16), ((0, CARRY - 1), (0, LANES - lengths.shape[1]))
            )
            lanes = jnp.concatenate([lanes, carried])[None]
            for axis in ("y", "c", "x"):
                lanes = jnp.concatenate([lanes, swap(lanes, axis)])
            where_at = jnp.stack([plane[0], team_at, y_at, c_at]).astype(jnp.int32)
            norms = [shape((2, width), F32)] * 5
            params = kernel_call(
                functools.partial(channel_kernel, planes, sides, head_size),
                norms
                + [
                    shape((tap_count + 1, team_width), F32),
                    shape((2, team_width), F32),
                    shape((2, team_width), F32),
                    shape((team, lengths.shape[1]), jnp.int32),
                ],
                plane_pieces(lanes),
                scalars=(where_at,),
                scratch=[pltpu.VMEM((width, LANES), F32)],
            )
            norms, (taps, batch_rows, bias_rows, team_lengths) = params[:5], params[5:]
        else:
            team_lengths = jnp.concatenate(chunk_order(gather(lengths)))
            chan_float = lax.all_gather(chan_low, ALL, axis=1, tiled=True).astype(F32)

            def own_hidden(rows):
                rows = rows.reshape(rows.shape[0], planes, team, -1)
                rows = lax.dynamic_index_in_dim(rows, team_at, axis=2, keepdims=False)
                return rows.reshape(rows.shape[0], team_width)

            taps = own_hidden(chan_float[: tap_count + 1])
            batch_rows = own_hidden(chan_float[tap_count + 10 : tap_count + 12])
            bias_rows = lax.dynamic_index_in_dim(
                split_heads(chan_float[tap_count + 12 : tap_count + 14]), team_at, 0, False
            )
            norms = [
                jnp.stack([chan_float[tap_count + j], chan_float[tap_count + 5 + j]])
                for j in range(5)
            ]

        columns, up_two = team_swap(columns), team_swap(up_two)
        if head_aligned:
            head_rows = sides * rows_in
            per_side = planes // sides
            depth = team * rows_in
            lines = [2 * depth + width // BLOCK * head_rows, 2 * depth]
            mix_pack, conv_pack = kernel_call(
                square_pack_kernel,
                [shape((n, BLOCK), BF16) for n in lines],
                [columns, mix, swap(mix, "y"), conv_out],
                scalars=(side,),
            )
            second = kernel_call(
                feed_pack_kernel,
                [shape((depth + down_two.shape[0], team_hidden), BF16)],
                [up_two, down_two],
            )[0]
        else:
            per_side = 0
            mix = lax.all_gather(mix, ALL, axis=0, tiled=True)
            mix = lax.dynamic_slice_in_dim(mix, team_at * team_width, team_width, axis=0)
            columns = columns.reshape(-1, 6 * team_width)
            mix_pack = to_blocks(columns[:, : 4 * team_width], BLOCK)
            conv_pack = jnp.concatenate(
                [to_blocks(columns[:, 4 * team_width :], BLOCK), to_blocks(conv_out, BLOCK)]
            )
            second = jnp.concatenate([up_two.reshape(-1, team_hidden), down_two])
        table = offset_table(slots, width).astype(BF16)

        ready = (packs_one, groups, norms, taps, team_lengths, table)
        ready, mix_pack, conv_pack, second, mix = lax.optimization_barrier(
            (ready, mix_pack, conv_pack, second, mix)
        )
        packs_one, groups, norms, taps, team_lengths, table = ready
        mix_pack = plane_gather(mix_pack)
        mix_packs = (mix_pack,) if head_aligned else (mix_pack, mix)

        def columns_of(results, i):
            return [result[i] for result in results]

        at = [0]
        for group in groups:
            at.append(at[-1] + 2 * len(group[0]))

        results = [forward_call(group, packs_one, norms[0]) for group in groups]
        saved_one = [columns_of(columns_of(results, 1), i) for i in (1, 0)]
        parts, _ = scatter(columns_of(results, 0))
        stream_one, normed = join_call(frames, parts, 0.5, norms[1])
        normed, conv_pack, second = lax.optimization_barrier((normed, conv_pack, second))
        conv_pack = plane_gather(conv_pack)
        pack_two = plane_gather(second)

        place = kernel_call(
            place_kernel,
            [shape((table.shape[0], team_width), BF16)],
            [table, mix_pack],
            flops=2 * table.shape[0] * width * team_width,
        )[0]

        def attention(i, group):
            return attention_call(
                group, team_lengths, at[i], side, mix_packs, per_side, bias_rows, place, head_size
            )

        groups, results = spread(normed, attention)
        saved_two = columns_of(results, 1)
        parts, _ = scatter(columns_of(results, 0))
        stream_two, normed = join_call(stream_one, parts, 1.0, norms[2])

        def gates(i, group):
            return gate_call(group, team_lengths, at[i], conv_pack, taps, tap_count)

        groups, saved_three = spread(normed, gates)
        stats = outer_merge(merge(columns_of(saved_three, 2)), merge)
        results = [
            batch_call(len(group[0]), saved[0], stats, batch_rows, conv_pack, slots, width)
            for group, saved in reversed(list(zip(groups, saved_three)))
        ][::-1]
        parts, _ = scatter(results)
        stream_three, normed = join_call(stream_two, parts, 1.0, norms[3])
        normed, pack_two = lax.optimization_barrier((normed, pack_two))

        groups, results = spread(normed, lambda i, group: forward_call(group, (pack_two,)))
        saved_four = [chunk_order(groups), columns_of(columns_of(results, 1), 0)]
        parts, _ = scatter(columns_of(results, 0))
        output, grad_four, low, norm_four = turn_call(
            stream_three, parts, 0.5, norms[4], out_grad, lengths
        )

        def feed_backward(low, packs, saved):
            normed, before = saved
            groups, results = spread(
                low, lambda i, group: backward_call(group, packs, before[i])
            )
            grads, active = [columns_of(columns_of(results, 1), i) for i in (0, 1)]
            term = feed_weight_call(normed, grads, active, chunk_order(groups), planes)
            return scatter(columns_of(results, 0), term)

        parts, second_term = feed_backward(low, (pack_two,), saved_four)
        grad_three, low, norm_three = join_back_call(stream_three, grad_four, parts, 1.0, norms[3])
        low, second_term = lax.optimization_barrier((low, second_term))
        second_term = plane_reduce(second_term)

        def batch_back(i, group):
            return batch_back_call(
                group, team_lengths, at[i], saved_three[i][0], stats, batch_rows, conv_pack
            )

        groups, grads = spread(low, batch_back)
        local_sums = sum_call(columns_of(grads, 2))
        sums = outer_merge(local_sums, sum_call)
        def gate_back(sums, numbers):
            return [
                gate_back_call(
                    len(groups[i][0]), team_lengths, at[i], grads[i][0], saved_three[i][0], stats,
                    sums, conv_pack, taps, tap_count, slots, width,
                )
                for i in numbers
            ]

        results = gate_back(sums, [len(groups) - 1])

        def gate_back_near(sums):
            results[:0] = gate_back(sums, range(len(groups) - 1))
            return columns_of(results, 0)

        parts, _ = scatter(columns_of(results, 0), near=(sums, gate_back_near))
        tap_terms = columns_of(columns_of(results, 1), 1)
        conv_term = conv_weight_call(
            columns_of(saved_three, 1), columns_of(columns_of(results, 1), 0), columns_of(grads, 1),
            chunk_order(groups), planes,
        )
        parts, conv_term = lax.optimization_barrier((parts, conv_term))
        grad_two, low, norm_two = join_back_call(stream_two, grad_three, parts, 1.0, norms[2])
        low, conv_term, second_term = lax.optimization_barrier((low, conv_term, second_term))
        conv_term = plane_reduce(conv_term)

        def attention_back(i, group):
            return attention_back_call(
                group, side, mix_packs, per_side, place, saved_two[i], head_size
            )

        groups, results = spread(low, attention_back)
        rows = chunk_order(groups)
        grads = columns_of(results, 1)
        bias_terms = columns_of(grads, 2)
        mix_term = mix_weight_call(
            saved_two, columns_of(grads, 0), rows, [table] + columns_of(grads, 1), side, planes,
            per_side,
        )
        parts, mix_term = scatter(columns_of(results, 0), mix_term)
        if not head_aligned:
            mixed = jnp.concatenate([saved[:, -team_width:] for saved in saved_two])
            mix_own = mm_tn(mixed, jnp.concatenate(rows)).astype(BF16)
            mix_own = lax.dynamic_update_slice_in_dim(
                jnp.zeros((width, width), BF16), mix_own, team_at * team_width, axis=0
            )
        grad_one, low, norm_one = join_back_call(stream_one, grad_two, parts, 0.5, norms[1])
        low, conv_term = lax.optimization_barrier((low, conv_term))
        mix_term = plane_reduce(mix_term)

        parts, first_term = feed_backward(low, packs_one, saved_one)
        first_term = plane_reduce(first_term)
        frames_grad, norm_zero = join_back_call(frames, grad_one, parts, 1.0, norms[0], keep=False)

        late = (second_term, conv_term, mix_term)
        frames_grad, late = lax.optimization_barrier((frames_grad, late))
        second_term, conv_term, mix_term = late
        depth = width // planes
        rate_scale = lax.rsqrt(stats[0:1])

        def from_team(rows, columns):
            return team_swap(rows.astype(BF16).reshape(team, -1, columns))

        def finish_channels(chan_term):
            chan_term = outer_merge(chan_term, sum_call).reshape(chan_rows, planes, -1)
            chan_term = lax.dynamic_index_in_dim(chan_term, lax.axis_index("z"), 1, keepdims=False)
            if not wide_team:
                chan_term = lax.dynamic_index_in_dim(
                    chan_term.reshape(chan_rows, sides, -1), y_at, 1, keepdims=False
                )
            return chan_term

        norm_terms = [norm_zero, norm_one, norm_two, norm_three, norm_four]
        if head_aligned:
            second_up = from_team(second_term[:depth], team_hidden)
            features = kernel_call(
                functools.partial(feature_grad_kernel, planes, sides),
                [shape((team, 12, team_width), F32)],
                norm_terms + bias_terms,
                scalars=(team_at.reshape(1).astype(jnp.int32),),
            )[0]
            chan_term = kernel_call(
                functools.partial(channel_grad_kernel, tap_count),
                [shape((chan_rows, team_width), F32)],
                [team_swap(features), local_sums] + tap_terms,
            )[0]
            chan_grad = finish_channels(chan_term)
            blocks = kernel_call(
                column_grad_kernel,
                [shape((team, rows_in, 6 * team_width), BF16)],
                [mix_term, conv_term],
            )[0]
            square_all = update_call(
                functools.partial(update_square_kernel, planes, sides, head_size),
                rate_scale,
                [
                    team_swap(blocks),
                    mix_term,
                    swap(mix_term[4 * team_width // BLOCK * depth :], "y"),
                    conv_term,
                ],
                square_weight,
                square_moment,
                square_average,
                scalars=(side,),
            )
            first_term, square_all, second_up = lax.optimization_barrier(
                (first_term, square_all, second_up)
            )
            down_all = update_call(
                update_down_kernel,
                rate_scale,
                [first_term, second_term],
                down_weight,
                down_moment,
                down_average,
            )
            up_all = update_call(
                update_up_kernel,
                rate_scale,
                [from_team(first_term[:depth], team_hidden), second_up],
                up_weight,
                up_moment,
                up_average,
            )
            up_grad, up_new = up_all[0], up_all[1:]
            down_grad, down_new = down_all[0], down_all[1:]
            square_grad, square_new = square_all[0], square_all[1:]
            rate_scale = rate_scale[0, 0]
        else:
            column_blocks = 4 * team_width // BLOCK
            qkv_term = from_blocks(mix_term[: column_blocks * depth], column_blocks)
            gate_blocks = 2 * team_width // BLOCK
            gate_term = from_blocks(conv_term[: gate_blocks * depth], gate_blocks)
            conv_out_term = from_blocks(conv_term[gate_blocks * depth :], width // BLOCK)
            mix_grad = lax.psum_scatter(mix_own, ALL, scatter_dimension=0, tiled=True).astype(F32)
            blocks = from_team(jnp.concatenate([qkv_term, gate_term], axis=1), 6 * team_width)

            def block(i):
                return blocks[:, :, i * team_width : (i + 1) * team_width]

            square_grad = jnp.stack(
                [side_scatter(join_heads(block(i))).astype(F32) for i in range(3)]
                + [mix_grad, side_scatter(join_heads(block(3))).astype(F32)]
                + [side_scatter(join_hidden(block(i))).astype(F32) for i in (4, 5)]
                + [side_scatter(conv_out_term).astype(F32)]
            )
            bias_rows = join_heads(
                lax.dynamic_update_slice_in_dim(
                    jnp.zeros((team, 2, team_width), F32), sum(bias_terms)[None], team_at, 0
                )
            )
            features = jnp.concatenate(
                [t[0:1] for t in norm_terms] + [t[1:2] for t in norm_terms] + [bias_rows]
            )
            features = jnp.sum(team_swap(split_hidden(features)), axis=0)
            chan_grad = finish_channels(
                jnp.concatenate(
                    [
                        sum(tap_terms)[:tap_count],
                        features[:10],
                        local_sums[:2],
                        features[10:],
                    ]
                )
            )
            feed_terms = (first_term, second_term)
            up_grad = jnp.stack(
                [
                    side_scatter(join_hidden(from_team(rows[:depth], team_hidden))).astype(F32)
                    for rows in feed_terms
                ]
            )
            down_grad = jnp.stack(
                [
                    side_scatter(from_blocks(rows[depth:], width // team_hidden)).astype(F32)
                    for rows in feed_terms
                ]
            )
            rate_scale = rate_scale[0, 0]
            up_new = nesterov(up_weight, up_moment, up_average, up_grad, RATE_UP, rate_scale)
            down_new = nesterov(
                down_weight, down_moment, down_average, down_grad, RATE_DOWN, rate_scale
            )
            square_new = nesterov(
                square_weight, square_moment, square_average, square_grad, RATE_SQUARE, rate_scale
            )
        chan_new = nesterov(
            chan_weight, chan_moment, chan_average, chan_grad, RATE_CHANNEL, rate_scale
        )
        bias_grad = chan_grad[tap_count + 12 : tap_count + 14]
        return (
            output,
            frames_grad,
            up_grad,
            down_grad,
            square_grad,
            chan_grad,
            up_new[0],
            down_new[0],
            square_new[0],
            chan_new[0],
            up_new[1],
            down_new[1],
            square_new[1],
            chan_new[1],
            up_new[2],
            down_new[2],
            square_new[2],
            chan_new[2],
            bias_grad,
        )

    return step


def solution(mesh):
    wide, narrow = mesh.shape["wide"], mesh.shape["narrow"]
    planes = wide // 4
    inner = Mesh(mesh.devices.reshape(planes, 2, 2, narrow), ALL)
    token = P(ALL, None)
    matrix = P(None, ALL, None)
    vector = P(None, ALL)
    group = (matrix, matrix, matrix, vector)
    return jax.shard_map(
        make_step(planes, narrow),
        mesh=inner,
        in_specs=(token, token, token) + group * 3,
        out_specs=(token, token) + group * 4 + (vector,),
        check_vma=False,
    )
```
